32 devices in a mesh: head: 4 (over x, core), blk: 8 (over z, y).
Axes of the slice: x: 2, y: 2, z: 4, core: 2. Of those that a mesh axis runs over, the one named last changes fastest.
Arguments:
- inputs: bfloat16 [4096, 1024], P(('head', 'blk')), may hold values from -6 to 6
- encoded: bfloat16 [4096, 1024], P(('head', 'blk')), may hold values from -6 to 6
- d_output: bfloat16 [4096, 1024], P(('head', 'blk')), may hold values from -6 to 6
- target_lengths: int32 [16], replicated, may hold values from 1 to 2048, 4096 in all
- source_lengths: int32 [16], replicated, may hold values from 1 to 2048, 4096 in all
- norm_gain: bfloat16 [3, 1024], P(None, ('head', 'blk')), may hold values from 0.5 to 1.5
- norm_shift: bfloat16 [3, 1024], P(None, ('head', 'blk')), may hold values from -1.75 to 1.75
- self_qkv: bfloat16 [1024, 3, 1024], P(('head', 'blk')), may hold values from -0.1875 to 0.1875
- self_bias: bfloat16 [2, 1024], P(None, ('head', 'blk')), may hold values from -1.75 to 1.75
- self_out: bfloat16 [1024, 1024], P(('head', 'blk')), may hold values from -1.5 to 1.5
- cross_q: bfloat16 [1024, 1024], P(('head', 'blk')), may hold values from -0.1875 to 0.1875
- cross_kv: bfloat16 [1024, 2, 1024], P(('head', 'blk')), may hold values from -0.1875 to 0.1875
- cross_bias: bfloat16 [2, 1024], P(None, ('head', 'blk')), may hold values from -1.75 to 1.75
- cross_out: bfloat16 [1024, 1024], P(('head', 'blk')), may hold values from -1.5 to 1.5
- out_bias: bfloat16 [3, 1024], P(None, ('head', 'blk')), may hold values from -1.75 to 1.75
- ffn_in: bfloat16 [1024, 4096], P(('head', 'blk')), may hold values from -0.1875 to 0.1875
- ffn_in_bias: bfloat16 [4096], P(('head', 'blk')), may hold values from -3 to 3
- ffn_out: bfloat16 [4096, 1024], P(('head', 'blk')), may hold values from -0.09375 to 0.09375
Outputs:
- layer_output: bfloat16 [4096, 1024], P(('head', 'blk'))
- d_inputs: float32 [4096, 1024], P(('head', 'blk'))
- d_encoded: float32 [4096, 1024], P(('head', 'blk'))
- grad_norm_gain: float32 [3, 1024], P(None, ('head', 'blk'))
- grad_norm_shift: float32 [3, 1024], P(None, ('head', 'blk'))
- grad_self_qkv: float32 [1024, 3, 1024], P(('head', 'blk'))
- grad_self_bias: float32 [2, 1024], P(None, ('head', 'blk'))
- grad_self_out: float32 [1024, 1024], P(('head', 'blk'))
- grad_cross_q: float32 [1024, 1024], P(('head', 'blk'))
- grad_cross_kv: float32 [1024, 2, 1024], P(('head', 'blk'))
- grad_cross_bias: float32 [2, 1024], P(None, ('head', 'blk'))
- grad_cross_out: float32 [1024, 1024], P(('head', 'blk'))
- grad_out_bias: float32 [3, 1024], P(None, ('head', 'blk'))
- grad_ffn_in: float32 [1024, 4096], P(('head', 'blk'))
- grad_ffn_in_bias: float32 [4096], P(('head', 'blk'))
- grad_ffn_out: float32 [4096, 1024], P(('head', 'blk'))
The draws below stay inside these ranges and needn't reach their ends.
Inputs may be any that keep to these rules, and one draw needn't show every extreme that they name: `target_lengths`: 16 document lengths adding up to 4096; the longest is exactly 2048; target document j is aligned with source document j. `source_lengths`: 16 document lengths adding up to 4096; the longest is exactly 2048.
All inputs are finite; a program needn't handle non-finite values.
Results may differ from the reference program's by a relative error of at most 0.023.
Values may be sent and summed in bfloat16 or wider, within the bound.
A program may use at most 192 MiB of HBM per device.

```python
import math
import jax
import jax.numpy as jnp
import numpy as np
from jax import lax

D = 1024
HEADS = 16
HEAD_DIM = 64
FF = 4096
NDOC = 16
TOKENS = 4096
DOC_MAX = 2048


def steps_of(stream_key, dims, pieces, smallest, high):
    factor_of, own = 1.0, jax.random.fold_in(stream_key, 6)
    for position, parts in pieces:
        heights = jnp.exp(jax.random.uniform(jax.random.fold_in(own, position), (parts,), jnp.float32, smallest / len(pieces), high / len(pieces)))
        factor_of = factor_of * jnp.repeat(heights, dims[position] // parts).reshape([-1 if axis == position else 1 for axis in range(len(dims))])
    return factor_of


def length_profile(amount, total, limit, skew):
    weights = [(1 << 20) // math.isqrt(standing ** skew) + 1 for standing in range(2, amount + 1)]
    rest, given = total - limit - (amount - 1), [1] * (amount - 1)
    while rest > 0:
        candidates = [i for i in range(amount - 1) if given[i] < limit]
        pool, budget = sum([weights[i] for i in candidates]), rest
        for i in candidates:
            extra = min(limit - given[i], max(1, budget * weights[i] // pool), rest)
            given[i] = given[i] + extra
            rest = rest - extra
    return np.array([limit] + given)


def uneven_parts(own_key, number_of, total, reach, slope):
    if number_of == 2:
        one = jax.random.randint(own_key, (), max(1, total - reach), min(reach, total - 1) + 1)
        return jnp.stack([one, total - one])
    tallies = jnp.asarray(length_profile(number_of, total, reach, slope), jnp.int32)
    pairs = (number_of - 1) // 2
    donor, sink = tallies[1:1 + 2 * pairs:2], tallies[2:2 + 2 * pairs:2]
    margin = jnp.minimum(donor - 1, reach - sink)
    passed = jax.random.randint(jax.random.fold_in(own_key, 1), (pairs,), 0, 1 << 20) % (margin + 1)
    tallies = tallies.at[1:1 + 2 * pairs:2].set(donor - passed).at[2:2 + 2 * pairs:2].set(sink + passed)
    return tallies[jax.random.permutation(jax.random.fold_in(own_key, 2), number_of)]


def gaussian(rng, shape, width, reach, shards=(), kind=jnp.bfloat16):
    level = steps_of(rng, shape, shards, -0.22, 0.18) if shards else 1.0
    entries = jax.random.normal(rng, shape, jnp.float32) * width * level
    return jnp.minimum(jnp.maximum(entries, -reach), reach).astype(kind)


def setup_inputs(seed: int = 0) -> dict:
    key_of = jax.random.split(jax.random.key(seed), 19)
    return {
        "inputs": gaussian(key_of[0], (TOKENS, D), 1.0, 6.0, ((0, 32),)),
        "encoded": gaussian(key_of[1], (TOKENS, D), 1.0, 6.0, ((0, 32),)),
        "d_output": gaussian(key_of[2], (TOKENS, D), 1.0, 6.0, ((0, 32),)),
        "target_lengths": uneven_parts(key_of[3], NDOC, TOKENS, DOC_MAX, 2).astype(jnp.int32),
        "source_lengths": uneven_parts(key_of[4], NDOC, TOKENS, DOC_MAX, 2).astype(jnp.int32),
        "norm_gain": jnp.clip(1.0 + 0.1 * jax.random.normal(key_of[5], (3, D), jnp.float32), 0.5, 1.5).astype(jnp.bfloat16),
        "norm_shift": gaussian(key_of[6], (3, D), 0.3, 1.75, ((1, 32),)),
        "self_qkv": gaussian(key_of[7], (D, 3, D), D ** -0.5, 0.1875, ((0, 32),)),
        "self_bias": gaussian(key_of[8], (2, D), 0.3, 1.75, ((1, 32),)),
        "self_out": gaussian(key_of[9], (D, D), (HEAD_DIM // 4) ** -0.5, 1.5, ((0, 32),)),
        "cross_q": gaussian(key_of[10], (D, D), D ** -0.5, 0.1875, ((0, 32),)),
        "cross_kv": gaussian(key_of[11], (D, 2, D), D ** -0.5, 0.1875, ((0, 32),)),
        "cross_bias": gaussian(key_of[12], (2, D), 0.3, 1.75, ((1, 32),)),
        "cross_out": gaussian(key_of[13], (D, D), (HEAD_DIM // 4) ** -0.5, 1.5, ((0, 32),)),
        "out_bias": gaussian(key_of[14], (3, D), 0.3, 1.75, ((1, 32),)),
        "ffn_in": gaussian(key_of[15], (D, FF), D ** -0.5, 0.1875, ((0, 32),)),
        "ffn_in_bias": gaussian(key_of[16], (FF,), 0.5, 3.0, ((0, 32),)),
        "ffn_out": gaussian(key_of[17], (FF, D), FF ** -0.5, 0.09375, ((0, 32),)),
    }


@jax.custom_vjp
def low(v):
    return lax.optimization_barrier(v.astype(jnp.bfloat16)).astype(jnp.float32)

@jax.custom_vjp
def low_back(v):
    return v

def low_keep(v):
    return (low(v), None)

def low_pass(kept, grad):
    return (grad,)

def back_keep(v):
    return (v, None)

def back_low(kept, grad):
    return (low(grad),)
low.defvjp(low_keep, low_pass)
low_back.defvjp(back_keep, back_low)

def rounded_both(values):
    return low_back(low(values))

def layer_norm(activity, scaling, offset):
    average = lax.optimization_barrier(jnp.mean(activity, axis=-1, keepdims=True))
    centred = activity - average
    spread = lax.optimization_barrier(jnp.mean(centred * centred, axis=-1, keepdims=True))
    return centred * lax.rsqrt(spread + 1e-05) * scaling + offset

def segment_ids(lengths, total_rows):
    doc_ends = jnp.cumsum(lengths, dtype=jnp.int32)
    positions = jnp.arange(total_rows, dtype=jnp.int32)
    return lax.optimization_barrier(jnp.sum((positions[:, None] >= doc_ends[None, :]).astype(jnp.int32), axis=1, dtype=jnp.int32))

def attend(queries, key_rows, value_rows, query_seg, key_seg, causal):
    total_rows = queries.shape[0]
    block_rows = min(512, total_rows)
    block_count = total_rows // block_rows
    key_heads = key_rows.reshape(total_rows, HEADS, HEAD_DIM)
    value_heads = value_rows.reshape(total_rows, HEADS, HEAD_DIM)
    key_pos = jnp.arange(total_rows, dtype=jnp.int32)

    def one_block(block_items):
        query_block, seg_block, first_row = block_items
        query_heads = query_block.reshape(block_rows, HEADS, HEAD_DIM)
        products = jnp.einsum('qhd,khd->hqk', query_heads, key_heads, precision=lax.Precision.HIGHEST)
        scores = low_back(products) * HEAD_DIM ** (-0.5)
        allowed = seg_block[:, None] == key_seg[None, :]
        if causal:
            query_pos = first_row + jnp.arange(block_rows, dtype=jnp.int32)
            allowed = allowed & (key_pos[None, :] <= query_pos[:, None])
        scores = jnp.where(allowed[None], scores, -1e+30)
        highest = lax.optimization_barrier(jnp.max(scores, axis=-1, keepdims=True))
        weights = jnp.exp(scores - highest)
        weights = low(weights / lax.optimization_barrier(jnp.sum(weights, axis=-1, keepdims=True)))
        mixture = jnp.einsum('hqk,khd->qhd', weights, value_heads, precision=lax.Precision.HIGHEST)
        return mixture.reshape(block_rows, HEADS * HEAD_DIM)
    starts = jnp.arange(block_count, dtype=jnp.int32) * block_rows
    outputs = lax.map(jax.checkpoint(one_block), (queries.reshape(block_count, block_rows, HEADS * HEAD_DIM), query_seg.reshape(block_count, block_rows), starts))
    return outputs.reshape(total_rows, HEADS * HEAD_DIM)

def forward(inputs, encoded, norm_gain, norm_shift, self_qkv, self_bias, self_out, cross_q, cross_kv, cross_bias, cross_out, out_bias, ffn_in, ffn_in_bias, ffn_out, target_seg, source_seg):
    precise = lax.Precision.HIGHEST
    normed = low(layer_norm(inputs, norm_gain[0], norm_shift[0]))
    joined = jnp.einsum('td,dcf->tcf', normed, self_qkv, precision=precise)
    queries = rounded_both(joined[:, 0] + self_bias[0])
    key_rows = rounded_both(joined[:, 1])
    value_rows = rounded_both(joined[:, 2] + self_bias[1])
    mixture = rounded_both(attend(queries, key_rows, value_rows, target_seg, target_seg, True))
    first_sum = inputs + low_back(jnp.dot(mixture, self_out, precision=precise) + out_bias[0])
    normed = low(layer_norm(first_sum, norm_gain[1], norm_shift[1]))
    queries = rounded_both(jnp.dot(normed, cross_q, precision=precise) + cross_bias[0])
    key_value = jnp.einsum('td,dcf->tcf', encoded, cross_kv, precision=precise)
    key_rows = rounded_both(key_value[:, 0])
    value_rows = rounded_both(key_value[:, 1] + cross_bias[1])
    mixture = rounded_both(attend(queries, key_rows, value_rows, target_seg, source_seg, False))
    second_sum = first_sum + low_back(jnp.dot(mixture, cross_out, precision=precise) + out_bias[1])
    normed = low(layer_norm(second_sum, norm_gain[2], norm_shift[2]))
    hidden = low_back(jnp.dot(normed, ffn_in, precision=precise) + ffn_in_bias)
    active = low(jax.nn.gelu(hidden, approximate=False))
    return second_sum + low_back(jnp.dot(active, ffn_out, precision=precise) + out_bias[2])

def reference(inputs, encoded, d_output, target_lengths, source_lengths, norm_gain, norm_shift, self_qkv, self_bias, self_out, cross_q, cross_kv, cross_bias, cross_out, out_bias, ffn_in, ffn_in_bias, ffn_out):
    target_seg = segment_ids(target_lengths, TOKENS)
    source_seg = segment_ids(source_lengths, TOKENS)
    floats = tuple((argument.astype(jnp.float32) for argument in (inputs, encoded, norm_gain, norm_shift, self_qkv, self_bias, self_out, cross_q, cross_kv, cross_bias, cross_out, out_bias, ffn_in, ffn_in_bias, ffn_out)))

    def apply_layer(*arrays_in):
        return forward(*arrays_in, target_seg, source_seg)
    result, pullback = jax.vjp(apply_layer, *floats)
    grads = pullback(d_output.astype(jnp.float32))
    return (result.astype(jnp.bfloat16), grads[0], grads[1], grads[2], grads[3], grads[4], grads[5], grads[6], grads[7], grads[8], grads[9], grads[10], grads[11], grads[12], grads[13], grads[14])
```

```python
from functools import partial

import jax
import jax.numpy as jnp
from jax import lax
from jax.experimental import pallas as pl
from jax.experimental.pallas import tpu as pltpu
from jax.sharding import PartitionSpec as P

HEAD_DIM = 64
HEADS_HERE = 4
KEY_BLOCK = 256
MESH = pl.DeviceIdType.MESH
ANY = pl.BlockSpec(memory_space=pl.ANY)
VMEM = pl.BlockSpec(memory_space=pltpu.VMEM)
SMEM = pl.BlockSpec(memory_space=pltpu.SMEM)
DMA = pltpu.SemaphoreType.DMA
f32 = jnp.float32
bf16 = jnp.bfloat16
NT = (((1,), (1,)), ((), ()))
NN = (((1,), (0,)), ((), ()))
TN = (((0,), (0,)), ((), ()))


def dot(a, b, dims=NN):
    return lax.dot_general(a, b, dims, preferred_element_type=f32)


def params(cid):
    return pltpu.CompilerParams(
        collective_id=cid, has_side_effects=True, vmem_limit_bytes=56 * 2**20
    )


def remote(src, dst, ssem, rsem, device):
    return pltpu.make_async_remote_copy(
        src, dst, ssem, rsem, device_id=device, device_id_type=MESH
    )


class Head:
    def __init__(self):
        self.me = lax.axis_index("head")
        self.core = self.me % 2
        self.x = self.me // 2
        self.sib = self.me + 1 - 2 * self.core
        self.far = self.me + 2 - 4 * self.x
        self.far_sib = self.sib + 2 - 4 * self.x


class Blk:
    def __init__(self, count):
        self.me = lax.axis_index("blk")
        self.z = self.me // 2
        self.y = self.me % 2
        self.Z = count // 2
        self.across = self.me + 1 - 2 * self.y


def signal(bar, **device):
    pl.semaphore_signal(bar, inc=1, device_id=device, device_id_type=MESH)


def greet_head(bar, hd):
    for k in range(1, 4):
        signal(bar, head=(hd.me + k) % 4)
    return 3


def greet_blk(bar, bk):
    signal(bar, blk=bk.across)

    @pl.when(bk.z > 0)
    def _():
        signal(bar, blk=bk.me - 2)

    @pl.when(bk.z < bk.Z - 1)
    def _():
        signal(bar, blk=bk.me + 2)

    return 1 + jnp.where(bk.z > 0, 1, 0) + jnp.where(bk.z < bk.Z - 1, 1, 0)


class BlkGather:
    def __init__(self, bk, outs, ssem, rsem):
        self.bk, self.outs, self.ssem, self.rsem = bk, outs, ssem, rsem

    def copy(self, a, slot, way, device, src=None):
        view = self.outs[a].at[:, slot]
        return remote(
            view if src is None else src,
            view,
            self.ssem.at[a, way, slot // 2],
            self.rsem.at[a, slot],
            {"blk": device},
        )

    def start(self, a, src=None):
        bk = self.bk

        @pl.when(bk.z < bk.Z - 1)
        def _():
            self.copy(a, bk.me, 0, bk.me + 2, src).start()

        @pl.when(bk.z > 0)
        def _():
            self.copy(a, bk.me, 1, bk.me - 2, src).start()

        self.copy(a, bk.me, 2, bk.across, src).start()

    def pass_on(self):
        bk = self.bk
        for k in range(1, bk.Z):
            for a in range(len(self.outs)):

                @pl.when(bk.z - k >= 0)
                def _():
                    slot = bk.me - 2 * k
                    self.copy(a, slot, 0, bk.me).wait_recv()

                    @pl.when(bk.z < bk.Z - 1)
                    def _():
                        self.copy(a, slot, 0, bk.me + 2).start()

                    self.copy(a, slot, 2, bk.across).start()

                @pl.when(bk.z + k < bk.Z)
                def _():
                    slot = bk.me + 2 * k
                    self.copy(a, slot, 0, bk.me).wait_recv()

                    @pl.when(bk.z > 0)
                    def _():
                        self.copy(a, slot, 1, bk.me - 2).start()

                    self.copy(a, slot, 2, bk.across).start()

    def finish(self):
        bk = self.bk
        for a in range(len(self.outs)):
            for s in range(bk.Z):
                self.copy(a, 2 * s + 1 - bk.y, 0, bk.me).wait_recv()
                slot = 2 * s + bk.y

                @pl.when((s <= bk.z) & (bk.z < bk.Z - 1))
                def _():
                    self.copy(a, slot, 0, bk.me).wait_send()

                @pl.when((s >= bk.z) & (bk.z > 0))
                def _():
                    self.copy(a, slot, 1, bk.me).wait_send()

                self.copy(a, slot, 2, bk.me).wait_send()


def weights_kernel(count, n_col, n_row, n_act, *refs):
    n_in = n_col + 1 + n_row + n_act
    ins, outs = refs[:n_in], refs[n_in : 2 * n_in]
    lsem, hs, hr, ssem, rsem = refs[2 * n_in :]
    hd, bk = Head(), Blk(count)
    bar = pltpu.get_barrier_semaphore()
    greeted = greet_head(bar, hd) + greet_blk(bar, bk)
    pl.semaphore_wait(bar, greeted)
    n_blk = n_col + 1 + n_row
    ring = BlkGather(bk, outs[:n_blk], ssem, rsem)

    def own(a):
        if a < n_col:
            return pltpu.make_async_copy(
                ins[a].at[hd.me], outs[a].at[hd.me, bk.me], lsem.at[a]
            )
        if a == n_col:
            return pltpu.make_async_copy(ins[a], outs[a].at[hd.me, bk.me], lsem.at[a])
        if a < n_blk:
            return pltpu.make_async_copy(ins[a], outs[a].at[:, bk.me], lsem.at[a])
        return pltpu.make_async_copy(ins[a], outs[a].at[hd.me], lsem.at[a])

    def across_head(a, k, back):
        to = (hd.me + k) % 4
        if a < n_col:
            src, dst = ins[a].at[to], outs[a].at[to if back else hd.me, bk.me]
        elif a == n_col:
            src, dst = ins[a], outs[a].at[to if back else hd.me, bk.me]
        else:
            src, dst = ins[a], outs[a].at[to if back else hd.me]
        return remote(
            src, dst, hs.at[a, k], hr.at[a, to if back else hd.me], {"head": to}
        )

    headed = list(range(n_col + 1)) + list(range(n_blk, n_in))
    for a in headed:
        for k in range(1, 4):
            across_head(a, k, False).start()
    for a in range(n_in):
        own(a).start()
    for a in range(n_col + 1, n_blk):
        ring.start(a, ins[a])
    for a in range(n_col + 1):
        own(a).wait()
        for k in range(1, 4):
            across_head(a, k, True).wait_recv()
        ring.start(a)
    ring.pass_on()
    ring.finish()
    for a in range(n_blk, n_in):
        for k in range(1, 4):
            across_head(a, k, True).wait_recv()
    for a in range(n_col + 1, n_in):
        own(a).wait()
    for a in headed:
        for k in range(1, 4):
            across_head(a, k, False).wait_send()


def gather_weights(cols, small, rows, acts, count, cid):
    n_in = len(cols) + 1 + len(rows) + len(acts)
    n_blk = n_in - len(acts)
    shapes = (
        [(4, count) + a.shape[1:] for a in cols]
        + [(4, count) + small.shape]
        + [(1, count) + a.shape[1:] for a in rows]
        + [(4,) + a.shape for a in acts]
    )
    ops = list(cols) + [small] + list(rows) + list(acts)
    outs = pl.pallas_call(
        partial(weights_kernel, count, len(cols), len(rows), len(acts)),
        out_shape=[jax.ShapeDtypeStruct(s, a.dtype) for s, a in zip(shapes, ops)],
        in_specs=[ANY] * n_in,
        out_specs=[ANY] * n_in,
        scratch_shapes=[
            DMA((n_in,)),
            DMA((n_in, 4)),
            DMA((n_in, 4)),
            DMA((n_blk, 3, count // 2)),
            DMA((n_blk, count)),
        ],
        compiler_params=params(cid),
        name="gather_weights",
    )(*ops)
    a, b, c = len(cols), len(cols) + 1 + len(rows), n_in
    return outs[:a], outs[a], outs[a + 1 : b], outs[b:c]


def gather_blk_kernel(count, n, *refs):
    ins, outs = refs[:n], refs[n : 2 * n]
    lsem, ssem, rsem = refs[2 * n :]
    bk = Blk(count)
    bar = pltpu.get_barrier_semaphore()
    pl.semaphore_wait(bar, greet_blk(bar, bk))
    ring = BlkGather(bk, outs, ssem, rsem)
    for a in range(n):
        ring.start(a, ins[a])
    for a in range(n):
        pltpu.make_async_copy(ins[a], outs[a].at[:, bk.me], lsem.at[a]).start()
    ring.pass_on()
    ring.finish()
    for a in range(n):
        pltpu.make_async_copy(ins[a], outs[a].at[:, bk.me], lsem.at[a]).wait()


def gather_blk(items, count, cid):
    n = len(items)
    return pl.pallas_call(
        partial(gather_blk_kernel, count, n),
        out_shape=[
            jax.ShapeDtypeStruct((a.shape[0], count) + a.shape[1:], a.dtype) for a in items
        ],
        in_specs=[ANY] * n,
        out_specs=[ANY] * n,
        scratch_shapes=[DMA((n,)), DMA((n, 3, count // 2)), DMA((n, count))],
        compiler_params=params(cid),
        name="gather_blk",
    )(*items)


class BlkScatter:
    def __init__(self, bk, ins, bufs, sems):
        self.bk, self.ins = bk, ins
        self.own, self.over, self.side = bufs
        self.lsem, self.ys, self.yr, self.zs, self.ur, self.dr = sems

    def load(self, a, s):
        return pltpu.make_async_copy(
            self.ins[a].at[:, 2 * s + self.bk.y], self.own[a].at[s], self.lsem.at[a, s]
        )

    def cross(self, a, s):
        return remote(
            self.ins[a].at[:, 2 * s + 1 - self.bk.y],
            self.over[a].at[s],
            self.ys.at[a, s],
            self.yr.at[a, s],
            {"blk": self.bk.across},
        )

    def send(self, a, s, upward, slot=None):
        if slot is None:
            slot = s if upward else jnp.where(s == self.bk.z - 1, self.bk.Z, s)
        return remote(
            self.own[a].at[s],
            self.side[a].at[slot],
            self.zs.at[a, s],
            (self.ur if upward else self.dr).at[a, s],
            {"blk": self.bk.me + (2 if upward else -2)},
        )

    def order(self):
        for k in range((self.bk.Z + 1) // 2):
            yield self.bk.Z - 1 - k
            if k != self.bk.Z - 1 - k:
                yield k

    def begin(self):
        for s in self.order():
            for a in range(len(self.ins)):
                self.cross(a, s).start()
                self.load(a, s).start()

    def add(self, a, s, extra, store):
        groups, rows = self.own[a].shape[1:3]
        step = min(rows, 32)

        def one(g, carry):
            for r in range(0, rows, step):
                part = pl.ds(r, step)
                total = self.own[a][s, g, part].astype(f32) + self.over[a][s, g, part].astype(f32)
                for slot in extra:
                    total = total + self.side[a][slot, g, part].astype(f32)
                store(g, part, total)
            return carry

        lax.fori_loop(0, groups, one, 0)

    def relay(self, a, s, upward):
        bk = self.bk
        self.load(a, s).wait()
        self.cross(a, s).wait_recv()
        inner = (bk.z > 0) if upward else (bk.z < bk.Z - 1)

        def store(g, part, total):
            self.own[a][s, g, part] = total.astype(bf16)

        @pl.when(inner)
        def _():
            self.send(a, s, upward, s).wait_recv()
            self.add(a, s, (s,), store)

        @pl.when(jnp.logical_not(inner))
        def _():
            self.add(a, s, (), store)

        self.send(a, s, upward).start()

    def run(self):
        bk = self.bk
        for k in range(bk.Z - 1):
            for a in range(len(self.ins)):

                @pl.when(bk.Z - 1 - k > bk.z)
                def _():
                    self.relay(a, bk.Z - 1 - k, True)

                @pl.when(k < bk.z)
                def _():
                    self.relay(a, k, False)

    def last(self, a, store):
        bk, s = self.bk, self.bk.z
        self.load(a, s).wait()
        self.cross(a, s).wait_recv()

        @pl.when(bk.z > 0)
        def _():
            self.send(a, s, True, s).wait_recv()

        @pl.when(bk.z < bk.Z - 1)
        def _():
            self.send(a, s, False, bk.Z).wait_recv()

        @pl.when((bk.z > 0) & (bk.z < bk.Z - 1))
        def _():
            self.add(a, s, (s, bk.Z), store)

        @pl.when((bk.z > 0) & (bk.z == bk.Z - 1))
        def _():
            self.add(a, s, (s,), store)

        @pl.when((bk.z == 0) & (bk.z < bk.Z - 1))
        def _():
            self.add(a, s, (bk.Z,), store)

    def finish(self):
        bk = self.bk
        for a in range(len(self.ins)):
            for s in range(bk.Z):
                self.cross(a, s).wait_send()

                @pl.when(s != bk.z)
                def _():
                    self.send(a, s, True, s).wait_send()


def scatter_scratch(items, count):
    Z = count // 2
    kinds = [
        pltpu.VMEM((slots, a.shape[0]) + a.shape[2:], bf16)
        for slots in (Z, Z, Z + 1)
        for a in items
    ]
    return kinds + [DMA((len(items), Z)) for _ in range(6)]


def scatter_parts(refs, n):
    bufs = tuple(refs[k * n : (k + 1) * n] for k in range(3))
    return bufs, refs[3 * n : 3 * n + 6], refs[3 * n + 6 :]


def scatter_blk_kernel(count, n, *refs):
    ins, outs = refs[:n], refs[n : 2 * n]
    bufs, sems, _ = scatter_parts(refs[2 * n :], n)
    bk = Blk(count)
    bar = pltpu.get_barrier_semaphore()
    pl.semaphore_wait(bar, greet_blk(bar, bk))
    ring = BlkScatter(bk, ins, bufs, sems)
    ring.begin()
    ring.run()
    for a in range(n):

        def store(g, part, total, a=a):
            outs[a][g, part] = total.astype(outs[a].dtype)

        ring.last(a, store)
    ring.finish()


def scatter_blk(items, count, cid):
    n = len(items)
    return pl.pallas_call(
        partial(scatter_blk_kernel, count, n),
        out_shape=[
            jax.ShapeDtypeStruct((a.shape[0],) + a.shape[2:], a.dtype) for a in items
        ],
        in_specs=[ANY] * n,
        out_specs=[VMEM] * n,
        scratch_shapes=scatter_scratch(items, count),
        compiler_params=params(cid),
        name="scatter_blk",
    )(*items)


def grads_kernel(count, n_col, n_row, *refs):
    n = n_col + n_row
    ins, small_in = refs[:n], refs[n]
    outs, small_out = refs[n + 1 : 2 * n + 1], refs[2 * n + 1]
    bufs, sems, rest = scatter_parts(refs[2 * n + 2 :], n)
    done = rest[:n_col]
    hs, hr, ls, ss, sr = rest[n_col:]
    hd, bk = Head(), Blk(count)
    devices = 4 * count
    me = hd.me * count + bk.me
    bar = pltpu.get_barrier_semaphore()

    def place(k):
        to = (me + k) % devices
        return to, {"head": to // count, "blk": to % count}

    def greet(k, carry):
        signal(bar, **place(k)[1])
        return carry

    lax.fori_loop(1, devices, greet, 0)
    pl.semaphore_wait(bar, devices - 1)
    ring = BlkScatter(bk, ins, bufs, sems)
    ring.begin()
    mine = pltpu.make_async_copy(small_in.at[me], small_out.at[me], ls)
    mine.start()

    def small(k, back):
        to, device = place(k)
        return remote(
            small_in.at[to],
            small_out.at[to if back else me],
            ss.at[k],
            sr.at[to if back else me],
            device,
        )

    def start_small(k, carry):
        small(k, False).start()
        return carry

    lax.fori_loop(1, devices, start_small, 0)
    ring.run()

    def across_head(a, k, back):
        to = (hd.me + k) % 4
        return remote(
            done[a].at[to],
            outs[a].at[to if back else hd.me],
            hs.at[a, k],
            hr.at[a, to if back else hd.me],
            {"head": to},
        )

    for a in range(n_col):

        def store(g, part, total, a=a):
            done[a][g, part] = total.astype(bf16)

        ring.last(a, store)
        for k in range(1, 4):
            across_head(a, k, False).start()
        outs[a][hd.me] = done[a][hd.me]
    for a in range(n_col, n):

        def store(g, part, total, a=a):
            outs[a][g, part] = total

        ring.last(a, store)
    ring.finish()
    for a in range(n_col):
        for k in range(1, 4):
            across_head(a, k, False).wait_send()
            across_head(a, k, True).wait_recv()
    mine.wait()

    def end_small(k, carry):
        small(k, False).wait_send()
        small(k, True).wait_recv()
        return carry

    lax.fori_loop(1, devices, end_small, 0)


def scatter_grads(cols, rows, small, count, cid):
    items = list(cols) + list(rows)
    devices = 4 * count
    outs = pl.pallas_call(
        partial(grads_kernel, count, len(cols), len(rows)),
        out_shape=[jax.ShapeDtypeStruct((4,) + a.shape[2:], bf16) for a in cols]
        + [jax.ShapeDtypeStruct((1,) + a.shape[2:], f32) for a in rows]
        + [jax.ShapeDtypeStruct(small.shape, f32)],
        in_specs=[ANY] * len(items) + [VMEM],
        out_specs=[VMEM] * len(items) + [VMEM],
        scratch_shapes=scatter_scratch(items, count)
        + [pltpu.VMEM((4,) + a.shape[2:], bf16) for a in cols]
        + [
            DMA((len(cols), 4)),
            DMA((len(cols), 4)),
            DMA,
            DMA((devices,)),
            DMA((devices,)),
        ],
        compiler_params=params(cid),
        name="scatter_grads",
    )(*items, small)
    return outs[: len(cols)], outs[len(cols) : -1], outs[-1]


class HeadSum:
    def __init__(self, hd, part, near, mid, far, sems):
        self.hd, self.part, self.near, self.mid, self.far = hd, part, near, mid, far
        self.ss, self.rs = sems

    def near_copy(self, i):
        hd = self.hd
        block = hd.far_sib if i == 0 else hd.sib
        return remote(
            self.part.at[block], self.near.at[i], self.ss.at[i], self.rs.at[i], {"head": hd.sib}
        )

    def far_copy(self):
        return remote(self.mid, self.far, self.ss.at[2], self.rs.at[2], {"head": self.hd.far})

    def begin(self):
        self.near_copy(0).start()
        self.near_copy(1).start()

    def middle(self):
        self.near_copy(0).wait_recv()
        mine = self.part[self.hd.far].astype(f32)
        self.mid[...] = (mine + self.near[0].astype(f32)).astype(bf16)
        self.far_copy().start()

    def total(self):
        self.near_copy(1).wait_recv()
        mine = self.part[self.hd.me].astype(f32) + self.near[1].astype(f32)
        self.far_copy().wait_recv()
        return mine + self.far[...].astype(f32)

    def finish(self):
        self.near_copy(0).wait_send()
        self.near_copy(1).wait_send()
        self.far_copy().wait_send()


def head_sum_scratch(rows, width):
    return [
        pltpu.VMEM((2, rows, width), bf16),
        pltpu.VMEM((rows, width), bf16),
        pltpu.VMEM((rows, width), bf16),
        DMA((3,)),
        DMA((3,)),
    ]


class HeadGather:
    def __init__(self, hd, out, ss, rs):
        self.hd, self.out, self.ss, self.rs = hd, out, ss, rs

    def copy(self, slot, way, device):
        view = self.out.at[slot]
        return remote(view, view, self.ss.at[way], self.rs.at[slot], {"head": device})

    def run(self):
        hd = self.hd
        self.copy(hd.me, 0, hd.far).start()
        self.copy(hd.me, 1, hd.sib).start()
        self.copy(hd.far, 0, hd.me).wait_recv()
        self.copy(hd.far, 2, hd.sib).start()

    def finish(self):
        hd = self.hd
        self.copy(hd.sib, 0, hd.me).wait_recv()
        self.copy(hd.far_sib, 0, hd.me).wait_recv()
        self.copy(hd.me, 0, hd.far).wait_send()
        self.copy(hd.me, 1, hd.sib).wait_send()
        self.copy(hd.far, 2, hd.sib).wait_send()


def row_stats(v):
    average = jnp.mean(v, axis=-1, keepdims=True)
    centred = v - average
    spread = jnp.mean(centred * centred, axis=-1, keepdims=True)
    return centred, lax.rsqrt(spread + 1e-05)


def layer_norm(v, gain, shift):
    centred, r = row_stats(v)
    return centred * r * gain + shift


def layer_norm_back(v, g, gain):
    centred, r = row_stats(v)
    u = centred * r
    c = g * gain
    dv = r * (c - jnp.mean(c, axis=-1, keepdims=True) - u * jnp.mean(c * u, axis=-1, keepdims=True))
    return dv, jnp.sum(g * u, axis=0, keepdims=True), jnp.sum(g, axis=0, keepdims=True)


def forward_kernel(part, base, vecs, total, normed, near, mid, far, ss, rs, gs, gr):
    hd = Head()
    bar = pltpu.get_barrier_semaphore()
    pl.semaphore_wait(bar, greet_head(bar, hd))
    summed = HeadSum(hd, part, near, mid, far, (ss, rs))
    summed.begin()
    summed.middle()
    v = base[...].astype(f32) + summed.total() + vecs[0:1]
    total[...] = v
    normed[hd.me] = layer_norm(v, vecs[1:2], vecs[2:3]).astype(bf16)
    spread = HeadGather(hd, normed, gs, gr)
    spread.run()
    spread.finish()
    summed.finish()


def join_forward(part, base, bias, gain, shift, cid):
    rows, width = base.shape
    vecs = jnp.stack((bias, gain, shift))
    return pl.pallas_call(
        forward_kernel,
        out_shape=(
            jax.ShapeDtypeStruct((rows, width), f32),
            jax.ShapeDtypeStruct((4, rows, width), bf16),
        ),
        in_specs=[VMEM] * 3,
        out_specs=(VMEM, VMEM),
        scratch_shapes=head_sum_scratch(rows, width) + [DMA((3,)), DMA((4,))],
        compiler_params=params(cid),
        name="join_forward",
    )(part, base, vecs)


def backward_kernel(
    out_term, gathers, part, extra, onward, v, vecs, back, other, grad_all, stats, *scratch
):
    hd = Head()
    bar = pltpu.get_barrier_semaphore()
    pl.semaphore_wait(bar, greet_head(bar, hd))
    summed = HeadSum(hd, part, *scratch[:3], scratch[3:5])
    scratch = scratch[5:]
    second = None
    if extra is not None:
        second = HeadSum(hd, extra, *scratch[:3], scratch[3:5])
        scratch = scratch[5:]
    summed.begin()
    summed.middle()
    if second is not None:
        second.begin()
        second.middle()
    dv, d_gain, d_shift = layer_norm_back(v[...], summed.total(), vecs[0:1])
    d = dv + onward[...].astype(f32)
    back[...] = d
    rounded = d.astype(bf16)
    if gathers:
        grad_all[hd.me] = rounded
        spread = HeadGather(hd, grad_all, *scratch)
        spread.run()
    if second is not None:
        more = second.total()
        if out_term:
            more = v[...] + more + vecs[1:2]
        other[...] = more.astype(other.dtype)
    stats[0:1] = d_gain
    stats[1:2] = d_shift
    stats[2:3] = jnp.sum(rounded.astype(f32), axis=0, keepdims=True)
    if gathers:
        spread.finish()
    summed.finish()
    if second is not None:
        second.finish()


def join_backward(part, onward, v, gain, cid, extra=None, bias=None, gathers=True):
    rows, width = onward.shape
    has_extra = extra is not None
    out_term = bias is not None
    vecs = jnp.stack((gain, bias if out_term else gain))

    def kernel(*refs):
        refs = list(refs)
        part_ref = refs.pop(0)
        extra_ref = refs.pop(0) if has_extra else None
        onward_ref, v_ref, vecs_ref, back = (refs.pop(0) for _ in range(4))
        other = refs.pop(0) if has_extra else None
        grad_all = refs.pop(0) if gathers else None
        stats = refs.pop(0)
        backward_kernel(
            out_term, gathers, part_ref, extra_ref, onward_ref, v_ref, vecs_ref,
            back, other, grad_all, stats, *refs,
        )

    shapes = [jax.ShapeDtypeStruct((rows, width), f32)]
    if has_extra:
        shapes.append(jax.ShapeDtypeStruct((rows, width), bf16 if out_term else f32))
    if gathers:
        shapes.append(jax.ShapeDtypeStruct((4, rows, width), bf16))
    shapes.append(jax.ShapeDtypeStruct((8, width), f32))
    scratch = head_sum_scratch(rows, width)
    if has_extra:
        scratch = scratch + head_sum_scratch(rows, width)
    if gathers:
        scratch = scratch + [DMA((3,)), DMA((4,))]
    ops = [part] + ([extra] if has_extra else []) + [onward, v, vecs]
    return pl.pallas_call(
        kernel,
        out_shape=shapes,
        in_specs=[VMEM] * len(ops),
        out_specs=[VMEM] * len(shapes),
        scratch_shapes=scratch,
        compiler_params=params(cid),
        name="join_backward",
    )(*ops)


def stack_heads(rows, scale):
    lane = lax.broadcasted_iota(jnp.int32, rows.shape, 1) // HEAD_DIM
    pieces = [
        jnp.where(lane == h, rows.astype(f32) * scale, 0.0).astype(bf16) for h in range(HEADS_HERE)
    ]
    return jnp.concatenate(pieces, axis=0)


def take_heads(wide, rows):
    pieces = [
        wide[h * HEAD_DIM : (h + 1) * HEAD_DIM, h * rows : (h + 1) * rows]
        for h in range(HEADS_HERE)
    ]
    return jnp.concatenate(pieces, axis=0).T


def masked_scores(keys, stacked, first, low, high):
    scores = dot(keys, stacked, NT)
    key_pos = first + lax.broadcasted_iota(jnp.int32, scores.shape, 0)
    return jnp.where((key_pos >= low) & (key_pos < high), scores, -1e30)


def attend_kernel(bounds, q, k, v, low, high, o, mix, lse, acc):
    chunks, rows, width = q.shape

    def chunk(i, carry):
        stacked = stack_heads(q[i], HEAD_DIM ** (-0.5))
        lo, hi = low[i], high[i]
        acc[...] = jnp.zeros_like(acc)

        def step(kb, state):
            top, total = state
            first = pl.multiple_of(kb * KEY_BLOCK, KEY_BLOCK)
            scores = masked_scores(k[pl.ds(first, KEY_BLOCK), :], stacked, first, lo, hi)
            new_top = jnp.maximum(top, jnp.max(scores, axis=0, keepdims=True))
            fading = jnp.exp(top - new_top)
            weights = jnp.exp(scores - new_top)
            total = total * fading + jnp.sum(weights, axis=0, keepdims=True)
            acc[...] = acc[...] * fading + dot(
                v[pl.ds(first, KEY_BLOCK), :], weights.astype(bf16), TN
            )
            return new_top, total

        wide = HEADS_HERE * rows
        top, total = lax.fori_loop(
            bounds[0, i],
            bounds[1, i],
            step,
            (jnp.full((1, wide), -1e30, f32), jnp.zeros((1, wide), f32)),
        )
        lse[i] = top + jnp.log(total)
        result = take_heads(acc[...] / total, rows)
        o[i] = result
        mix[i] = result.astype(bf16)
        return carry

    lax.fori_loop(0, chunks, chunk, 0)


def attend(q, k, v, spans):
    bounds, low, high = spans
    chunks, rows, width = q.shape
    wide = HEADS_HERE * rows
    return pl.pallas_call(
        attend_kernel,
        out_shape=(
            jax.ShapeDtypeStruct(q.shape, f32),
            jax.ShapeDtypeStruct(q.shape, bf16),
            jax.ShapeDtypeStruct((chunks, 1, wide), f32),
        ),
        in_specs=[SMEM] + [VMEM] * 5,
        out_specs=(VMEM,) * 3,
        scratch_shapes=[pltpu.VMEM((width, wide), f32)],
        compiler_params=pltpu.CompilerParams(vmem_limit_bytes=56 * 2**20),
        name="attend",
    )(bounds, q, k, v, low, high)


def attend_back_kernel(
    bounds, q, k, v, low, high, d_o, o, lse, dq, dk, dv, qs, dos, delta, dq_acc, dk_acc, dv_acc
):
    chunks, rows, width = q.shape
    for i in range(chunks):
        qs[i] = stack_heads(q[i], HEAD_DIM ** (-0.5))
        dos[i] = stack_heads(d_o[i], 1.0)
        product = (d_o[i].astype(f32) * o[i]).T
        delta[i] = jnp.concatenate(
            [
                jnp.sum(product[h * HEAD_DIM : (h + 1) * HEAD_DIM], axis=0, keepdims=True)
                for h in range(HEADS_HERE)
            ],
            axis=1,
        )
    dq_acc[...] = jnp.zeros_like(dq_acc)

    def block(kb, carry):
        first = pl.multiple_of(kb * KEY_BLOCK, KEY_BLOCK)
        part = pl.ds(first, KEY_BLOCK)
        dk_acc[...] = jnp.zeros_like(dk_acc)
        dv_acc[...] = jnp.zeros_like(dv_acc)

        def chunk(i, inner):
            @pl.when((kb >= bounds[0, i]) & (kb < bounds[1, i]))
            def _():
                keys = k[part, :]
                scores = masked_scores(keys, qs[i], first, low[i], high[i])
                weights = jnp.exp(scores - lse[i])
                d_weights = dot(v[part, :], dos[i], NT)
                d_scores = (weights * (d_weights - delta[i])).astype(bf16)
                dv_acc[...] += dot(weights.astype(bf16), dos[i])
                dk_acc[...] += dot(d_scores, qs[i])
                dq_acc[i] += dot(keys, d_scores, TN)

            return inner

        lax.fori_loop(0, chunks, chunk, 0)
        dk[part, :] = dk_acc[...].astype(bf16)
        dv[part, :] = dv_acc[...].astype(bf16)
        return carry

    lax.fori_loop(0, k.shape[0] // KEY_BLOCK, block, 0)
    for i in range(chunks):
        dq[i] = (take_heads(dq_acc[i], rows) * HEAD_DIM ** (-0.5)).astype(bf16)


def attend_back(q, k, v, spans, d_o, o, lse):
    bounds, low, high = spans
    chunks, rows, width = q.shape
    wide = HEADS_HERE * rows
    return pl.pallas_call(
        attend_back_kernel,
        out_shape=(
            jax.ShapeDtypeStruct(q.shape, bf16),
            jax.ShapeDtypeStruct(k.shape, bf16),
            jax.ShapeDtypeStruct(k.shape, bf16),
        ),
        in_specs=[SMEM] + [VMEM] * 8,
        out_specs=(VMEM,) * 3,
        scratch_shapes=[
            pltpu.VMEM((chunks, wide, width), bf16),
            pltpu.VMEM((chunks, wide, width), bf16),
            pltpu.VMEM((chunks, 1, wide), f32),
            pltpu.VMEM((chunks, width, wide), f32),
            pltpu.VMEM((KEY_BLOCK, width), f32),
            pltpu.VMEM((KEY_BLOCK, width), f32),
        ],
        compiler_params=pltpu.CompilerParams(vmem_limit_bytes=60 * 2**20),
        name="attend_back",
    )(bounds, q, k, v, low, high, d_o, o, lse)


def key_spans(target_lengths, source_lengths, rows, count):
    ends = jnp.cumsum(target_lengths, dtype=jnp.int32)
    starts = ends - target_lengths
    chunk = jnp.arange(4, dtype=jnp.int32) * count + lax.axis_index("blk")
    pos = chunk[:, None] * rows + jnp.arange(rows, dtype=jnp.int32)[None, :]
    past = (pos[..., None] >= ends).astype(jnp.int32)
    begun = (pos[..., None] >= starts).astype(jnp.int32)

    def spans(low, high):
        bounds = jnp.stack(
            (low[:, 0] // KEY_BLOCK, (high[:, -1] + KEY_BLOCK - 1) // KEY_BLOCK)
        ).astype(jnp.int32)
        wide = lambda a: jnp.tile(a[:, None, :], (1, 1, HEADS_HERE))
        return bounds, wide(low), wide(high)

    own = spans(jnp.sum(past * target_lengths, axis=-1), pos + 1)
    aligned = spans(
        jnp.sum(past * source_lengths, axis=-1), jnp.sum(begun * source_lengths, axis=-1)
    )
    return own, aligned


def body(
    count,
    inputs,
    encoded,
    d_output,
    target_lengths,
    source_lengths,
    norm_gain,
    norm_shift,
    self_qkv,
    self_bias,
    self_out,
    cross_q,
    cross_kv,
    cross_bias,
    cross_out,
    out_bias,
    ffn_in,
    ffn_in_bias,
    ffn_out,
):
    rows, width = inputs.shape
    devices = 4 * count
    share = width // devices
    head_width = width // 4
    hidden_width = ffn_in.shape[1]
    hidden_here = hidden_width // 4
    hidden_rows = hidden_width // width
    tokens_here = 4 * rows

    def split_cols(w):
        return jnp.transpose(w.reshape(share, -1, 4, w.shape[-1] // 4), (2, 0, 1, 3)).reshape(
            4, share, -1
        )

    small = jnp.concatenate(
        (
            norm_gain,
            norm_shift,
            self_bias,
            cross_bias,
            out_bias,
            ffn_in_bias.reshape(hidden_rows, share),
        )
    )
    n_small = small.shape[0]
    small = jnp.pad(small.reshape(-1), (0, 1024 - n_small * share)).reshape(8, 128)
    cols, small, row_weights, acts = gather_weights(
        [split_cols(w) for w in (self_qkv, cross_q, cross_kv, ffn_in)],
        small,
        [w[None] for w in (self_out, cross_out, ffn_out)],
        [inputs, encoded, d_output],
        count,
        0,
    )
    w_qkv, w_cross_q, w_cross_kv, w_ffn_in = (w.reshape(width, -1) for w in cols)
    w_self_out, w_cross_out = (w.reshape(head_width, width) for w in row_weights[:2])
    w_ffn_out = row_weights[2].reshape(hidden_here, width)
    inputs_all, encoded_all, d_output_all = (a.reshape(tokens_here, width) for a in acts)
    small = small.reshape(devices, 1024)[:, : n_small * share].reshape(devices, n_small, share)
    small = small.astype(f32)
    vectors = jnp.transpose(small[:, :13], (1, 0, 2)).reshape(13, width)
    gains, shifts, b_out = vectors[0:3], vectors[3:6], vectors[10:13]
    head = lax.axis_index("head")
    here = lax.dynamic_slice_in_dim(vectors[6:10], head * head_width, head_width, axis=1)
    b_hidden = lax.dynamic_slice_in_dim(
        small[:, 13:].reshape(1, hidden_width), head * hidden_here, hidden_here, axis=1
    )

    own, aligned = key_spans(target_lengths, source_lengths, rows, count)

    def chunks(a):
        return a.reshape(4, rows, a.shape[-1])

    normed_one = layer_norm(inputs_all.astype(f32), gains[0:1], shifts[0:1]).astype(bf16)
    joined = dot(normed_one, w_qkv)
    q1 = (joined[:, :head_width] + here[0:1]).astype(bf16)
    k1 = joined[:, head_width : 2 * head_width].astype(bf16)
    v1 = (joined[:, 2 * head_width :] + here[1:2]).astype(bf16)
    pair = dot(encoded_all, w_cross_kv)
    k2 = pair[:, :head_width].astype(bf16)
    v2 = (pair[:, head_width:] + here[3:4]).astype(bf16)
    k1, v1, k2, v2 = (
        a.reshape(-1, head_width)
        for a in gather_blk([chunks(k1), chunks(v1), chunks(k2), chunks(v2)], count, 1)
    )
    q1 = chunks(q1)
    o1, mix1, lse1 = attend(q1, k1, v1, own)
    mix1 = mix1.reshape(tokens_here, head_width)
    first, normed_two = join_forward(
        chunks(dot(mix1, w_self_out).astype(bf16)), inputs, b_out[0], gains[1], shifts[1], 2
    )
    normed_two = normed_two.reshape(tokens_here, width)
    q2 = chunks((dot(normed_two, w_cross_q) + here[2:3]).astype(bf16))
    o2, mix2, lse2 = attend(q2, k2, v2, aligned)
    mix2 = mix2.reshape(tokens_here, head_width)
    second, normed_three = join_forward(
        chunks(dot(mix2, w_cross_out).astype(bf16)), first, b_out[1], gains[2], shifts[2], 3
    )
    normed_three = normed_three.reshape(tokens_here, width)

    hidden = dot(normed_three, w_ffn_in) + b_hidden
    active, gelu_back = jax.vjp(partial(jax.nn.gelu, approximate=False), hidden)
    active = active.astype(bf16)
    out_part = dot(active, w_ffn_out).astype(bf16)
    grad_ffn_out = dot(active, d_output_all, TN)
    d_active = dot(d_output_all, w_ffn_out, NT)
    d_hidden = gelu_back(d_active)[0].astype(bf16)
    grad_ffn_in = dot(normed_three, d_hidden, TN)
    d_part = dot(d_hidden, w_ffn_in, NT).astype(bf16)
    d_second, layer_output, d_cross, stats_three = join_backward(
        chunks(d_part), d_output, second, gains[2], 4, extra=chunks(out_part), bias=b_out[2]
    )
    d_cross = d_cross.reshape(tokens_here, width)

    grad_cross_out = dot(mix2, d_cross, TN)
    d_o2 = chunks(dot(d_cross, w_cross_out, NT).astype(bf16))
    dq2, dk2, dv2 = attend_back(q2, k2, v2, aligned, d_o2, o2, lse2)
    dq2 = dq2.reshape(tokens_here, head_width)
    grad_cross_q = dot(normed_two, dq2, TN)
    d_first, d_self, stats_two = join_backward(
        chunks(dot(dq2, w_cross_q, NT).astype(bf16)), d_second, first, gains[1], 5
    )
    d_self = d_self.reshape(tokens_here, width)

    grad_self_out = dot(mix1, d_self, TN)
    d_o1 = chunks(dot(d_self, w_self_out, NT).astype(bf16))
    dq1, dk1, dv1 = attend_back(q1, k1, v1, own, d_o1, o1, lse1)
    dq1 = dq1.reshape(tokens_here, head_width)
    dk1, dv1, dk2, dv2 = (
        a.reshape(tokens_here, head_width)
        for a in scatter_blk(
            [a.reshape(4, count, rows, head_width) for a in (dk1, dv1, dk2, dv2)], count, 6
        )
    )
    d_joined = jnp.concatenate((dq1, dk1, dv1), axis=1)
    d_pair = jnp.concatenate((dk2, dv2), axis=1)
    d_inputs, d_encoded, stats_one = join_backward(
        chunks(dot(d_joined, w_qkv, NT).astype(bf16)),
        d_first,
        inputs.astype(f32),
        gains[0],
        7,
        extra=chunks(dot(d_pair, w_cross_kv, NT).astype(bf16)),
        gathers=False,
    )
    grad_qkv = dot(normed_one, d_joined, TN)
    grad_cross_kv = dot(encoded_all, d_pair, TN)

    def column_sum(gradient):
        return jnp.sum(gradient.astype(f32), axis=0, keepdims=True)

    def placed(part):
        whole = jnp.zeros((part.shape[0], 4 * part.shape[1]), f32)
        return lax.dynamic_update_slice_in_dim(whole, part, head * part.shape[1], axis=1)

    sums = placed(
        jnp.concatenate((column_sum(dq1), column_sum(dv1), column_sum(dq2), column_sum(dv2)))
    )
    table = jnp.concatenate(
        (
            stats_one[0:1],
            stats_two[0:1],
            stats_three[0:1],
            stats_one[1:2],
            stats_two[1:2],
            stats_three[1:2],
            sums,
            stats_two[2:3],
            stats_three[2:3],
            column_sum(d_output),
        )
    )
    table = jnp.transpose(table.reshape(13, devices, share), (1, 0, 2)).reshape(devices, -1)
    table = jnp.concatenate(
        (table, placed(column_sum(d_hidden)).reshape(devices, hidden_rows * share)), axis=1
    )
    table = jnp.pad(table, ((0, 0), (0, 1024 - n_small * share))).reshape(devices, 8, 128)

    col_grads, row_grads, table = scatter_grads(
        [
            g.astype(bf16).reshape(4, count, share, -1)
            for g in (grad_qkv, grad_cross_q, grad_cross_kv, grad_ffn_in)
        ],
        [
            g.astype(bf16).reshape(1, count, -1, width)
            for g in (grad_self_out, grad_cross_out, grad_ffn_out)
        ],
        table,
        count,
        8,
    )

    def join_cols(g, shape):
        parts = shape[1] if len(shape) == 3 else 1
        return (
            jnp.transpose(g.reshape(4, share, parts, -1), (1, 2, 0, 3)).reshape(shape).astype(f32)
        )

    table = jnp.sum(table, axis=0).reshape(-1)[: n_small * share].reshape(n_small, share)
    return (
        layer_output,
        d_inputs,
        d_encoded,
        table[0:3],
        table[3:6],
        join_cols(col_grads[0], self_qkv.shape),
        table[6:8],
        row_grads[0][0],
        join_cols(col_grads[1], cross_q.shape),
        join_cols(col_grads[2], cross_kv.shape),
        table[8:10],
        row_grads[1][0],
        table[10:13],
        join_cols(col_grads[3], ffn_in.shape),
        table[13:].reshape(-1),
        row_grads[2][0],
    )


def solution(mesh):
    both = ("head", "blk")
    rows2, rows3, cols2 = P(both, None), P(both, None, None), P(None, both)
    return jax.shard_map(
        partial(body, mesh.shape["blk"]),
        mesh=mesh,
        in_specs=(
            rows2, rows2, rows2, P(), P(), cols2, cols2, rows3, cols2, rows2, rows2, rows3,
            cols2, rows2, cols2, rows2, P(both), rows2,
        ),
        out_specs=(
            rows2, rows2, rows2, cols2, cols2, rows3, cols2, rows2, rows2, rows3, cols2, rows2,
            cols2, rows2, P(both), rows2,
        ),
        check_vma=False,
    )
```

```python
from functools import partial

import jax
import jax.numpy as jnp
from jax import lax
from jax.experimental import pallas as pl
from jax.experimental.pallas import tpu as pltpu
from jax.sharding import PartitionSpec as P

HEAD_DIM = 64
HEADS_HERE = 4
KEY_BLOCK = 256
AHEAD = 2
MESH = pl.DeviceIdType.MESH
ANY = pl.BlockSpec(memory_space=pl.ANY)
VMEM = pl.BlockSpec(memory_space=pltpu.VMEM)
SMEM = pl.BlockSpec(memory_space=pltpu.SMEM)
DMA = pltpu.SemaphoreType.DMA
f32 = jnp.float32
bf16 = jnp.bfloat16
NT = (((1,), (1,)), ((), ()))
NN = (((1,), (0,)), ((), ()))
TN = (((0,), (0,)), ((), ()))


def dot(a, b, dims=NN):
    return lax.dot_general(a, b, dims, preferred_element_type=f32)


def params(cid):
    return pltpu.CompilerParams(
        collective_id=cid, has_side_effects=True, vmem_limit_bytes=56 * 2**20
    )


def lasts(us):
    return pl.CostEstimate(flops=int(us * 1e9), bytes_accessed=int(us * 1e6), transcendentals=0)


def remote(src, dst, ssem, rsem, device):
    return pltpu.make_async_remote_copy(
        src, dst, ssem, rsem, device_id=device, device_id_type=MESH
    )


class Head:
    def __init__(self):
        self.me = lax.axis_index("head")
        self.core = self.me % 2
        self.x = self.me // 2
        self.sib = self.me + 1 - 2 * self.core
        self.far = self.me + 2 - 4 * self.x
        self.far_sib = self.sib + 2 - 4 * self.x


class Blk:
    def __init__(self, count):
        self.me = lax.axis_index("blk")
        self.z = self.me // 2
        self.y = self.me % 2
        self.Z = count // 2
        self.across = self.me + 1 - 2 * self.y


def signal(bar, **device):
    pl.semaphore_signal(bar, inc=1, device_id=device, device_id_type=MESH)


def greet_head(bar, hd):
    for k in range(1, 4):
        signal(bar, head=(hd.me + k) % 4)
    return 3


def greet_blk(bar, bk):
    signal(bar, blk=bk.across)

    @pl.when(bk.z > 0)
    def _():
        signal(bar, blk=bk.me - 2)

    @pl.when(bk.z < bk.Z - 1)
    def _():
        signal(bar, blk=bk.me + 2)

    return 1 + jnp.where(bk.z > 0, 1, 0) + jnp.where(bk.z < bk.Z - 1, 1, 0)


class BlkGather:
    def __init__(self, bk, outs, ssem, rsem):
        self.bk, self.outs, self.ssem, self.rsem = bk, outs, ssem, rsem

    def copy(self, a, slot, way, device, src=None):
        view = self.outs[a].at[:, slot]
        return remote(
            view if src is None else src,
            view,
            self.ssem.at[a, way, slot // 2],
            self.rsem.at[a, slot],
            {"blk": device},
        )

    def start(self, a, src=None):
        bk = self.bk

        @pl.when(bk.z < bk.Z - 1)
        def _():
            self.copy(a, bk.me, 0, bk.me + 2, src).start()

        @pl.when(bk.z > 0)
        def _():
            self.copy(a, bk.me, 1, bk.me - 2, src).start()

        self.copy(a, bk.me, 2, bk.across, src).start()

    def pass_on(self):
        bk = self.bk
        for k in range(1, bk.Z):
            for a in range(len(self.outs)):

                @pl.when(bk.z - k >= 0)
                def _():
                    slot = bk.me - 2 * k
                    self.copy(a, slot, 0, bk.me).wait_recv()

                    @pl.when(bk.z < bk.Z - 1)
                    def _():
                        self.copy(a, slot, 0, bk.me + 2).start()

                    self.copy(a, slot, 2, bk.across).start()

                @pl.when(bk.z + k < bk.Z)
                def _():
                    slot = bk.me + 2 * k
                    self.copy(a, slot, 0, bk.me).wait_recv()

                    @pl.when(bk.z > 0)
                    def _():
                        self.copy(a, slot, 1, bk.me - 2).start()

                    self.copy(a, slot, 2, bk.across).start()

    def finish(self):
        bk = self.bk
        for a in range(len(self.outs)):
            for s in range(bk.Z):
                self.copy(a, 2 * s + 1 - bk.y, 0, bk.me).wait_recv()
                slot = 2 * s + bk.y

                @pl.when((s <= bk.z) & (bk.z < bk.Z - 1))
                def _():
                    self.copy(a, slot, 0, bk.me).wait_send()

                @pl.when((s >= bk.z) & (bk.z > 0))
                def _():
                    self.copy(a, slot, 1, bk.me).wait_send()

                self.copy(a, slot, 2, bk.me).wait_send()


def weights_kernel(count, n_col, n_row, n_act, n_swap, *refs):
    n_in = n_col + 1 + n_row + n_act + n_swap
    first_swap = n_in - n_swap
    ins, outs = refs[:n_in], refs[n_in : 2 * n_in]
    lsem, hs, hr, ssem, rsem = refs[2 * n_in :]
    hd, bk = Head(), Blk(count)
    bar = pltpu.get_barrier_semaphore()
    greeted = greet_head(bar, hd) + greet_blk(bar, bk)
    pl.semaphore_wait(bar, greeted)
    n_blk = n_col + 1 + n_row
    ring = BlkGather(bk, outs[:n_blk], ssem, rsem)

    def own(a):
        if a < n_col:
            return pltpu.make_async_copy(
                ins[a].at[hd.me], outs[a].at[hd.me, bk.me], lsem.at[a]
            )
        if a == n_col:
            return pltpu.make_async_copy(ins[a], outs[a].at[hd.me, bk.me], lsem.at[a])
        if a < n_blk:
            return pltpu.make_async_copy(ins[a], outs[a].at[:, bk.me], lsem.at[a])
        src = ins[a].at[hd.me] if a >= first_swap else ins[a]
        return pltpu.make_async_copy(src, outs[a].at[hd.me], lsem.at[a])

    def across_head(a, k, back):
        to = (hd.me + k) % 4
        if a < n_col:
            src, dst = ins[a].at[to], outs[a].at[to if back else hd.me, bk.me]
        elif a == n_col:
            src, dst = ins[a], outs[a].at[to if back else hd.me, bk.me]
        else:
            src = ins[a].at[to] if a >= first_swap else ins[a]
            dst = outs[a].at[to if back else hd.me]
        return remote(
            src, dst, hs.at[a, k], hr.at[a, to if back else hd.me], {"head": to}
        )

    headed = list(range(n_col + 1)) + list(range(n_blk, n_in))
    for a in headed:
        for k in range(1, 4):
            across_head(a, k, False).start()
    for a in range(n_in):
        own(a).start()
    for a in range(n_col + 1, n_blk):
        ring.start(a, ins[a])
    for a in range(n_col + 1):
        own(a).wait()
        for k in range(1, 4):
            across_head(a, k, True).wait_recv()
        ring.start(a)
    ring.pass_on()
    ring.finish()
    for a in range(n_blk, n_in):
        for k in range(1, 4):
            across_head(a, k, True).wait_recv()
    for a in range(n_col + 1, n_in):
        own(a).wait()
    for a in headed:
        for k in range(1, 4):
            across_head(a, k, False).wait_send()


def gather_weights(cols, small, rows, acts, swaps, count, cid):
    n_in = len(cols) + 1 + len(rows) + len(acts) + len(swaps)
    n_blk = n_in - len(acts) - len(swaps)
    shapes = (
        [(4, count) + a.shape[1:] for a in cols]
        + [(4, count) + small.shape]
        + [(1, count) + a.shape[1:] for a in rows]
        + [(4,) + a.shape for a in acts]
        + [a.shape for a in swaps]
    )
    ops = list(cols) + [small] + list(rows) + list(acts) + list(swaps)
    outs = pl.pallas_call(
        partial(weights_kernel, count, len(cols), len(rows), len(acts), len(swaps)),
        out_shape=[jax.ShapeDtypeStruct(s, a.dtype) for s, a in zip(shapes, ops)],
        in_specs=[ANY] * n_in,
        out_specs=[ANY] * n_in,
        scratch_shapes=[
            DMA((n_in,)),
            DMA((n_in, 4)),
            DMA((n_in, 4)),
            DMA((n_blk, 3, count // 2)),
            DMA((n_blk, count)),
        ],
        compiler_params=params(cid),
        name="gather_weights",
        cost_estimate=lasts(55),
    )(*ops)
    a, b, c = len(cols), len(cols) + 1 + len(rows), n_in - len(swaps)
    return outs[:a], outs[a], outs[a + 1 : b], outs[b:c], outs[c:]


def gather_blk_kernel(count, n, *refs):
    ins, outs = refs[:n], refs[n : 2 * n]
    lsem, ssem, rsem = refs[2 * n :]
    bk = Blk(count)
    bar = pltpu.get_barrier_semaphore()
    pl.semaphore_wait(bar, greet_blk(bar, bk))
    ring = BlkGather(bk, outs, ssem, rsem)
    for a in range(n):
        ring.start(a, ins[a])
    for a in range(n):
        pltpu.make_async_copy(ins[a], outs[a].at[:, bk.me], lsem.at[a]).start()
    ring.pass_on()
    ring.finish()
    for a in range(n):
        pltpu.make_async_copy(ins[a], outs[a].at[:, bk.me], lsem.at[a]).wait()


def gather_blk(items, count, cid):
    n = len(items)
    return pl.pallas_call(
        partial(gather_blk_kernel, count, n),
        out_shape=[
            jax.ShapeDtypeStruct((a.shape[0], count) + a.shape[1:], a.dtype) for a in items
        ],
        in_specs=[ANY] * n,
        out_specs=[ANY] * n,
        scratch_shapes=[DMA((n,)), DMA((n, 3, count // 2)), DMA((n, count))],
        compiler_params=params(cid),
        name="gather_blk",
        cost_estimate=lasts(47),
    )(*items)


class BlkScatter:
    def __init__(self, bk, ins, bufs, sems):
        self.bk, self.ins = bk, ins
        self.own, self.over, self.side = bufs
        self.lsem, self.ys, self.yr, self.zs, self.ur, self.dr = sems

    def load(self, a, s):
        return pltpu.make_async_copy(
            self.ins[a].at[:, 2 * s + self.bk.y], self.own[a].at[s], self.lsem.at[a, s]
        )

    def cross(self, a, s):
        return remote(
            self.ins[a].at[:, 2 * s + 1 - self.bk.y],
            self.over[a].at[s],
            self.ys.at[a, s],
            self.yr.at[a, s],
            {"blk": self.bk.across},
        )

    def send(self, a, s, upward, slot=None):
        if slot is None:
            slot = s if upward else jnp.where(s == self.bk.z - 1, self.bk.Z, s)
        return remote(
            self.own[a].at[s],
            self.side[a].at[slot],
            self.zs.at[a, s],
            (self.ur if upward else self.dr).at[a, s],
            {"blk": self.bk.me + (2 if upward else -2)},
        )

    def order(self):
        for k in range((self.bk.Z + 1) // 2):
            yield self.bk.Z - 1 - k
            if k != self.bk.Z - 1 - k:
                yield k

    def begin(self, a):
        if a < len(self.ins):
            for s in self.order():
                self.cross(a, s).start()
                self.load(a, s).start()

    def add(self, a, s, extra, store):
        groups, rows = self.own[a].shape[1:3]
        step = min(rows, 32)

        def one(g, carry):
            for r in range(0, rows, step):
                part = pl.ds(r, step)
                total = self.own[a][s, g, part].astype(f32) + self.over[a][s, g, part].astype(f32)
                for slot in extra:
                    total = total + self.side[a][slot, g, part].astype(f32)
                store(g, part, total)
            return carry

        lax.fori_loop(0, groups, one, 0)

    def relay(self, a, s, upward):
        bk = self.bk
        self.load(a, s).wait()
        self.cross(a, s).wait_recv()
        inner = (bk.z > 0) if upward else (bk.z < bk.Z - 1)

        def store(g, part, total):
            self.own[a][s, g, part] = total.astype(bf16)

        @pl.when(inner)
        def _():
            self.send(a, s, upward, s).wait_recv()
            self.add(a, s, (s,), store)

        @pl.when(jnp.logical_not(inner))
        def _():
            self.add(a, s, (), store)

        self.send(a, s, upward).start()

    def run(self, finish):
        bk, n = self.bk, len(self.ins)
        for a in range(n):
            self.begin(a + AHEAD)
            for k in range(bk.Z - 1):

                @pl.when(bk.Z - 1 - k > bk.z)
                def _():
                    self.relay(a, bk.Z - 1 - k, True)

                @pl.when(k < bk.z)
                def _():
                    self.relay(a, k, False)

            if a > 0:
                finish(a - 1)
        finish(n - 1)

    def last(self, a, store):
        bk, s = self.bk, self.bk.z
        self.load(a, s).wait()
        self.cross(a, s).wait_recv()

        @pl.when(bk.z > 0)
        def _():
            self.send(a, s, True, s).wait_recv()

        @pl.when(bk.z < bk.Z - 1)
        def _():
            self.send(a, s, False, bk.Z).wait_recv()

        @pl.when((bk.z > 0) & (bk.z < bk.Z - 1))
        def _():
            self.add(a, s, (s, bk.Z), store)

        @pl.when((bk.z > 0) & (bk.z == bk.Z - 1))
        def _():
            self.add(a, s, (s,), store)

        @pl.when((bk.z == 0) & (bk.z < bk.Z - 1))
        def _():
            self.add(a, s, (bk.Z,), store)

    def finish(self):
        bk = self.bk
        for a in range(len(self.ins)):
            for s in range(bk.Z):
                self.cross(a, s).wait_send()

                @pl.when(s != bk.z)
                def _():
                    self.send(a, s, True, s).wait_send()


def scatter_scratch(items, count):
    Z = count // 2
    kinds = [
        pltpu.VMEM((slots, a.shape[0]) + a.shape[2:], bf16)
        for slots in (Z, Z, Z + 1)
        for a in items
    ]
    return kinds + [DMA((len(items), Z)) for _ in range(6)]


def scatter_parts(refs, n):
    bufs = tuple(refs[k * n : (k + 1) * n] for k in range(3))
    return bufs, refs[3 * n : 3 * n + 6], refs[3 * n + 6 :]


def scatter_blk_kernel(count, n, *refs):
    ins, outs = refs[:n], refs[n : 2 * n]
    bufs, sems, _ = scatter_parts(refs[2 * n :], n)
    bk = Blk(count)
    bar = pltpu.get_barrier_semaphore()
    pl.semaphore_wait(bar, greet_blk(bar, bk))
    ring = BlkScatter(bk, ins, bufs, sems)
    for a in range(AHEAD):
        ring.begin(a)

    def finish(a):
        def store(g, part, total):
            outs[a][g, part] = total.astype(outs[a].dtype)

        ring.last(a, store)

    ring.run(finish)
    ring.finish()


def scatter_blk(items, count, cid):
    n = len(items)
    return pl.pallas_call(
        partial(scatter_blk_kernel, count, n),
        out_shape=[
            jax.ShapeDtypeStruct((a.shape[0],) + a.shape[2:], a.dtype) for a in items
        ],
        in_specs=[ANY] * n,
        out_specs=[VMEM] * n,
        scratch_shapes=scatter_scratch(items, count),
        compiler_params=params(cid),
        name="scatter_blk",
        cost_estimate=lasts(60),
    )(*items)


def grads_kernel(count, n_col, n_row, *refs):
    n = n_col + n_row
    ins, small_in = refs[:n], refs[n]
    outs, small_out = refs[n + 1 : 2 * n + 1], refs[2 * n + 1]
    bufs, sems, rest = scatter_parts(refs[2 * n + 2 :], n)
    done = rest[:n_col]
    hs, hr, ls, ss, sr = rest[n_col:]
    hd, bk = Head(), Blk(count)
    devices = 4 * count
    me = hd.me * count + bk.me
    bar = pltpu.get_barrier_semaphore()

    def place(k):
        to = (me + k) % devices
        return to, {"head": to // count, "blk": to % count}

    def greet(k, carry):
        signal(bar, **place(k)[1])
        return carry

    lax.fori_loop(1, devices, greet, 0)
    pl.semaphore_wait(bar, devices - 1)
    ring = BlkScatter(bk, ins, bufs, sems)
    for a in range(AHEAD):
        ring.begin(a)
    mine = pltpu.make_async_copy(small_in.at[me], small_out.at[me], ls)
    mine.start()

    def small(k, back):
        to, device = place(k)
        return remote(
            small_in.at[to],
            small_out.at[to if back else me],
            ss.at[k],
            sr.at[to if back else me],
            device,
        )

    def start_small(k, carry):
        small(k, False).start()
        return carry

    lax.fori_loop(1, devices, start_small, 0)

    def across_head(a, k, back):
        to = (hd.me + k) % 4
        return remote(
            done[a].at[to],
            outs[a].at[to if back else hd.me],
            hs.at[a, k],
            hr.at[a, to if back else hd.me],
            {"head": to},
        )

    def finish(a):
        def store(g, part, total):
            if a < n_col:
                done[a][g, part] = total.astype(bf16)
            else:
                outs[a][g, part] = total

        ring.last(a, store)
        if a < n_col:
            for k in range(1, 4):
                across_head(a, k, False).start()
            outs[a][hd.me] = done[a][hd.me]

    ring.run(finish)
    ring.finish()
    for a in range(n_col):
        for k in range(1, 4):
            across_head(a, k, False).wait_send()
            across_head(a, k, True).wait_recv()
    mine.wait()

    def end_small(k, carry):
        small(k, False).wait_send()
        small(k, True).wait_recv()
        return carry

    lax.fori_loop(1, devices, end_small, 0)


def scatter_grads(cols, rows, small, count, cid):
    items = list(cols) + list(rows)
    devices = 4 * count
    outs = pl.pallas_call(
        partial(grads_kernel, count, len(cols), len(rows)),
        out_shape=[jax.ShapeDtypeStruct((4,) + a.shape[2:], bf16) for a in cols]
        + [jax.ShapeDtypeStruct((1,) + a.shape[2:], f32) for a in rows]
        + [jax.ShapeDtypeStruct(small.shape, f32)],
        in_specs=[ANY] * len(items) + [VMEM],
        out_specs=[VMEM] * len(items) + [VMEM],
        scratch_shapes=scatter_scratch(items, count)
        + [pltpu.VMEM((4,) + a.shape[2:], bf16) for a in cols]
        + [
            DMA((len(cols), 4)),
            DMA((len(cols), 4)),
            DMA,
            DMA((devices,)),
            DMA((devices,)),
        ],
        compiler_params=params(cid),
        name="scatter_grads",
        cost_estimate=lasts(70),
    )(*items, small)
    return outs[: len(cols)], outs[len(cols) : -1], outs[-1]


class HeadSum:
    def __init__(self, hd, part, near, mid, far, sems):
        self.hd, self.part, self.near, self.mid, self.far = hd, part, near, mid, far
        self.ss, self.rs = sems

    def near_copy(self, i):
        hd = self.hd
        block = hd.far_sib if i == 0 else hd.sib
        return remote(
            self.part.at[block], self.near.at[i], self.ss.at[i], self.rs.at[i], {"head": hd.sib}
        )

    def far_copy(self):
        return remote(self.mid, self.far, self.ss.at[2], self.rs.at[2], {"head": self.hd.far})

    def begin(self):
        self.near_copy(0).start()
        self.near_copy(1).start()

    def middle(self):
        self.near_copy(0).wait_recv()
        mine = self.part[self.hd.far].astype(f32)
        self.mid[...] = (mine + self.near[0].astype(f32)).astype(bf16)
        self.far_copy().start()

    def total(self):
        self.near_copy(1).wait_recv()
        mine = self.part[self.hd.me].astype(f32) + self.near[1].astype(f32)
        self.far_copy().wait_recv()
        return mine + self.far[...].astype(f32)

    def finish(self):
        self.near_copy(0).wait_send()
        self.near_copy(1).wait_send()
        self.far_copy().wait_send()


def head_sum_scratch(rows, width):
    return [
        pltpu.VMEM((2, rows, width), bf16),
        pltpu.VMEM((rows, width), bf16),
        pltpu.VMEM((rows, width), bf16),
        DMA((3,)),
        DMA((3,)),
    ]


class HeadGather:
    def __init__(self, hd, out, ss, rs):
        self.hd, self.out, self.ss, self.rs = hd, out, ss, rs

    def copy(self, slot, way, device):
        view = self.out.at[slot]
        return remote(view, view, self.ss.at[way], self.rs.at[slot], {"head": device})

    def run(self):
        hd = self.hd
        self.copy(hd.me, 0, hd.far).start()
        self.copy(hd.me, 1, hd.sib).start()
        self.copy(hd.far, 0, hd.me).wait_recv()
        self.copy(hd.far, 2, hd.sib).start()

    def finish(self):
        hd = self.hd
        self.copy(hd.sib, 0, hd.me).wait_recv()
        self.copy(hd.far_sib, 0, hd.me).wait_recv()
        self.copy(hd.me, 0, hd.far).wait_send()
        self.copy(hd.me, 1, hd.sib).wait_send()
        self.copy(hd.far, 2, hd.sib).wait_send()


def row_stats(v):
    average = jnp.mean(v, axis=-1, keepdims=True)
    centred = v - average
    spread = jnp.mean(centred * centred, axis=-1, keepdims=True)
    return centred, lax.rsqrt(spread + 1e-05)


def layer_norm(v, gain, shift):
    centred, r = row_stats(v)
    return centred * r * gain + shift


def layer_norm_back(v, g, gain):
    centred, r = row_stats(v)
    u = centred * r
    c = g * gain
    dv = r * (c - jnp.mean(c, axis=-1, keepdims=True) - u * jnp.mean(c * u, axis=-1, keepdims=True))
    return dv, jnp.sum(g * u, axis=0, keepdims=True), jnp.sum(g, axis=0, keepdims=True)


def forward_kernel(part, base, vecs, total, normed, near, mid, far, ss, rs, gs, gr):
    hd = Head()
    bar = pltpu.get_barrier_semaphore()
    pl.semaphore_wait(bar, greet_head(bar, hd))
    summed = HeadSum(hd, part, near, mid, far, (ss, rs))
    summed.begin()
    summed.middle()
    v = base[...].astype(f32) + summed.total() + vecs[0:1]
    total[...] = v
    normed[hd.me] = layer_norm(v, vecs[1:2], vecs[2:3]).astype(bf16)
    spread = HeadGather(hd, normed, gs, gr)
    spread.run()
    spread.finish()
    summed.finish()


def join_forward(part, base, bias, gain, shift, cid):
    rows, width = base.shape
    vecs = jnp.stack((bias, gain, shift))
    return pl.pallas_call(
        forward_kernel,
        out_shape=(
            jax.ShapeDtypeStruct((rows, width), f32),
            jax.ShapeDtypeStruct((4, rows, width), bf16),
        ),
        in_specs=[VMEM] * 3,
        out_specs=(VMEM, VMEM),
        scratch_shapes=head_sum_scratch(rows, width) + [DMA((3,)), DMA((4,))],
        compiler_params=params(cid),
        name="join_forward",
        cost_estimate=lasts(22),
    )(part, base, vecs)


def backward_kernel(
    out_term, gathers, part, extra, onward, v, vecs, back, other, grad_all, stats, *scratch
):
    hd = Head()
    bar = pltpu.get_barrier_semaphore()
    pl.semaphore_wait(bar, greet_head(bar, hd))
    summed = HeadSum(hd, part, *scratch[:3], scratch[3:5])
    scratch = scratch[5:]
    second = None
    if extra is not None:
        second = HeadSum(hd, extra, *scratch[:3], scratch[3:5])
        scratch = scratch[5:]
    summed.begin()
    summed.middle()
    if second is not None:
        second.begin()
        second.middle()
    dv, d_gain, d_shift = layer_norm_back(v[...], summed.total(), vecs[0:1])
    d = dv + onward[...].astype(f32)
    back[...] = d
    rounded = d.astype(bf16)
    if gathers:
        grad_all[hd.me] = rounded
        spread = HeadGather(hd, grad_all, *scratch)
        spread.run()
    if second is not None:
        more = second.total()
        if out_term:
            more = v[...] + more + vecs[1:2]
        other[...] = more.astype(other.dtype)
    stats[0:1] = d_gain
    stats[1:2] = d_shift
    stats[2:3] = jnp.sum(rounded.astype(f32), axis=0, keepdims=True)
    if gathers:
        spread.finish()
    summed.finish()
    if second is not None:
        second.finish()


def join_backward(part, onward, v, gain, cid, extra=None, bias=None, gathers=True):
    rows, width = onward.shape
    has_extra = extra is not None
    out_term = bias is not None
    vecs = jnp.stack((gain, bias if out_term else gain))

    def kernel(*refs):
        refs = list(refs)
        part_ref = refs.pop(0)
        extra_ref = refs.pop(0) if has_extra else None
        onward_ref, v_ref, vecs_ref, back = (refs.pop(0) for _ in range(4))
        other = refs.pop(0) if has_extra else None
        grad_all = refs.pop(0) if gathers else None
        stats = refs.pop(0)
        backward_kernel(
            out_term, gathers, part_ref, extra_ref, onward_ref, v_ref, vecs_ref,
            back, other, grad_all, stats, *refs,
        )

    shapes = [jax.ShapeDtypeStruct((rows, width), f32)]
    if has_extra:
        shapes.append(jax.ShapeDtypeStruct((rows, width), bf16 if out_term else f32))
    if gathers:
        shapes.append(jax.ShapeDtypeStruct((4, rows, width), bf16))
    shapes.append(jax.ShapeDtypeStruct((8, width), f32))
    scratch = head_sum_scratch(rows, width)
    if has_extra:
        scratch = scratch + head_sum_scratch(rows, width)
    if gathers:
        scratch = scratch + [DMA((3,)), DMA((4,))]
    ops = [part] + ([extra] if has_extra else []) + [onward, v, vecs]
    return pl.pallas_call(
        kernel,
        out_shape=shapes,
        in_specs=[VMEM] * len(ops),
        out_specs=[VMEM] * len(shapes),
        scratch_shapes=scratch,
        compiler_params=params(cid),
        name="join_backward",
        cost_estimate=lasts(24),
    )(*ops)


def exchange(grads, count):
    return [
        lax.all_to_all(g, "blk", 1, 1, tiled=True) if g.shape[0] > 1
        else lax.all_to_all(g[0], "blk", 0, 0, tiled=True)[None]
        for g in grads
    ]


def tie(value, *others):
    return lax.optimization_barrier((value,) + others)


def stack_heads(rows, scale):
    lane = lax.broadcasted_iota(jnp.int32, rows.shape, 1) // HEAD_DIM
    pieces = [
        jnp.where(lane == h, rows.astype(f32) * scale, 0.0).astype(bf16) for h in range(HEADS_HERE)
    ]
    return jnp.concatenate(pieces, axis=0)


def take_heads(wide, rows):
    pieces = [
        wide[h * HEAD_DIM : (h + 1) * HEAD_DIM, h * rows : (h + 1) * rows]
        for h in range(HEADS_HERE)
    ]
    return jnp.concatenate(pieces, axis=0).T


def masked_scores(keys, stacked, first, low, high):
    scores = dot(keys, stacked, NT)
    key_pos = first + lax.broadcasted_iota(jnp.int32, scores.shape, 0)
    return jnp.where((key_pos >= low) & (key_pos < high), scores, -1e30)


def attend_kernel(bounds, q, k, v, low, high, o, mix, lse, acc):
    chunks, rows, width = q.shape

    def chunk(i, carry):
        stacked = stack_heads(q[i], HEAD_DIM ** (-0.5))
        lo, hi = low[i], high[i]
        acc[...] = jnp.zeros_like(acc)

        def step(kb, state):
            top, total = state
            first = pl.multiple_of(kb * KEY_BLOCK, KEY_BLOCK)
            scores = masked_scores(k[pl.ds(first, KEY_BLOCK), :], stacked, first, lo, hi)
            new_top = jnp.maximum(top, jnp.max(scores, axis=0, keepdims=True))
            fading = jnp.exp(top - new_top)
            weights = jnp.exp(scores - new_top)
            total = total * fading + jnp.sum(weights, axis=0, keepdims=True)
            acc[...] = acc[...] * fading + dot(
                v[pl.ds(first, KEY_BLOCK), :], weights.astype(bf16), TN
            )
            return new_top, total

        wide = HEADS_HERE * rows
        top, total = lax.fori_loop(
            bounds[0, i],
            bounds[1, i],
            step,
            (jnp.full((1, wide), -1e30, f32), jnp.zeros((1, wide), f32)),
        )
        lse[i] = top + jnp.log(total)
        result = take_heads(acc[...] / total, rows)
        o[i] = result
        mix[i] = result.astype(bf16)
        return carry

    lax.fori_loop(0, chunks, chunk, 0)


def attend(q, k, v, spans):
    bounds, low, high = spans
    chunks, rows, width = q.shape
    wide = HEADS_HERE * rows
    return pl.pallas_call(
        attend_kernel,
        out_shape=(
            jax.ShapeDtypeStruct(q.shape, f32),
            jax.ShapeDtypeStruct(q.shape, bf16),
            jax.ShapeDtypeStruct((chunks, 1, wide), f32),
        ),
        in_specs=[SMEM] + [VMEM] * 5,
        out_specs=(VMEM,) * 3,
        scratch_shapes=[pltpu.VMEM((width, wide), f32)],
        compiler_params=pltpu.CompilerParams(vmem_limit_bytes=56 * 2**20),
        name="attend",
        cost_estimate=lasts(12),
    )(bounds, q, k, v, low, high)


def attend_back_kernel(
    bounds, q, k, v, low, high, d_o, o, lse, dq, dk, dv, qs, dos, delta, dq_acc, dk_acc, dv_acc
):
    chunks, rows, width = q.shape
    for i in range(chunks):
        qs[i] = stack_heads(q[i], HEAD_DIM ** (-0.5))
        dos[i] = stack_heads(d_o[i], 1.0)
        product = (d_o[i].astype(f32) * o[i]).T
        delta[i] = jnp.concatenate(
            [
                jnp.sum(product[h * HEAD_DIM : (h + 1) * HEAD_DIM], axis=0, keepdims=True)
                for h in range(HEADS_HERE)
            ],
            axis=1,
        )
    dq_acc[...] = jnp.zeros_like(dq_acc)

    def block(kb, carry):
        first = pl.multiple_of(kb * KEY_BLOCK, KEY_BLOCK)
        part = pl.ds(first, KEY_BLOCK)
        dk_acc[...] = jnp.zeros_like(dk_acc)
        dv_acc[...] = jnp.zeros_like(dv_acc)

        def chunk(i, inner):
            @pl.when((kb >= bounds[0, i]) & (kb < bounds[1, i]))
            def _():
                keys = k[part, :]
                scores = masked_scores(keys, qs[i], first, low[i], high[i])
                weights = jnp.exp(scores - lse[i])
                d_weights = dot(v[part, :], dos[i], NT)
                d_scores = (weights * (d_weights - delta[i])).astype(bf16)
                dv_acc[...] += dot(weights.astype(bf16), dos[i])
                dk_acc[...] += dot(d_scores, qs[i])
                dq_acc[i] += dot(keys, d_scores, TN)

            return inner

        lax.fori_loop(0, chunks, chunk, 0)
        dk[part, :] = dk_acc[...].astype(bf16)
        dv[part, :] = dv_acc[...].astype(bf16)
        return carry

    lax.fori_loop(0, k.shape[0] // KEY_BLOCK, block, 0)
    for i in range(chunks):
        dq[i] = (take_heads(dq_acc[i], rows) * HEAD_DIM ** (-0.5)).astype(bf16)


def attend_back(q, k, v, spans, d_o, o, lse):
    bounds, low, high = spans
    chunks, rows, width = q.shape
    wide = HEADS_HERE * rows
    return pl.pallas_call(
        attend_back_kernel,
        out_shape=(
            jax.ShapeDtypeStruct(q.shape, bf16),
            jax.ShapeDtypeStruct(k.shape, bf16),
            jax.ShapeDtypeStruct(k.shape, bf16),
        ),
        in_specs=[SMEM] + [VMEM] * 8,
        out_specs=(VMEM,) * 3,
        scratch_shapes=[
            pltpu.VMEM((chunks, wide, width), bf16),
            pltpu.VMEM((chunks, wide, width), bf16),
            pltpu.VMEM((chunks, 1, wide), f32),
            pltpu.VMEM((chunks, width, wide), f32),
            pltpu.VMEM((KEY_BLOCK, width), f32),
            pltpu.VMEM((KEY_BLOCK, width), f32),
        ],
        compiler_params=pltpu.CompilerParams(vmem_limit_bytes=60 * 2**20),
        name="attend_back",
        cost_estimate=lasts(14),
    )(bounds, q, k, v, low, high, d_o, o, lse)


def key_spans(target_lengths, source_lengths, rows, count):
    ends = jnp.cumsum(target_lengths, dtype=jnp.int32)
    starts = ends - target_lengths
    chunk = jnp.arange(4, dtype=jnp.int32) * count + lax.axis_index("blk")
    pos = chunk[:, None] * rows + jnp.arange(rows, dtype=jnp.int32)[None, :]
    past = (pos[..., None] >= ends).astype(jnp.int32)
    begun = (pos[..., None] >= starts).astype(jnp.int32)

    def spans(low, high):
        bounds = jnp.stack(
            (low[:, 0] // KEY_BLOCK, (high[:, -1] + KEY_BLOCK - 1) // KEY_BLOCK)
        ).astype(jnp.int32)
        wide = lambda a: jnp.tile(a[:, None, :], (1, 1, HEADS_HERE))
        return bounds, wide(low), wide(high)

    own = spans(jnp.sum(past * target_lengths, axis=-1), pos + 1)
    aligned = spans(
        jnp.sum(past * source_lengths, axis=-1), jnp.sum(begun * source_lengths, axis=-1)
    )
    return own, aligned


def body(
    count,
    inputs,
    encoded,
    d_output,
    target_lengths,
    source_lengths,
    norm_gain,
    norm_shift,
    self_qkv,
    self_bias,
    self_out,
    cross_q,
    cross_kv,
    cross_bias,
    cross_out,
    out_bias,
    ffn_in,
    ffn_in_bias,
    ffn_out,
):
    rows, width = inputs.shape
    devices = 4 * count
    share = width // devices
    head_width = width // 4
    hidden_width = ffn_in.shape[1]
    hidden_here = hidden_width // 4
    hidden_rows = hidden_width // width
    tokens_here = 4 * rows

    def split_cols(w):
        return jnp.transpose(w.reshape(share, -1, 4, w.shape[-1] // 4), (2, 0, 1, 3)).reshape(
            4, share, -1
        )

    small = jnp.concatenate(
        (
            norm_gain,
            norm_shift,
            self_bias,
            cross_bias,
            out_bias,
            ffn_in_bias.reshape(hidden_rows, share),
        )
    )
    n_small = small.shape[0]
    small = jnp.pad(small.reshape(-1), (0, 1024 - n_small * share)).reshape(8, 128)
    cols, small, row_weights, acts, swaps = gather_weights(
        [split_cols(w) for w in (self_qkv, cross_q, cross_kv)],
        small,
        [w[None] for w in (self_out, cross_out)],
        [inputs, encoded, d_output],
        [split_cols(ffn_in)],
        count,
        0,
    )
    w_qkv, w_cross_q, w_cross_kv = (w.reshape(width, -1) for w in cols)
    w_self_out, w_cross_out = (w.reshape(head_width, width) for w in row_weights[:2])
    w_ffn_out = lax.all_gather(ffn_out, "blk", axis=0, tiled=True)
    inputs_all, encoded_all, d_output_all = (a.reshape(tokens_here, width) for a in acts)
    small = small.reshape(devices, 1024)[:, : n_small * share].reshape(devices, n_small, share)
    small = small.astype(f32)
    vectors = jnp.transpose(small[:, :13], (1, 0, 2)).reshape(13, width)
    gains, shifts, b_out = vectors[0:3], vectors[3:6], vectors[10:13]
    head = lax.axis_index("head")
    here = lax.dynamic_slice_in_dim(vectors[6:10], head * head_width, head_width, axis=1)
    b_hidden = lax.dynamic_slice_in_dim(
        small[:, 13:].reshape(1, hidden_width), head * hidden_here, hidden_here, axis=1
    )

    own, aligned = key_spans(target_lengths, source_lengths, rows, count)

    def chunks(a):
        return a.reshape(4, rows, a.shape[-1])

    normed_one = layer_norm(inputs_all.astype(f32), gains[0:1], shifts[0:1]).astype(bf16)
    joined = dot(normed_one, w_qkv)
    q1 = (joined[:, :head_width] + here[0:1]).astype(bf16)
    k1 = joined[:, head_width : 2 * head_width].astype(bf16)
    v1 = (joined[:, 2 * head_width :] + here[1:2]).astype(bf16)
    pair = dot(encoded_all, w_cross_kv)
    k2 = pair[:, :head_width].astype(bf16)
    v2 = (pair[:, head_width:] + here[3:4]).astype(bf16)
    k2, v2, w_ffn_out = lax.optimization_barrier((k2, v2, w_ffn_out))
    k2, v2 = (
        lax.all_gather(chunks(a), "blk", axis=1, tiled=True).reshape(-1, head_width) for a in (k2, v2)
    )
    k2, v2, w_ffn_in = lax.optimization_barrier((k2, v2, swaps[0]))
    w_ffn_in = lax.all_gather(w_ffn_in, "blk", axis=1, tiled=True).reshape(width, -1)
    k1, v1 = (
        a.reshape(-1, head_width) for a in gather_blk([chunks(k1), chunks(v1)], count, 1)
    )
    q1 = chunks(q1)
    o1, mix1, lse1 = attend(q1, k1, v1, own)
    mix1 = mix1.reshape(tokens_here, head_width)
    first, normed_two = join_forward(
        chunks(dot(mix1, w_self_out).astype(bf16)), inputs, b_out[0], gains[1], shifts[1], 2
    )
    normed_two = normed_two.reshape(tokens_here, width)
    q2 = chunks((dot(normed_two, w_cross_q) + here[2:3]).astype(bf16))
    o2, mix2, lse2 = attend(q2, k2, v2, aligned)
    mix2 = mix2.reshape(tokens_here, head_width)
    second, normed_three = join_forward(
        chunks(dot(mix2, w_cross_out).astype(bf16)), first, b_out[1], gains[2], shifts[2], 3
    )
    normed_three = normed_three.reshape(tokens_here, width)

    hidden = dot(normed_three, w_ffn_in) + b_hidden
    active, gelu_back = jax.vjp(partial(jax.nn.gelu, approximate=False), hidden)
    active = active.astype(bf16)
    out_part = dot(active, w_ffn_out).astype(bf16)
    grad_ffn_out = dot(active, d_output_all, TN)
    d_active = dot(d_output_all, w_ffn_out, NT)
    d_hidden = gelu_back(d_active)[0].astype(bf16)
    grad_ffn_in = dot(normed_three, d_hidden, TN)
    d_part = dot(d_hidden, w_ffn_in, NT).astype(bf16)
    ffn_terms = exchange(
        [
            grad_ffn_in.astype(bf16).reshape(4, count, share, hidden_here),
            grad_ffn_out.astype(bf16).reshape(1, count, hidden_rows * share, width),
        ],
        count,
    )
    d_second, layer_output, d_cross, stats_three = join_backward(
        chunks(d_part), d_output, second, gains[2], 4, extra=chunks(out_part), bias=b_out[2]
    )
    d_cross = d_cross.reshape(tokens_here, width)

    grad_cross_out = dot(mix2, d_cross, TN)
    d_o2 = chunks(dot(d_cross, w_cross_out, NT).astype(bf16))
    dq2, dk2, dv2 = attend_back(q2, k2, v2, aligned, d_o2, o2, lse2)
    dq2 = dq2.reshape(tokens_here, head_width)
    grad_cross_q = dot(normed_two, dq2, TN)
    d_first, d_self, stats_two = join_backward(
        chunks(dot(dq2, w_cross_q, NT).astype(bf16)), d_second, first, gains[1], 5
    )
    d_self = d_self.reshape(tokens_here, width)

    grad_self_out = dot(mix1, d_self, TN)
    d_o1 = chunks(dot(d_self, w_self_out, NT).astype(bf16))
    dq1, dk1, dv1 = attend_back(q1, k1, v1, own, d_o1, o1, lse1)
    dk1, ffn_terms = tie(dk1, ffn_terms)
    dq1 = dq1.reshape(tokens_here, head_width)
    dk1, dv1, dk2, dv2 = (
        a.reshape(tokens_here, head_width)
        for a in scatter_blk(
            [a.reshape(4, count, rows, head_width) for a in (dk1, dv1, dk2, dv2)], count, 6
        )
    )
    d_joined = jnp.concatenate((dq1, dk1, dv1), axis=1)
    d_pair = jnp.concatenate((dk2, dv2), axis=1)
    d_inputs, d_encoded, stats_one = join_backward(
        chunks(dot(d_joined, w_qkv, NT).astype(bf16)),
        d_first,
        inputs.astype(f32),
        gains[0],
        7,
        extra=chunks(dot(d_pair, w_cross_kv, NT).astype(bf16)),
        gathers=False,
    )
    grad_qkv = dot(normed_one, d_joined, TN)
    grad_cross_kv = dot(encoded_all, d_pair, TN)

    def column_sum(gradient):
        return jnp.sum(gradient.astype(f32), axis=0, keepdims=True)

    def placed(part):
        whole = jnp.zeros((part.shape[0], 4 * part.shape[1]), f32)
        return lax.dynamic_update_slice_in_dim(whole, part, head * part.shape[1], axis=1)

    sums = placed(
        jnp.concatenate((column_sum(dq1), column_sum(dv1), column_sum(dq2), column_sum(dv2)))
    )
    table = jnp.concatenate(
        (
            stats_one[0:1],
            stats_two[0:1],
            stats_three[0:1],
            stats_one[1:2],
            stats_two[1:2],
            stats_three[1:2],
            sums,
            stats_two[2:3],
            stats_three[2:3],
            column_sum(d_output),
        )
    )
    table = jnp.transpose(table.reshape(13, devices, share), (1, 0, 2)).reshape(devices, -1)
    table = jnp.concatenate(
        (table, placed(column_sum(d_hidden)).reshape(devices, hidden_rows * share)), axis=1
    )
    table = jnp.pad(table, ((0, 0), (0, 1024 - n_small * share))).reshape(devices, 8, 128)

    grad_ffn_in, grad_ffn_out = (jnp.sum(g.astype(f32), axis=1) for g in ffn_terms)
    grad_ffn_in = lax.all_to_all(grad_ffn_in.astype(bf16), "head", 0, 0, tiled=True)
    col_grads, row_grads, table = scatter_grads(
        [
            g.astype(bf16).reshape(4, count, share, -1)
            for g in (grad_qkv, grad_cross_kv, grad_cross_q)
        ],
        [
            g.astype(bf16).reshape(1, count, -1, width)
            for g in (grad_cross_out, grad_self_out)
        ],
        table,
        count,
        8,
    )

    def join_cols(g, shape):
        parts = shape[1] if len(shape) == 3 else 1
        return (
            jnp.transpose(g.reshape(4, share, parts, -1), (1, 2, 0, 3)).reshape(shape).astype(f32)
        )

    table = jnp.sum(table, axis=0).reshape(-1)[: n_small * share].reshape(n_small, share)
    return (
        layer_output,
        d_inputs,
        d_encoded,
        table[0:3],
        table[3:6],
        join_cols(col_grads[0], self_qkv.shape),
        table[6:8],
        row_grads[1][0],
        join_cols(col_grads[2], cross_q.shape),
        join_cols(col_grads[1], cross_kv.shape),
        table[8:10],
        row_grads[0][0],
        table[10:13],
        join_cols(grad_ffn_in, ffn_in.shape),
        table[13:].reshape(-1),
        grad_ffn_out[0],
    )


def solution(mesh):
    both = ("head", "blk")
    rows2, rows3, cols2 = P(both, None), P(both, None, None), P(None, both)
    return jax.shard_map(
        partial(body, mesh.shape["blk"]),
        mesh=mesh,
        in_specs=(
            rows2, rows2, rows2, P(), P(), cols2, cols2, rows3, cols2, rows2, rows2, rows3,
            cols2, rows2, cols2, rows2, P(both), rows2,
        ),
        out_specs=(
            rows2, rows2, rows2, cols2, cols2, rows3, cols2, rows2, rows2, rows3, cols2, rows2,
            cols2, rows2, P(both), rows2,
        ),
        check_vma=False,
    )
```

```python
from functools import partial

import jax
import jax.numpy as jnp
from jax import lax
from jax.experimental import pallas as pl
from jax.experimental.pallas import tpu as pltpu
from jax.sharding import PartitionSpec as P

HEAD_DIM = 64
HEADS_HERE = 4
KEY_BLOCK = 256
AHEAD = 2
MESH = pl.DeviceIdType.MESH
ANY = pl.BlockSpec(memory_space=pl.ANY)
VMEM = pl.BlockSpec(memory_space=pltpu.VMEM)
SMEM = pl.BlockSpec(memory_space=pltpu.SMEM)
DMA = pltpu.SemaphoreType.DMA
f32 = jnp.float32
bf16 = jnp.bfloat16
NT = (((1,), (1,)), ((), ()))
NN = (((1,), (0,)), ((), ()))
TN = (((0,), (0,)), ((), ()))


def dot(a, b, dims=NN):
    return lax.dot_general(a, b, dims, preferred_element_type=f32)


def params(cid):
    return pltpu.CompilerParams(
        collective_id=cid, has_side_effects=True, vmem_limit_bytes=56 * 2**20
    )


def lasts(us):
    return pl.CostEstimate(flops=int(us * 3e8), bytes_accessed=int(us * 3e5), transcendentals=0)


def remote(src, dst, ssem, rsem, device):
    return pltpu.make_async_remote_copy(
        src, dst, ssem, rsem, device_id=device, device_id_type=MESH
    )


class Head:
    def __init__(self):
        self.me = lax.axis_index("head")
        self.core = self.me % 2
        self.x = self.me // 2
        self.sib = self.me + 1 - 2 * self.core
        self.far = self.me + 2 - 4 * self.x
        self.far_sib = self.sib + 2 - 4 * self.x


class Blk:
    def __init__(self, count):
        self.me = lax.axis_index("blk")
        self.z = self.me // 2
        self.y = self.me % 2
        self.Z = count // 2
        self.across = self.me + 1 - 2 * self.y


def signal(bar, **device):
    pl.semaphore_signal(bar, inc=1, device_id=device, device_id_type=MESH)


def greet_head(bar, hd):
    for k in range(1, 4):
        signal(bar, head=(hd.me + k) % 4)
    return 3


def greet_blk(bar, bk):
    signal(bar, blk=bk.across)

    @pl.when(bk.z > 0)
    def _():
        signal(bar, blk=bk.me - 2)

    @pl.when(bk.z < bk.Z - 1)
    def _():
        signal(bar, blk=bk.me + 2)

    return 1 + jnp.where(bk.z > 0, 1, 0) + jnp.where(bk.z < bk.Z - 1, 1, 0)


class BlkGather:
    def __init__(self, bk, outs, ssem, rsem):
        self.bk, self.outs, self.ssem, self.rsem = bk, outs, ssem, rsem

    def copy(self, a, slot, way, device, src=None):
        view = self.outs[a].at[:, slot]
        return remote(
            view if src is None else src,
            view,
            self.ssem.at[a, way, slot // 2],
            self.rsem.at[a, slot],
            {"blk": device},
        )

    def start(self, a, src=None):
        bk = self.bk

        @pl.when(bk.z < bk.Z - 1)
        def _():
            self.copy(a, bk.me, 0, bk.me + 2, src).start()

        @pl.when(bk.z > 0)
        def _():
            self.copy(a, bk.me, 1, bk.me - 2, src).start()

        self.copy(a, bk.me, 2, bk.across, src).start()

    def step(self, a, k):
        bk = self.bk

        @pl.when(bk.z - k >= 0)
        def _():
            slot = bk.me - 2 * k
            self.copy(a, slot, 0, bk.me).wait_recv()

            @pl.when(bk.z < bk.Z - 1)
            def _():
                self.copy(a, slot, 0, bk.me + 2).start()

            self.copy(a, slot, 2, bk.across).start()

        @pl.when(bk.z + k < bk.Z)
        def _():
            slot = bk.me + 2 * k
            self.copy(a, slot, 0, bk.me).wait_recv()

            @pl.when(bk.z > 0)
            def _():
                self.copy(a, slot, 1, bk.me - 2).start()

            self.copy(a, slot, 2, bk.across).start()

    def arrive(self, a):
        for s in range(self.bk.Z):
            self.copy(a, 2 * s + 1 - self.bk.y, 0, self.bk.me).wait_recv()

    def drain(self, a):
        bk = self.bk
        for s in range(bk.Z):
            slot = 2 * s + bk.y

            @pl.when((s <= bk.z) & (bk.z < bk.Z - 1))
            def _():
                self.copy(a, slot, 0, bk.me).wait_send()

            @pl.when((s >= bk.z) & (bk.z > 0))
            def _():
                self.copy(a, slot, 1, bk.me).wait_send()

            self.copy(a, slot, 2, bk.me).wait_send()


N_SMALL = 24


def front_kernel(
    count, small, qkv, ckv, cq, so, co, ffn_in, inputs, encoded, d_output, *refs
):
    (
        vectors, w_qkv, w_ckv, w_cq, w_so, w_co, swapped, inputs_all, encoded_all, d_output_all,
        normed, q1, k1, v1, k2, v2, small_all, bias, lsem, hs, hr, ssem, rsem,
    ) = refs
    hd, bk = Head(), Blk(count)
    share, head_width = qkv.shape[1], q1.shape[2]
    rows, width = inputs.shape
    bar = pltpu.get_barrier_semaphore()
    pl.semaphore_wait(bar, greet_head(bar, hd) + greet_blk(bar, bk))
    ring = BlkGather(bk, (small_all, w_qkv, w_ckv, w_cq, w_so, w_co, k1, v1), ssem, rsem)
    K1, V1 = 6, 7
    pairs = (
        (small, small_all), (qkv, w_qkv), (ckv, w_ckv), (cq, w_cq), (so, w_so), (co, w_co),
        (inputs, inputs_all), (encoded, encoded_all), (ffn_in, swapped), (d_output, d_output_all),
    )
    SMALL, QKV, CKV, CQ, SO, CO, INPUTS, ENCODED, FFN_IN, D_OUTPUT = range(10)
    rows_only = (SO, CO)

    def source(a, to):
        return pairs[a][0].at[to] if a in (QKV, CKV, CQ, FFN_IN) else pairs[a][0]

    def target(a, h):
        if a in rows_only:
            return pairs[a][1].at[:, bk.me]
        return pairs[a][1].at[h] if a >= INPUTS else pairs[a][1].at[h, bk.me]

    def own(a):
        return pltpu.make_async_copy(source(a, hd.me), target(a, hd.me), lsem.at[a])

    def across_head(a, k, back):
        to = (hd.me + k) % 4
        return remote(
            source(a, to),
            target(a, to if back else hd.me),
            hs.at[a, k],
            hr.at[a, to if back else hd.me],
            {"head": to},
        )

    def headed(a):
        own(a).wait()
        for k in range(1, 4):
            across_head(a, k, True).wait_recv()

    everything = (SMALL, QKV, INPUTS, CKV, CQ, ENCODED, FFN_IN, D_OUTPUT)
    for a in everything:
        own(a).start()
        for k in (2, 1, 3):
            across_head(a, k, False).start()
    for a in rows_only:
        own(a).start()
    headed(SMALL)
    ring.start(SMALL)
    headed(QKV)
    ring.start(QKV)
    headed(CKV)
    ring.start(CKV)
    for k in range(1, bk.Z):
        ring.step(SMALL, k)
        if k < bk.Z - 1:
            ring.step(QKV, k)
    for a in rows_only:
        ring.start(a, pairs[a][0])
    headed(CQ)
    ring.start(CQ)
    ring.arrive(0)
    lane = lax.broadcasted_iota(jnp.int32, (N_SMALL, 128), 1)

    def assemble(h, carry):
        for group in range(head_width // 128):
            total = jnp.zeros((N_SMALL, 128), f32)
            for i in range(128 // share):
                piece = small_all[h, group * (128 // share) + i].astype(f32)
                if i:
                    piece = pltpu.roll(piece, i * share, 1)
                total = jnp.where(lane // share == i, piece, total)
            vectors[h, :, group * 128 : (group + 1) * 128] = total
        return carry

    lax.fori_loop(0, 4, assemble, 0)

    def whole(n):
        return jnp.concatenate([vectors[h, n : n + 1, :] for h in range(4)], axis=1)

    gain, shift = whole(0), whole(3)
    bias[...] = vectors[hd.me]
    headed(INPUTS)

    def norm(j, carry):
        normed[j] = layer_norm(inputs_all[j].astype(f32), gain, shift).astype(bf16)
        return carry

    lax.fori_loop(0, 4, norm, 0)
    ring.step(QKV, bk.Z - 1)
    for k in range(1, bk.Z - 1):
        ring.step(CKV, k)
    ring.arrive(QKV)

    def project(features, w, c, bias_row, store):
        cols = w[:, :, :, c * head_width : (c + 1) * head_width].reshape(width, head_width)

        def one(j, carry):
            out = dot(features[j], cols)
            if bias_row is not None:
                out = out + bias[bias_row : bias_row + 1, :]
            store(j, out.astype(bf16))
            return carry

        lax.fori_loop(0, 4, one, 0)

    def into(ref):
        def store(j, value):
            ref[j] = value

        return store

    def into_own(ref):
        def store(j, value):
            ref[j, bk.me] = value

        return store

    project(normed, w_qkv, 1, None, into_own(k1))
    ring.start(K1)
    project(normed, w_qkv, 2, 7, into_own(v1))
    ring.start(V1)
    project(normed, w_qkv, 0, 6, into(q1))
    ring.step(CKV, bk.Z - 1)
    headed(ENCODED)
    for a in (SO, CO, CQ):
        for k in range(1, bk.Z):
            ring.step(a, k)
    ring.step(K1, 1)
    ring.step(V1, 1)
    ring.arrive(CKV)
    project(encoded_all, w_ckv, 0, None, into(k2))
    project(encoded_all, w_ckv, 1, 9, into(v2))
    for k in range(2, bk.Z):
        ring.step(K1, k)
        ring.step(V1, k)
    for a in rows_only:
        own(a).wait()
    for a in (FFN_IN, D_OUTPUT):
        headed(a)
    for a in (CQ, SO, CO, K1, V1):
        ring.arrive(a)
    for a in range(8):
        ring.drain(a)
    for a in everything:
        for k in range(1, 4):
            across_head(a, k, False).wait_send()


def front(small, cols, so, co, ffn_in, acts, count, cid):
    rows, width = acts[0].shape
    share, head_width = cols[0].shape[1], width // 4
    keys = (4, count, rows, head_width)
    tokens = (4, rows, width)
    block = (4, rows, head_width)
    bf = [(4, count) + a.shape[1:] for a in cols] + [(1, count) + a.shape[1:] for a in (so, co)]
    bf += [ffn_in.shape] + [tokens] * 4 + [block, keys, keys, block, block]
    return pl.pallas_call(
        partial(front_kernel, count),
        out_shape=[jax.ShapeDtypeStruct((4, N_SMALL, head_width), f32)]
        + [jax.ShapeDtypeStruct(s, bf16) for s in bf],
        in_specs=[ANY] * 10,
        out_specs=[VMEM] * 3 + [ANY] * 4 + [VMEM] * 2 + [ANY] + [VMEM] * 6,
        scratch_shapes=[
            pltpu.VMEM((4, count, N_SMALL, 128), bf16),
            pltpu.VMEM((N_SMALL, head_width), f32),
            DMA((10,)),
            DMA((10, 4)),
            DMA((10, 4)),
            DMA((8, 3, count // 2)),
            DMA((8, count)),
        ],
        compiler_params=params(cid),
        name="front",
        cost_estimate=lasts(90),
    )(small, *cols, so, co, ffn_in, *acts)


class BlkScatter:
    def __init__(self, bk, ins, bufs, sems):
        self.bk, self.ins = bk, ins
        self.own, self.over, self.side = bufs
        self.lsem, self.ys, self.yr, self.zs, self.ur, self.dr = sems

    def load(self, a, s):
        return pltpu.make_async_copy(
            self.ins[a].at[:, 2 * s + self.bk.y], self.own[a].at[s], self.lsem.at[a, s]
        )

    def cross(self, a, s):
        return remote(
            self.ins[a].at[:, 2 * s + 1 - self.bk.y],
            self.over[a].at[s],
            self.ys.at[a, s],
            self.yr.at[a, s],
            {"blk": self.bk.across},
        )

    def send(self, a, s, upward, slot=None):
        if slot is None:
            slot = s if upward else jnp.where(s == self.bk.z - 1, self.bk.Z, s)
        return remote(
            self.own[a].at[s],
            self.side[a].at[slot],
            self.zs.at[a, s],
            (self.ur if upward else self.dr).at[a, s],
            {"blk": self.bk.me + (2 if upward else -2)},
        )

    def order(self):
        for k in range((self.bk.Z + 1) // 2):
            yield self.bk.Z - 1 - k
            if k != self.bk.Z - 1 - k:
                yield k

    def begin(self, a):
        if a < len(self.ins):
            for s in self.order():
                self.cross(a, s).start()
                self.load(a, s).start()

    def add(self, a, s, extra, store):
        groups, rows = self.own[a].shape[1:3]
        step = min(rows, 32)

        def one(g, carry):
            for r in range(0, rows, step):
                part = pl.ds(r, step)
                total = self.own[a][s, g, part].astype(f32) + self.over[a][s, g, part].astype(f32)
                for slot in extra:
                    total = total + self.side[a][slot, g, part].astype(f32)
                store(g, part, total)
            return carry

        lax.fori_loop(0, groups, one, 0)

    def relay(self, a, s, upward):
        bk = self.bk
        self.load(a, s).wait()
        self.cross(a, s).wait_recv()
        inner = (bk.z > 0) if upward else (bk.z < bk.Z - 1)

        def store(g, part, total):
            self.own[a][s, g, part] = total.astype(bf16)

        @pl.when(inner)
        def _():
            self.send(a, s, upward, s).wait_recv()
            self.add(a, s, (s,), store)

        @pl.when(jnp.logical_not(inner))
        def _():
            self.add(a, s, (), store)

        self.send(a, s, upward).start()

    def run(self, finish):
        bk, n = self.bk, len(self.ins)
        for a in range(n):
            self.begin(a + AHEAD)
            for k in range(bk.Z - 1):

                @pl.when(bk.Z - 1 - k > bk.z)
                def _():
                    self.relay(a, bk.Z - 1 - k, True)

                @pl.when(k < bk.z)
                def _():
                    self.relay(a, k, False)

            if a > 0:
                finish(a - 1)
        finish(n - 1)

    def last(self, a, store):
        bk, s = self.bk, self.bk.z
        self.load(a, s).wait()
        self.cross(a, s).wait_recv()

        @pl.when(bk.z > 0)
        def _():
            self.send(a, s, True, s).wait_recv()

        @pl.when(bk.z < bk.Z - 1)
        def _():
            self.send(a, s, False, bk.Z).wait_recv()

        @pl.when((bk.z > 0) & (bk.z < bk.Z - 1))
        def _():
            self.add(a, s, (s, bk.Z), store)

        @pl.when((bk.z > 0) & (bk.z == bk.Z - 1))
        def _():
            self.add(a, s, (s,), store)

        @pl.when((bk.z == 0) & (bk.z < bk.Z - 1))
        def _():
            self.add(a, s, (bk.Z,), store)

    def finish(self):
        bk = self.bk
        for a in range(len(self.ins)):
            for s in range(bk.Z):
                self.cross(a, s).wait_send()

                @pl.when(s != bk.z)
                def _():
                    self.send(a, s, True, s).wait_send()


def scatter_scratch(items, count):
    Z = count // 2
    kinds = [
        pltpu.VMEM((slots, a.shape[0]) + a.shape[2:], bf16)
        for slots in (Z, Z, Z + 1)
        for a in items
    ]
    return kinds + [DMA((len(items), Z)) for _ in range(6)]


def scatter_parts(refs, n):
    bufs = tuple(refs[k * n : (k + 1) * n] for k in range(3))
    return bufs, refs[3 * n : 3 * n + 6], refs[3 * n + 6 :]


def scatter_blk_kernel(count, n, *refs):
    ins, outs = refs[:n], refs[n : 2 * n]
    bufs, sems, _ = scatter_parts(refs[2 * n :], n)
    bk = Blk(count)
    bar = pltpu.get_barrier_semaphore()
    pl.semaphore_wait(bar, greet_blk(bar, bk))
    ring = BlkScatter(bk, ins, bufs, sems)
    for a in range(AHEAD):
        ring.begin(a)

    def finish(a):
        def store(g, part, total):
            outs[a][g, part] = total.astype(outs[a].dtype)

        ring.last(a, store)

    ring.run(finish)
    ring.finish()


def scatter_blk(items, count, cid):
    n = len(items)
    return pl.pallas_call(
        partial(scatter_blk_kernel, count, n),
        out_shape=[
            jax.ShapeDtypeStruct((a.shape[0],) + a.shape[2:], a.dtype) for a in items
        ],
        in_specs=[ANY] * n,
        out_specs=[VMEM] * n,
        scratch_shapes=scatter_scratch(items, count),
        compiler_params=params(cid),
        name="scatter_blk",
        cost_estimate=lasts(60),
    )(*items)


class HeadSum:
    def __init__(self, hd, part, near, mid, far, sems):
        self.hd, self.part, self.near, self.mid, self.far = hd, part, near, mid, far
        self.ss, self.rs = sems

    def near_copy(self, i):
        hd = self.hd
        block = hd.far_sib if i == 0 else hd.sib
        return remote(
            self.part.at[block], self.near.at[i], self.ss.at[i], self.rs.at[i], {"head": hd.sib}
        )

    def far_copy(self):
        return remote(self.mid, self.far, self.ss.at[2], self.rs.at[2], {"head": self.hd.far})

    def begin(self):
        self.near_copy(0).start()
        self.near_copy(1).start()

    def middle(self):
        self.near_copy(0).wait_recv()
        mine = self.part[self.hd.far].astype(f32)
        self.mid[...] = (mine + self.near[0].astype(f32)).astype(bf16)
        self.far_copy().start()

    def total(self):
        self.near_copy(1).wait_recv()
        mine = self.part[self.hd.me].astype(f32) + self.near[1].astype(f32)
        self.far_copy().wait_recv()
        return mine + self.far[...].astype(f32)

    def finish(self):
        self.near_copy(0).wait_send()
        self.near_copy(1).wait_send()
        self.far_copy().wait_send()


def head_sum_scratch(rows, width):
    return [
        pltpu.VMEM((2, rows, width), bf16),
        pltpu.VMEM((rows, width), bf16),
        pltpu.VMEM((rows, width), bf16),
        DMA((3,)),
        DMA((3,)),
    ]


class HeadGather:
    def __init__(self, hd, out, ss, rs):
        self.hd, self.out, self.ss, self.rs = hd, out, ss, rs

    def copy(self, slot, way, device):
        view = self.out.at[slot]
        return remote(view, view, self.ss.at[way], self.rs.at[slot], {"head": device})

    def begin(self):
        hd = self.hd
        self.copy(hd.me, 0, hd.far).start()
        self.copy(hd.me, 1, hd.sib).start()

    def forward(self):
        hd = self.hd
        self.copy(hd.far, 0, hd.me).wait_recv()
        self.copy(hd.far, 2, hd.sib).start()

    def arrive(self):
        hd = self.hd
        self.copy(hd.sib, 0, hd.me).wait_recv()
        self.copy(hd.far_sib, 0, hd.me).wait_recv()

    def drain(self):
        hd = self.hd
        self.copy(hd.me, 0, hd.far).wait_send()
        self.copy(hd.me, 1, hd.sib).wait_send()
        self.copy(hd.far, 2, hd.sib).wait_send()


def row_stats(v):
    average = jnp.mean(v, axis=-1, keepdims=True)
    centred = v - average
    spread = jnp.mean(centred * centred, axis=-1, keepdims=True)
    return centred, lax.rsqrt(spread + 1e-05)


def layer_norm(v, gain, shift):
    centred, r = row_stats(v)
    return centred * r * gain + shift


def layer_norm_back(v, g, gain):
    centred, r = row_stats(v)
    u = centred * r
    c = g * gain
    dv = r * (c - jnp.mean(c, axis=-1, keepdims=True) - u * jnp.mean(c * u, axis=-1, keepdims=True))
    return dv, jnp.sum(g * u, axis=0, keepdims=True), jnp.sum(g, axis=0, keepdims=True)


PAIRS = ("dk1", "dv1", "dk2", "dv2")


def finale_kernel(count, inside, names_in, names_out, names_scratch, *refs):
    n_in, n_out = len(names_in), len(names_out)
    r = dict(zip(names_in + names_out + names_scratch, refs))
    hd, bk = Head(), Blk(count)
    devices = 4 * count
    me = hd.me * count + bk.me
    rows = r["d_first"].shape[0]
    width = r["d_first"].shape[1]
    items = [n[4:] for n in names_scratch if n.startswith("own_")]
    sources = [r["grad_" + n] if n in ("qkv", "ckv") else r[n] for n in items]
    bufs = tuple([r[k + n] for n in items] for k in ("own_", "over_", "side_"))
    ring = BlkScatter(bk, sources, bufs, [r["ring%d" % i] for i in range(6)])
    bar = pltpu.get_barrier_semaphore()

    def place(k):
        to = (me + k) % devices
        return to, {"head": to // count, "blk": to % count}

    def greet(k, carry):
        signal(bar, **place(k)[1])
        return carry

    lax.fori_loop(1, devices, greet, 0)
    pl.semaphore_wait(bar, devices - 1)

    def tiles(src, dst, which):
        local = pltpu.make_async_copy(src.at[me], dst.at[me], r["tile_local"].at[which])

        def copy(k, back):
            to, device = place(k)
            return remote(
                src.at[to],
                dst.at[to if back else me],
                r["tile_send"].at[which, k],
                r["tile_recv"].at[which, to if back else me],
                device,
            )

        def start(k, carry):
            copy(k, False).start()
            return carry

        def end(k, carry):
            copy(k, False).wait_send()
            copy(k, True).wait_recv()
            return carry

        def begin():
            local.start()
            lax.fori_loop(1, devices, start, 0)

        def finish():
            local.wait()
            lax.fori_loop(1, devices, end, 0)

        return begin, finish

    headed = ["ffn_in", "cq", "qkv", "ckv"]

    def across_head(n, k, back):
        a = headed.index(n)
        to = (hd.me + k) % 4
        src = r["ffn_in"] if n == "ffn_in" else r["done_" + n]
        return remote(
            src.at[to],
            r["out_" + n].at[to if back else hd.me],
            r["head_send"].at[a, k],
            r["head_recv"].at[a, to if back else hd.me],
            {"head": to},
        )

    def send_heads(n):
        for k in range(1, 4):
            across_head(n, k, False).start()
        src = r["ffn_in"] if n == "ffn_in" else r["done_" + n]
        r["out_" + n][hd.me] = src[hd.me]

    at = items.index

    def begin(n):
        ring.begin(at(n))

    def relays(n):
        a = at(n)
        for k in range(bk.Z - 1):

            @pl.when(bk.Z - 1 - k > bk.z)
            def _():
                ring.relay(a, bk.Z - 1 - k, True)

            @pl.when(k < bk.z)
            def _():
                ring.relay(a, k, False)

    def finish(n):
        def store(g, part, total):
            if n in PAIRS:
                r["sum_" + n][g, part] = total.astype(bf16)
            elif n in headed:
                r["done_" + n][g, part] = total.astype(bf16)
            else:
                r["out_" + n][g, part] = total

        ring.last(at(n), store)
        if n in headed:
            send_heads(n)

    def summed(n):
        return r["sum_" + n] if inside else r[n]

    def project(parts, w, out, joined, features, grad):
        for j in range(4):
            block = jnp.concatenate([p[j] for p in parts], axis=1)
            joined[j * rows : (j + 1) * rows, :] = block
            out[j] = dot(block, w[...], NT).astype(bf16)
        step = width // 4
        for g in range(4):
            lhs = features[:, :, g * step : (g + 1) * step].reshape(4 * rows, step)
            total = dot(lhs, joined[...], TN)
            grad[g] = total.reshape(grad.shape[1:]).astype(bf16)

    table_begin, table_finish = tiles(r["table"], r["out_table"], 0)
    stats_begin, stats_finish = tiles(r["stats_tab"], r["out_stats"], 1)
    near = [r["near%d" % i] for i in range(2)]
    first = HeadSum(
        hd, r["part1"], near[0], r["mid0"], r["far0"], (r["sum_send0"], r["sum_recv0"])
    )
    second = HeadSum(
        hd, r["part2"], near[1], r["mid1"], r["far1"], (r["sum_send1"], r["sum_recv1"])
    )

    def self_part():
        project(
            [r["dq1"], summed("dk1"), summed("dv1")],
            r["w_qkv"], r["part1"], r["joined1"], r["normed"], r["grad_qkv"],
        )
        first.begin()

    def cross_part():
        project(
            [summed("dk2"), summed("dv2")],
            r["w_ckv"], r["part2"], r["joined2"], r["encoded"], r["grad_ckv"],
        )
        second.begin()

    def self_end():
        dv, d_gain, d_shift = layer_norm_back(
            r["inputs"][...].astype(f32), first.total(), r["gain"][...]
        )
        r["out_d_inputs"][...] = dv + r["d_first"][...]
        both = jnp.concatenate((d_gain, d_shift, jnp.zeros((6, width), f32)), axis=0)
        share = width // devices
        for d in range(devices):
            lane = d * share // 128 * 128
            turn = d * share - lane
            tile = both[:, lane : lane + 128]
            if turn:
                tile = pltpu.roll(tile, 128 - turn, 1)
            r["stats_tab"][d] = tile
        stats_begin()

    if inside:
        begin("dk1")
        begin("dv1")
    else:
        begin("co")
        begin("so")
    table_begin()
    send_heads("ffn_in")
    if inside:
        begin("co")
        relays("dk1")
        begin("so")
        relays("dv1")
        finish("dk1")
        begin("cq")
        relays("co")
        finish("dv1")
        begin("dk2")
        self_part()
        begin("dv2")
        relays("so")
        finish("co")
        begin("qkv")
        first.middle()
        relays("cq")
        finish("so")
        relays("dk2")
        finish("cq")
        self_end()
        relays("dv2")
        finish("dk2")
        relays("qkv")
        finish("dv2")
        cross_part()
        begin("ckv")
        finish("qkv")
    else:
        begin("cq")
        self_part()
        begin("qkv")
        relays("co")
        cross_part()
        begin("ckv")
        relays("so")
        finish("co")
        first.middle()
        relays("cq")
        finish("so")
        self_end()
        relays("qkv")
        finish("cq")
        finish("qkv")
    second.middle()
    relays("ckv")
    r["out_d_encoded"][...] = second.total()
    finish("ckv")
    ring.finish()
    first.finish()
    second.finish()
    for n in headed:
        for k in range(1, 4):
            across_head(n, k, False).wait_send()
            across_head(n, k, True).wait_recv()
    table_finish()
    stats_finish()


def finale(count, pairs, co, so, cq, ffn_in, table, dq1, normed, encoded, w_qkv, w_ckv, inputs, d_first, gain, cid):
    inside = pairs[0].ndim == 4
    devices, Z = 4 * count, count // 2
    rows, width = inputs.shape
    share = width // devices
    head_width = w_ckv.shape[1] // 2
    ins = dict(zip(PAIRS, pairs))
    ins.update(co=co, so=so, cq=cq)
    in_specs = [ANY if inside else VMEM] * 4 + [ANY] * 3
    rest = dict(
        ffn_in=ffn_in, table=table, dq1=dq1, normed=normed, encoded=encoded, w_qkv=w_qkv,
        w_ckv=w_ckv, inputs=inputs, d_first=d_first, gain=gain,
    )
    ins.update(rest)
    in_specs += [VMEM] * len(rest)
    outs = dict(
        out_d_inputs=((rows, width), f32),
        out_d_encoded=((rows, width), f32),
        out_qkv=((4, share, 3 * head_width), bf16),
        out_ckv=((4, share, 2 * head_width), bf16),
        out_cq=((4, share, head_width), bf16),
        out_ffn_in=(ffn_in.shape, bf16),
        out_co=((1, share, width), f32),
        out_so=((1, share, width), f32),
        out_table=(table.shape, f32),
        out_stats=(table.shape, f32),
    )
    grads = dict(
        grad_qkv=(4, count, share, 3 * head_width), grad_ckv=(4, count, share, 2 * head_width)
    )
    shapes = {n: a.shape for n, a in zip(PAIRS, pairs)} if inside else {}
    shapes.update(co=co.shape, so=so.shape, cq=cq.shape, qkv=grads["grad_qkv"], ckv=grads["grad_ckv"])
    scratch = {}
    for kind, slots in (("own_", Z), ("over_", Z), ("side_", Z + 1)):
        for n, shape in shapes.items():
            scratch[kind + n] = pltpu.VMEM((slots, shape[0]) + shape[2:], bf16)
    for n in ("cq", "qkv", "ckv"):
        scratch["done_" + n] = pltpu.VMEM((4,) + shapes[n][2:], bf16)
    if inside:
        for n in PAIRS:
            scratch["sum_" + n] = pltpu.VMEM((4, rows, head_width), bf16)
    for n, shape in grads.items():
        scratch[n] = pltpu.VMEM(shape, bf16)
    for i, n in enumerate(("1", "2")):
        scratch["part" + n] = pltpu.VMEM((4, rows, width), bf16)
        scratch["joined" + n] = pltpu.VMEM((4 * rows, (3 - i) * head_width), bf16)
        kinds = head_sum_scratch(rows, width)
        for name, kind in zip(("near", "mid", "far", "sum_send", "sum_recv"), kinds):
            scratch[name + str(i)] = kind
    scratch["stats_tab"] = pltpu.VMEM(table.shape, f32)
    for i in range(6):
        scratch["ring%d" % i] = DMA((len(shapes), Z))
    scratch["tile_local"] = DMA((2,))
    scratch["tile_send"] = DMA((2, devices))
    scratch["tile_recv"] = DMA((2, devices))
    scratch["head_send"] = DMA((4, 4))
    scratch["head_recv"] = DMA((4, 4))
    got = pl.pallas_call(
        partial(finale_kernel, count, inside, tuple(ins), tuple(outs), tuple(scratch)),
        out_shape=[jax.ShapeDtypeStruct(*o) for o in outs.values()],
        in_specs=in_specs,
        out_specs=[VMEM] * len(outs),
        scratch_shapes=list(scratch.values()),
        compiler_params=params(cid),
        name="finale",
        cost_estimate=lasts(150),
    )(*ins.values())
    return dict(zip(outs, got))


def forward_kernel(count, n_stream, has_query, *refs):
    refs = list(refs)
    mix, w_out, base, vecs = (refs.pop(0) for _ in range(4))
    w_query, b_query = (refs.pop(0) for _ in range(2)) if has_query else (None, None)
    stream_in = [refs.pop(0) for _ in range(n_stream)]
    total, normed = (refs.pop(0) for _ in range(2))
    query = refs.pop(0) if has_query else None
    stream_out = [refs.pop(0) for _ in range(n_stream)]
    part, near, mid, far, ss, rs, gs, gr = (refs.pop(0) for _ in range(8))
    hd, bk = Head(), Blk(count)
    bar = pltpu.get_barrier_semaphore()
    greeted = greet_head(bar, hd)
    if n_stream:
        greeted = greeted + greet_blk(bar, bk)
    pl.semaphore_wait(bar, greeted)
    ring = None
    if n_stream:
        lsem, ssem, rsem = refs
        ring = BlkGather(bk, stream_out, ssem, rsem)
        for a in range(n_stream):
            ring.start(a, stream_in[a])
            pltpu.make_async_copy(stream_in[a], stream_out[a].at[:, bk.me], lsem.at[a]).start()

    def term(j):
        part[j] = dot(mix[j], w_out[...]).astype(bf16)

    summed = HeadSum(hd, part, near, mid, far, (ss, rs))
    term(hd.far_sib)
    summed.near_copy(0).start()
    term(hd.sib)
    summed.near_copy(1).start()
    term(hd.far)
    summed.middle()
    term(hd.me)
    v = base[...].astype(f32) + summed.total() + vecs[0:1]
    total[...] = v
    normed[hd.me] = layer_norm(v, vecs[1:2], vecs[2:3]).astype(bf16)
    spread = HeadGather(hd, normed, gs, gr)
    spread.begin()

    def ask(j):
        if has_query:
            query[j] = (dot(normed[j], w_query[...]) + b_query[...]).astype(bf16)

    def step(k):
        for a in range(n_stream):
            ring.step(a, k)

    ask(hd.me)
    if n_stream:
        step(1)
    spread.forward()
    ask(hd.far)
    spread.arrive()
    ask(hd.sib)
    ask(hd.far_sib)
    if n_stream:
        for k in range(2, bk.Z):
            step(k)
        for a in range(n_stream):
            ring.arrive(a)
            ring.drain(a)
            pltpu.make_async_copy(stream_in[a], stream_out[a].at[:, bk.me], lsem.at[a]).wait()
    spread.drain()
    summed.finish()


def join_forward(mix, w_out, base, bias, gain, shift, count, cid, query=None, stream=()):
    rows, width = base.shape
    n = len(stream)
    vecs = jnp.stack((bias, gain, shift))
    ops = [mix, w_out, base, vecs] + list(query or ()) + list(stream)
    shapes = [
        jax.ShapeDtypeStruct((rows, width), f32),
        jax.ShapeDtypeStruct((4, rows, width), bf16),
    ]
    if query:
        shapes.append(jax.ShapeDtypeStruct(mix.shape, bf16))
    n_vmem = len(shapes)
    shapes += [jax.ShapeDtypeStruct((4, count) + a.shape[1:], bf16) for a in stream]
    scratch = [pltpu.VMEM((4, rows, width), bf16)] + head_sum_scratch(rows, width)
    scratch += [DMA((3,)), DMA((4,))]
    if n:
        scratch += [DMA((n,)), DMA((n, 3, count // 2)), DMA((n, count))]
    return pl.pallas_call(
        partial(forward_kernel, count, n, query is not None),
        out_shape=shapes,
        in_specs=[VMEM] * (len(ops) - n) + [ANY] * n,
        out_specs=[VMEM] * n_vmem + [ANY] * n,
        scratch_shapes=scratch,
        compiler_params=params(cid),
        name="join_forward",
        cost_estimate=lasts(50 if n else 22),
    )(*ops)


def backward_kernel(
    out_term, gathers, part, extra, onward, v, vecs, back, other, grad_all, stats, *scratch
):
    hd = Head()
    bar = pltpu.get_barrier_semaphore()
    pl.semaphore_wait(bar, greet_head(bar, hd))
    summed = HeadSum(hd, part, *scratch[:3], scratch[3:5])
    scratch = scratch[5:]
    second = None
    if extra is not None:
        second = HeadSum(hd, extra, *scratch[:3], scratch[3:5])
        scratch = scratch[5:]
    summed.begin()
    summed.middle()
    if second is not None:
        second.begin()
        second.middle()
    dv, d_gain, d_shift = layer_norm_back(v[...], summed.total(), vecs[0:1])
    d = dv + onward[...].astype(f32)
    back[...] = d
    rounded = d.astype(bf16)
    if gathers:
        grad_all[hd.me] = rounded
        spread = HeadGather(hd, grad_all, *scratch)
        spread.begin()
        spread.forward()
    if second is not None:
        more = second.total()
        if out_term:
            more = v[...] + more + vecs[1:2]
        other[...] = more.astype(other.dtype)
    stats[0:1] = d_gain
    stats[1:2] = d_shift
    stats[2:3] = jnp.sum(rounded.astype(f32), axis=0, keepdims=True)
    if gathers:
        spread.arrive()
        spread.drain()
    summed.finish()
    if second is not None:
        second.finish()


def join_backward(part, onward, v, gain, cid, extra=None, bias=None, gathers=True):
    rows, width = onward.shape
    has_extra = extra is not None
    out_term = bias is not None
    vecs = jnp.stack((gain, bias if out_term else gain))

    def kernel(*refs):
        refs = list(refs)
        part_ref = refs.pop(0)
        extra_ref = refs.pop(0) if has_extra else None
        onward_ref, v_ref, vecs_ref, back = (refs.pop(0) for _ in range(4))
        other = refs.pop(0) if has_extra else None
        grad_all = refs.pop(0) if gathers else None
        stats = refs.pop(0)
        backward_kernel(
            out_term, gathers, part_ref, extra_ref, onward_ref, v_ref, vecs_ref,
            back, other, grad_all, stats, *refs,
        )

    shapes = [jax.ShapeDtypeStruct((rows, width), f32)]
    if has_extra:
        shapes.append(jax.ShapeDtypeStruct((rows, width), bf16 if out_term else f32))
    if gathers:
        shapes.append(jax.ShapeDtypeStruct((4, rows, width), bf16))
    shapes.append(jax.ShapeDtypeStruct((8, width), f32))
    scratch = head_sum_scratch(rows, width)
    if has_extra:
        scratch = scratch + head_sum_scratch(rows, width)
    if gathers:
        scratch = scratch + [DMA((3,)), DMA((4,))]
    ops = [part] + ([extra] if has_extra else []) + [onward, v, vecs]
    return pl.pallas_call(
        kernel,
        out_shape=shapes,
        in_specs=[VMEM] * len(ops),
        out_specs=[VMEM] * len(shapes),
        scratch_shapes=scratch,
        compiler_params=params(cid),
        name="join_backward",
        cost_estimate=lasts(24),
    )(*ops)


def tie(value, *others):
    return lax.optimization_barrier((value,) + others)


def stack_heads(rows, scale):
    lane = lax.broadcasted_iota(jnp.int32, rows.shape, 1) // HEAD_DIM
    pieces = [
        jnp.where(lane == h, rows.astype(f32) * scale, 0.0).astype(bf16) for h in range(HEADS_HERE)
    ]
    return jnp.concatenate(pieces, axis=0)


def take_heads(wide, rows):
    pieces = [
        wide[h * HEAD_DIM : (h + 1) * HEAD_DIM, h * rows : (h + 1) * rows]
        for h in range(HEADS_HERE)
    ]
    return jnp.concatenate(pieces, axis=0).T


def masked_scores(keys, stacked, first, low, high):
    scores = dot(keys, stacked, NT)
    key_pos = first + lax.broadcasted_iota(jnp.int32, scores.shape, 0)
    return jnp.where((key_pos >= low) & (key_pos < high), scores, -1e30)


def attend_kernel(bounds, q, k, v, low, high, o, mix, lse, acc):
    chunks, rows, width = q.shape

    def chunk(i, carry):
        stacked = stack_heads(q[i], HEAD_DIM ** (-0.5))
        lo, hi = low[i], high[i]
        acc[...] = jnp.zeros_like(acc)

        def step(kb, state):
            top, total = state
            first = pl.multiple_of(kb * KEY_BLOCK, KEY_BLOCK)
            scores = masked_scores(k[pl.ds(first, KEY_BLOCK), :], stacked, first, lo, hi)
            new_top = jnp.maximum(top, jnp.max(scores, axis=0, keepdims=True))
            fading = jnp.exp(top - new_top)
            weights = jnp.exp(scores - new_top)
            total = total * fading + jnp.sum(weights, axis=0, keepdims=True)
            acc[...] = acc[...] * fading + dot(
                v[pl.ds(first, KEY_BLOCK), :], weights.astype(bf16), TN
            )
            return new_top, total

        wide = HEADS_HERE * rows
        top, total = lax.fori_loop(
            bounds[0, i],
            bounds[1, i],
            step,
            (jnp.full((1, wide), -1e30, f32), jnp.zeros((1, wide), f32)),
        )
        lse[i] = top + jnp.log(total)
        result = take_heads(acc[...] / total, rows)
        o[i] = result
        mix[i] = result.astype(bf16)
        return carry

    lax.fori_loop(0, chunks, chunk, 0)


def attend(q, k, v, spans):
    bounds, low, high = spans
    chunks, rows, width = q.shape
    wide = HEADS_HERE * rows
    return pl.pallas_call(
        attend_kernel,
        out_shape=(
            jax.ShapeDtypeStruct(q.shape, f32),
            jax.ShapeDtypeStruct(q.shape, bf16),
            jax.ShapeDtypeStruct((chunks, 1, wide), f32),
        ),
        in_specs=[SMEM] + [VMEM] * 5,
        out_specs=(VMEM,) * 3,
        scratch_shapes=[pltpu.VMEM((width, wide), f32)],
        compiler_params=pltpu.CompilerParams(vmem_limit_bytes=56 * 2**20),
        name="attend",
        cost_estimate=lasts(12),
    )(bounds, q, k, v, low, high)


def attend_back_kernel(
    bounds, q, k, v, low, high, d_o, o, lse, dq, dk, dv, dv_sum, qs, dos, delta, dq_acc, dk_acc, dv_acc
):
    chunks, rows, width = q.shape
    dv_sum[...] = jnp.zeros_like(dv_sum)
    for i in range(chunks):
        qs[i] = stack_heads(q[i], HEAD_DIM ** (-0.5))
        dos[i] = stack_heads(d_o[i], 1.0)
        product = (d_o[i].astype(f32) * o[i]).T
        delta[i] = jnp.concatenate(
            [
                jnp.sum(product[h * HEAD_DIM : (h + 1) * HEAD_DIM], axis=0, keepdims=True)
                for h in range(HEADS_HERE)
            ],
            axis=1,
        )
    dq_acc[...] = jnp.zeros_like(dq_acc)

    def block(kb, carry):
        first = pl.multiple_of(kb * KEY_BLOCK, KEY_BLOCK)
        part = pl.ds(first, KEY_BLOCK)
        dk_acc[...] = jnp.zeros_like(dk_acc)
        dv_acc[...] = jnp.zeros_like(dv_acc)

        def chunk(i, inner):
            @pl.when((kb >= bounds[0, i]) & (kb < bounds[1, i]))
            def _():
                keys = k[part, :]
                scores = masked_scores(keys, qs[i], first, low[i], high[i])
                weights = jnp.exp(scores - lse[i])
                d_weights = dot(v[part, :], dos[i], NT)
                d_scores = (weights * (d_weights - delta[i])).astype(bf16)
                dv_acc[...] += dot(weights.astype(bf16), dos[i])
                dk_acc[...] += dot(d_scores, qs[i])
                dq_acc[i] += dot(keys, d_scores, TN)

            return inner

        lax.fori_loop(0, chunks, chunk, 0)
        dk[part, :] = dk_acc[...].astype(bf16)
        dv[part, :] = dv_acc[...].astype(bf16)
        dv_sum[...] += jnp.sum(dv_acc[...], axis=0, keepdims=True)
        return carry

    lax.fori_loop(0, k.shape[0] // KEY_BLOCK, block, 0)
    for i in range(chunks):
        dq[i] = (take_heads(dq_acc[i], rows) * HEAD_DIM ** (-0.5)).astype(bf16)


def attend_back(q, k, v, spans, d_o, o, lse):
    bounds, low, high = spans
    chunks, rows, width = q.shape
    wide = HEADS_HERE * rows
    return pl.pallas_call(
        attend_back_kernel,
        out_shape=(
            jax.ShapeDtypeStruct(q.shape, bf16),
            jax.ShapeDtypeStruct(k.shape, bf16),
            jax.ShapeDtypeStruct(k.shape, bf16),
            jax.ShapeDtypeStruct((1, width), f32),
        ),
        in_specs=[SMEM] + [VMEM] * 8,
        out_specs=(VMEM,) * 4,
        scratch_shapes=[
            pltpu.VMEM((chunks, wide, width), bf16),
            pltpu.VMEM((chunks, wide, width), bf16),
            pltpu.VMEM((chunks, 1, wide), f32),
            pltpu.VMEM((chunks, width, wide), f32),
            pltpu.VMEM((KEY_BLOCK, width), f32),
            pltpu.VMEM((KEY_BLOCK, width), f32),
        ],
        compiler_params=pltpu.CompilerParams(vmem_limit_bytes=60 * 2**20),
        name="attend_back",
        cost_estimate=lasts(14),
    )(bounds, q, k, v, low, high, d_o, o, lse)


def key_spans(target_lengths, source_lengths, rows, count):
    ends = jnp.cumsum(target_lengths, dtype=jnp.int32)
    starts = ends - target_lengths
    chunk = jnp.arange(4, dtype=jnp.int32) * count + lax.axis_index("blk")
    pos = chunk[:, None] * rows + jnp.arange(rows, dtype=jnp.int32)[None, :]
    past = (pos[..., None] >= ends).astype(jnp.int32)
    begun = (pos[..., None] >= starts).astype(jnp.int32)

    def spans(low, high):
        bounds = jnp.stack(
            (low[:, 0] // KEY_BLOCK, (high[:, -1] + KEY_BLOCK - 1) // KEY_BLOCK)
        ).astype(jnp.int32)
        wide = lambda a: jnp.tile(a[:, None, :], (1, 1, HEADS_HERE))
        return bounds, wide(low), wide(high)

    own = spans(jnp.sum(past * target_lengths, axis=-1), pos + 1)
    aligned = spans(
        jnp.sum(past * source_lengths, axis=-1), jnp.sum(begun * source_lengths, axis=-1)
    )
    return own, aligned


def body(
    count,
    inputs,
    encoded,
    d_output,
    target_lengths,
    source_lengths,
    norm_gain,
    norm_shift,
    self_qkv,
    self_bias,
    self_out,
    cross_q,
    cross_kv,
    cross_bias,
    cross_out,
    out_bias,
    ffn_in,
    ffn_in_bias,
    ffn_out,
):
    rows, width = inputs.shape
    devices = 4 * count
    share = width // devices
    head_width = width // 4
    hidden_width = ffn_in.shape[1]
    hidden_here = hidden_width // 4
    hidden_rows = hidden_width // width
    tokens_here = 4 * rows

    def split_cols(w):
        return jnp.transpose(w.reshape(share, -1, 4, w.shape[-1] // 4), (2, 0, 1, 3)).reshape(
            4, share, -1
        )

    w_ffn_out = lax.all_gather(ffn_out, "blk", axis=0, tiled=True)
    small = jnp.concatenate(
        (
            norm_gain,
            norm_shift,
            self_bias,
            cross_bias,
            out_bias,
            ffn_in_bias.reshape(hidden_rows, share),
        )
    )
    n_small = small.shape[0]
    small = jnp.pad(small, ((0, N_SMALL - n_small), (0, 128 - share)))
    (
        vectors, w_qkv, w_cross_kv, w_cross_q, w_self_out, w_cross_out, w_ffn_in, inputs_all,
        encoded_all, d_output_all, normed_one, q1, k1, v1, k2, v2,
    ) = front(
        small,
        [split_cols(w) for w in (self_qkv, cross_kv, cross_q)],
        self_out[None],
        cross_out[None],
        split_cols(ffn_in),
        [inputs, encoded, d_output],
        count,
        0,
    )
    w_ffn_in = lax.all_gather(w_ffn_in, "blk", axis=1, tiled=True).reshape(width, -1)
    w_qkv, w_cross_kv, w_cross_q, w_self_out, w_cross_out = (
        w.reshape(-1, w.shape[-1]) for w in (w_qkv, w_cross_kv, w_cross_q, w_self_out, w_cross_out)
    )
    encoded_all, d_output_all, normed_one = (
        a.reshape(tokens_here, width) for a in (encoded_all, d_output_all, normed_one)
    )
    head = lax.axis_index("head")
    here = lax.dynamic_index_in_dim(vectors, head, 0, keepdims=False)
    b_query = here[8:9]
    b_hidden = jnp.transpose(here[13:17].reshape(hidden_rows, count, share), (1, 0, 2)).reshape(
        1, hidden_here
    )
    vectors = jnp.transpose(vectors[:, :13], (1, 0, 2)).reshape(13, width)
    gains, shifts, b_out = vectors[0:3], vectors[3:6], vectors[10:13]

    own, aligned = key_spans(target_lengths, source_lengths, rows, count)

    def chunks(a):
        return a.reshape(4, rows, a.shape[-1])

    k1, v1 = (a.reshape(-1, head_width) for a in (k1, v1))
    o1, mix1, lse1 = attend(q1, k1, v1, own)
    first, normed_two, q2, k2, v2 = join_forward(
        mix1, w_self_out, inputs, b_out[0], gains[1], shifts[1], count, 2,
        query=(w_cross_q, b_query), stream=(k2, v2),
    )
    mix1 = mix1.reshape(tokens_here, head_width)
    normed_two = normed_two.reshape(tokens_here, width)
    k2, v2 = (a.reshape(-1, head_width) for a in (k2, v2))
    o2, mix2, lse2 = attend(q2, k2, v2, aligned)
    second, normed_three = join_forward(
        mix2, w_cross_out, first, b_out[1], gains[2], shifts[2], count, 3
    )
    mix2 = mix2.reshape(tokens_here, head_width)
    normed_three = normed_three.reshape(tokens_here, width)

    hidden = dot(normed_three, w_ffn_in) + b_hidden
    active, gelu_back = jax.vjp(partial(jax.nn.gelu, approximate=False), hidden)
    active = active.astype(bf16)
    out_part = dot(active, w_ffn_out).astype(bf16)
    grad_ffn_out = dot(active, d_output_all, TN)
    d_active = dot(d_output_all, w_ffn_out, NT)
    d_hidden = gelu_back(d_active)[0].astype(bf16)
    grad_ffn_in = dot(normed_three, d_hidden, TN)
    d_part = dot(d_hidden, w_ffn_in, NT).astype(bf16)
    ffn_grads = jnp.concatenate(
        (
            jnp.transpose(
                grad_ffn_in.astype(bf16).reshape(4, count, share, hidden_here), (1, 0, 2, 3)
            ).reshape(count, 4 * share, hidden_here),
            grad_ffn_out.astype(bf16).reshape(count, hidden_rows * share, width),
        ),
        axis=1,
    )
    d_part, ffn_grads = tie(d_part, ffn_grads)
    ffn_terms = lax.all_to_all(ffn_grads, "blk", 0, 0, tiled=True)
    d_second, layer_output, d_cross, stats_three = join_backward(
        chunks(d_part), d_output, second, gains[2], 4, extra=chunks(out_part), bias=b_out[2]
    )
    d_cross = d_cross.reshape(tokens_here, width)

    grad_cross_out = dot(mix2, d_cross, TN)
    d_o2 = chunks(dot(d_cross, w_cross_out, NT).astype(bf16))
    dq2, dk2, dv2, dv2_sum = attend_back(q2, k2, v2, aligned, d_o2, o2, lse2)
    dq2 = dq2.reshape(tokens_here, head_width)
    grad_cross_q = dot(normed_two, dq2, TN)
    d_first, d_self, stats_two = join_backward(
        chunks(dot(dq2, w_cross_q, NT).astype(bf16)), d_second, first, gains[1], 5
    )
    d_self = d_self.reshape(tokens_here, width)

    grad_self_out = dot(mix1, d_self, TN)
    d_o1 = chunks(dot(d_self, w_self_out, NT).astype(bf16))
    dq1, dk1, dv1, dv1_sum = attend_back(q1, k1, v1, own, d_o1, o1, lse1)
    dk1, ffn_terms = tie(dk1, ffn_terms)
    ffn_terms = jnp.sum(ffn_terms.astype(f32), axis=0)
    grad_ffn_in = ffn_terms[: 4 * share].reshape(4, share, hidden_here)
    grad_ffn_out = ffn_terms[4 * share :]
    pairs = [a.reshape(4, count, rows, head_width) for a in (dk1, dv1, dk2, dv2)]
    if count > 8:
        pairs = scatter_blk(pairs, count, 6)

    def column_sum(gradient):
        return jnp.sum(gradient.astype(f32), axis=0, keepdims=True)

    def placed(part):
        whole = jnp.zeros((part.shape[0], 4 * part.shape[1]), f32)
        return lax.dynamic_update_slice_in_dim(whole, part, head * part.shape[1], axis=1)

    sums = placed(
        jnp.concatenate(
            (column_sum(dq1.reshape(tokens_here, -1)), dv1_sum, column_sum(dq2), dv2_sum)
        )
    )
    nothing = jnp.zeros((1, width), f32)
    vectors = jnp.concatenate(
        (
            nothing, stats_two[0:1], stats_three[0:1], nothing, stats_two[1:2], stats_three[1:2],
            sums, stats_two[2:3], stats_three[2:3], column_sum(d_output),
        )
    )
    table = jnp.transpose(vectors.reshape(13, devices, share), (1, 0, 2)).reshape(devices, -1)
    table = jnp.concatenate(
        (table, placed(column_sum(d_hidden)).reshape(devices, hidden_rows * share)), axis=1
    )
    table = jnp.pad(table, ((0, 0), (0, 1024 - n_small * share))).reshape(devices, 8, 128)

    got = finale(
        count,
        pairs,
        grad_cross_out.astype(bf16).reshape(1, count, share, width),
        grad_self_out.astype(bf16).reshape(1, count, share, width),
        grad_cross_q.astype(bf16).reshape(4, count, share, head_width),
        grad_ffn_in.astype(bf16),
        table,
        dq1,
        chunks(normed_one),
        chunks(encoded_all),
        w_qkv,
        w_cross_kv,
        inputs,
        d_first,
        gains[0:1],
        7,
    )

    def join_cols(g, shape):
        parts = shape[1] if len(shape) == 3 else 1
        return (
            jnp.transpose(g.reshape(4, share, parts, -1), (1, 2, 0, 3)).reshape(shape).astype(f32)
        )

    table = jnp.sum(got["out_table"], axis=0).reshape(-1)[: n_small * share].reshape(n_small, share)
    stats_one = jnp.sum(got["out_stats"], axis=0)[:2, :share]
    return (
        layer_output,
        got["out_d_inputs"],
        got["out_d_encoded"],
        jnp.concatenate((stats_one[0:1], table[1:3])),
        jnp.concatenate((stats_one[1:2], table[4:6])),
        join_cols(got["out_qkv"], self_qkv.shape),
        table[6:8],
        got["out_so"][0],
        join_cols(got["out_cq"], cross_q.shape),
        join_cols(got["out_ckv"], cross_kv.shape),
        table[8:10],
        got["out_co"][0],
        table[10:13],
        join_cols(got["out_ffn_in"], ffn_in.shape),
        table[13:].reshape(-1),
        grad_ffn_out,
    )


def solution(mesh):
    both = ("head", "blk")
    rows2, rows3, cols2 = P(both, None), P(both, None, None), P(None, both)
    return jax.shard_map(
        partial(body, mesh.shape["blk"]),
        mesh=mesh,
        in_specs=(
            rows2, rows2, rows2, P(), P(), cols2, cols2, rows3, cols2, rows2, rows2, rows3,
            cols2, rows2, cols2, rows2, P(both), rows2,
        ),
        out_specs=(
            rows2, rows2, rows2, cols2, cols2, rows3, cols2, rows2, rows2, rows3, cols2, rows2,
            cols2, rows2, P(both), rows2,
        ),
        check_vma=False,
    )
```

```python
from functools import partial

import jax
import jax.numpy as jnp
from jax import lax
from jax.experimental import pallas as pl
from jax.experimental.pallas import tpu as pltpu
from jax.sharding import PartitionSpec as P

HEAD_DIM = 64
HEADS_HERE = 4
KEY_BLOCK = 256
AHEAD = 2
SKEW = 2
MESH = pl.DeviceIdType.MESH
ANY = pl.BlockSpec(memory_space=pl.ANY)
VMEM = pl.BlockSpec(memory_space=pltpu.VMEM)
SMEM = pl.BlockSpec(memory_space=pltpu.SMEM)
DMA = pltpu.SemaphoreType.DMA
f32 = jnp.float32
bf16 = jnp.bfloat16
NT = (((1,), (1,)), ((), ()))
NN = (((1,), (0,)), ((), ()))
TN = (((0,), (0,)), ((), ()))


def dot(a, b, dims=NN):
    return lax.dot_general(a, b, dims, preferred_element_type=f32)


def params(cid):
    return pltpu.CompilerParams(
        collective_id=cid, has_side_effects=True, vmem_limit_bytes=56 * 2**20
    )


def lasts(us):
    return pl.CostEstimate(flops=int(us * 3e8), bytes_accessed=int(us * 3e5), transcendentals=0)


def remote(src, dst, ssem, rsem, device):
    return pltpu.make_async_remote_copy(
        src, dst, ssem, rsem, device_id=device, device_id_type=MESH
    )


class Head:
    def __init__(self):
        self.me = lax.axis_index("head")
        self.core = self.me % 2
        self.x = self.me // 2
        self.sib = self.me + 1 - 2 * self.core
        self.far = self.me + 2 - 4 * self.x
        self.far_sib = self.sib + 2 - 4 * self.x


class Blk:
    def __init__(self, count):
        self.me = lax.axis_index("blk")
        self.z = self.me // 2
        self.y = self.me % 2
        self.Z = count // 2
        self.across = self.me + 1 - 2 * self.y


def signal(bar, **device):
    pl.semaphore_signal(bar, inc=1, device_id=device, device_id_type=MESH)


def greet_head(bar, hd):
    for k in range(1, 4):
        signal(bar, head=(hd.me + k) % 4)
    return 3


def greet_blk(bar, bk):
    signal(bar, blk=bk.across)

    @pl.when(bk.z > 0)
    def _():
        signal(bar, blk=bk.me - 2)

    @pl.when(bk.z < bk.Z - 1)
    def _():
        signal(bar, blk=bk.me + 2)

    return 1 + jnp.where(bk.z > 0, 1, 0) + jnp.where(bk.z < bk.Z - 1, 1, 0)


class BlkGather:
    def __init__(self, bk, outs, ssem, rsem):
        self.bk, self.outs, self.ssem, self.rsem = bk, outs, ssem, rsem

    def copy(self, a, slot, way, device, src=None):
        view = self.outs[a].at[:, slot]
        return remote(
            view if src is None else src,
            view,
            self.ssem.at[a, way, slot // 2],
            self.rsem.at[a, slot],
            {"blk": device},
        )

    def start(self, a, src=None):
        bk = self.bk

        @pl.when(bk.z < bk.Z - 1)
        def _():
            self.copy(a, bk.me, 0, bk.me + 2, src).start()

        @pl.when(bk.z > 0)
        def _():
            self.copy(a, bk.me, 1, bk.me - 2, src).start()

        self.copy(a, bk.me, 2, bk.across, src).start()

    def step(self, a, k):
        bk = self.bk

        @pl.when(bk.z - k >= 0)
        def _():
            slot = bk.me - 2 * k
            self.copy(a, slot, 0, bk.me).wait_recv()

            @pl.when(bk.z < bk.Z - 1)
            def _():
                self.copy(a, slot, 0, bk.me + 2).start()

            self.copy(a, slot, 2, bk.across).start()

        @pl.when(bk.z + k < bk.Z)
        def _():
            slot = bk.me + 2 * k
            self.copy(a, slot, 0, bk.me).wait_recv()

            @pl.when(bk.z > 0)
            def _():
                self.copy(a, slot, 1, bk.me - 2).start()

            self.copy(a, slot, 2, bk.across).start()

    def arrive(self, a):
        for s in range(self.bk.Z):
            self.copy(a, 2 * s + 1 - self.bk.y, 0, self.bk.me).wait_recv()

    def drain(self, a):
        bk = self.bk
        for s in range(bk.Z):
            slot = 2 * s + bk.y

            @pl.when((s <= bk.z) & (bk.z < bk.Z - 1))
            def _():
                self.copy(a, slot, 0, bk.me).wait_send()

            @pl.when((s >= bk.z) & (bk.z > 0))
            def _():
                self.copy(a, slot, 1, bk.me).wait_send()

            self.copy(a, slot, 2, bk.me).wait_send()


N_SMALL = 24


def front_kernel(
    count, small, qkv, ckv, cq, so, co, ffn_in, inputs, encoded, d_output, *refs
):
    (
        vectors, w_qkv, w_ckv, w_cq, w_so, w_co, swapped, inputs_all, encoded_all, d_output_all,
        normed, q1, k1, v1, k2, v2, small_all, bias, lsem, hs, hr, ssem, rsem,
    ) = refs
    hd, bk = Head(), Blk(count)
    share, head_width = qkv.shape[1], q1.shape[2]
    rows, width = inputs.shape
    bar = pltpu.get_barrier_semaphore()
    pl.semaphore_wait(bar, greet_head(bar, hd) + greet_blk(bar, bk))
    ring = BlkGather(bk, (small_all, w_qkv, w_ckv, w_cq, w_so, w_co, k1, v1), ssem, rsem)
    K1, V1 = 6, 7
    pairs = (
        (small, small_all), (qkv, w_qkv), (ckv, w_ckv), (cq, w_cq), (so, w_so), (co, w_co),
        (inputs, inputs_all), (encoded, encoded_all), (ffn_in, swapped), (d_output, d_output_all),
    )
    SMALL, QKV, CKV, CQ, SO, CO, INPUTS, ENCODED, FFN_IN, D_OUTPUT = range(10)
    rows_only = (SO, CO)

    def source(a, to):
        return pairs[a][0].at[to] if a in (QKV, CKV, CQ, FFN_IN) else pairs[a][0]

    def target(a, h):
        if a in rows_only:
            return pairs[a][1].at[:, bk.me]
        return pairs[a][1].at[h] if a >= INPUTS else pairs[a][1].at[h, bk.me]

    def own(a):
        return pltpu.make_async_copy(source(a, hd.me), target(a, hd.me), lsem.at[a])

    def across_head(a, k, back):
        to = (hd.me + k) % 4
        return remote(
            source(a, to),
            target(a, to if back else hd.me),
            hs.at[a, k],
            hr.at[a, to if back else hd.me],
            {"head": to},
        )

    def headed(a):
        own(a).wait()
        for k in range(1, 4):
            across_head(a, k, True).wait_recv()

    everything = (SMALL, QKV, CKV, CQ, INPUTS, ENCODED, FFN_IN, D_OUTPUT)
    for a in everything:
        own(a).start()
        for k in (2, 1, 3):
            across_head(a, k, False).start()
    for a in rows_only:
        own(a).start()
    headed(SMALL)
    ring.start(SMALL)
    headed(QKV)
    ring.start(QKV)
    for a in rows_only:
        ring.start(a, pairs[a][0])
    headed(CKV)
    ring.start(CKV)
    headed(CQ)
    ring.start(CQ)
    for k in range(1, bk.Z):
        for a in (SMALL, QKV) + ((SO, CO, CKV, CQ) if k < bk.Z - 1 else ()):
            ring.step(a, k)
    ring.arrive(0)
    lane = lax.broadcasted_iota(jnp.int32, (N_SMALL, 128), 1)

    def assemble(h, carry):
        for group in range(head_width // 128):
            total = jnp.zeros((N_SMALL, 128), f32)
            for i in range(128 // share):
                piece = small_all[h, group * (128 // share) + i].astype(f32)
                if i:
                    piece = pltpu.roll(piece, i * share, 1)
                total = jnp.where(lane // share == i, piece, total)
            vectors[h, :, group * 128 : (group + 1) * 128] = total
        return carry

    lax.fori_loop(0, 4, assemble, 0)

    def whole(n):
        return jnp.concatenate([vectors[h, n : n + 1, :] for h in range(4)], axis=1)

    gain, shift = whole(0), whole(3)
    bias[...] = vectors[hd.me]
    headed(INPUTS)

    def norm(j, carry):
        normed[j] = layer_norm(inputs_all[j].astype(f32), gain, shift).astype(bf16)
        return carry

    lax.fori_loop(0, 4, norm, 0)
    for a in (SO, CO, CKV, CQ):
        ring.step(a, bk.Z - 1)
    ring.arrive(QKV)

    def project(features, w, c, bias_row, store):
        cols = w[:, :, :, c * head_width : (c + 1) * head_width].reshape(width, head_width)

        def one(j, carry):
            out = dot(features[j], cols)
            if bias_row is not None:
                out = out + bias[bias_row : bias_row + 1, :]
            store(j, out.astype(bf16))
            return carry

        lax.fori_loop(0, 4, one, 0)

    def into(ref):
        def store(j, value):
            ref[j] = value

        return store

    def into_own(ref):
        def store(j, value):
            ref[j, bk.me] = value

        return store

    project(normed, w_qkv, 1, None, into_own(k1))
    ring.start(K1)
    project(normed, w_qkv, 2, 7, into_own(v1))
    ring.start(V1)
    project(normed, w_qkv, 0, 6, into(q1))
    headed(ENCODED)
    ring.step(K1, 1)
    ring.step(V1, 1)
    ring.arrive(CKV)
    project(encoded_all, w_ckv, 0, None, into(k2))
    project(encoded_all, w_ckv, 1, 9, into(v2))
    for k in range(2, bk.Z):
        ring.step(K1, k)
        ring.step(V1, k)
    for a in rows_only:
        own(a).wait()
    for a in (FFN_IN, D_OUTPUT):
        headed(a)
    for a in (CQ, SO, CO, K1, V1):
        ring.arrive(a)
    for a in range(8):
        ring.drain(a)
    for a in everything:
        for k in range(1, 4):
            across_head(a, k, False).wait_send()


def front(small, cols, so, co, ffn_in, acts, count, cid):
    rows, width = acts[0].shape
    share, head_width = cols[0].shape[1], width // 4
    keys = (4, count, rows, head_width)
    tokens = (4, rows, width)
    block = (4, rows, head_width)
    bf = [(4, count) + a.shape[1:] for a in cols] + [(1, count) + a.shape[1:] for a in (so, co)]
    bf += [ffn_in.shape] + [tokens] * 4 + [block, keys, keys, block, block]
    return pl.pallas_call(
        partial(front_kernel, count),
        out_shape=[jax.ShapeDtypeStruct((4, N_SMALL, head_width), f32)]
        + [jax.ShapeDtypeStruct(s, bf16) for s in bf],
        in_specs=[ANY] * 10,
        out_specs=[VMEM] * 3 + [ANY] * 4 + [VMEM] * 2 + [ANY] + [VMEM] * 6,
        scratch_shapes=[
            pltpu.VMEM((4, count, N_SMALL, 128), bf16),
            pltpu.VMEM((N_SMALL, head_width), f32),
            DMA((10,)),
            DMA((10, 4)),
            DMA((10, 4)),
            DMA((8, 3, count // 2)),
            DMA((8, count)),
        ],
        compiler_params=params(cid),
        name="front",
        cost_estimate=lasts(90),
    )(small, *cols, so, co, ffn_in, *acts)


class BlkScatter:
    def __init__(self, bk, ins, bufs, sems):
        self.bk, self.ins = bk, ins
        self.own, self.over, self.side = bufs
        self.lsem, self.ys, self.yr, self.zs, self.ur, self.dr = sems

    def load(self, a, s):
        return pltpu.make_async_copy(
            self.ins[a].at[:, 2 * s + self.bk.y], self.own[a].at[s], self.lsem.at[a, s]
        )

    def cross(self, a, s):
        return remote(
            self.ins[a].at[:, 2 * s + 1 - self.bk.y],
            self.over[a].at[s],
            self.ys.at[a, s],
            self.yr.at[a, s],
            {"blk": self.bk.across},
        )

    def send(self, a, s, upward, slot=None):
        if slot is None:
            slot = s if upward else jnp.where(s == self.bk.z - 1, self.bk.Z, s)
        return remote(
            self.own[a].at[s],
            self.side[a].at[slot],
            self.zs.at[a, s],
            (self.ur if upward else self.dr).at[a, s],
            {"blk": self.bk.me + (2 if upward else -2)},
        )

    def order(self):
        for k in range((self.bk.Z + 1) // 2):
            yield self.bk.Z - 1 - k
            if k != self.bk.Z - 1 - k:
                yield k

    def begin(self, a):
        if a < len(self.ins):
            for s in self.order():
                self.cross(a, s).start()
                self.load(a, s).start()

    def add(self, a, s, extra, store):
        groups, rows = self.own[a].shape[1:3]
        step = min(rows, 32)

        def one(g, carry):
            for r in range(0, rows, step):
                part = pl.ds(r, step)
                total = self.own[a][s, g, part].astype(f32) + self.over[a][s, g, part].astype(f32)
                for slot in extra:
                    total = total + self.side[a][slot, g, part].astype(f32)
                store(g, part, total)
            return carry

        lax.fori_loop(0, groups, one, 0)

    def relay(self, a, s, upward):
        bk = self.bk
        self.load(a, s).wait()
        self.cross(a, s).wait_recv()
        inner = (bk.z > 0) if upward else (bk.z < bk.Z - 1)

        def store(g, part, total):
            self.own[a][s, g, part] = total.astype(bf16)

        @pl.when(inner)
        def _():
            self.send(a, s, upward, s).wait_recv()
            self.add(a, s, (s,), store)

        @pl.when(jnp.logical_not(inner))
        def _():
            self.add(a, s, (), store)

        self.send(a, s, upward).start()

    def run(self, finish):
        bk, n = self.bk, len(self.ins)
        for a in range(n):
            self.begin(a + AHEAD)
            for k in range(bk.Z - 1):

                @pl.when(bk.Z - 1 - k > bk.z)
                def _():
                    self.relay(a, bk.Z - 1 - k, True)

                @pl.when(k < bk.z)
                def _():
                    self.relay(a, k, False)

            if a > 0:
                finish(a - 1)
        finish(n - 1)

    def last(self, a, store):
        bk, s = self.bk, self.bk.z
        self.load(a, s).wait()
        self.cross(a, s).wait_recv()

        @pl.when(bk.z > 0)
        def _():
            self.send(a, s, True, s).wait_recv()

        @pl.when(bk.z < bk.Z - 1)
        def _():
            self.send(a, s, False, bk.Z).wait_recv()

        @pl.when((bk.z > 0) & (bk.z < bk.Z - 1))
        def _():
            self.add(a, s, (s, bk.Z), store)

        @pl.when((bk.z > 0) & (bk.z == bk.Z - 1))
        def _():
            self.add(a, s, (s,), store)

        @pl.when((bk.z == 0) & (bk.z < bk.Z - 1))
        def _():
            self.add(a, s, (bk.Z,), store)

    def finish(self):
        bk = self.bk
        for a in range(len(self.ins)):
            for s in range(bk.Z):
                self.cross(a, s).wait_send()

                @pl.when(s != bk.z)
                def _():
                    self.send(a, s, True, s).wait_send()


def scatter_scratch(items, count):
    Z = count // 2
    kinds = [
        pltpu.VMEM((slots, a.shape[0]) + a.shape[2:], bf16)
        for slots in (Z, Z, Z + 1)
        for a in items
    ]
    return kinds + [DMA((len(items), Z)) for _ in range(6)]


def scatter_parts(refs, n):
    bufs = tuple(refs[k * n : (k + 1) * n] for k in range(3))
    return bufs, refs[3 * n : 3 * n + 6], refs[3 * n + 6 :]


def scatter_blk_kernel(count, n, *refs):
    ins, outs = refs[:n], refs[n : 2 * n]
    bufs, sems, _ = scatter_parts(refs[2 * n :], n)
    bk = Blk(count)
    bar = pltpu.get_barrier_semaphore()
    pl.semaphore_wait(bar, greet_blk(bar, bk))
    ring = BlkScatter(bk, ins, bufs, sems)
    for a in range(AHEAD):
        ring.begin(a)

    def finish(a):
        def store(g, part, total):
            outs[a][g, part] = total.astype(outs[a].dtype)

        ring.last(a, store)

    ring.run(finish)
    ring.finish()


def scatter_blk(items, count, cid):
    n = len(items)
    return pl.pallas_call(
        partial(scatter_blk_kernel, count, n),
        out_shape=[
            jax.ShapeDtypeStruct((a.shape[0],) + a.shape[2:], a.dtype) for a in items
        ],
        in_specs=[ANY] * n,
        out_specs=[VMEM] * n,
        scratch_shapes=scatter_scratch(items, count),
        compiler_params=params(cid),
        name="scatter_blk",
        cost_estimate=lasts(60),
    )(*items)


class HeadSum:
    def __init__(self, hd, part, near, mid, far, sems):
        self.hd, self.part, self.near, self.mid, self.far = hd, part, near, mid, far
        self.ss, self.rs = sems

    def near_copy(self, i):
        hd = self.hd
        block = hd.far_sib if i == 0 else hd.sib
        return remote(
            self.part.at[block], self.near.at[i], self.ss.at[i], self.rs.at[i], {"head": hd.sib}
        )

    def far_copy(self):
        return remote(self.mid, self.far, self.ss.at[2], self.rs.at[2], {"head": self.hd.far})

    def begin(self):
        self.near_copy(0).start()
        self.near_copy(1).start()

    def middle(self):
        self.near_copy(0).wait_recv()
        mine = self.part[self.hd.far].astype(f32)
        self.mid[...] = (mine + self.near[0].astype(f32)).astype(bf16)
        self.far_copy().start()

    def total(self):
        self.near_copy(1).wait_recv()
        mine = self.part[self.hd.me].astype(f32) + self.near[1].astype(f32)
        self.far_copy().wait_recv()
        return mine + self.far[...].astype(f32)

    def finish(self):
        self.near_copy(0).wait_send()
        self.near_copy(1).wait_send()
        self.far_copy().wait_send()


def head_sum_scratch(rows, width):
    return [
        pltpu.VMEM((2, rows, width), bf16),
        pltpu.VMEM((rows, width), bf16),
        pltpu.VMEM((rows, width), bf16),
        DMA((3,)),
        DMA((3,)),
    ]


class HeadGather:
    def __init__(self, hd, out, ss, rs):
        self.hd, self.out, self.ss, self.rs = hd, out, ss, rs

    def copy(self, slot, way, device):
        view = self.out.at[slot]
        return remote(view, view, self.ss.at[way], self.rs.at[slot], {"head": device})

    def begin(self):
        hd = self.hd
        self.copy(hd.me, 0, hd.far).start()
        self.copy(hd.me, 1, hd.sib).start()

    def forward(self):
        hd = self.hd
        self.copy(hd.far, 0, hd.me).wait_recv()
        self.copy(hd.far, 2, hd.sib).start()

    def arrive(self):
        hd = self.hd
        self.copy(hd.sib, 0, hd.me).wait_recv()
        self.copy(hd.far_sib, 0, hd.me).wait_recv()

    def drain(self):
        hd = self.hd
        self.copy(hd.me, 0, hd.far).wait_send()
        self.copy(hd.me, 1, hd.sib).wait_send()
        self.copy(hd.far, 2, hd.sib).wait_send()


def row_stats(v):
    average = jnp.mean(v, axis=-1, keepdims=True)
    centred = v - average
    spread = jnp.mean(centred * centred, axis=-1, keepdims=True)
    return centred, lax.rsqrt(spread + 1e-05)


def layer_norm(v, gain, shift):
    centred, r = row_stats(v)
    return centred * r * gain + shift


def layer_norm_back(v, g, gain):
    centred, r = row_stats(v)
    u = centred * r
    c = g * gain
    dv = r * (c - jnp.mean(c, axis=-1, keepdims=True) - u * jnp.mean(c * u, axis=-1, keepdims=True))
    return dv, jnp.sum(g * u, axis=0, keepdims=True), jnp.sum(g, axis=0, keepdims=True)


PAIRS = ("dk1", "dv1", "dk2", "dv2")


class PageScatter:
    def __init__(self, bk, feeds, bufs, sems, ready, crossed):
        self.bk, self.feeds, self.ready, self.crossed = bk, feeds, ready, crossed
        self.own, self.over, self.side = bufs
        self.lsem, self.ys, self.yr, self.zs, self.ur, self.dr = sems
        self.n = len(feeds)

    def load(self, a, s):
        copies = [
            pltpu.make_async_copy(src(s, True), self.own.at[(a, s) + dst], self.lsem.at[a, s, i])
            for i, (src, dst) in enumerate(self.feeds[a])
        ]
        if a in self.crossed:
            copies += [
                pltpu.make_async_copy(
                    src(s, False), self.over.at[(a, s) + dst], self.yr.at[a, s, i]
                )
                for i, (src, dst) in enumerate(self.feeds[a])
            ]
        return copies

    def cross(self, a, s):
        if a in self.crossed:
            return []
        return [
            remote(
                src(s, False),
                self.over.at[(a, s) + dst],
                self.ys.at[a, s, i],
                self.yr.at[a, s, i],
                {"blk": self.bk.across},
            )
            for i, (src, dst) in enumerate(self.feeds[a])
        ]

    def begin(self, a):
        Z = self.bk.Z
        for k in range(Z):
            s = Z - 1 - k // 2 if k % 2 == 0 else k // 2
            for copy in self.cross(a, s) + self.load(a, s):
                copy.start()

    def send(self, a, s, upward, slot=None):
        bk = self.bk
        if slot is None:
            slot = s if upward else jnp.where(s == bk.z - 1, bk.Z, s)
        return remote(
            self.own.at[a, s],
            self.side.at[a, slot],
            self.zs.at[a, s],
            (self.ur if upward else self.dr).at[a, s],
            {"blk": bk.me + (2 if upward else -2)},
        )

    def gathered(self, a):
        for s in range(self.bk.Z):
            for copy in self.load(a, s):
                copy.wait()
            for copy in self.cross(a, s):
                copy.wait_recv()

    def relay(self, a, s, upward):
        bk = self.bk
        inner = (bk.z > 0) if upward else (bk.z < bk.Z - 1)

        @pl.when(inner)
        def _():
            self.send(a, s, upward, s).wait_recv()
            self.own[a, s] = (
                self.own[a, s].astype(f32)
                + self.over[a, s].astype(f32)
                + self.side[a, s].astype(f32)
            ).astype(bf16)

        @pl.when(jnp.logical_not(inner))
        def _():
            self.own[a, s] = (
                self.own[a, s].astype(f32) + self.over[a, s].astype(f32)
            ).astype(bf16)

        self.send(a, s, upward).start()

    def wave(self, t):
        bk = self.bk
        if t < self.n:
            self.gathered(t)
        up, down = t - SKEW * bk.z, t - SKEW * (bk.Z - 1 - bk.z)

        @pl.when((up >= 0) & (up < self.n))
        def _():
            def one(i, carry):
                self.relay(up, bk.Z - 1 - i, True)
                return carry

            lax.fori_loop(0, bk.Z - 1 - bk.z, one, 0)

        @pl.when((down >= 0) & (down < self.n))
        def _():
            def one(i, carry):
                self.relay(down, i, False)
                return carry

            lax.fori_loop(0, bk.z, one, 0)

        a = t - SKEW * (bk.Z - 1)
        if a >= 0:
            self.last(a)

    def last(self, a):
        bk, s = self.bk, self.bk.z
        total = self.own[a, s].astype(f32) + self.over[a, s].astype(f32)

        @pl.when(bk.z > 0)
        def _():
            self.send(a, s, True, s).wait_recv()

        @pl.when(bk.z < bk.Z - 1)
        def _():
            self.send(a, s, False, bk.Z).wait_recv()

        total = total + jnp.where(bk.z > 0, self.side[a, s].astype(f32), 0.0)
        total = total + jnp.where(bk.z < bk.Z - 1, self.side[a, bk.Z].astype(f32), 0.0)
        self.ready[a](total)

    def drain(self):
        bk = self.bk
        for a in range(self.n):
            for s in range(bk.Z):
                for copy in self.cross(a, s):
                    copy.wait_send()

                @pl.when(s != bk.z)
                def _():
                    self.send(a, s, True, s).wait_send()


def finale_kernel(count, inside, names_in, names_out, names_scratch, *refs):
    r = dict(zip(names_in + names_out + names_scratch, refs))
    hd, bk = Head(), Blk(count)
    devices = 4 * count
    me = hd.me * count + bk.me
    rows, width = r["d_first"].shape
    head_width = width // 4
    share = width // devices
    bar = pltpu.get_barrier_semaphore()

    def place(k):
        to = (me + k) % devices
        return to, {"head": to // count, "blk": to % count}

    def greet(k, carry):
        signal(bar, **place(k)[1])
        return carry

    lax.fori_loop(1, devices, greet, 0)
    pl.semaphore_wait(bar, devices - 1)

    def tiles(src, dst, which):
        local = pltpu.make_async_copy(src.at[me], dst.at[me], r["tile_local"].at[which])

        def copy(k, back):
            to, device = place(k)
            return remote(
                src.at[to],
                dst.at[to if back else me],
                r["tile_send"].at[which, k],
                r["tile_recv"].at[which, to if back else me],
                device,
            )

        def start(k, carry):
            copy(k, False).start()
            return carry

        def end(k, carry):
            copy(k, False).wait_send()
            copy(k, True).wait_recv()
            return carry

        def begin():
            local.start()
            lax.fori_loop(1, devices, start, 0)

        def finish():
            local.wait()
            lax.fori_loop(1, devices, end, 0)

        return begin, finish

    headed = ["ffn_in", "cq", "qkv", "ckv"]

    def across_head(n, k, back):
        a = headed.index(n)
        to = (hd.me + k) % 4
        src = r["ffn_in"] if n == "ffn_in" else r["done_" + n]
        return remote(
            src.at[to],
            r["out_" + n].at[to if back else hd.me],
            r["head_send"].at[a, k],
            r["head_recv"].at[a, to if back else hd.me],
            {"head": to},
        )

    def send_heads(n):
        for k in range(1, 4):
            across_head(n, k, False).start()
        src = r["ffn_in"] if n == "ffn_in" else r["done_" + n]
        r["out_" + n][hd.me] = src[hd.me]

    def place_of(s, mine):
        return 2 * s + (bk.y if mine else 1 - bk.y)

    def col_page(ref, c):
        def src(s, mine):
            return ref.at[:, place_of(s, mine), :, c * head_width : (c + 1) * head_width]

        return [(src, ())]

    def row_page(ref):
        def src(j):
            return lambda s, mine: ref.at[
                0, place_of(s, mine), :, j * head_width : (j + 1) * head_width
            ]

        return [(src(j), (j,)) for j in range(4)]

    def pair_page(n, h):
        return [(lambda s, mine: r[n if mine else n + "_over"].at[h, s], ())]

    def store_pair(n, h):
        def store(total):
            r["sum_" + n][h] = total.reshape(rows, head_width).astype(bf16)

        return store

    def store_col(n, c):
        def store(total):
            r["done_" + n][:, :, c * head_width : (c + 1) * head_width] = total.astype(bf16)

        return store

    def store_row(n):
        def store(total):
            for j in range(4):
                r["out_" + n][0, :, j * head_width : (j + 1) * head_width] = total[j]

        return store

    feeds, ready, crossed, index = [], [], [], {}

    def item(name, feed, store):
        index[name] = len(feeds)
        feeds.append(feed)
        ready.append(store)

    if inside:
        for n in ("dk2", "dv2", "dk1", "dv1"):
            for h in range(4):
                if n in ("dk2", "dv2"):
                    crossed.append(len(feeds))
                item(n, pair_page(n, h), store_pair(n, h))
    for n in ("so", "co"):
        item(n, row_page(r[n]), store_row(n))
    item("cq", col_page(r["cq"], 0), store_col("cq", 0))
    item("qkv0", col_page(r["grad_qkv"], 0), store_col("qkv", 0))
    for c in range(2):
        item("ckv%d" % c, col_page(r["grad_ckv"], c), store_col("ckv", c))
    for c in (1, 2):
        item("qkv%d" % c, col_page(r["grad_qkv"], c), store_col("qkv", c))
    ring = PageScatter(
        bk, feeds, (r["own"], r["over"], r["side"]), [r["ring%d" % i] for i in range(6)], ready,
        crossed,
    )

    def summed(n):
        return r["sum_" + n] if inside else r[n]

    def fill(joined, parts, first):
        cols = slice(first, first + len(parts) * head_width)
        for j in range(4):
            joined[j * rows : (j + 1) * rows, cols] = jnp.concatenate([p[j] for p in parts], axis=1)
        return cols

    def weight_grad(joined, cols, features, grad):
        def one(g, carry):
            lhs = features[:, :, pl.ds(pl.multiple_of(g * head_width, head_width), head_width)]
            total = dot(lhs.reshape(4 * rows, head_width), joined[:, cols], TN)
            grad[g, :, :, cols] = total.reshape(grad.shape[1:3] + (-1,)).astype(bf16)
            return carry

        lax.fori_loop(0, 4, one, 0)

    def project(joined, w, out, summed_over_head):
        def term(j, carry):
            block = joined[pl.ds(pl.multiple_of(j * rows, rows), rows), :]
            out[j] = dot(block, w[...], NT).astype(bf16)
            return carry

        lax.fori_loop(0, 4, term, 0)
        summed_over_head.begin()

    table_begin, table_finish = tiles(r["table"], r["out_table"], 0)
    stats_begin, stats_finish = tiles(r["stats_tab"], r["out_stats"], 1)
    first, second = (
        HeadSum(
            hd, r["part%d" % (i + 1)], r["near%d" % i], r["mid%d" % i], r["far%d" % i],
            (r["sum_send%d" % i], r["sum_recv%d" % i]),
        )
        for i in range(2)
    )

    def query_part():
        cols = fill(r["joined1"], [r["dq1"]], 0)
        weight_grad(r["joined1"], cols, r["normed"], r["grad_qkv"])
        ring.begin(index["qkv0"])

    def self_part():
        cols = fill(r["joined1"], [summed("dk1"), summed("dv1")], head_width)
        weight_grad(r["joined1"], cols, r["normed"], r["grad_qkv"])
        for c in (1, 2):
            ring.begin(index["qkv%d" % c])
        project(r["joined1"], r["w_qkv"], r["part1"], first)

    def cross_part():
        cols = fill(r["joined2"], [summed("dk2"), summed("dv2")], 0)
        weight_grad(r["joined2"], cols, r["encoded"], r["grad_ckv"])
        for c in range(2):
            ring.begin(index["ckv%d" % c])
        project(r["joined2"], r["w_ckv"], r["part2"], second)

    def self_end():
        dv, d_gain, d_shift = layer_norm_back(
            r["inputs"][...].astype(f32), first.total(), r["gain"][...]
        )
        r["out_d_inputs"][...] = dv + r["d_first"][...]
        both = jnp.concatenate((d_gain, d_shift, jnp.zeros((6, width), f32)), axis=0)
        for d in range(devices):
            lane = d * share // 128 * 128
            turn = d * share - lane
            tile = both[:, lane : lane + 128]
            if turn:
                tile = pltpu.roll(tile, 128 - turn, 1)
            r["stats_tab"][d] = tile
        stats_begin()

    lag = SKEW * (bk.Z - 1)
    for a in range(index["cq"] + 1):
        ring.begin(a)
    table_begin()
    send_heads("ffn_in")
    query_part()
    if inside:
        after_cross, after_self = index["dv2"] + lag, index["dv1"] + lag
    else:
        cross_part()
        self_part()
        after_cross, after_self = 0, 3
    for t in range(ring.n + lag):
        ring.wave(t)
        if inside and t == after_cross:
            cross_part()
        if inside and t == after_self:
            self_part()
        if t == after_cross + 3:
            second.middle()
        if t == min(after_self + 2, ring.n + lag - 1):
            first.middle()
            r["out_d_encoded"][...] = second.total()
        if t == min(after_self + 5, ring.n + lag - 1):
            self_end()
        if t == index["cq"] + lag:
            send_heads("cq")
        if t == index["ckv1"] + lag:
            send_heads("ckv")
    send_heads("qkv")
    ring.drain()
    first.finish()
    second.finish()
    table_finish()
    stats_finish()
    for n in headed:
        for k in range(1, 4):
            across_head(n, k, False).wait_send()
            across_head(n, k, True).wait_recv()


def finale(count, pairs, co, so, cq, ffn_in, table, dq1, normed, encoded, w_qkv, w_ckv, inputs, d_first, gain, cid):
    inside = len(pairs) == 8
    devices, Z = 4 * count, count // 2
    rows, width = inputs.shape
    share = width // devices
    head_width = w_ckv.shape[1] // 2
    ins = dict(zip(PAIRS + tuple(n + "_over" for n in PAIRS), pairs))
    ins.update(co=co, so=so, cq=cq)
    in_specs = [ANY if inside else VMEM] * len(pairs) + [ANY] * 3
    rest = dict(
        ffn_in=ffn_in, table=table, dq1=dq1, normed=normed, encoded=encoded, w_qkv=w_qkv,
        w_ckv=w_ckv, inputs=inputs, d_first=d_first, gain=gain,
    )
    ins.update(rest)
    in_specs += [VMEM] * len(rest)
    outs = dict(
        out_d_inputs=((rows, width), f32),
        out_d_encoded=((rows, width), f32),
        out_qkv=((4, share, 3 * head_width), bf16),
        out_ckv=((4, share, 2 * head_width), bf16),
        out_cq=((4, share, head_width), bf16),
        out_ffn_in=(ffn_in.shape, bf16),
        out_co=((1, share, width), f32),
        out_so=((1, share, width), f32),
        out_table=(table.shape, f32),
        out_stats=(table.shape, f32),
    )
    grads = dict(
        grad_qkv=(4, count, share, 3 * head_width), grad_ckv=(4, count, share, 2 * head_width)
    )
    scratch = {}
    n_items = 24 if inside else 8
    for kind, slots in (("own", Z), ("over", Z), ("side", Z + 1)):
        scratch[kind] = pltpu.VMEM((n_items, slots, 4, share, head_width), bf16)
    for n, wide in (("cq", 1), ("qkv", 3), ("ckv", 2)):
        scratch["done_" + n] = pltpu.VMEM((4, share, wide * head_width), bf16)
    if inside:
        for n in PAIRS:
            scratch["sum_" + n] = pltpu.VMEM((4, rows, head_width), bf16)
    for n, shape in grads.items():
        scratch[n] = pltpu.VMEM(shape, bf16)
    for i, n in enumerate(("1", "2")):
        scratch["part" + n] = pltpu.VMEM((4, rows, width), bf16)
        scratch["joined" + n] = pltpu.VMEM((4 * rows, (3 - i) * head_width), bf16)
        kinds = head_sum_scratch(rows, width)
        for name, kind in zip(("near", "mid", "far", "sum_send", "sum_recv"), kinds):
            scratch[name + str(i)] = kind
    scratch["stats_tab"] = pltpu.VMEM(table.shape, f32)
    for i in range(6):
        scratch["ring%d" % i] = DMA((n_items, Z, 4) if i < 3 else (n_items, Z))
    scratch["tile_local"] = DMA((2,))
    scratch["tile_send"] = DMA((2, devices))
    scratch["tile_recv"] = DMA((2, devices))
    scratch["head_send"] = DMA((4, 4))
    scratch["head_recv"] = DMA((4, 4))
    got = pl.pallas_call(
        partial(finale_kernel, count, inside, tuple(ins), tuple(outs), tuple(scratch)),
        out_shape=[jax.ShapeDtypeStruct(*o) for o in outs.values()],
        in_specs=in_specs,
        out_specs=[VMEM] * len(outs),
        scratch_shapes=list(scratch.values()),
        compiler_params=params(cid),
        name="finale",
        cost_estimate=lasts(150),
    )(*ins.values())
    return dict(zip(outs, got))


def forward_kernel(count, n_stream, has_query, *refs):
    refs = list(refs)
    mix, w_out, base, vecs = (refs.pop(0) for _ in range(4))
    w_query, b_query = (refs.pop(0) for _ in range(2)) if has_query else (None, None)
    stream_in = [refs.pop(0) for _ in range(n_stream)]
    total, normed = (refs.pop(0) for _ in range(2))
    query = refs.pop(0) if has_query else None
    stream_out = [refs.pop(0) for _ in range(n_stream)]
    part, near, mid, far, ss, rs, gs, gr = (refs.pop(0) for _ in range(8))
    hd, bk = Head(), Blk(count)
    bar = pltpu.get_barrier_semaphore()
    greeted = greet_head(bar, hd)
    if n_stream:
        greeted = greeted + greet_blk(bar, bk)
    pl.semaphore_wait(bar, greeted)
    ring = None
    if n_stream:
        lsem, ssem, rsem = refs
        ring = BlkGather(bk, stream_out, ssem, rsem)
        for a in range(n_stream):
            ring.start(a, stream_in[a])
            pltpu.make_async_copy(stream_in[a], stream_out[a].at[:, bk.me], lsem.at[a]).start()

    def term(j):
        part[j] = dot(mix[j], w_out[...]).astype(bf16)

    summed = HeadSum(hd, part, near, mid, far, (ss, rs))
    term(hd.far_sib)
    summed.near_copy(0).start()
    term(hd.sib)
    summed.near_copy(1).start()
    term(hd.far)
    summed.middle()
    term(hd.me)
    v = base[...].astype(f32) + summed.total() + vecs[0:1]
    total[...] = v
    normed[hd.me] = layer_norm(v, vecs[1:2], vecs[2:3]).astype(bf16)
    spread = HeadGather(hd, normed, gs, gr)
    spread.begin()

    def ask(j):
        if has_query:
            query[j] = (dot(normed[j], w_query[...]) + b_query[...]).astype(bf16)

    def step(k):
        for a in range(n_stream):
            ring.step(a, k)

    ask(hd.me)
    if n_stream:
        step(1)
    spread.forward()
    ask(hd.far)
    spread.arrive()
    ask(hd.sib)
    ask(hd.far_sib)
    if n_stream:
        for k in range(2, bk.Z):
            step(k)
        for a in range(n_stream):
            ring.arrive(a)
            ring.drain(a)
            pltpu.make_async_copy(stream_in[a], stream_out[a].at[:, bk.me], lsem.at[a]).wait()
    spread.drain()
    summed.finish()


def join_forward(mix, w_out, base, bias, gain, shift, count, cid, query=None, stream=()):
    rows, width = base.shape
    n = len(stream)
    vecs = jnp.stack((bias, gain, shift))
    ops = [mix, w_out, base, vecs] + list(query or ()) + list(stream)
    shapes = [
        jax.ShapeDtypeStruct((rows, width), f32),
        jax.ShapeDtypeStruct((4, rows, width), bf16),
    ]
    if query:
        shapes.append(jax.ShapeDtypeStruct(mix.shape, bf16))
    n_vmem = len(shapes)
    shapes += [jax.ShapeDtypeStruct((4, count) + a.shape[1:], bf16) for a in stream]
    scratch = [pltpu.VMEM((4, rows, width), bf16)] + head_sum_scratch(rows, width)
    scratch += [DMA((3,)), DMA((4,))]
    if n:
        scratch += [DMA((n,)), DMA((n, 3, count // 2)), DMA((n, count))]
    return pl.pallas_call(
        partial(forward_kernel, count, n, query is not None),
        out_shape=shapes,
        in_specs=[VMEM] * (len(ops) - n) + [ANY] * n,
        out_specs=[VMEM] * n_vmem + [ANY] * n,
        scratch_shapes=scratch,
        compiler_params=params(cid),
        name="join_forward",
        cost_estimate=lasts(50 if n else 22),
    )(*ops)


def backward_kernel(
    out_term, gathers, part, extra, onward, v, vecs, back, other, grad_all, stats, *scratch
):
    hd = Head()
    bar = pltpu.get_barrier_semaphore()
    pl.semaphore_wait(bar, greet_head(bar, hd))
    summed = HeadSum(hd, part, *scratch[:3], scratch[3:5])
    scratch = scratch[5:]
    second = None
    if extra is not None:
        second = HeadSum(hd, extra, *scratch[:3], scratch[3:5])
        scratch = scratch[5:]
    summed.begin()
    summed.middle()
    if second is not None:
        second.begin()
        second.middle()
    dv, d_gain, d_shift = layer_norm_back(v[...], summed.total(), vecs[0:1])
    d = dv + onward[...].astype(f32)
    back[...] = d
    rounded = d.astype(bf16)
    if gathers:
        grad_all[hd.me] = rounded
        spread = HeadGather(hd, grad_all, *scratch)
        spread.begin()
        spread.forward()
    if second is not None:
        more = second.total()
        if out_term:
            more = v[...] + more + vecs[1:2]
        other[...] = more.astype(other.dtype)
    stats[0:1] = d_gain
    stats[1:2] = d_shift
    stats[2:3] = jnp.sum(rounded.astype(f32), axis=0, keepdims=True)
    if gathers:
        spread.arrive()
        spread.drain()
    summed.finish()
    if second is not None:
        second.finish()


def join_backward(part, onward, v, gain, cid, extra=None, bias=None, gathers=True):
    rows, width = onward.shape
    has_extra = extra is not None
    out_term = bias is not None
    vecs = jnp.stack((gain, bias if out_term else gain))

    def kernel(*refs):
        refs = list(refs)
        part_ref = refs.pop(0)
        extra_ref = refs.pop(0) if has_extra else None
        onward_ref, v_ref, vecs_ref, back = (refs.pop(0) for _ in range(4))
        other = refs.pop(0) if has_extra else None
        grad_all = refs.pop(0) if gathers else None
        stats = refs.pop(0)
        backward_kernel(
            out_term, gathers, part_ref, extra_ref, onward_ref, v_ref, vecs_ref,
            back, other, grad_all, stats, *refs,
        )

    shapes = [jax.ShapeDtypeStruct((rows, width), f32)]
    if has_extra:
        shapes.append(jax.ShapeDtypeStruct((rows, width), bf16 if out_term else f32))
    if gathers:
        shapes.append(jax.ShapeDtypeStruct((4, rows, width), bf16))
    shapes.append(jax.ShapeDtypeStruct((8, width), f32))
    scratch = head_sum_scratch(rows, width)
    if has_extra:
        scratch = scratch + head_sum_scratch(rows, width)
    if gathers:
        scratch = scratch + [DMA((3,)), DMA((4,))]
    ops = [part] + ([extra] if has_extra else []) + [onward, v, vecs]
    return pl.pallas_call(
        kernel,
        out_shape=shapes,
        in_specs=[VMEM] * len(ops),
        out_specs=[VMEM] * len(shapes),
        scratch_shapes=scratch,
        compiler_params=params(cid),
        name="join_backward",
        cost_estimate=lasts(24),
    )(*ops)


def tie(value, *others):
    return lax.optimization_barrier((value,) + others)


def stack_heads(rows, scale):
    lane = lax.broadcasted_iota(jnp.int32, rows.shape, 1) // HEAD_DIM
    pieces = [
        jnp.where(lane == h, rows.astype(f32) * scale, 0.0).astype(bf16) for h in range(HEADS_HERE)
    ]
    return jnp.concatenate(pieces, axis=0)


def take_heads(wide, rows):
    pieces = [
        wide[h * HEAD_DIM : (h + 1) * HEAD_DIM, h * rows : (h + 1) * rows]
        for h in range(HEADS_HERE)
    ]
    return jnp.concatenate(pieces, axis=0).T


def masked_scores(keys, stacked, first, low, high):
    scores = dot(keys, stacked, NT)
    key_pos = first + lax.broadcasted_iota(jnp.int32, scores.shape, 0)
    return jnp.where((key_pos >= low) & (key_pos < high), scores, -1e30)


def attend_kernel(bounds, q, k, v, low, high, o, mix, lse, acc):
    chunks, rows, width = q.shape

    def chunk(i, carry):
        stacked = stack_heads(q[i], HEAD_DIM ** (-0.5))
        lo, hi = low[i], high[i]
        acc[...] = jnp.zeros_like(acc)

        def step(kb, state):
            top, total = state
            first = pl.multiple_of(kb * KEY_BLOCK, KEY_BLOCK)
            scores = masked_scores(k[pl.ds(first, KEY_BLOCK), :], stacked, first, lo, hi)
            new_top = jnp.maximum(top, jnp.max(scores, axis=0, keepdims=True))
            fading = jnp.exp(top - new_top)
            weights = jnp.exp(scores - new_top)
            total = total * fading + jnp.sum(weights, axis=0, keepdims=True)
            acc[...] = acc[...] * fading + dot(
                v[pl.ds(first, KEY_BLOCK), :], weights.astype(bf16), TN
            )
            return new_top, total

        wide = HEADS_HERE * rows
        top, total = lax.fori_loop(
            bounds[0, i],
            bounds[1, i],
            step,
            (jnp.full((1, wide), -1e30, f32), jnp.zeros((1, wide), f32)),
        )
        lse[i] = top + jnp.log(total)
        result = take_heads(acc[...] / total, rows)
        o[i] = result
        mix[i] = result.astype(bf16)
        return carry

    lax.fori_loop(0, chunks, chunk, 0)


def attend(q, k, v, spans):
    bounds, low, high = spans
    chunks, rows, width = q.shape
    wide = HEADS_HERE * rows
    return pl.pallas_call(
        attend_kernel,
        out_shape=(
            jax.ShapeDtypeStruct(q.shape, f32),
            jax.ShapeDtypeStruct(q.shape, bf16),
            jax.ShapeDtypeStruct((chunks, 1, wide), f32),
        ),
        in_specs=[SMEM] + [VMEM] * 5,
        out_specs=(VMEM,) * 3,
        scratch_shapes=[pltpu.VMEM((width, wide), f32)],
        compiler_params=pltpu.CompilerParams(vmem_limit_bytes=56 * 2**20),
        name="attend",
        cost_estimate=lasts(12),
    )(bounds, q, k, v, low, high)


def attend_back_kernel(
    bounds, q, k, v, low, high, d_o, o, lse, dq, dk, dk_over, dv, dv_over, dv_sum,
    qs, dos, delta, dq_acc, dk_acc, dv_acc
):
    chunks, rows, width = q.shape
    y = lax.axis_index("blk") % 2
    mine = pl.ds(pl.multiple_of(y * rows, rows), rows)
    theirs = pl.ds(pl.multiple_of((1 - y) * rows, rows), rows)
    dv_sum[...] = jnp.zeros_like(dv_sum)
    for i in range(chunks):
        qs[i] = stack_heads(q[i], HEAD_DIM ** (-0.5))
        dos[i] = stack_heads(d_o[i], 1.0)
        product = (d_o[i].astype(f32) * o[i]).T
        delta[i] = jnp.concatenate(
            [
                jnp.sum(product[h * HEAD_DIM : (h + 1) * HEAD_DIM], axis=0, keepdims=True)
                for h in range(HEADS_HERE)
            ],
            axis=1,
        )
    dq_acc[...] = jnp.zeros_like(dq_acc)

    def block(kb, carry):
        first = pl.multiple_of(kb * KEY_BLOCK, KEY_BLOCK)
        part = pl.ds(first, KEY_BLOCK)
        dk_acc[...] = jnp.zeros_like(dk_acc)
        dv_acc[...] = jnp.zeros_like(dv_acc)

        def chunk(i, inner):
            @pl.when((kb >= bounds[0, i]) & (kb < bounds[1, i]))
            def _():
                keys = k[part, :]
                scores = masked_scores(keys, qs[i], first, low[i], high[i])
                weights = jnp.exp(scores - lse[i])
                d_weights = dot(v[part, :], dos[i], NT)
                d_scores = (weights * (d_weights - delta[i])).astype(bf16)
                dv_acc[...] += dot(weights.astype(bf16), dos[i])
                dk_acc[...] += dot(d_scores, qs[i])
                dq_acc[i] += dot(keys, d_scores, TN)

            return inner

        lax.fori_loop(0, chunks, chunk, 0)
        dk[kb] = dk_acc[mine, :].astype(bf16)
        dk_over[kb] = dk_acc[theirs, :].astype(bf16)
        dv[kb] = dv_acc[mine, :].astype(bf16)
        dv_over[kb] = dv_acc[theirs, :].astype(bf16)
        dv_sum[...] += jnp.sum(dv_acc[...], axis=0, keepdims=True)
        return carry

    lax.fori_loop(0, k.shape[0] // KEY_BLOCK, block, 0)
    for i in range(chunks):
        dq[i] = (take_heads(dq_acc[i], rows) * HEAD_DIM ** (-0.5)).astype(bf16)


def attend_back(q, k, v, spans, d_o, o, lse):
    bounds, low, high = spans
    chunks, rows, width = q.shape
    wide = HEADS_HERE * rows
    half = (k.shape[0] // KEY_BLOCK, rows, width)
    return pl.pallas_call(
        attend_back_kernel,
        out_shape=(
            jax.ShapeDtypeStruct(q.shape, bf16),
            jax.ShapeDtypeStruct(half, bf16),
            jax.ShapeDtypeStruct(half, bf16),
            jax.ShapeDtypeStruct(half, bf16),
            jax.ShapeDtypeStruct(half, bf16),
            jax.ShapeDtypeStruct((1, width), f32),
        ),
        in_specs=[SMEM] + [VMEM] * 8,
        out_specs=(VMEM,) * 6,
        scratch_shapes=[
            pltpu.VMEM((chunks, wide, width), bf16),
            pltpu.VMEM((chunks, wide, width), bf16),
            pltpu.VMEM((chunks, 1, wide), f32),
            pltpu.VMEM((chunks, width, wide), f32),
            pltpu.VMEM((KEY_BLOCK, width), f32),
            pltpu.VMEM((KEY_BLOCK, width), f32),
        ],
        compiler_params=pltpu.CompilerParams(vmem_limit_bytes=60 * 2**20),
        name="attend_back",
        cost_estimate=lasts(14),
    )(bounds, q, k, v, low, high, d_o, o, lse)


def key_spans(target_lengths, source_lengths, rows, count):
    ends = jnp.cumsum(target_lengths, dtype=jnp.int32)
    starts = ends - target_lengths
    chunk = jnp.arange(4, dtype=jnp.int32) * count + lax.axis_index("blk")
    pos = chunk[:, None] * rows + jnp.arange(rows, dtype=jnp.int32)[None, :]
    past = (pos[..., None] >= ends).astype(jnp.int32)
    begun = (pos[..., None] >= starts).astype(jnp.int32)

    def spans(low, high):
        bounds = jnp.stack(
            (low[:, 0] // KEY_BLOCK, (high[:, -1] + KEY_BLOCK - 1) // KEY_BLOCK)
        ).astype(jnp.int32)
        wide = lambda a: jnp.tile(a[:, None, :], (1, 1, HEADS_HERE))
        return bounds, wide(low), wide(high)

    own = spans(jnp.sum(past * target_lengths, axis=-1), pos + 1)
    aligned = spans(
        jnp.sum(past * source_lengths, axis=-1), jnp.sum(begun * source_lengths, axis=-1)
    )
    return own, aligned


def body(
    count,
    inputs,
    encoded,
    d_output,
    target_lengths,
    source_lengths,
    norm_gain,
    norm_shift,
    self_qkv,
    self_bias,
    self_out,
    cross_q,
    cross_kv,
    cross_bias,
    cross_out,
    out_bias,
    ffn_in,
    ffn_in_bias,
    ffn_out,
):
    rows, width = inputs.shape
    devices = 4 * count
    share = width // devices
    head_width = width // 4
    hidden_width = ffn_in.shape[1]
    hidden_here = hidden_width // 4
    hidden_rows = hidden_width // width
    tokens_here = 4 * rows

    def split_cols(w):
        return jnp.transpose(w.reshape(share, -1, 4, w.shape[-1] // 4), (2, 0, 1, 3)).reshape(
            4, share, -1
        )

    w_ffn_out = lax.all_gather(ffn_out, "blk", axis=0, tiled=True)
    small = jnp.concatenate(
        (
            norm_gain,
            norm_shift,
            self_bias,
            cross_bias,
            out_bias,
            ffn_in_bias.reshape(hidden_rows, share),
        )
    )
    n_small = small.shape[0]
    small = jnp.pad(small, ((0, N_SMALL - n_small), (0, 128 - share)))
    (
        vectors, w_qkv, w_cross_kv, w_cross_q, w_self_out, w_cross_out, w_ffn_in, inputs_all,
        encoded_all, d_output_all, normed_one, q1, k1, v1, k2, v2,
    ) = front(
        small,
        [split_cols(w) for w in (self_qkv, cross_kv, cross_q)],
        self_out[None],
        cross_out[None],
        split_cols(ffn_in),
        [inputs, encoded, d_output],
        count,
        0,
    )
    w_ffn_in = lax.all_gather(w_ffn_in, "blk", axis=1, tiled=True).reshape(width, -1)
    w_qkv, w_cross_kv, w_cross_q, w_self_out, w_cross_out = (
        w.reshape(-1, w.shape[-1]) for w in (w_qkv, w_cross_kv, w_cross_q, w_self_out, w_cross_out)
    )
    encoded_all, d_output_all, normed_one = (
        a.reshape(tokens_here, width) for a in (encoded_all, d_output_all, normed_one)
    )
    head = lax.axis_index("head")
    here = lax.dynamic_index_in_dim(vectors, head, 0, keepdims=False)
    b_query = here[8:9]
    b_hidden = jnp.transpose(here[13:17].reshape(hidden_rows, count, share), (1, 0, 2)).reshape(
        1, hidden_here
    )
    vectors = jnp.transpose(vectors[:, :13], (1, 0, 2)).reshape(13, width)
    gains, shifts, b_out = vectors[0:3], vectors[3:6], vectors[10:13]

    own, aligned = key_spans(target_lengths, source_lengths, rows, count)

    def chunks(a):
        return a.reshape(4, rows, a.shape[-1])

    k1, v1 = (a.reshape(-1, head_width) for a in (k1, v1))
    o1, mix1, lse1 = attend(q1, k1, v1, own)
    first, normed_two, q2, k2, v2 = join_forward(
        mix1, w_self_out, inputs, b_out[0], gains[1], shifts[1], count, 2,
        query=(w_cross_q, b_query), stream=(k2, v2),
    )
    mix1 = mix1.reshape(tokens_here, head_width)
    normed_two = normed_two.reshape(tokens_here, width)
    k2, v2 = (a.reshape(-1, head_width) for a in (k2, v2))
    o2, mix2, lse2 = attend(q2, k2, v2, aligned)
    second, normed_three = join_forward(
        mix2, w_cross_out, first, b_out[1], gains[2], shifts[2], count, 3
    )
    mix2 = mix2.reshape(tokens_here, head_width)
    normed_three = normed_three.reshape(tokens_here, width)

    hidden = dot(normed_three, w_ffn_in) + b_hidden
    active, gelu_back = jax.vjp(partial(jax.nn.gelu, approximate=False), hidden)
    active = active.astype(bf16)
    out_part = dot(active, w_ffn_out).astype(bf16)
    grad_ffn_out = dot(active, d_output_all, TN)
    d_active = dot(d_output_all, w_ffn_out, NT)
    d_hidden = gelu_back(d_active)[0].astype(bf16)
    grad_ffn_in = dot(normed_three, d_hidden, TN)
    d_part = dot(d_hidden, w_ffn_in, NT).astype(bf16)
    ffn_grads = jnp.concatenate(
        (
            jnp.transpose(
                grad_ffn_in.astype(bf16).reshape(4, count, share, hidden_here), (1, 0, 2, 3)
            ).reshape(count, 4 * share, hidden_here),
            grad_ffn_out.astype(bf16).reshape(count, hidden_rows * share, width),
        ),
        axis=1,
    )
    d_part, ffn_grads = tie(d_part, ffn_grads)
    ffn_terms = lax.all_to_all(ffn_grads, "blk", 0, 0, tiled=True)
    d_second, layer_output, d_cross, stats_three = join_backward(
        chunks(d_part), d_output, second, gains[2], 4, extra=chunks(out_part), bias=b_out[2]
    )
    d_cross = d_cross.reshape(tokens_here, width)

    grad_cross_out = dot(mix2, d_cross, TN)
    d_o2 = chunks(dot(d_cross, w_cross_out, NT).astype(bf16))
    dq2, dk2, dk2_over, dv2, dv2_over, dv2_sum = attend_back(q2, k2, v2, aligned, d_o2, o2, lse2)
    inside = rows == 4 * share
    if inside:
        swap = [(i, i ^ 1) for i in range(count)]
        dk2_over, dv2_over = lax.ppermute((dk2_over, dv2_over), "blk", swap)
    dq2 = dq2.reshape(tokens_here, head_width)
    grad_cross_q = dot(normed_two, dq2, TN)
    d_first, d_self, stats_two = join_backward(
        chunks(dot(dq2, w_cross_q, NT).astype(bf16)), d_second, first, gains[1], 5
    )
    d_self = d_self.reshape(tokens_here, width)

    grad_self_out = dot(mix1, d_self, TN)
    d_o1 = chunks(dot(d_self, w_self_out, NT).astype(bf16))
    dq1, dk1, dk1_over, dv1, dv1_over, dv1_sum = attend_back(q1, k1, v1, own, d_o1, o1, lse1)
    ffn_terms = jnp.sum(ffn_terms.astype(f32), axis=0)
    grad_ffn_in = ffn_terms[: 4 * share].reshape(4, share, hidden_here)
    grad_ffn_out = ffn_terms[4 * share :]
    pairs = (dk1, dv1, dk2, dv2, dk1_over, dv1_over, dk2_over, dv2_over)
    if inside:
        pairs = [a.reshape(4, count // 2, 4, share, head_width) for a in pairs]
    else:
        y = lax.axis_index("blk") % 2
        pairs = [
            jnp.where(y == 0, jnp.stack((a, b), axis=1), jnp.stack((b, a), axis=1)).reshape(
                4, count, rows, head_width
            )
            for a, b in zip(pairs[:4], pairs[4:])
        ]
        pairs = scatter_blk(pairs, count, 6)

    def column_sum(gradient):
        return jnp.sum(gradient.astype(f32), axis=0, keepdims=True)

    def placed(part):
        whole = jnp.zeros((part.shape[0], 4 * part.shape[1]), f32)
        return lax.dynamic_update_slice_in_dim(whole, part, head * part.shape[1], axis=1)

    sums = placed(
        jnp.concatenate(
            (column_sum(dq1.reshape(tokens_here, -1)), dv1_sum, column_sum(dq2), dv2_sum)
        )
    )
    nothing = jnp.zeros((1, width), f32)
    vectors = jnp.concatenate(
        (
            nothing, stats_two[0:1], stats_three[0:1], nothing, stats_two[1:2], stats_three[1:2],
            sums, stats_two[2:3], stats_three[2:3], column_sum(d_output),
        )
    )
    table = jnp.transpose(vectors.reshape(13, devices, share), (1, 0, 2)).reshape(devices, -1)
    table = jnp.concatenate(
        (table, placed(column_sum(d_hidden)).reshape(devices, hidden_rows * share)), axis=1
    )
    table = jnp.pad(table, ((0, 0), (0, 1024 - n_small * share))).reshape(devices, 8, 128)

    got = finale(
        count,
        pairs,
        grad_cross_out.astype(bf16).reshape(1, count, share, width),
        grad_self_out.astype(bf16).reshape(1, count, share, width),
        grad_cross_q.astype(bf16).reshape(4, count, share, head_width),
        grad_ffn_in.astype(bf16),
        table,
        dq1,
        chunks(normed_one),
        chunks(encoded_all),
        w_qkv,
        w_cross_kv,
        inputs,
        d_first,
        gains[0:1],
        7,
    )

    def join_cols(g, shape):
        parts = shape[1] if len(shape) == 3 else 1
        return (
            jnp.transpose(g.reshape(4, share, parts, -1), (1, 2, 0, 3)).reshape(shape).astype(f32)
        )

    table = jnp.sum(got["out_table"], axis=0).reshape(-1)[: n_small * share].reshape(n_small, share)
    stats_one = jnp.sum(got["out_stats"], axis=0)[:2, :share]
    return (
        layer_output,
        got["out_d_inputs"],
        got["out_d_encoded"],
        jnp.concatenate((stats_one[0:1], table[1:3])),
        jnp.concatenate((stats_one[1:2], table[4:6])),
        join_cols(got["out_qkv"], self_qkv.shape),
        table[6:8],
        got["out_so"][0],
        join_cols(got["out_cq"], cross_q.shape),
        join_cols(got["out_ckv"], cross_kv.shape),
        table[8:10],
        got["out_co"][0],
        table[10:13],
        join_cols(got["out_ffn_in"], ffn_in.shape),
        table[13:].reshape(-1),
        grad_ffn_out,
    )


def solution(mesh):
    both = ("head", "blk")
    rows2, rows3, cols2 = P(both, None), P(both, None, None), P(None, both)
    return jax.shard_map(
        partial(body, mesh.shape["blk"]),
        mesh=mesh,
        in_specs=(
            rows2, rows2, rows2, P(), P(), cols2, cols2, rows3, cols2, rows2, rows2, rows3,
            cols2, rows2, cols2, rows2, P(both), rows2,
        ),
        out_specs=(
            rows2, rows2, rows2, cols2, cols2, rows3, cols2, rows2, rows2, rows3, cols2, rows2,
            cols2, rows2, P(both), rows2,
        ),
        check_vma=False,
    )
```

```python
from functools import partial

import jax
import jax.numpy as jnp
from jax import lax
from jax.experimental import pallas as pl
from jax.experimental.pallas import tpu as pltpu
from jax.sharding import PartitionSpec as P

HEAD_DIM = 64
HEADS_HERE = 4
KEY_BLOCK = 256
AHEAD = 2
SKEW = 2
MESH = pl.DeviceIdType.MESH
ANY = pl.BlockSpec(memory_space=pl.ANY)
VMEM = pl.BlockSpec(memory_space=pltpu.VMEM)
SMEM = pl.BlockSpec(memory_space=pltpu.SMEM)
DMA = pltpu.SemaphoreType.DMA
f32 = jnp.float32
bf16 = jnp.bfloat16
NT = (((1,), (1,)), ((), ()))
NN = (((1,), (0,)), ((), ()))
TN = (((0,), (0,)), ((), ()))


def dot(a, b, dims=NN):
    return lax.dot_general(a, b, dims, preferred_element_type=f32)


def params(cid):
    return pltpu.CompilerParams(
        collective_id=cid, has_side_effects=True, vmem_limit_bytes=56 * 2**20
    )


def lasts(us):
    return pl.CostEstimate(flops=int(us * 3e8), bytes_accessed=int(us * 3e5), transcendentals=0)


def remote(src, dst, ssem, rsem, device):
    return pltpu.make_async_remote_copy(
        src, dst, ssem, rsem, device_id=device, device_id_type=MESH
    )


class Head:
    def __init__(self):
        self.me = lax.axis_index("head")
        self.core = self.me % 2
        self.x = self.me // 2
        self.sib = self.me + 1 - 2 * self.core
        self.far = self.me + 2 - 4 * self.x
        self.far_sib = self.sib + 2 - 4 * self.x


class Blk:
    def __init__(self, count):
        self.me = lax.axis_index("blk")
        self.z = self.me // 2
        self.y = self.me % 2
        self.Z = count // 2
        self.across = self.me + 1 - 2 * self.y


def signal(bar, **device):
    pl.semaphore_signal(bar, inc=1, device_id=device, device_id_type=MESH)


def greet_head(bar, hd):
    for k in range(1, 4):
        signal(bar, head=(hd.me + k) % 4)
    return 3


def greet_blk(bar, bk):
    signal(bar, blk=bk.across)

    @pl.when(bk.z > 0)
    def _():
        signal(bar, blk=bk.me - 2)

    @pl.when(bk.z < bk.Z - 1)
    def _():
        signal(bar, blk=bk.me + 2)

    return 1 + jnp.where(bk.z > 0, 1, 0) + jnp.where(bk.z < bk.Z - 1, 1, 0)


class BlkGather:
    def __init__(self, bk, outs, ssem, rsem):
        self.bk, self.outs, self.ssem, self.rsem = bk, outs, ssem, rsem

    def copy(self, a, slot, way, device, src=None):
        view = self.outs[a].at[:, slot]
        return remote(
            view if src is None else src,
            view,
            self.ssem.at[a, way, slot // 2],
            self.rsem.at[a, slot],
            {"blk": device},
        )

    def start(self, a, src=None):
        bk = self.bk

        @pl.when(bk.z < bk.Z - 1)
        def _():
            self.copy(a, bk.me, 0, bk.me + 2, src).start()

        @pl.when(bk.z > 0)
        def _():
            self.copy(a, bk.me, 1, bk.me - 2, src).start()

        self.copy(a, bk.me, 2, bk.across, src).start()

    def step(self, a, k):
        bk = self.bk

        @pl.when(bk.z - k >= 0)
        def _():
            slot = bk.me - 2 * k
            self.copy(a, slot, 0, bk.me).wait_recv()

            @pl.when(bk.z < bk.Z - 1)
            def _():
                self.copy(a, slot, 0, bk.me + 2).start()

            self.copy(a, slot, 2, bk.across).start()

        @pl.when(bk.z + k < bk.Z)
        def _():
            slot = bk.me + 2 * k
            self.copy(a, slot, 0, bk.me).wait_recv()

            @pl.when(bk.z > 0)
            def _():
                self.copy(a, slot, 1, bk.me - 2).start()

            self.copy(a, slot, 2, bk.across).start()

    def arrive(self, a):
        for s in range(self.bk.Z):
            self.copy(a, 2 * s + 1 - self.bk.y, 0, self.bk.me).wait_recv()

    def drain(self, a):
        bk = self.bk
        for s in range(bk.Z):
            slot = 2 * s + bk.y

            @pl.when((s <= bk.z) & (bk.z < bk.Z - 1))
            def _():
                self.copy(a, slot, 0, bk.me).wait_send()

            @pl.when((s >= bk.z) & (bk.z > 0))
            def _():
                self.copy(a, slot, 1, bk.me).wait_send()

            self.copy(a, slot, 2, bk.me).wait_send()


N_SMALL = 24


def front_kernel(
    count, small, qkv, ckv, cq, so, co, ffn_in, inputs, encoded, d_output, *refs
):
    (
        table, bias, b_hidden, w_qkv, w_ckv, w_cq, w_so, w_co, swapped, inputs_all, encoded_all,
        d_output_all, normed, q1, k1, v1, k2, v2, small_all, vectors, lsem, hs, hr, ssem, rsem,
    ) = refs
    hd, bk = Head(), Blk(count)
    share, head_width = qkv.shape[1], q1.shape[2]
    rows, width = inputs.shape
    bar = pltpu.get_barrier_semaphore()
    pl.semaphore_wait(bar, greet_head(bar, hd) + greet_blk(bar, bk))
    ring = BlkGather(bk, (small_all, w_qkv, w_ckv, w_cq, w_so, w_co, k1, v1), ssem, rsem)
    K1, V1 = 6, 7
    pairs = (
        (small, small_all), (qkv, w_qkv), (ckv, w_ckv), (cq, w_cq), (so, w_so), (co, w_co),
        (inputs, inputs_all), (encoded, encoded_all), (ffn_in, swapped), (d_output, d_output_all),
    )
    SMALL, QKV, CKV, CQ, SO, CO, INPUTS, ENCODED, FFN_IN, D_OUTPUT = range(10)
    rows_only = (SO, CO)

    def source(a, to):
        return pairs[a][0].at[to] if a in (QKV, CKV, CQ, FFN_IN) else pairs[a][0]

    def target(a, h):
        if a in rows_only:
            return pairs[a][1].at[:, bk.me]
        return pairs[a][1].at[h] if a >= INPUTS else pairs[a][1].at[h, bk.me]

    def own(a):
        return pltpu.make_async_copy(source(a, hd.me), target(a, hd.me), lsem.at[a])

    def across_head(a, k, back):
        to = (hd.me + k) % 4
        return remote(
            source(a, to),
            target(a, to if back else hd.me),
            hs.at[a, k],
            hr.at[a, to if back else hd.me],
            {"head": to},
        )

    def headed(a):
        own(a).wait()
        for k in range(1, 4):
            across_head(a, k, True).wait_recv()

    everything = (SMALL, QKV, CKV, CQ, INPUTS, ENCODED, FFN_IN, D_OUTPUT)
    for a in everything:
        own(a).start()
        for k in (2, 1, 3):
            across_head(a, k, False).start()
    for a in rows_only:
        own(a).start()
    headed(SMALL)
    ring.start(SMALL)
    headed(QKV)
    ring.start(QKV)
    for a in rows_only:
        ring.start(a, pairs[a][0])
    headed(CKV)
    ring.start(CKV)
    headed(CQ)
    ring.start(CQ)
    for k in range(1, bk.Z):
        for a in (SMALL, QKV) + ((SO, CO, CKV, CQ) if k < bk.Z - 1 else ()):
            ring.step(a, k)
    ring.arrive(0)
    lane = lax.broadcasted_iota(jnp.int32, (N_SMALL, 128), 1)

    def assemble(h, carry):
        for group in range(head_width // 128):
            total = jnp.zeros((N_SMALL, 128), f32)
            for i in range(128 // share):
                piece = small_all[h, group * (128 // share) + i].astype(f32)
                if i:
                    piece = pltpu.roll(piece, i * share, 1)
                total = jnp.where(lane // share == i, piece, total)
            vectors[h, :, group * 128 : (group + 1) * 128] = total
        return carry

    lax.fori_loop(0, 4, assemble, 0)

    for h in range(4):
        table[:, h * head_width : (h + 1) * head_width] = vectors[h]
    bias[...] = vectors[hd.me]
    first = lax.broadcasted_iota(jnp.int32, (1, 128), 1)
    per_group = 128 // share
    for group in range(4 * count // per_group):
        total = jnp.zeros((1, 128), f32)
        for i in range(per_group):
            b, run = divmod(group * per_group + i, 4)
            piece = small_all[hd.me, b].astype(f32)[13 + run : 14 + run]
            if i:
                piece = pltpu.roll(piece, i * share, 1)
            total = jnp.where(first // share == i, piece, total)
        b_hidden[:, group * 128 : (group + 1) * 128] = total
    gain, shift = table[0:1], table[3:4]
    headed(INPUTS)

    def norm(j, carry):
        normed[j] = layer_norm(inputs_all[j].astype(f32), gain, shift).astype(bf16)
        return carry

    lax.fori_loop(0, 4, norm, 0)
    for a in (SO, CO, CKV, CQ):
        ring.step(a, bk.Z - 1)
    ring.arrive(QKV)

    def project(features, w, c, bias_row, store):
        cols = w[:, :, :, c * head_width : (c + 1) * head_width].reshape(width, head_width)

        def one(j, carry):
            out = dot(features[j], cols)
            if bias_row is not None:
                out = out + bias[bias_row : bias_row + 1, :]
            store(j, out.astype(bf16))
            return carry

        lax.fori_loop(0, 4, one, 0)

    def into(ref):
        def store(j, value):
            ref[j] = value

        return store

    def into_own(ref):
        def store(j, value):
            ref[j, bk.me] = value

        return store

    project(normed, w_qkv, 1, None, into_own(k1))
    ring.start(K1)
    project(normed, w_qkv, 2, 7, into_own(v1))
    ring.start(V1)
    project(normed, w_qkv, 0, 6, into(q1))
    headed(ENCODED)
    ring.step(K1, 1)
    ring.step(V1, 1)
    ring.arrive(CKV)
    project(encoded_all, w_ckv, 0, None, into(k2))
    project(encoded_all, w_ckv, 1, 9, into(v2))
    for k in range(2, bk.Z):
        ring.step(K1, k)
        ring.step(V1, k)
    for a in rows_only:
        own(a).wait()
    for a in (FFN_IN, D_OUTPUT):
        headed(a)
    for a in (CQ, SO, CO, K1, V1):
        ring.arrive(a)
    for a in range(8):
        ring.drain(a)
    for a in everything:
        for k in range(1, 4):
            across_head(a, k, False).wait_send()


def front(small, cols, so, co, ffn_in, acts, count, cid):
    rows, width = acts[0].shape
    share, head_width = cols[0].shape[1], width // 4
    keys = (4, count, rows, head_width)
    tokens = (4, rows, width)
    block = (4, rows, head_width)
    bf = [(4, count) + a.shape[1:] for a in cols] + [(1, count) + a.shape[1:] for a in (so, co)]
    bf += [ffn_in.shape] + [tokens] * 4 + [block, keys, keys, block, block]
    return pl.pallas_call(
        partial(front_kernel, count),
        out_shape=[
            jax.ShapeDtypeStruct((N_SMALL, width), f32),
            jax.ShapeDtypeStruct((N_SMALL, head_width), f32),
            jax.ShapeDtypeStruct((1, ffn_in.shape[2]), f32),
        ]
        + [jax.ShapeDtypeStruct(s, bf16) for s in bf],
        in_specs=[ANY] * 10,
        out_specs=[VMEM] * 5 + [ANY] * 4 + [VMEM] * 2 + [ANY] + [VMEM] * 6,
        scratch_shapes=[
            pltpu.VMEM((4, count, N_SMALL, 128), bf16),
            pltpu.VMEM((4, N_SMALL, head_width), f32),
            DMA((10,)),
            DMA((10, 4)),
            DMA((10, 4)),
            DMA((8, 3, count // 2)),
            DMA((8, count)),
        ],
        compiler_params=params(cid),
        name="front",
        cost_estimate=lasts(90),
    )(small, *cols, so, co, ffn_in, *acts)


class BlkScatter:
    def __init__(self, bk, ins, bufs, sems):
        self.bk, self.ins = bk, ins
        self.own, self.over, self.side = bufs
        self.lsem, self.ys, self.yr, self.zs, self.ur, self.dr = sems

    def load(self, a, s):
        return pltpu.make_async_copy(
            self.ins[a].at[:, 2 * s + self.bk.y], self.own[a].at[s], self.lsem.at[a, s]
        )

    def cross(self, a, s):
        return remote(
            self.ins[a].at[:, 2 * s + 1 - self.bk.y],
            self.over[a].at[s],
            self.ys.at[a, s],
            self.yr.at[a, s],
            {"blk": self.bk.across},
        )

    def send(self, a, s, upward, slot=None):
        if slot is None:
            slot = s if upward else jnp.where(s == self.bk.z - 1, self.bk.Z, s)
        return remote(
            self.own[a].at[s],
            self.side[a].at[slot],
            self.zs.at[a, s],
            (self.ur if upward else self.dr).at[a, s],
            {"blk": self.bk.me + (2 if upward else -2)},
        )

    def order(self):
        for k in range((self.bk.Z + 1) // 2):
            yield self.bk.Z - 1 - k
            if k != self.bk.Z - 1 - k:
                yield k

    def begin(self, a):
        if a < len(self.ins):
            for s in self.order():
                self.cross(a, s).start()
                self.load(a, s).start()

    def add(self, a, s, extra, store):
        groups, rows = self.own[a].shape[1:3]
        step = min(rows, 32)

        def one(g, carry):
            for r in range(0, rows, step):
                part = pl.ds(r, step)
                total = self.own[a][s, g, part].astype(f32) + self.over[a][s, g, part].astype(f32)
                for slot in extra:
                    total = total + self.side[a][slot, g, part].astype(f32)
                store(g, part, total)
            return carry

        lax.fori_loop(0, groups, one, 0)

    def relay(self, a, s, upward):
        bk = self.bk
        self.load(a, s).wait()
        self.cross(a, s).wait_recv()
        inner = (bk.z > 0) if upward else (bk.z < bk.Z - 1)

        def store(g, part, total):
            self.own[a][s, g, part] = total.astype(bf16)

        @pl.when(inner)
        def _():
            self.send(a, s, upward, s).wait_recv()
            self.add(a, s, (s,), store)

        @pl.when(jnp.logical_not(inner))
        def _():
            self.add(a, s, (), store)

        self.send(a, s, upward).start()

    def run(self, finish):
        bk, n = self.bk, len(self.ins)
        for a in range(n):
            self.begin(a + AHEAD)
            for k in range(bk.Z - 1):

                @pl.when(bk.Z - 1 - k > bk.z)
                def _():
                    self.relay(a, bk.Z - 1 - k, True)

                @pl.when(k < bk.z)
                def _():
                    self.relay(a, k, False)

            if a > 0:
                finish(a - 1)
        finish(n - 1)

    def last(self, a, store):
        bk, s = self.bk, self.bk.z
        self.load(a, s).wait()
        self.cross(a, s).wait_recv()

        @pl.when(bk.z > 0)
        def _():
            self.send(a, s, True, s).wait_recv()

        @pl.when(bk.z < bk.Z - 1)
        def _():
            self.send(a, s, False, bk.Z).wait_recv()

        @pl.when((bk.z > 0) & (bk.z < bk.Z - 1))
        def _():
            self.add(a, s, (s, bk.Z), store)

        @pl.when((bk.z > 0) & (bk.z == bk.Z - 1))
        def _():
            self.add(a, s, (s,), store)

        @pl.when((bk.z == 0) & (bk.z < bk.Z - 1))
        def _():
            self.add(a, s, (bk.Z,), store)

    def finish(self):
        bk = self.bk
        for a in range(len(self.ins)):
            for s in range(bk.Z):
                self.cross(a, s).wait_send()

                @pl.when(s != bk.z)
                def _():
                    self.send(a, s, True, s).wait_send()


def scatter_scratch(items, count):
    Z = count // 2
    kinds = [
        pltpu.VMEM((slots, a.shape[0]) + a.shape[2:], bf16)
        for slots in (Z, Z, Z + 1)
        for a in items
    ]
    return kinds + [DMA((len(items), Z)) for _ in range(6)]


def scatter_parts(refs, n):
    bufs = tuple(refs[k * n : (k + 1) * n] for k in range(3))
    return bufs, refs[3 * n : 3 * n + 6], refs[3 * n + 6 :]


def scatter_blk_kernel(count, n, *refs):
    ins, outs = refs[:n], refs[n : 2 * n]
    bufs, sems, _ = scatter_parts(refs[2 * n :], n)
    bk = Blk(count)
    bar = pltpu.get_barrier_semaphore()
    pl.semaphore_wait(bar, greet_blk(bar, bk))
    ring = BlkScatter(bk, ins, bufs, sems)
    for a in range(AHEAD):
        ring.begin(a)

    def finish(a):
        def store(g, part, total):
            outs[a][g, part] = total.astype(outs[a].dtype)

        ring.last(a, store)

    ring.run(finish)
    ring.finish()


def scatter_blk(items, count, cid):
    n = len(items)
    return pl.pallas_call(
        partial(scatter_blk_kernel, count, n),
        out_shape=[
            jax.ShapeDtypeStruct((a.shape[0],) + a.shape[2:], a.dtype) for a in items
        ],
        in_specs=[ANY] * n,
        out_specs=[VMEM] * n,
        scratch_shapes=scatter_scratch(items, count),
        compiler_params=params(cid),
        name="scatter_blk",
        cost_estimate=lasts(60),
    )(*items)


class HeadSum:
    def __init__(self, hd, part, near, mid, far, sems):
        self.hd, self.part, self.near, self.mid, self.far = hd, part, near, mid, far
        self.ss, self.rs = sems

    def near_copy(self, i):
        hd = self.hd
        block = hd.far_sib if i == 0 else hd.sib
        return remote(
            self.part.at[block], self.near.at[i], self.ss.at[i], self.rs.at[i], {"head": hd.sib}
        )

    def far_copy(self):
        return remote(self.mid, self.far, self.ss.at[2], self.rs.at[2], {"head": self.hd.far})

    def begin(self):
        self.near_copy(0).start()
        self.near_copy(1).start()

    def middle(self):
        self.near_copy(0).wait_recv()
        mine = self.part[self.hd.far].astype(f32)
        self.mid[...] = (mine + self.near[0].astype(f32)).astype(bf16)
        self.far_copy().start()

    def total(self):
        self.near_copy(1).wait_recv()
        mine = self.part[self.hd.me].astype(f32) + self.near[1].astype(f32)
        self.far_copy().wait_recv()
        return mine + self.far[...].astype(f32)

    def finish(self):
        self.near_copy(0).wait_send()
        self.near_copy(1).wait_send()
        self.far_copy().wait_send()


def head_sum_scratch(rows, width):
    return [
        pltpu.VMEM((2, rows, width), bf16),
        pltpu.VMEM((rows, width), bf16),
        pltpu.VMEM((rows, width), bf16),
        DMA((3,)),
        DMA((3,)),
    ]


class HeadGather:
    def __init__(self, hd, out, ss, rs):
        self.hd, self.out, self.ss, self.rs = hd, out, ss, rs

    def copy(self, slot, way, device):
        view = self.out.at[slot]
        return remote(view, view, self.ss.at[way], self.rs.at[slot], {"head": device})

    def begin(self):
        hd = self.hd
        self.copy(hd.me, 0, hd.far).start()
        self.copy(hd.me, 1, hd.sib).start()

    def forward(self):
        hd = self.hd
        self.copy(hd.far, 0, hd.me).wait_recv()
        self.copy(hd.far, 2, hd.sib).start()

    def arrive(self):
        hd = self.hd
        self.copy(hd.sib, 0, hd.me).wait_recv()
        self.copy(hd.far_sib, 0, hd.me).wait_recv()

    def drain(self):
        hd = self.hd
        self.copy(hd.me, 0, hd.far).wait_send()
        self.copy(hd.me, 1, hd.sib).wait_send()
        self.copy(hd.far, 2, hd.sib).wait_send()


def row_stats(v):
    average = jnp.mean(v, axis=-1, keepdims=True)
    centred = v - average
    spread = jnp.mean(centred * centred, axis=-1, keepdims=True)
    return centred, lax.rsqrt(spread + 1e-05)


def layer_norm(v, gain, shift):
    centred, r = row_stats(v)
    return centred * r * gain + shift


def layer_norm_back(v, g, gain):
    centred, r = row_stats(v)
    u = centred * r
    c = g * gain
    dv = r * (c - jnp.mean(c, axis=-1, keepdims=True) - u * jnp.mean(c * u, axis=-1, keepdims=True))
    return dv, jnp.sum(g * u, axis=0, keepdims=True), jnp.sum(g, axis=0, keepdims=True)


SMALL_ROWS = (
    ("gain", 3), ("shift", 3), ("self_bias", 2), ("cross_bias", 2), ("out_bias", 3), ("ffn_bias", 4)
)
PAIRS = ("dk1", "dv1", "dk2", "dv2")


class PageScatter:
    def __init__(self, bk, feeds, bufs, sems, ready, crossed):
        self.bk, self.feeds, self.ready, self.crossed = bk, feeds, ready, crossed
        self.own, self.over, self.side = bufs
        self.lsem, self.ys, self.yr, self.zs, self.ur, self.dr = sems
        self.n = len(feeds)

    def load(self, a, s):
        copies = [
            pltpu.make_async_copy(src(s, True), self.own.at[(a, s) + dst], self.lsem.at[a, s, i])
            for i, (src, dst) in enumerate(self.feeds[a])
        ]
        if a in self.crossed:
            copies += [
                pltpu.make_async_copy(
                    src(s, False), self.over.at[(a, s) + dst], self.yr.at[a, s, i]
                )
                for i, (src, dst) in enumerate(self.feeds[a])
            ]
        return copies

    def cross(self, a, s):
        if a in self.crossed:
            return []
        return [
            remote(
                src(s, False),
                self.over.at[(a, s) + dst],
                self.ys.at[a, s, i],
                self.yr.at[a, s, i],
                {"blk": self.bk.across},
            )
            for i, (src, dst) in enumerate(self.feeds[a])
        ]

    def begin(self, a):
        Z = self.bk.Z
        for k in range(Z):
            s = Z - 1 - k // 2 if k % 2 == 0 else k // 2
            for copy in self.cross(a, s) + self.load(a, s):
                copy.start()

    def send(self, a, s, upward, slot=None):
        bk = self.bk
        if slot is None:
            slot = s if upward else jnp.where(s == bk.z - 1, bk.Z, s)
        return remote(
            self.own.at[a, s],
            self.side.at[a, slot],
            self.zs.at[a, s],
            (self.ur if upward else self.dr).at[a, s],
            {"blk": bk.me + (2 if upward else -2)},
        )

    def gathered(self, a):
        for s in range(self.bk.Z):
            for copy in self.load(a, s):
                copy.wait()
            for copy in self.cross(a, s):
                copy.wait_recv()

    def relay(self, a, s, upward):
        bk = self.bk
        inner = (bk.z > 0) if upward else (bk.z < bk.Z - 1)

        @pl.when(inner)
        def _():
            self.send(a, s, upward, s).wait_recv()
            self.own[a, s] = (
                self.own[a, s].astype(f32)
                + self.over[a, s].astype(f32)
                + self.side[a, s].astype(f32)
            ).astype(bf16)

        @pl.when(jnp.logical_not(inner))
        def _():
            self.own[a, s] = (
                self.own[a, s].astype(f32) + self.over[a, s].astype(f32)
            ).astype(bf16)

        self.send(a, s, upward).start()

    def wave(self, t):
        bk = self.bk
        if t < self.n:
            self.gathered(t)
        up, down = t - SKEW * bk.z, t - SKEW * (bk.Z - 1 - bk.z)

        @pl.when((up >= 0) & (up < self.n))
        def _():
            def one(i, carry):
                self.relay(up, bk.Z - 1 - i, True)
                return carry

            lax.fori_loop(0, bk.Z - 1 - bk.z, one, 0)

        @pl.when((down >= 0) & (down < self.n))
        def _():
            def one(i, carry):
                self.relay(down, i, False)
                return carry

            lax.fori_loop(0, bk.z, one, 0)

        a = t - SKEW * (bk.Z - 1)
        if a >= 0:
            self.last(a)

    def last(self, a):
        bk, s = self.bk, self.bk.z
        total = self.own[a, s].astype(f32) + self.over[a, s].astype(f32)

        @pl.when(bk.z > 0)
        def _():
            self.send(a, s, True, s).wait_recv()

        @pl.when(bk.z < bk.Z - 1)
        def _():
            self.send(a, s, False, bk.Z).wait_recv()

        total = total + jnp.where(bk.z > 0, self.side[a, s].astype(f32), 0.0)
        total = total + jnp.where(bk.z < bk.Z - 1, self.side[a, bk.Z].astype(f32), 0.0)
        self.ready[a](total)

    def drain(self):
        bk = self.bk
        for a in range(self.n):
            for s in range(bk.Z):
                for copy in self.cross(a, s):
                    copy.wait_send()

                @pl.when(s != bk.z)
                def _():
                    self.send(a, s, True, s).wait_send()


def finale_kernel(count, inside, names_in, names_out, names_scratch, *refs):
    r = dict(zip(names_in + names_out + names_scratch, refs))
    hd, bk = Head(), Blk(count)
    devices = 4 * count
    me = hd.me * count + bk.me
    rows, width = r["d_first"].shape
    head_width = width // 4
    share = width // devices
    bar = pltpu.get_barrier_semaphore()

    def place(k):
        to = (me + k) % devices
        return to, {"head": to // count, "blk": to % count}

    def greet(k, carry):
        signal(bar, **place(k)[1])
        return carry

    lax.fori_loop(1, devices, greet, 0)
    pl.semaphore_wait(bar, devices - 1)

    def tiles(src, dst, which):
        local = pltpu.make_async_copy(src.at[me], dst.at[me], r["tile_local"].at[which])

        def copy(k, back):
            to, device = place(k)
            return remote(
                src.at[to],
                dst.at[to if back else me],
                r["tile_send"].at[which, k],
                r["tile_recv"].at[which, to if back else me],
                device,
            )

        def start(k, carry):
            copy(k, False).start()
            return carry

        def end(k, carry):
            copy(k, False).wait_send()
            copy(k, True).wait_recv()
            return carry

        def begin():
            local.start()
            lax.fori_loop(1, devices, start, 0)

        def finish():
            local.wait()
            lax.fori_loop(1, devices, end, 0)

        return begin, finish

    headed = ["ffn_in", "cq", "qkv", "ckv"]

    def across_head(n, k, back):
        a = headed.index(n)
        to = (hd.me + k) % 4
        src = r["ffn_in"] if n == "ffn_in" else r["done_" + n]
        return remote(
            src.at[to],
            r["out_" + n].at[to if back else hd.me],
            r["head_send"].at[a, k],
            r["head_recv"].at[a, to if back else hd.me],
            {"head": to},
        )

    def send_heads(n):
        for k in range(1, 4):
            across_head(n, k, False).start()
        src = r["ffn_in"] if n == "ffn_in" else r["done_" + n]
        r["out_" + n][hd.me] = src[hd.me]

    def place_of(s, mine):
        return 2 * s + (bk.y if mine else 1 - bk.y)

    def col_page(ref, c):
        def src(s, mine):
            return ref.at[:, place_of(s, mine), :, c * head_width : (c + 1) * head_width]

        return [(src, ())]

    def row_page(ref):
        def src(j):
            return lambda s, mine: ref.at[
                0, place_of(s, mine), :, j * head_width : (j + 1) * head_width
            ]

        return [(src(j), (j,)) for j in range(4)]

    def pair_page(n, h):
        return [(lambda s, mine: r[n if mine else n + "_over"].at[h, s], ())]

    def store_pair(n, h):
        def store(total):
            r["sum_" + n][h] = total.reshape(rows, head_width).astype(bf16)

        return store

    def store_col(n, c):
        def store(total):
            r["done_" + n][:, :, c * head_width : (c + 1) * head_width] = total.astype(bf16)

        return store

    def store_row(n):
        def store(total):
            for j in range(4):
                r["out_" + n][0, :, j * head_width : (j + 1) * head_width] = total[j]

        return store

    feeds, ready, crossed, index = [], [], [], {}

    def item(name, feed, store):
        index[name] = len(feeds)
        feeds.append(feed)
        ready.append(store)

    if inside:
        for n, h in [(n, h) for h in range(4) for n in ("dk1", "dk2")] + [
            (n, h) for n in ("dv1", "dv2") for h in range(4)
        ]:
            if n in ("dk2", "dv2"):
                crossed.append(len(feeds))
            item(n, pair_page(n, h), store_pair(n, h))
    for n in ("so", "co"):
        item(n, row_page(r[n]), store_row(n))
    item("cq", col_page(r["cq"], 0), store_col("cq", 0))
    item("qkv0", col_page(r["grad_qkv"], 0), store_col("qkv", 0))
    for c in (1, 2):
        item("qkv%d" % c, col_page(r["grad_qkv"], c), store_col("qkv", c))
    for c in range(2):
        item("ckv%d" % c, col_page(r["grad_ckv"], c), store_col("ckv", c))
    ring = PageScatter(
        bk, feeds, (r["own"], r["over"], r["side"]), [r["ring%d" % i] for i in range(6)], ready,
        crossed,
    )

    def summed(n):
        return r["sum_" + n] if inside else r[n]

    def fill(joined, parts, first):
        cols = slice(first, first + len(parts) * head_width)
        for j in range(4):
            joined[j * rows : (j + 1) * rows, cols] = jnp.concatenate([p[j] for p in parts], axis=1)
        return cols

    def weight_grad(joined, cols, features, grad):
        def one(g, carry):
            lhs = features[:, :, pl.ds(pl.multiple_of(g * head_width, head_width), head_width)]
            total = dot(lhs.reshape(4 * rows, head_width), joined[:, cols], TN)
            grad[g, :, :, cols] = total.reshape(grad.shape[1:3] + (-1,)).astype(bf16)
            return carry

        lax.fori_loop(0, 4, one, 0)

    def project(joined, w, out, summed_over_head):
        def term(j, carry):
            block = joined[pl.ds(pl.multiple_of(j * rows, rows), rows), :]
            out[j] = dot(block, w[...], NT).astype(bf16)
            return carry

        lax.fori_loop(0, 4, term, 0)
        summed_over_head.begin()

    stats_begin, stats_finish = tiles(r["stats_tab"], r["stats_got"], 0)
    first, second = (
        HeadSum(
            hd, r["part%d" % (i + 1)], r["near%d" % i], r["mid%d" % i], r["far%d" % i],
            (r["sum_send%d" % i], r["sum_recv%d" % i]),
        )
        for i in range(2)
    )

    def query_part():
        cols = fill(r["joined1"], [r["dq1"]], 0)
        weight_grad(r["joined1"], cols, r["normed"], r["grad_qkv"])
        ring.begin(index["qkv0"])

    def self_part():
        cols = fill(r["joined1"], [summed("dk1"), summed("dv1")], head_width)
        weight_grad(r["joined1"], cols, r["normed"], r["grad_qkv"])
        for c in (1, 2):
            ring.begin(index["qkv%d" % c])
        project(r["joined1"], r["w_qkv"], r["part1"], first)

    def cross_part():
        cols = fill(r["joined2"], [summed("dk2"), summed("dv2")], 0)
        weight_grad(r["joined2"], cols, r["encoded"], r["grad_ckv"])
        for c in range(2):
            ring.begin(index["ckv%d" % c])
        project(r["joined2"], r["w_ckv"], r["part2"], second)

    def self_end():
        dv, d_gain, d_shift = layer_norm_back(
            r["inputs"][...].astype(f32), first.total(), r["gain"][...]
        )
        r["out_d_inputs"][...] = dv + r["d_first"][...]
        two, three = r["stats_two"], r["stats_three"]

        def placed(row):
            return jnp.concatenate(
                [jnp.where(hd.me == h, row, 0.0) for h in range(4)], axis=1
            )

        rows_of = [
            d_gain, two[0:1], three[0:1], d_shift, two[1:2], three[1:2],
            placed(r["sums_one"][0:1]), placed(r["sums_one"][1:2]),
            placed(r["sums_two"][0:1]), placed(r["sums_two"][1:2]),
            two[2:3], three[2:3], three[3:4],
        ]
        whole = jnp.concatenate(rows_of + [jnp.zeros((N_SMALL - 13, width), f32)], axis=0)
        hidden = r["d_hidden"][...]

        def turned(value, lane):
            tile = value[:, lane // 128 * 128 : lane // 128 * 128 + 128]
            return pltpu.roll(tile, 128 - lane % 128, 1) if lane % 128 else tile

        for d in range(devices):
            r["stats_tab"][d] = turned(whole, d * share)
            h, b = divmod(d, count)
            for run in range(4):
                mine = turned(hidden, (4 * b + run) * share)
                r["stats_tab"][d, 13 + run : 14 + run, :] = jnp.where(hd.me == h, mine, 0.0)
        stats_begin()

    def sum_ffn():
        def one(i, carry):
            part = pl.ds(pl.multiple_of(i * share, share), share)
            total = r["ffn_terms"][0, part, :].astype(f32)
            for b in range(1, count // 2):
                total = total + r["ffn_terms"][b, part, :].astype(f32)

            @pl.when(i < 4)
            def _():
                r["ffn_in"][i] = total.astype(bf16)

            @pl.when(i >= 4)
            def _():
                r["out_ffn_out"][pl.ds(pl.multiple_of((i - 4) * share, share), share), :] = total

            return carry

        lax.fori_loop(0, 8, one, 0)
        send_heads("ffn_in")

    lag = SKEW * (bk.Z - 1)
    for a in range(index["cq"] + 1):
        ring.begin(a)
    sum_ffn()
    query_part()
    if inside:
        after_cross, after_self = index["dv2"] + lag, index["dv1"] + lag
    else:
        self_part()
        cross_part()
        after_cross, after_self = 3, 0
    for t in range(ring.n + lag):
        ring.wave(t)
        if inside and t == after_self:
            self_part()
        if t == after_self + 2:
            first.middle()
        if inside and t == after_cross:
            cross_part()
        if t == after_cross + 1:
            self_end()
        if t == after_cross + 3:
            second.middle()
        if t == index["cq"] + lag:
            send_heads("cq")
        if t == index["qkv2"] + lag:
            send_heads("qkv")
    send_heads("ckv")
    r["out_d_encoded"][...] = second.total()
    ring.drain()
    first.finish()
    second.finish()
    for n in headed:
        for k in range(1, 4):
            across_head(n, k, False).wait_send()
            across_head(n, k, True).wait_recv()
    stats_finish()
    total = r["stats_got"][0]
    for d in range(1, devices):
        total = total + r["stats_got"][d]
    r["out_stats"][...] = total


def settle_kernel(names, *refs):
    r = dict(zip(names, refs[:-1]))
    sems = refs[-1]
    copies = [
        pltpu.make_async_copy(r[name], r["here_" + name[4:]], sems.at[i])
        for i, name in enumerate([n for n in names if n.startswith("got_")])
    ]
    for copy in copies:
        copy.start()
    for copy in copies:
        copy.wait()
    for name in ("ffn_in", "cq", "ckv", "qkv"):
        got, out = r["here_" + name], r["out_" + name]
        parts = out.shape[1] if len(out.shape) == 3 else 1
        step = got.shape[2] // parts
        for h in range(4):
            for c in range(parts):
                value = got[h, :, c * step : (c + 1) * step].astype(f32)
                if parts == 1:
                    out[:, h * step : (h + 1) * step] = value
                else:
                    out[:, c, h * step : (h + 1) * step] = value
    for name in ("d_inputs", "d_encoded", "ffn_out", "layer"):
        r["out_" + name][...] = r["here_" + name][...]
    for name in ("co", "so"):
        r["out_" + name][...] = r["here_" + name][0]
    row = 0
    for name, number in SMALL_ROWS:
        out = r["out_" + name]
        out[...] = r["here_stats"][row : row + number, : out.shape[1]]
        row += number


def settle(got, layer_output, share, width, hidden_width):
    rows = layer_output.shape[0]
    ins = {"got_" + n[4:]: a for n, a in got.items()}
    ins["got_layer"] = layer_output
    outs = dict(
        out_layer=((rows, width), bf16),
        out_d_inputs=((rows, width), f32),
        out_d_encoded=((rows, width), f32),
        out_qkv=((share, 3, width), f32),
        out_ckv=((share, 2, width), f32),
        out_cq=((share, width), f32),
        out_ffn_in=((share, hidden_width), f32),
        out_ffn_out=(got["out_ffn_out"].shape, f32),
        out_co=((share, width), f32),
        out_so=((share, width), f32),
    )
    outs.update({"out_" + n: ((number, share), f32) for n, number in SMALL_ROWS})
    here = {"here_" + n[4:]: pltpu.VMEM(a.shape, a.dtype) for n, a in ins.items()}
    done = pl.pallas_call(
        partial(settle_kernel, tuple(ins) + tuple(outs) + tuple(here)),
        out_shape=[jax.ShapeDtypeStruct(*o) for o in outs.values()],
        in_specs=[ANY] * len(ins),
        out_specs=[VMEM] * len(outs),
        scratch_shapes=list(here.values()) + [DMA((len(ins),))],
        compiler_params=pltpu.CompilerParams(vmem_limit_bytes=60 * 2**20),
        name="settle",
        cost_estimate=lasts(4),
    )(*ins.values())
    return dict(zip(outs, done))


def finale(
    count, pairs, co, so, cq, ffn_terms, dq1, normed, encoded, w_qkv, w_ckv, inputs, d_first, gain,
    stats_two, stats_three, sums_one, sums_two, d_hidden, cid,
):
    inside = len(pairs) == 8
    devices, Z = 4 * count, count // 2
    rows, width = inputs.shape
    share = width // devices
    head_width = w_ckv.shape[1] // 2
    hidden_width = ffn_terms.shape[2]
    ins = dict(zip(PAIRS + tuple(n + "_over" for n in PAIRS), pairs))
    ins.update(co=co, so=so, cq=cq)
    in_specs = [ANY if inside else VMEM] * len(pairs) + [ANY] * 3
    rest = dict(
        ffn_terms=ffn_terms, dq1=dq1, normed=normed, encoded=encoded, w_qkv=w_qkv, w_ckv=w_ckv,
        inputs=inputs, d_first=d_first, gain=gain, stats_two=stats_two, stats_three=stats_three,
        sums_one=sums_one, sums_two=sums_two, d_hidden=d_hidden,
    )
    ins.update(rest)
    in_specs += [VMEM] * len(rest)
    outs = dict(
        out_d_inputs=((rows, width), f32),
        out_d_encoded=((rows, width), f32),
        out_qkv=((4, share, 3 * head_width), bf16),
        out_ckv=((4, share, 2 * head_width), bf16),
        out_cq=((4, share, head_width), bf16),
        out_ffn_in=((4, share, hidden_width), bf16),
        out_ffn_out=((4 * share, width), f32),
        out_co=((1, share, width), f32),
        out_so=((1, share, width), f32),
        out_stats=((N_SMALL, 128), f32),
    )
    grads = dict(
        grad_qkv=(4, count, share, 3 * head_width), grad_ckv=(4, count, share, 2 * head_width)
    )
    scratch = {}
    n_items = 24 if inside else 8
    for kind, slots in (("own", Z), ("over", Z), ("side", Z + 1)):
        scratch[kind] = pltpu.VMEM((n_items, slots, 4, share, head_width), bf16)
    for n, wide in (("cq", 1), ("qkv", 3), ("ckv", 2)):
        scratch["done_" + n] = pltpu.VMEM((4, share, wide * head_width), bf16)
    scratch["ffn_in"] = pltpu.VMEM((4, share, hidden_width), bf16)
    if inside:
        for n in PAIRS:
            scratch["sum_" + n] = pltpu.VMEM((4, rows, head_width), bf16)
    for n, shape in grads.items():
        scratch[n] = pltpu.VMEM(shape, bf16)
    for i, n in enumerate(("1", "2")):
        scratch["part" + n] = pltpu.VMEM((4, rows, width), bf16)
        scratch["joined" + n] = pltpu.VMEM((4 * rows, (3 - i) * head_width), bf16)
        kinds = head_sum_scratch(rows, width)
        for name, kind in zip(("near", "mid", "far", "sum_send", "sum_recv"), kinds):
            scratch[name + str(i)] = kind
    for n in ("stats_tab", "stats_got"):
        scratch[n] = pltpu.VMEM((devices, N_SMALL, 128), f32)
    for i in range(6):
        scratch["ring%d" % i] = DMA((n_items, Z, 4) if i < 3 else (n_items, Z))
    scratch["tile_local"] = DMA((1,))
    scratch["tile_send"] = DMA((1, devices))
    scratch["tile_recv"] = DMA((1, devices))
    scratch["head_send"] = DMA((4, 4))
    scratch["head_recv"] = DMA((4, 4))
    got = pl.pallas_call(
        partial(finale_kernel, count, inside, tuple(ins), tuple(outs), tuple(scratch)),
        out_shape=[jax.ShapeDtypeStruct(*o) for o in outs.values()],
        in_specs=in_specs,
        out_specs=[VMEM] * len(outs),
        scratch_shapes=list(scratch.values()),
        compiler_params=params(cid),
        name="finale",
        cost_estimate=lasts(150),
    )(*ins.values())
    return dict(zip(outs, got))


def forward_kernel(count, n_stream, has_query, layer, *refs):
    refs = list(refs)
    mix, w_out, base, table = (refs.pop(0) for _ in range(4))
    w_query, b_query = (refs.pop(0) for _ in range(2)) if has_query else (None, None)
    stream_in = [refs.pop(0) for _ in range(n_stream)]
    total, normed = (refs.pop(0) for _ in range(2))
    query = refs.pop(0) if has_query else None
    stream_out = [refs.pop(0) for _ in range(n_stream)]
    part, near, mid, far, ss, rs, gs, gr = (refs.pop(0) for _ in range(8))
    hd, bk = Head(), Blk(count)
    bar = pltpu.get_barrier_semaphore()
    greeted = greet_head(bar, hd)
    if n_stream:
        greeted = greeted + greet_blk(bar, bk)
    pl.semaphore_wait(bar, greeted)
    ring = None
    if n_stream:
        lsem, ssem, rsem = refs
        ring = BlkGather(bk, stream_out, ssem, rsem)
        for a in range(n_stream):
            ring.start(a, stream_in[a])
            pltpu.make_async_copy(stream_in[a], stream_out[a].at[:, bk.me], lsem.at[a]).start()

    def term(j):
        part[j] = dot(mix[j], w_out[...]).astype(bf16)

    summed = HeadSum(hd, part, near, mid, far, (ss, rs))
    term(hd.far_sib)
    summed.near_copy(0).start()
    term(hd.sib)
    summed.near_copy(1).start()
    term(hd.far)
    summed.middle()
    term(hd.me)
    v = base[...].astype(f32) + summed.total() + table[10 + layer : 11 + layer]
    total[...] = v
    gain, shift = table[layer + 1 : layer + 2], table[layer + 4 : layer + 5]
    normed[hd.me] = layer_norm(v, gain, shift).astype(bf16)
    spread = HeadGather(hd, normed, gs, gr)
    spread.begin()

    def ask(j):
        if has_query:
            query[j] = (dot(normed[j], w_query[...]) + b_query[8:9]).astype(bf16)

    def step(k):
        for a in range(n_stream):
            ring.step(a, k)

    ask(hd.me)
    if n_stream:
        step(1)
    spread.forward()
    ask(hd.far)
    spread.arrive()
    ask(hd.sib)
    ask(hd.far_sib)
    if n_stream:
        for k in range(2, bk.Z):
            step(k)
        for a in range(n_stream):
            ring.arrive(a)
            ring.drain(a)
            pltpu.make_async_copy(stream_in[a], stream_out[a].at[:, bk.me], lsem.at[a]).wait()
    spread.drain()
    summed.finish()


def join_forward(mix, w_out, base, table, layer, count, cid, query=None, stream=()):
    rows, width = base.shape
    n = len(stream)
    ops = [mix, w_out, base, table] + list(query or ()) + list(stream)
    shapes = [
        jax.ShapeDtypeStruct((rows, width), f32),
        jax.ShapeDtypeStruct((4, rows, width), bf16),
    ]
    if query:
        shapes.append(jax.ShapeDtypeStruct(mix.shape, bf16))
    n_vmem = len(shapes)
    shapes += [jax.ShapeDtypeStruct((4, count) + a.shape[1:], bf16) for a in stream]
    scratch = [pltpu.VMEM((4, rows, width), bf16)] + head_sum_scratch(rows, width)
    scratch += [DMA((3,)), DMA((4,))]
    if n:
        scratch += [DMA((n,)), DMA((n, 3, count // 2)), DMA((n, count))]
    return pl.pallas_call(
        partial(forward_kernel, count, n, query is not None, layer),
        out_shape=shapes,
        in_specs=[VMEM] * (len(ops) - n) + [ANY] * n,
        out_specs=[VMEM] * n_vmem + [ANY] * n,
        scratch_shapes=scratch,
        compiler_params=params(cid),
        name="join_forward",
        cost_estimate=lasts(50 if n else 22),
    )(*ops)


def backward_kernel(count, layer, has_extra, *refs):
    refs = list(refs)
    if has_extra:
        part, extra = (refs.pop(0) for _ in range(2))
    else:
        dq, w_in, normed = (refs.pop(0) for _ in range(3))
    onward, v, table, w_out, mix = (refs.pop(0) for _ in range(5))
    back, stats, d_o, grad_out = (refs.pop(0) for _ in range(4))
    other = refs.pop(0)
    grad_all = refs.pop(0)
    sums = [refs.pop(0) for _ in range(5)]
    hd = Head()
    head_width = mix.shape[2]
    tokens = 4 * mix.shape[1]
    bar = pltpu.get_barrier_semaphore()
    pl.semaphore_wait(bar, greet_head(bar, hd))
    if has_extra:
        second = HeadSum(hd, extra, *refs[:3], refs[3:5])
        refs = refs[5:]
    else:
        part = refs.pop(0)
    summed = HeadSum(hd, part, *sums[:3], sums[3:])
    if has_extra:
        summed.begin()
        summed.middle()
        second.begin()
        second.middle()
    else:

        def term(j):
            part[j] = dot(dq[j], w_in[...], NT).astype(bf16)

        term(hd.far_sib)
        summed.near_copy(0).start()
        term(hd.sib)
        summed.near_copy(1).start()
        term(hd.far)
        summed.middle()
        term(hd.me)
        all_dq = dq[...].reshape(tokens, head_width)

        def weight(g, carry):
            lhs = normed[:, :, pl.ds(pl.multiple_of(g * head_width, head_width), head_width)]
            other[g] = (
                dot(lhs.reshape(tokens, head_width), all_dq, TN).reshape(other.shape[1:]).astype(bf16)
            )
            return carry

        lax.fori_loop(0, 4, weight, 0)
    gain = table[layer : layer + 1]
    dv, d_gain, d_shift = layer_norm_back(v[...], summed.total(), gain)
    d = dv + onward[...].astype(f32)
    back[...] = d
    rounded = d.astype(bf16)
    grad_all[hd.me] = rounded
    spread = HeadGather(hd, grad_all, *refs)
    spread.begin()
    stats[0:1] = d_gain
    stats[1:2] = d_shift
    stats[2:3] = jnp.sum(rounded.astype(f32), axis=0, keepdims=True)
    stats[3:4] = jnp.sum(onward[...].astype(f32), axis=0, keepdims=True)

    def out(j):
        d_o[j] = dot(grad_all[j], w_out[...], NT).astype(bf16)

    out(hd.me)
    if has_extra:
        other[...] = (v[...] + second.total() + table[10 + layer : 11 + layer]).astype(bf16)
    spread.forward()
    out(hd.far)
    spread.arrive()
    out(hd.sib)
    out(hd.far_sib)
    grad = dot(mix[...].reshape(tokens, head_width), grad_all[...].reshape(tokens, -1), TN)
    grad_out[0] = grad.reshape(grad_out.shape[1:]).astype(bf16)
    spread.drain()
    summed.finish()
    if has_extra:
        second.finish()


def join_backward(terms, onward, v, table, layer, w_out, mix, count, cid):
    rows, width = onward.shape
    share, head_width = width // (4 * count), mix.shape[2]
    has_extra = len(terms) == 2
    ops = list(terms) + [onward, v, table, w_out, mix]
    other = ((rows, width), bf16) if has_extra else ((4, count, share, head_width), bf16)
    shapes = [
        ((rows, width), f32),
        ((8, width), f32),
        (mix.shape, bf16),
        ((1, count, share, width), bf16),
        other,
    ]
    scratch = [pltpu.VMEM((4, rows, width), bf16)] + head_sum_scratch(rows, width)
    if has_extra:
        scratch += head_sum_scratch(rows, width)
    else:
        scratch += [pltpu.VMEM((4, rows, width), bf16)]
    scratch += [DMA((3,)), DMA((4,))]
    return pl.pallas_call(
        partial(backward_kernel, count, layer, has_extra),
        out_shape=[jax.ShapeDtypeStruct(*s) for s in shapes],
        in_specs=[VMEM] * len(ops),
        out_specs=[VMEM] * len(shapes),
        scratch_shapes=scratch,
        compiler_params=params(cid),
        name="join_backward",
        cost_estimate=lasts(24),
    )(*ops)


def feed_forward_kernel(
    normed, d_output, w_in, w_out, b_hidden, out_part, d_part, mine, theirs, d_sum, act, dh
):
    rows, width = normed.shape[1:]
    tokens = 4 * rows
    share = mine.shape[1] // 8
    first = lax.axis_index("blk") % 2 == 0
    d_sum[...] = jnp.zeros_like(d_sum)

    def block(j, carry):
        hidden = dot(normed[j], w_in[...]) + b_hidden[...]
        phi = 0.5 * (1.0 + lax.erf(hidden * (0.5**0.5)))
        active = (hidden * phi).astype(bf16)
        slope = phi + hidden * jnp.exp(-0.5 * hidden * hidden) * ((0.5 / jnp.pi) ** 0.5)
        d_hidden = (dot(d_output[j], w_out[...], NT) * slope).astype(bf16)
        act[j] = active
        dh[j] = d_hidden
        d_sum[...] += jnp.sum(d_hidden.astype(f32), axis=0, keepdims=True)
        out_part[j] = dot(active, w_out[...]).astype(bf16)
        d_part[j] = dot(d_hidden, w_in[...], NT).astype(bf16)
        return carry

    lax.fori_loop(0, 4, block, 0)
    step = width // 4
    runs = step // (8 * share)

    def weight(g, carry):
        part = pl.ds(pl.multiple_of(g * step, step), step)
        def split(total, place):
            even, odd = total[:, 0].astype(bf16), total[:, 1].astype(bf16)
            mine[place] = jnp.where(first, even, odd)
            theirs[place] = jnp.where(first, odd, even)

        total = dot(normed[:, :, part].reshape(tokens, step), dh[...].reshape(tokens, -1), TN)
        place = (slice(None), pl.ds(pl.multiple_of(g * share, share), share))
        split(total.reshape(mine.shape[0], 2, share, -1), place)
        total = dot(act[:, :, part].reshape(tokens, step), d_output[...].reshape(tokens, -1), TN)
        place = (pl.ds(g * runs, runs), slice(4 * share, None))
        split(total.reshape(runs, 2, 4 * share, -1), place)
        return carry

    lax.fori_loop(0, 4, weight, 0)


def feed_forward(normed, d_output, w_in, w_out, b_hidden, count):
    rows, width = normed.shape[1:]
    share = width // (4 * count)
    return pl.pallas_call(
        feed_forward_kernel,
        out_shape=(
            jax.ShapeDtypeStruct(normed.shape, bf16),
            jax.ShapeDtypeStruct(normed.shape, bf16),
            jax.ShapeDtypeStruct((count // 2, 8 * share, width), bf16),
            jax.ShapeDtypeStruct((count // 2, 8 * share, width), bf16),
            jax.ShapeDtypeStruct((1, w_in.shape[1]), f32),
        ),
        in_specs=[VMEM] * 5,
        out_specs=(VMEM,) * 5,
        scratch_shapes=[
            pltpu.VMEM((4, rows, w_in.shape[1]), bf16),
            pltpu.VMEM((4, rows, w_in.shape[1]), bf16),
        ],
        compiler_params=pltpu.CompilerParams(vmem_limit_bytes=56 * 2**20),
        name="feed_forward",
        cost_estimate=lasts(15),
    )(normed, d_output, w_in, w_out, b_hidden)


def tie(value, *others):
    return lax.optimization_barrier((value,) + others)


def stack_heads(rows, scale):
    lane = lax.broadcasted_iota(jnp.int32, rows.shape, 1) // HEAD_DIM
    pieces = [
        jnp.where(lane == h, rows.astype(f32) * scale, 0.0).astype(bf16) for h in range(HEADS_HERE)
    ]
    return jnp.concatenate(pieces, axis=0)


def take_heads(wide, rows):
    pieces = [
        wide[h * HEAD_DIM : (h + 1) * HEAD_DIM, h * rows : (h + 1) * rows]
        for h in range(HEADS_HERE)
    ]
    return jnp.concatenate(pieces, axis=0).T


def wide_span(spans, which, i):
    return [jnp.concatenate([spans[which, e, i]] * HEADS_HERE, axis=1) for e in range(2)]


def masked_scores(keys, stacked, first, low, high):
    scores = dot(keys, stacked, NT)
    key_pos = first + lax.broadcasted_iota(jnp.int32, scores.shape, 0)
    return jnp.where((key_pos >= low) & (key_pos < high), scores, -1e30)


def attend_kernel(which, bounds, spans, q, k, v, o, mix, lse, acc):
    chunks, rows, width = q.shape

    def chunk(i, carry):
        stacked = stack_heads(q[i], HEAD_DIM ** (-0.5))
        lo, hi = wide_span(spans, which, i)
        acc[...] = jnp.zeros_like(acc)

        def step(kb, state):
            top, total = state
            first = pl.multiple_of(kb * KEY_BLOCK, KEY_BLOCK)
            scores = masked_scores(k[pl.ds(first, KEY_BLOCK), :], stacked, first, lo, hi)
            new_top = jnp.maximum(top, jnp.max(scores, axis=0, keepdims=True))
            fading = jnp.exp(top - new_top)
            weights = jnp.exp(scores - new_top)
            total = total * fading + jnp.sum(weights, axis=0, keepdims=True)
            acc[...] = acc[...] * fading + dot(
                v[pl.ds(first, KEY_BLOCK), :], weights.astype(bf16), TN
            )
            return new_top, total

        wide = HEADS_HERE * rows
        top, total = lax.fori_loop(
            bounds[which, 0, i],
            bounds[which, 1, i],
            step,
            (jnp.full((1, wide), -1e30, f32), jnp.zeros((1, wide), f32)),
        )
        lse[i] = top + jnp.log(total)
        result = take_heads(acc[...] / total, rows)
        o[i] = result
        mix[i] = result.astype(bf16)
        return carry

    lax.fori_loop(0, chunks, chunk, 0)


def attend(q, k, v, spans, which):
    bounds, spans = spans
    chunks, rows, width = q.shape
    wide = HEADS_HERE * rows
    return pl.pallas_call(
        partial(attend_kernel, which),
        out_shape=(
            jax.ShapeDtypeStruct(q.shape, f32),
            jax.ShapeDtypeStruct(q.shape, bf16),
            jax.ShapeDtypeStruct((chunks, 1, wide), f32),
        ),
        in_specs=[SMEM] + [VMEM] * 4,
        out_specs=(VMEM,) * 3,
        scratch_shapes=[pltpu.VMEM((width, wide), f32)],
        compiler_params=pltpu.CompilerParams(vmem_limit_bytes=56 * 2**20),
        name="attend",
        cost_estimate=lasts(12),
    )(bounds, spans, q, k, v)


def attend_back_kernel(
    which, bounds, spans, q, k, v, d_o, o, lse, dq, dk, dk_over, dv, dv_over, sums,
    qs, dos, delta, dq_acc, dk_acc, dv_acc
):
    chunks, rows, width = q.shape
    y = lax.axis_index("blk") % 2
    mine = pl.ds(pl.multiple_of(y * rows, rows), rows)
    theirs = pl.ds(pl.multiple_of((1 - y) * rows, rows), rows)
    sums[...] = jnp.zeros_like(sums)
    for i in range(chunks):
        qs[i] = stack_heads(q[i], HEAD_DIM ** (-0.5))
        dos[i] = stack_heads(d_o[i], 1.0)
        product = (d_o[i].astype(f32) * o[i]).T
        delta[i] = jnp.concatenate(
            [
                jnp.sum(product[h * HEAD_DIM : (h + 1) * HEAD_DIM], axis=0, keepdims=True)
                for h in range(HEADS_HERE)
            ],
            axis=1,
        )
    dq_acc[...] = jnp.zeros_like(dq_acc)

    def block(kb, carry):
        first = pl.multiple_of(kb * KEY_BLOCK, KEY_BLOCK)
        part = pl.ds(first, KEY_BLOCK)
        dk_acc[...] = jnp.zeros_like(dk_acc)
        dv_acc[...] = jnp.zeros_like(dv_acc)

        def chunk(i, inner):
            @pl.when((kb >= bounds[which, 0, i]) & (kb < bounds[which, 1, i]))
            def _():
                keys = k[part, :]
                lo, hi = wide_span(spans, which, i)
                scores = masked_scores(keys, qs[i], first, lo, hi)
                weights = jnp.exp(scores - lse[i])
                d_weights = dot(v[part, :], dos[i], NT)
                d_scores = (weights * (d_weights - delta[i])).astype(bf16)
                dv_acc[...] += dot(weights.astype(bf16), dos[i])
                dk_acc[...] += dot(d_scores, qs[i])
                dq_acc[i] += dot(keys, d_scores, TN)

            return inner

        lax.fori_loop(0, chunks, chunk, 0)
        dk[kb] = dk_acc[mine, :].astype(bf16)
        dk_over[kb] = dk_acc[theirs, :].astype(bf16)
        dv[kb] = dv_acc[mine, :].astype(bf16)
        dv_over[kb] = dv_acc[theirs, :].astype(bf16)
        sums[1:2] += jnp.sum(dv_acc[...], axis=0, keepdims=True)
        return carry

    lax.fori_loop(0, k.shape[0] // KEY_BLOCK, block, 0)
    for i in range(chunks):
        result = (take_heads(dq_acc[i], rows) * HEAD_DIM ** (-0.5)).astype(bf16)
        dq[i] = result
        sums[0:1] += jnp.sum(result.astype(f32), axis=0, keepdims=True)


def attend_back(q, k, v, spans, which, d_o, o, lse):
    bounds, spans = spans
    chunks, rows, width = q.shape
    wide = HEADS_HERE * rows
    half = (k.shape[0] // KEY_BLOCK, rows, width)
    return pl.pallas_call(
        partial(attend_back_kernel, which),
        out_shape=(
            jax.ShapeDtypeStruct(q.shape, bf16),
            jax.ShapeDtypeStruct(half, bf16),
            jax.ShapeDtypeStruct(half, bf16),
            jax.ShapeDtypeStruct(half, bf16),
            jax.ShapeDtypeStruct(half, bf16),
            jax.ShapeDtypeStruct((8, width), f32),
        ),
        in_specs=[SMEM] + [VMEM] * 7,
        out_specs=(VMEM,) * 6,
        scratch_shapes=[
            pltpu.VMEM((chunks, wide, width), bf16),
            pltpu.VMEM((chunks, wide, width), bf16),
            pltpu.VMEM((chunks, 1, wide), f32),
            pltpu.VMEM((chunks, width, wide), f32),
            pltpu.VMEM((KEY_BLOCK, width), f32),
            pltpu.VMEM((KEY_BLOCK, width), f32),
        ],
        compiler_params=pltpu.CompilerParams(vmem_limit_bytes=60 * 2**20),
        name="attend_back",
        cost_estimate=lasts(14),
    )(bounds, spans, q, k, v, d_o, o, lse)


def key_spans(target_lengths, source_lengths, rows, count):
    ends = jnp.cumsum(target_lengths, dtype=jnp.int32)
    starts = ends - target_lengths
    chunk = jnp.arange(4, dtype=jnp.int32) * count + lax.axis_index("blk")

    def at(pos):
        past = (pos[..., None] >= ends).astype(jnp.int32)
        begun = (pos[..., None] >= starts).astype(jnp.int32)
        return (
            (jnp.sum(past * target_lengths, axis=-1), pos + 1),
            (jnp.sum(past * source_lengths, axis=-1), jnp.sum(begun * source_lengths, axis=-1)),
        )

    first, last = at(chunk * rows), at(chunk * rows + rows - 1)
    bounds = jnp.stack(
        [
            jnp.stack((low // KEY_BLOCK, (high + KEY_BLOCK - 1) // KEY_BLOCK))
            for (low, _), (_, high) in zip(first, last)
        ]
    ).astype(jnp.int32)
    spans = at(chunk[:, None] * rows + jnp.arange(rows, dtype=jnp.int32)[None, :])
    spans = jnp.stack([jnp.stack(s) for s in spans])
    return bounds, spans[:, :, :, None, :]


def body(
    count,
    inputs,
    encoded,
    d_output,
    target_lengths,
    source_lengths,
    norm_gain,
    norm_shift,
    self_qkv,
    self_bias,
    self_out,
    cross_q,
    cross_kv,
    cross_bias,
    cross_out,
    out_bias,
    ffn_in,
    ffn_in_bias,
    ffn_out,
):
    rows, width = inputs.shape
    devices = 4 * count
    share = width // devices
    head_width = width // 4
    hidden_width = ffn_in.shape[1]
    hidden_here = hidden_width // 4
    hidden_rows = hidden_width // width
    tokens_here = 4 * rows

    def split_cols(w):
        return jnp.transpose(w.reshape(share, -1, 4, w.shape[-1] // 4), (2, 0, 1, 3)).reshape(
            4, share, -1
        )

    w_ffn_out = lax.all_gather(ffn_out, "blk", axis=0, tiled=True)
    small = jnp.concatenate(
        (
            norm_gain,
            norm_shift,
            self_bias,
            cross_bias,
            out_bias,
            ffn_in_bias.reshape(hidden_rows, share),
        )
    )
    n_small = small.shape[0]
    small = jnp.pad(small, ((0, N_SMALL - n_small), (0, 128 - share)))
    (
        table, here, b_hidden, w_qkv, w_cross_kv, w_cross_q, w_self_out, w_cross_out, w_ffn_in,
        inputs_all, encoded_all, d_output_all, normed_one, q1, k1, v1, k2, v2,
    ) = front(
        small,
        [split_cols(w) for w in (self_qkv, cross_kv, cross_q)],
        self_out[None],
        cross_out[None],
        split_cols(ffn_in),
        [inputs, encoded, d_output],
        count,
        0,
    )
    w_ffn_in = lax.all_gather(w_ffn_in, "blk", axis=1, tiled=True).reshape(width, -1)
    w_qkv, w_cross_kv, w_cross_q, w_self_out, w_cross_out = (
        w.reshape(-1, w.shape[-1]) for w in (w_qkv, w_cross_kv, w_cross_q, w_self_out, w_cross_out)
    )
    spans = key_spans(target_lengths, source_lengths, rows, count)

    k1, v1 = (a.reshape(-1, head_width) for a in (k1, v1))
    o1, mix1, lse1 = attend(q1, k1, v1, spans, 0)
    first, normed_two, q2, k2, v2 = join_forward(
        mix1, w_self_out, inputs, table, 0, count, 2, query=(w_cross_q, here), stream=(k2, v2)
    )
    k2, v2 = (a.reshape(-1, head_width) for a in (k2, v2))
    o2, mix2, lse2 = attend(q2, k2, v2, spans, 1)
    second, normed_three = join_forward(mix2, w_cross_out, first, table, 1, count, 3)

    out_part, d_part, ffn_mine, ffn_over, d_hidden = feed_forward(
        normed_three, d_output_all, w_ffn_in, w_ffn_out, b_hidden, count
    )
    swap = [(i, i ^ 1) for i in range(count)]
    ffn_over = lax.ppermute(ffn_over, "blk", swap)
    d_second, stats_three, d_o2, grad_cross_out, layer_output = join_backward(
        (d_part, out_part), d_output, second, table, 2, w_cross_out, mix2, count, 4
    )
    dq2, dk2, dk2_over, dv2, dv2_over, sums_two = attend_back(q2, k2, v2, spans, 1, d_o2, o2, lse2)
    inside = rows == 4 * share
    if inside:
        dk2_over, dv2_over = lax.ppermute((dk2_over, dv2_over), "blk", swap)
    dq2, ffn_over = tie(dq2, ffn_over)
    lines = [list(range(y, count, 2)) for y in range(2)]
    ffn_terms = lax.all_to_all(
        (ffn_mine.astype(f32) + ffn_over.astype(f32)).astype(bf16), "blk", 0, 0,
        axis_index_groups=lines, tiled=True,
    )
    d_first, stats_two, d_o1, grad_self_out, grad_cross_q = join_backward(
        (dq2, w_cross_q, normed_two), d_second, first, table, 1, w_self_out, mix1, count, 5
    )
    dq1, dk1, dk1_over, dv1, dv1_over, sums_one = attend_back(q1, k1, v1, spans, 0, d_o1, o1, lse1)
    pairs = (dk1, dv1, dk2, dv2, dk1_over, dv1_over, dk2_over, dv2_over)
    if inside:
        pairs = [a.reshape(4, count // 2, 4, share, head_width) for a in pairs]
    else:
        y = lax.axis_index("blk") % 2
        pairs = [
            jnp.where(y == 0, jnp.stack((a, b), axis=1), jnp.stack((b, a), axis=1)).reshape(
                4, count, rows, head_width
            )
            for a, b in zip(pairs[:4], pairs[4:])
        ]
        pairs = scatter_blk(pairs, count, 6)
    got = finale(
        count, pairs, grad_cross_out, grad_self_out, grad_cross_q, ffn_terms, dq1, normed_one,
        encoded_all, w_qkv, w_cross_kv, inputs, d_first, table[0:1], stats_two, stats_three,
        sums_one, sums_two, d_hidden, 7,
    )
    done = settle(got, layer_output, share, width, hidden_width)
    order = (
        "layer", "d_inputs", "d_encoded", "gain", "shift", "qkv", "self_bias", "so", "cq", "ckv",
        "cross_bias", "co", "out_bias", "ffn_in", "ffn_bias", "ffn_out",
    )
    outs = [done["out_" + n] for n in order]
    outs[14] = outs[14].reshape(-1)
    return tuple(outs)


def solution(mesh):
    both = ("head", "blk")
    rows2, rows3, cols2 = P(both, None), P(both, None, None), P(None, both)
    return jax.shard_map(
        partial(body, mesh.shape["blk"]),
        mesh=mesh,
        in_specs=(
            rows2, rows2, rows2, P(), P(), cols2, cols2, rows3, cols2, rows2, rows2, rows3,
            cols2, rows2, cols2, rows2, P(both), rows2,
        ),
        out_specs=(
            rows2, rows2, rows2, cols2, cols2, rows3, cols2, rows2, rows2, rows3, cols2, rows2,
            cols2, rows2, P(both), rows2,
        ),
        check_vma=False,
    )
```

```python
from functools import partial

import jax
import jax.numpy as jnp
from jax import lax
from jax.experimental import pallas as pl
from jax.experimental.pallas import tpu as pltpu
from jax.sharding import PartitionSpec as P

HEAD_DIM = 64
HEADS_HERE = 4
KEY_BLOCK = 512
AHEAD = 2
SKEW = 2
MESH = pl.DeviceIdType.MESH
ANY = pl.BlockSpec(memory_space=pl.ANY)
VMEM = pl.BlockSpec(memory_space=pltpu.VMEM)
SMEM = pl.BlockSpec(memory_space=pltpu.SMEM)
DMA = pltpu.SemaphoreType.DMA
f32 = jnp.float32
bf16 = jnp.bfloat16
NT = (((1,), (1,)), ((), ()))
NN = (((1,), (0,)), ((), ()))
TN = (((0,), (0,)), ((), ()))


def dot(a, b, dims=NN):
    return lax.dot_general(a, b, dims, preferred_element_type=f32)


def params(cid):
    return pltpu.CompilerParams(
        collective_id=cid, has_side_effects=True, vmem_limit_bytes=56 * 2**20
    )


def lasts(us):
    return pl.CostEstimate(flops=int(us * 3e8), bytes_accessed=int(us * 3e5), transcendentals=0)


def remote(src, dst, ssem, rsem, device):
    return pltpu.make_async_remote_copy(
        src, dst, ssem, rsem, device_id=device, device_id_type=MESH
    )


class Head:
    def __init__(self):
        self.me = lax.axis_index("head")
        self.core = self.me % 2
        self.x = self.me // 2
        self.sib = self.me + 1 - 2 * self.core
        self.far = self.me + 2 - 4 * self.x
        self.far_sib = self.sib + 2 - 4 * self.x


class Blk:
    def __init__(self, count):
        self.me = lax.axis_index("blk")
        self.z = self.me // 2
        self.y = self.me % 2
        self.Z = count // 2
        self.across = self.me + 1 - 2 * self.y


def signal(bar, **device):
    pl.semaphore_signal(bar, inc=1, device_id=device, device_id_type=MESH)


def greet_head(bar, hd):
    for k in range(1, 4):
        signal(bar, head=(hd.me + k) % 4)
    return 3


def greet_blk(bar, bk):
    signal(bar, blk=bk.across)

    @pl.when(bk.z > 0)
    def _():
        signal(bar, blk=bk.me - 2)

    @pl.when(bk.z < bk.Z - 1)
    def _():
        signal(bar, blk=bk.me + 2)

    return 1 + jnp.where(bk.z > 0, 1, 0) + jnp.where(bk.z < bk.Z - 1, 1, 0)


class BlkGather:
    def __init__(self, bk, outs, ssem, rsem):
        self.bk, self.outs, self.ssem, self.rsem = bk, outs, ssem, rsem

    def copy(self, a, slot, way, device, src=None):
        view = self.outs[a].at[:, slot]
        return remote(
            view if src is None else src,
            view,
            self.ssem.at[a, way, slot // 2],
            self.rsem.at[a, slot],
            {"blk": device},
        )

    def start(self, a, src=None):
        bk = self.bk

        @pl.when(bk.z < bk.Z - 1)
        def _():
            self.copy(a, bk.me, 0, bk.me + 2, src).start()

        @pl.when(bk.z > 0)
        def _():
            self.copy(a, bk.me, 1, bk.me - 2, src).start()

        self.copy(a, bk.me, 2, bk.across, src).start()

    def step(self, a, k):
        bk = self.bk

        @pl.when(bk.z - k >= 0)
        def _():
            slot = bk.me - 2 * k
            self.copy(a, slot, 0, bk.me).wait_recv()

            @pl.when(bk.z < bk.Z - 1)
            def _():
                self.copy(a, slot, 0, bk.me + 2).start()

            self.copy(a, slot, 2, bk.across).start()

        @pl.when(bk.z + k < bk.Z)
        def _():
            slot = bk.me + 2 * k
            self.copy(a, slot, 0, bk.me).wait_recv()

            @pl.when(bk.z > 0)
            def _():
                self.copy(a, slot, 1, bk.me - 2).start()

            self.copy(a, slot, 2, bk.across).start()

    def arrive(self, a):
        for s in range(self.bk.Z):
            self.copy(a, 2 * s + 1 - self.bk.y, 0, self.bk.me).wait_recv()

    def drain(self, a):
        bk = self.bk
        for s in range(bk.Z):
            slot = 2 * s + bk.y

            @pl.when((s <= bk.z) & (bk.z < bk.Z - 1))
            def _():
                self.copy(a, slot, 0, bk.me).wait_send()

            @pl.when((s >= bk.z) & (bk.z > 0))
            def _():
                self.copy(a, slot, 1, bk.me).wait_send()

            self.copy(a, slot, 2, bk.me).wait_send()


N_SMALL = 24


def front_kernel(
    count, small, qkv, ckv, cq, so, co, ffn_in, inputs, encoded, d_output, *refs
):
    (
        table, bias, b_hidden, w_qkv, w_ckv, w_cq, w_so, w_co, swapped, inputs_all, encoded_all,
        d_output_all, normed, q1, k1, v1, k2, v2, small_all, vectors, lsem, hs, hr, ssem, rsem,
    ) = refs
    hd, bk = Head(), Blk(count)
    share, head_width = qkv.shape[1], q1.shape[2]
    rows, width = inputs.shape
    bar = pltpu.get_barrier_semaphore()
    pl.semaphore_wait(bar, greet_head(bar, hd) + greet_blk(bar, bk))
    ring = BlkGather(bk, (small_all, w_qkv, w_ckv, w_cq, w_so, w_co, k1, v1), ssem, rsem)
    K1, V1 = 6, 7
    pairs = (
        (small, small_all), (qkv, w_qkv), (ckv, w_ckv), (cq, w_cq), (so, w_so), (co, w_co),
        (inputs, inputs_all), (encoded, encoded_all), (ffn_in, swapped), (d_output, d_output_all),
    )
    SMALL, QKV, CKV, CQ, SO, CO, INPUTS, ENCODED, FFN_IN, D_OUTPUT = range(10)
    rows_only = (SO, CO)

    def source(a, to):
        return pairs[a][0].at[to] if a in (QKV, CKV, CQ, FFN_IN) else pairs[a][0]

    def target(a, h):
        if a in rows_only:
            return pairs[a][1].at[:, bk.me]
        return pairs[a][1].at[h] if a >= INPUTS else pairs[a][1].at[h, bk.me]

    def own(a):
        return pltpu.make_async_copy(source(a, hd.me), target(a, hd.me), lsem.at[a])

    def across_head(a, k, back):
        to = (hd.me + k) % 4
        return remote(
            source(a, to),
            target(a, to if back else hd.me),
            hs.at[a, k],
            hr.at[a, to if back else hd.me],
            {"head": to},
        )

    def headed(a):
        own(a).wait()
        for k in range(1, 4):
            across_head(a, k, True).wait_recv()

    everything = (SMALL, QKV, CKV, CQ, INPUTS, ENCODED, FFN_IN, D_OUTPUT)
    for a in everything:
        own(a).start()
        for k in (2, 1, 3):
            across_head(a, k, False).start()
    for a in rows_only:
        own(a).start()
    headed(SMALL)
    ring.start(SMALL)
    headed(QKV)
    ring.start(QKV)
    for a in rows_only:
        ring.start(a, pairs[a][0])
    headed(CKV)
    ring.start(CKV)
    headed(CQ)
    ring.start(CQ)
    for k in range(1, bk.Z):
        for a in (SMALL, QKV) + ((SO, CO, CKV, CQ) if k < bk.Z - 1 else ()):
            ring.step(a, k)
    ring.arrive(0)
    lane = lax.broadcasted_iota(jnp.int32, (N_SMALL, 128), 1)

    def assemble(h, carry):
        for group in range(head_width // 128):
            total = jnp.zeros((N_SMALL, 128), f32)
            for i in range(128 // share):
                piece = small_all[h, group * (128 // share) + i].astype(f32)
                if i:
                    piece = pltpu.roll(piece, i * share, 1)
                total = jnp.where(lane // share == i, piece, total)
            vectors[h, :, group * 128 : (group + 1) * 128] = total
        return carry

    lax.fori_loop(0, 4, assemble, 0)

    for h in range(4):
        table[:, h * head_width : (h + 1) * head_width] = vectors[h]
    bias[...] = vectors[hd.me]
    first = lax.broadcasted_iota(jnp.int32, (1, 128), 1)
    per_group = 128 // share
    for group in range(4 * count // per_group):
        total = jnp.zeros((1, 128), f32)
        for i in range(per_group):
            b, run = divmod(group * per_group + i, 4)
            piece = small_all[hd.me, b].astype(f32)[13 + run : 14 + run]
            if i:
                piece = pltpu.roll(piece, i * share, 1)
            total = jnp.where(first // share == i, piece, total)
        b_hidden[:, group * 128 : (group + 1) * 128] = total
    gain, shift = table[0:1], table[3:4]
    headed(INPUTS)

    def norm(j, carry):
        normed[j] = layer_norm(inputs_all[j].astype(f32), gain, shift).astype(bf16)
        return carry

    lax.fori_loop(0, 4, norm, 0)
    for a in (SO, CO, CKV, CQ):
        ring.step(a, bk.Z - 1)
    ring.arrive(QKV)

    def project(features, w, c, bias_row, store):
        cols = w[:, :, :, c * head_width : (c + 1) * head_width].reshape(width, head_width)

        def one(j, carry):
            out = dot(features[j], cols)
            if bias_row is not None:
                out = out + bias[bias_row : bias_row + 1, :]
            store(j, out.astype(bf16))
            return carry

        lax.fori_loop(0, 4, one, 0)

    def into(ref):
        def store(j, value):
            ref[j] = value

        return store

    def into_own(ref):
        def store(j, value):
            ref[j, bk.me] = value

        return store

    project(normed, w_qkv, 1, None, into_own(k1))
    ring.start(K1)
    project(normed, w_qkv, 2, 7, into_own(v1))
    ring.start(V1)
    project(normed, w_qkv, 0, 6, into(q1))
    headed(ENCODED)
    ring.step(K1, 1)
    ring.step(V1, 1)
    ring.arrive(CKV)
    project(encoded_all, w_ckv, 0, None, into(k2))
    project(encoded_all, w_ckv, 1, 9, into(v2))
    for k in range(2, bk.Z):
        ring.step(K1, k)
        ring.step(V1, k)
    for a in rows_only:
        own(a).wait()
    for a in (FFN_IN, D_OUTPUT):
        headed(a)
    for a in (CQ, SO, CO, K1, V1):
        ring.arrive(a)
    for a in range(8):
        ring.drain(a)
    for a in everything:
        for k in range(1, 4):
            across_head(a, k, False).wait_send()


def front(small, cols, so, co, ffn_in, acts, count, cid):
    rows, width = acts[0].shape
    share, head_width = cols[0].shape[1], width // 4
    keys = (4, count, rows, head_width)
    tokens = (4, rows, width)
    block = (4, rows, head_width)
    bf = [(4, count) + a.shape[1:] for a in cols] + [(1, count) + a.shape[1:] for a in (so, co)]
    bf += [ffn_in.shape] + [tokens] * 4 + [block, keys, keys, block, block]
    return pl.pallas_call(
        partial(front_kernel, count),
        out_shape=[
            jax.ShapeDtypeStruct((N_SMALL, width), f32),
            jax.ShapeDtypeStruct((N_SMALL, head_width), f32),
            jax.ShapeDtypeStruct((1, ffn_in.shape[2]), f32),
        ]
        + [jax.ShapeDtypeStruct(s, bf16) for s in bf],
        in_specs=[ANY] * 10,
        out_specs=[VMEM] * 5 + [ANY] * 4 + [VMEM] * 2 + [ANY] + [VMEM] * 6,
        scratch_shapes=[
            pltpu.VMEM((4, count, N_SMALL, 128), bf16),
            pltpu.VMEM((4, N_SMALL, head_width), f32),
            DMA((10,)),
            DMA((10, 4)),
            DMA((10, 4)),
            DMA((8, 3, count // 2)),
            DMA((8, count)),
        ],
        compiler_params=params(cid),
        name="front",
        cost_estimate=lasts(90),
    )(small, *cols, so, co, ffn_in, *acts)


class BlkScatter:
    def __init__(self, bk, ins, bufs, sems):
        self.bk, self.ins = bk, ins
        self.own, self.over, self.side = bufs
        self.lsem, self.ys, self.yr, self.zs, self.ur, self.dr = sems

    def load(self, a, s):
        return pltpu.make_async_copy(
            self.ins[a].at[:, 2 * s + self.bk.y], self.own[a].at[s], self.lsem.at[a, s]
        )

    def cross(self, a, s):
        return remote(
            self.ins[a].at[:, 2 * s + 1 - self.bk.y],
            self.over[a].at[s],
            self.ys.at[a, s],
            self.yr.at[a, s],
            {"blk": self.bk.across},
        )

    def send(self, a, s, upward, slot=None):
        if slot is None:
            slot = s if upward else jnp.where(s == self.bk.z - 1, self.bk.Z, s)
        return remote(
            self.own[a].at[s],
            self.side[a].at[slot],
            self.zs.at[a, s],
            (self.ur if upward else self.dr).at[a, s],
            {"blk": self.bk.me + (2 if upward else -2)},
        )

    def order(self):
        for k in range((self.bk.Z + 1) // 2):
            yield self.bk.Z - 1 - k
            if k != self.bk.Z - 1 - k:
                yield k

    def begin(self, a):
        if a < len(self.ins):
            for s in self.order():
                self.cross(a, s).start()
                self.load(a, s).start()

    def add(self, a, s, extra, store):
        groups, rows = self.own[a].shape[1:3]
        step = min(rows, 32)

        def one(g, carry):
            for r in range(0, rows, step):
                part = pl.ds(r, step)
                total = self.own[a][s, g, part].astype(f32) + self.over[a][s, g, part].astype(f32)
                for slot in extra:
                    total = total + self.side[a][slot, g, part].astype(f32)
                store(g, part, total)
            return carry

        lax.fori_loop(0, groups, one, 0)

    def relay(self, a, s, upward):
        bk = self.bk
        self.load(a, s).wait()
        self.cross(a, s).wait_recv()
        inner = (bk.z > 0) if upward else (bk.z < bk.Z - 1)

        def store(g, part, total):
            self.own[a][s, g, part] = total.astype(bf16)

        @pl.when(inner)
        def _():
            self.send(a, s, upward, s).wait_recv()
            self.add(a, s, (s,), store)

        @pl.when(jnp.logical_not(inner))
        def _():
            self.add(a, s, (), store)

        self.send(a, s, upward).start()

    def run(self, finish):
        bk, n = self.bk, len(self.ins)
        for a in range(n):
            self.begin(a + AHEAD)
            for k in range(bk.Z - 1):

                @pl.when(bk.Z - 1 - k > bk.z)
                def _():
                    self.relay(a, bk.Z - 1 - k, True)

                @pl.when(k < bk.z)
                def _():
                    self.relay(a, k, False)

            if a > 0:
                finish(a - 1)
        finish(n - 1)

    def last(self, a, store):
        bk, s = self.bk, self.bk.z
        self.load(a, s).wait()
        self.cross(a, s).wait_recv()

        @pl.when(bk.z > 0)
        def _():
            self.send(a, s, True, s).wait_recv()

        @pl.when(bk.z < bk.Z - 1)
        def _():
            self.send(a, s, False, bk.Z).wait_recv()

        @pl.when((bk.z > 0) & (bk.z < bk.Z - 1))
        def _():
            self.add(a, s, (s, bk.Z), store)

        @pl.when((bk.z > 0) & (bk.z == bk.Z - 1))
        def _():
            self.add(a, s, (s,), store)

        @pl.when((bk.z == 0) & (bk.z < bk.Z - 1))
        def _():
            self.add(a, s, (bk.Z,), store)

    def finish(self):
        bk = self.bk
        for a in range(len(self.ins)):
            for s in range(bk.Z):
                self.cross(a, s).wait_send()

                @pl.when(s != bk.z)
                def _():
                    self.send(a, s, True, s).wait_send()


def scatter_scratch(items, count):
    Z = count // 2
    kinds = [
        pltpu.VMEM((slots, a.shape[0]) + a.shape[2:], bf16)
        for slots in (Z, Z, Z + 1)
        for a in items
    ]
    return kinds + [DMA((len(items), Z)) for _ in range(6)]


def scatter_parts(refs, n):
    bufs = tuple(refs[k * n : (k + 1) * n] for k in range(3))
    return bufs, refs[3 * n : 3 * n + 6], refs[3 * n + 6 :]


def scatter_blk_kernel(count, n, *refs):
    ins, outs = refs[:n], refs[n : 2 * n]
    bufs, sems, _ = scatter_parts(refs[2 * n :], n)
    bk = Blk(count)
    bar = pltpu.get_barrier_semaphore()
    pl.semaphore_wait(bar, greet_blk(bar, bk))
    ring = BlkScatter(bk, ins, bufs, sems)
    for a in range(AHEAD):
        ring.begin(a)

    def finish(a):
        def store(g, part, total):
            outs[a][g, part] = total.astype(outs[a].dtype)

        ring.last(a, store)

    ring.run(finish)
    ring.finish()


def scatter_blk(items, count, cid):
    n = len(items)
    return pl.pallas_call(
        partial(scatter_blk_kernel, count, n),
        out_shape=[
            jax.ShapeDtypeStruct((a.shape[0],) + a.shape[2:], a.dtype) for a in items
        ],
        in_specs=[ANY] * n,
        out_specs=[VMEM] * n,
        scratch_shapes=scatter_scratch(items, count),
        compiler_params=params(cid),
        name="scatter_blk",
        cost_estimate=lasts(60),
    )(*items)


PARTS = 2


class Halves:
    def half(self, p):
        rows = self.rows // PARTS
        return pl.ds(p * rows, rows)


class HeadSum(Halves):
    def __init__(self, hd, part, near, mid, far, sems):
        self.hd, self.part, self.near, self.mid, self.far = hd, part, near, mid, far
        self.ss, self.rs = sems
        self.rows = mid.shape[0]

    def near_copies(self, i):
        hd = self.hd
        block = hd.far_sib if i == 0 else hd.sib
        return [
            remote(
                self.part.at[block, self.half(p)],
                self.near.at[i, self.half(p)],
                self.ss.at[i, p],
                self.rs.at[i, p],
                {"head": hd.sib},
            )
            for p in range(PARTS)
        ]

    def near_start(self, i):
        for copy in self.near_copies(i):
            copy.start()

    def far_copy(self, p):
        return remote(
            self.mid.at[self.half(p)],
            self.far.at[self.half(p)],
            self.ss.at[2, p],
            self.rs.at[2, p],
            {"head": self.hd.far},
        )

    def begin(self):
        self.near_start(0)
        self.near_start(1)

    def middle(self):
        for p in range(PARTS):
            self.near_copies(0)[p].wait_recv()
            here = self.half(p)
            mine = self.part[self.hd.far, here].astype(f32)
            self.mid[here] = (mine + self.near[0, here].astype(f32)).astype(bf16)
            self.far_copy(p).start()

    def total(self, p):
        here = self.half(p)
        self.near_copies(1)[p].wait_recv()
        mine = self.part[self.hd.me, here].astype(f32) + self.near[1, here].astype(f32)
        self.far_copy(p).wait_recv()
        return mine + self.far[here].astype(f32)

    def whole(self):
        return jnp.concatenate([self.total(p) for p in range(PARTS)], axis=0)

    def finish(self):
        for p in range(PARTS):
            self.near_copies(0)[p].wait_send()
            self.near_copies(1)[p].wait_send()
            self.far_copy(p).wait_send()


def head_sum_scratch(rows, width):
    return [
        pltpu.VMEM((2, rows, width), bf16),
        pltpu.VMEM((rows, width), bf16),
        pltpu.VMEM((rows, width), bf16),
        DMA((3, PARTS)),
        DMA((3, PARTS)),
    ]


def head_gather_scratch():
    return [DMA((3, PARTS)), DMA((4, PARTS))]


class HeadGather(Halves):
    def __init__(self, hd, out, ss, rs):
        self.hd, self.out, self.ss, self.rs = hd, out, ss, rs
        self.rows = out.shape[1]

    def copy(self, slot, way, device, p):
        view = self.out.at[slot, self.half(p)]
        return remote(view, view, self.ss.at[way, p], self.rs.at[slot, p], {"head": device})

    def begin(self, p):
        hd = self.hd
        self.copy(hd.me, 0, hd.far, p).start()
        self.copy(hd.me, 1, hd.sib, p).start()

    def forward(self):
        hd = self.hd
        for p in range(PARTS):
            self.copy(hd.far, 0, hd.me, p).wait_recv()
            self.copy(hd.far, 2, hd.sib, p).start()

    def arrive(self):
        hd = self.hd
        for p in range(PARTS):
            self.copy(hd.sib, 0, hd.me, p).wait_recv()
            self.copy(hd.far_sib, 0, hd.me, p).wait_recv()

    def drain(self):
        hd = self.hd
        for p in range(PARTS):
            self.copy(hd.me, 0, hd.far, p).wait_send()
            self.copy(hd.me, 1, hd.sib, p).wait_send()
            self.copy(hd.far, 2, hd.sib, p).wait_send()


def row_stats(v):
    average = jnp.mean(v, axis=-1, keepdims=True)
    centred = v - average
    spread = jnp.mean(centred * centred, axis=-1, keepdims=True)
    return centred, lax.rsqrt(spread + 1e-05)


def layer_norm(v, gain, shift):
    centred, r = row_stats(v)
    return centred * r * gain + shift


def layer_norm_back(v, g, gain):
    centred, r = row_stats(v)
    u = centred * r
    c = g * gain
    dv = r * (c - jnp.mean(c, axis=-1, keepdims=True) - u * jnp.mean(c * u, axis=-1, keepdims=True))
    return dv, jnp.sum(g * u, axis=0, keepdims=True), jnp.sum(g, axis=0, keepdims=True)


SMALL_ROWS = (
    ("gain", 3), ("shift", 3), ("self_bias", 2), ("cross_bias", 2), ("out_bias", 3), ("ffn_bias", 4)
)
PAIRS = ("dk1", "dv1", "dk2", "dv2")


class PageScatter:
    def __init__(self, bk, feeds, bufs, sems, ready, crossed):
        self.bk, self.feeds, self.ready, self.crossed = bk, feeds, ready, crossed
        self.own, self.over, self.side = bufs
        self.lsem, self.ys, self.yr, self.zs, self.ur, self.dr = sems
        self.n = len(feeds)

    def load(self, a, s):
        copies = [
            pltpu.make_async_copy(src(s, True), self.own.at[(a, s) + dst], self.lsem.at[a, s, i])
            for i, (src, dst) in enumerate(self.feeds[a])
        ]
        if a in self.crossed:
            copies += [
                pltpu.make_async_copy(
                    src(s, False), self.over.at[(a, s) + dst], self.yr.at[a, s, i]
                )
                for i, (src, dst) in enumerate(self.feeds[a])
            ]
        return copies

    def cross(self, a, s):
        if a in self.crossed:
            return []
        return [
            remote(
                src(s, False),
                self.over.at[(a, s) + dst],
                self.ys.at[a, s, i],
                self.yr.at[a, s, i],
                {"blk": self.bk.across},
            )
            for i, (src, dst) in enumerate(self.feeds[a])
        ]

    def begin(self, a):
        Z = self.bk.Z
        for k in range(Z):
            s = Z - 1 - k // 2 if k % 2 == 0 else k // 2
            for copy in self.cross(a, s) + self.load(a, s):
                copy.start()

    def send(self, a, s, upward, slot=None):
        bk = self.bk
        if slot is None:
            slot = s if upward else jnp.where(s == bk.z - 1, bk.Z, s)
        return remote(
            self.own.at[a, s],
            self.side.at[a, slot],
            self.zs.at[a, s],
            (self.ur if upward else self.dr).at[a, s],
            {"blk": bk.me + (2 if upward else -2)},
        )

    def gathered(self, a):
        for s in range(self.bk.Z):
            for copy in self.load(a, s):
                copy.wait()
            for copy in self.cross(a, s):
                copy.wait_recv()

    def relay(self, a, s, upward):
        bk = self.bk
        inner = (bk.z > 0) if upward else (bk.z < bk.Z - 1)

        @pl.when(inner)
        def _():
            self.send(a, s, upward, s).wait_recv()
            self.own[a, s] = (
                self.own[a, s].astype(f32)
                + self.over[a, s].astype(f32)
                + self.side[a, s].astype(f32)
            ).astype(bf16)

        @pl.when(jnp.logical_not(inner))
        def _():
            self.own[a, s] = (
                self.own[a, s].astype(f32) + self.over[a, s].astype(f32)
            ).astype(bf16)

        self.send(a, s, upward).start()

    def wave(self, t):
        bk = self.bk
        if t < self.n:
            self.gathered(t)
        up, down = t - SKEW * bk.z, t - SKEW * (bk.Z - 1 - bk.z)

        @pl.when((up >= 0) & (up < self.n))
        def _():
            def one(i, carry):
                self.relay(up, bk.Z - 1 - i, True)
                return carry

            lax.fori_loop(0, bk.Z - 1 - bk.z, one, 0)

        @pl.when((down >= 0) & (down < self.n))
        def _():
            def one(i, carry):
                self.relay(down, i, False)
                return carry

            lax.fori_loop(0, bk.z, one, 0)

        a = t - SKEW * (bk.Z - 1)
        if a >= 0:
            self.last(a)

    def last(self, a):
        bk, s = self.bk, self.bk.z
        total = self.own[a, s].astype(f32) + self.over[a, s].astype(f32)

        @pl.when(bk.z > 0)
        def _():
            self.send(a, s, True, s).wait_recv()

        @pl.when(bk.z < bk.Z - 1)
        def _():
            self.send(a, s, False, bk.Z).wait_recv()

        total = total + jnp.where(bk.z > 0, self.side[a, s].astype(f32), 0.0)
        total = total + jnp.where(bk.z < bk.Z - 1, self.side[a, bk.Z].astype(f32), 0.0)
        self.ready[a](total)

    def drain(self):
        bk = self.bk
        for a in range(self.n):
            for s in range(bk.Z):
                for copy in self.cross(a, s):
                    copy.wait_send()

                @pl.when(s != bk.z)
                def _():
                    self.send(a, s, True, s).wait_send()


def finale_kernel(count, inside, names_in, names_out, names_scratch, *refs):
    r = dict(zip(names_in + names_out + names_scratch, refs))
    hd, bk = Head(), Blk(count)
    devices = 4 * count
    me = hd.me * count + bk.me
    rows, width = r["d_first"].shape
    head_width = width // 4
    share = width // devices
    bar = pltpu.get_barrier_semaphore()

    def place(k):
        to = (me + k) % devices
        return to, {"head": to // count, "blk": to % count}

    def greet(k, carry):
        signal(bar, **place(k)[1])
        return carry

    lax.fori_loop(1, devices, greet, 0)
    pl.semaphore_wait(bar, devices - 1)

    def tiles(src, dst, which):
        local = pltpu.make_async_copy(src.at[me], dst.at[me], r["tile_local"].at[which])

        def copy(k, back):
            to, device = place(k)
            return remote(
                src.at[to],
                dst.at[to if back else me],
                r["tile_send"].at[which, k],
                r["tile_recv"].at[which, to if back else me],
                device,
            )

        def start(k, carry):
            copy(k, False).start()
            return carry

        def end(k, carry):
            copy(k, False).wait_send()
            copy(k, True).wait_recv()
            return carry

        def begin():
            local.start()
            lax.fori_loop(1, devices, start, 0)

        def finish():
            local.wait()
            lax.fori_loop(1, devices, end, 0)

        return begin, finish

    headed = ["ffn_in", "cq", "qkv", "ckv"]

    def across_head(n, k, back):
        a = headed.index(n)
        to = (hd.me + k) % 4
        src = r["ffn_in"] if n == "ffn_in" else r["done_" + n]
        return remote(
            src.at[to],
            r["out_" + n].at[to if back else hd.me],
            r["head_send"].at[a, k],
            r["head_recv"].at[a, to if back else hd.me],
            {"head": to},
        )

    def send_heads(n):
        for k in range(1, 4):
            across_head(n, k, False).start()
        src = r["ffn_in"] if n == "ffn_in" else r["done_" + n]
        r["out_" + n][hd.me] = src[hd.me]

    def place_of(s, mine):
        return 2 * s + (bk.y if mine else 1 - bk.y)

    def col_page(ref, c):
        def src(s, mine):
            return ref.at[:, place_of(s, mine), :, c * head_width : (c + 1) * head_width]

        return [(src, ())]

    def row_page(ref):
        def src(j):
            return lambda s, mine: ref.at[
                0, place_of(s, mine), :, j * head_width : (j + 1) * head_width
            ]

        return [(src(j), (j,)) for j in range(4)]

    def pair_page(n, h):
        return [(lambda s, mine: r[n if mine else n + "_over"].at[h, s], ())]

    def store_pair(n, h):
        def store(total):
            r["sum_" + n][h] = total.reshape(rows, head_width).astype(bf16)

        return store

    def store_col(n, c):
        def store(total):
            r["done_" + n][:, :, c * head_width : (c + 1) * head_width] = total.astype(bf16)

        return store

    def store_row(n):
        def store(total):
            for j in range(4):
                r["out_" + n][0, :, j * head_width : (j + 1) * head_width] = total[j]

        return store

    feeds, ready, crossed, index = [], [], [], {}

    def item(name, feed, store):
        index[name] = len(feeds)
        feeds.append(feed)
        ready.append(store)

    if inside:
        for n, h in [(n, h) for n in ("dk2", "dk1", "dv1", "dv2") for h in range(4)]:
            if n in ("dk2", "dv2"):
                crossed.append(len(feeds))
            item(n, pair_page(n, h), store_pair(n, h))
    for n in ("so", "co"):
        item(n, row_page(r[n]), store_row(n))
    item("cq", col_page(r["cq"], 0), store_col("cq", 0))
    item("qkv0", col_page(r["grad_qkv"], 0), store_col("qkv", 0))
    item("ckv0", col_page(r["grad_ckv"], 0), store_col("ckv", 0))
    for c in (1, 2):
        item("qkv%d" % c, col_page(r["grad_qkv"], c), store_col("qkv", c))
    item("ckv1", col_page(r["grad_ckv"], 1), store_col("ckv", 1))
    ring = PageScatter(
        bk, feeds, (r["own"], r["over"], r["side"]), [r["ring%d" % i] for i in range(6)], ready,
        crossed,
    )

    def summed(n):
        return r["sum_" + n] if inside else r[n]

    def fill(joined, parts, first):
        for j in range(4):
            joined[j * rows : (j + 1) * rows, first : first + len(parts) * head_width] = (
                jnp.concatenate([p[j] for p in parts], axis=1)
            )

    def weight_grad(joined, cols, features, grad, g0, g1):
        def one(g, carry):
            lhs = features[:, :, pl.ds(pl.multiple_of(g * head_width, head_width), head_width)]
            total = dot(lhs.reshape(4 * rows, head_width), joined[:, cols], TN)
            grad[g, :, :, cols] = total.reshape(grad.shape[1:3] + (-1,)).astype(bf16)
            return carry

        lax.fori_loop(g0, g1, one, 0)

    def project(joined, w, summed_over_head):
        def term(j):
            def run():
                block = joined[pl.ds(pl.multiple_of(j * rows, rows), rows), :]
                summed_over_head.part[j] = dot(block, w[...], NT).astype(bf16)

            return run

        def near(i):
            return lambda: summed_over_head.near_start(i)

        return [
            [term(hd.far_sib), near(0)],
            [term(hd.sib), near(1)],
            [term(hd.far), summed_over_head.middle],
            [term(hd.me)],
        ]

    stats_begin, stats_finish = tiles(r["stats_tab"], r["stats_got"], 0)
    first, second = (
        HeadSum(
            hd, r["part%d" % (i + 1)], r["near%d" % i], r["mid%d" % i], r["far%d" % i],
            (r["sum_send%d" % i], r["sum_recv%d" % i]),
        )
        for i in range(2)
    )

    def query_part():
        fill(r["joined1"], [r["dq1"]], 0)
        weight_grad(r["joined1"], slice(0, head_width), r["normed"], r["grad_qkv"], 0, 4)
        ring.begin(index["qkv0"])

    def own_steps(n, c, joined, features, grad, page):
        cols = slice(c * head_width, (c + 1) * head_width)

        def half(g0, g1):
            return lambda: weight_grad(joined, cols, features, grad, g0, g1)

        return [
            [lambda: fill(joined, [summed(n)], c * head_width), half(0, 2)],
            [half(2, 4), lambda: ring.begin(index[page])],
        ]

    steps = dict(
        dk2=own_steps("dk2", 0, r["joined2"], r["encoded"], r["grad_ckv"], "ckv0"),
        dk1=own_steps("dk1", 1, r["joined1"], r["normed"], r["grad_qkv"], "qkv1"),
        dv1=own_steps("dv1", 2, r["joined1"], r["normed"], r["grad_qkv"], "qkv2"),
        dv2=own_steps("dv2", 1, r["joined2"], r["encoded"], r["grad_ckv"], "ckv1"),
    )
    steps["dv1"] += project(r["joined1"], r["w_qkv"], first)
    steps["dv2"] += project(r["joined2"], r["w_ckv"], second)

    def self_norm():
        dv, d_gain, d_shift = layer_norm_back(
            r["inputs"][...].astype(f32), first.whole(), r["table"][0:1]
        )
        r["out_d_inputs"][...] = dv + r["d_first"][...]
        r["own_stats"][0:1] = d_gain
        r["own_stats"][1:2] = d_shift

    def self_table():
        two, three = r["stats_two"], r["stats_three"]

        def placed(row):
            return jnp.concatenate(
                [jnp.where(hd.me == h, row, 0.0) for h in range(4)], axis=1
            )

        rows_of = [
            r["own_stats"][0:1], two[0:1], three[0:1], r["own_stats"][1:2], two[1:2], three[1:2],
            placed(r["sums_one"][0:1]), placed(r["sums_one"][1:2]),
            placed(r["sums_two"][0:1]), placed(r["sums_two"][1:2]),
            two[2:3], three[2:3], three[3:4],
        ]
        whole = jnp.concatenate(rows_of + [jnp.zeros((N_SMALL - 13, width), f32)], axis=0)
        hidden = r["d_hidden"][...]

        def turned(value, lane):
            tile = value[:, lane // 128 * 128 : lane // 128 * 128 + 128]
            return pltpu.roll(tile, 128 - lane % 128, 1) if lane % 128 else tile

        for d in range(devices):
            r["stats_tab"][d] = turned(whole, d * share)
            h, b = divmod(d, count)
            for run in range(4):
                mine = turned(hidden, (4 * b + run) * share)
                r["stats_tab"][d, 13 + run : 14 + run, :] = jnp.where(hd.me == h, mine, 0.0)

    def sum_ffn():
        def one(i, carry):
            part = pl.ds(pl.multiple_of(i * share, share), share)
            total = r["ffn_terms"][0, part, :].astype(f32)
            for b in range(1, count // 2):
                total = total + r["ffn_terms"][b, part, :].astype(f32)

            @pl.when(i < 4)
            def _():
                r["ffn_in"][i] = total.astype(bf16)

            @pl.when(i >= 4)
            def _():
                r["out_ffn_out"][pl.ds(pl.multiple_of((i - 4) * share, share), share), :] = total

            return carry

        lax.fori_loop(0, 8, one, 0)
        send_heads("ffn_in")

    lag = SKEW * (bk.Z - 1)
    lead = 4 if inside else index["cq"] + 1
    for a in range(lead):
        ring.begin(a)
    plan = {}

    def at(t, step):
        plan.setdefault(t, []).append(step)

    last = ring.n + lag - 1
    after_self = 0
    if inside:
        after_self = index["dv1"] + lag
        for n in PAIRS:
            for i, step in enumerate(steps[n]):
                at(index[n] + lag + (max(i - 1, 0) if n == "dv2" else i), step)
        at(3, [query_part])
        at(5, [sum_ffn])
    else:
        sum_ffn()
        query_part()
        for n in PAIRS:
            for step in steps[n]:
                for run in step:
                    run()
    for i, step in enumerate((self_norm, self_table, stats_begin)):
        at(min(after_self + 8 + i, last), [step])
    at(index["cq"] + lag, [lambda: send_heads("cq")])
    at(index["qkv2"] + lag, [lambda: send_heads("qkv")])
    for t in range(last + 1):
        for a in range(lead + 2 * t, min(lead + 2 * t + 2, index["cq"] + 1)):
            ring.begin(a)
        ring.wave(t)
        for step in plan.get(t, []):
            for run in step:
                run()
    send_heads("ckv")
    r["out_d_encoded"][...] = second.whole()
    ring.drain()
    first.finish()
    second.finish()
    for n in headed:
        for k in range(1, 4):
            across_head(n, k, False).wait_send()
            across_head(n, k, True).wait_recv()
    stats_finish()
    total = r["stats_got"][0]
    for d in range(1, devices):
        total = total + r["stats_got"][d]
    r["out_stats"][...] = total


def settle_kernel(names, *refs):
    r = dict(zip(names, refs[:-1]))
    sems = refs[-1]
    copies = [
        pltpu.make_async_copy(r[name], r["here_" + name[4:]], sems.at[i])
        for i, name in enumerate([n for n in names if n.startswith("got_")])
    ]
    for copy in copies:
        copy.start()
    for copy in copies:
        copy.wait()
    for name in ("ffn_in", "cq", "ckv", "qkv"):
        got, out = r["here_" + name], r["out_" + name]
        parts = out.shape[1] if len(out.shape) == 3 else 1
        step = got.shape[2] // parts
        for h in range(4):
            for c in range(parts):
                value = got[h, :, c * step : (c + 1) * step].astype(f32)
                if parts == 1:
                    out[:, h * step : (h + 1) * step] = value
                else:
                    out[:, c, h * step : (h + 1) * step] = value
    for name in ("d_inputs", "d_encoded", "ffn_out", "layer"):
        r["out_" + name][...] = r["here_" + name][...]
    for name in ("co", "so"):
        r["out_" + name][...] = r["here_" + name][0]
    row = 0
    for name, number in SMALL_ROWS:
        out = r["out_" + name]
        out[...] = r["here_stats"][row : row + number, : out.shape[1]]
        row += number


def settle(got, layer_output, share, width, hidden_width):
    rows = layer_output.shape[0]
    ins = {"got_" + n[4:]: a for n, a in got.items()}
    ins["got_layer"] = layer_output
    outs = dict(
        out_layer=((rows, width), bf16),
        out_d_inputs=((rows, width), f32),
        out_d_encoded=((rows, width), f32),
        out_qkv=((share, 3, width), f32),
        out_ckv=((share, 2, width), f32),
        out_cq=((share, width), f32),
        out_ffn_in=((share, hidden_width), f32),
        out_ffn_out=(got["out_ffn_out"].shape, f32),
        out_co=((share, width), f32),
        out_so=((share, width), f32),
    )
    outs.update({"out_" + n: ((number, share), f32) for n, number in SMALL_ROWS})
    here = {"here_" + n[4:]: pltpu.VMEM(a.shape, a.dtype) for n, a in ins.items()}
    done = pl.pallas_call(
        partial(settle_kernel, tuple(ins) + tuple(outs) + tuple(here)),
        out_shape=[jax.ShapeDtypeStruct(*o) for o in outs.values()],
        in_specs=[ANY] * len(ins),
        out_specs=[VMEM] * len(outs),
        scratch_shapes=list(here.values()) + [DMA((len(ins),))],
        compiler_params=pltpu.CompilerParams(vmem_limit_bytes=60 * 2**20),
        name="settle",
        cost_estimate=lasts(4),
    )(*ins.values())
    return dict(zip(outs, done))


def finale(
    count, pairs, co, so, cq, ffn_terms, dq1, normed, encoded, w_qkv, w_ckv, inputs, d_first, table,
    stats_two, stats_three, sums_one, sums_two, d_hidden, cid,
):
    inside = len(pairs) == 8
    devices, Z = 4 * count, count // 2
    rows, width = inputs.shape
    share = width // devices
    head_width = w_ckv.shape[1] // 2
    hidden_width = ffn_terms.shape[2]
    ins = dict(zip(PAIRS + tuple(n + "_over" for n in PAIRS), pairs))
    ins.update(co=co, so=so, cq=cq)
    in_specs = [ANY if inside else VMEM] * len(pairs) + [ANY] * 3
    rest = dict(
        ffn_terms=ffn_terms, dq1=dq1, normed=normed, encoded=encoded, w_qkv=w_qkv, w_ckv=w_ckv,
        inputs=inputs, d_first=d_first, table=table, stats_two=stats_two, stats_three=stats_three,
        sums_one=sums_one, sums_two=sums_two, d_hidden=d_hidden,
    )
    ins.update(rest)
    in_specs += [VMEM] * len(rest)
    outs = dict(
        out_d_inputs=((rows, width), f32),
        out_d_encoded=((rows, width), f32),
        out_qkv=((4, share, 3 * head_width), bf16),
        out_ckv=((4, share, 2 * head_width), bf16),
        out_cq=((4, share, head_width), bf16),
        out_ffn_in=((4, share, hidden_width), bf16),
        out_ffn_out=((4 * share, width), f32),
        out_co=((1, share, width), f32),
        out_so=((1, share, width), f32),
        out_stats=((N_SMALL, 128), f32),
    )
    grads = dict(
        grad_qkv=(4, count, share, 3 * head_width), grad_ckv=(4, count, share, 2 * head_width)
    )
    scratch = {}
    n_items = 24 if inside else 8
    for kind, slots in (("own", Z), ("over", Z), ("side", Z + 1)):
        scratch[kind] = pltpu.VMEM((n_items, slots, 4, share, head_width), bf16)
    for n, wide in (("cq", 1), ("qkv", 3), ("ckv", 2)):
        scratch["done_" + n] = pltpu.VMEM((4, share, wide * head_width), bf16)
    scratch["ffn_in"] = pltpu.VMEM((4, share, hidden_width), bf16)
    if inside:
        for n in PAIRS:
            scratch["sum_" + n] = pltpu.VMEM((4, rows, head_width), bf16)
    for n, shape in grads.items():
        scratch[n] = pltpu.VMEM(shape, bf16)
    for i, n in enumerate(("1", "2")):
        scratch["part" + n] = pltpu.VMEM((4, rows, width), bf16)
        scratch["joined" + n] = pltpu.VMEM((4 * rows, (3 - i) * head_width), bf16)
        kinds = head_sum_scratch(rows, width)
        for name, kind in zip(("near", "mid", "far", "sum_send", "sum_recv"), kinds):
            scratch[name + str(i)] = kind
    scratch["own_stats"] = pltpu.VMEM((8, width), f32)
    for n in ("stats_tab", "stats_got"):
        scratch[n] = pltpu.VMEM((devices, N_SMALL, 128), f32)
    for i in range(6):
        scratch["ring%d" % i] = DMA((n_items, Z, 4) if i < 3 else (n_items, Z))
    scratch["tile_local"] = DMA((1,))
    scratch["tile_send"] = DMA((1, devices))
    scratch["tile_recv"] = DMA((1, devices))
    scratch["head_send"] = DMA((4, 4))
    scratch["head_recv"] = DMA((4, 4))
    got = pl.pallas_call(
        partial(finale_kernel, count, inside, tuple(ins), tuple(outs), tuple(scratch)),
        out_shape=[jax.ShapeDtypeStruct(*o) for o in outs.values()],
        in_specs=in_specs,
        out_specs=[VMEM] * len(outs),
        scratch_shapes=list(scratch.values()),
        compiler_params=params(cid),
        name="finale",
        cost_estimate=lasts(150),
    )(*ins.values())
    return dict(zip(outs, got))


def forward_kernel(count, n_stream, has_query, layer, *refs):
    refs = list(refs)
    mix, w_out, base, table = (refs.pop(0) for _ in range(4))
    w_query, b_query = (refs.pop(0) for _ in range(2)) if has_query else (None, None)
    stream_in = [refs.pop(0) for _ in range(n_stream)]
    total, normed = (refs.pop(0) for _ in range(2))
    query = refs.pop(0) if has_query else None
    stream_out = [refs.pop(0) for _ in range(n_stream)]
    part, near, mid, far, ss, rs, gs, gr = (refs.pop(0) for _ in range(8))
    hd, bk = Head(), Blk(count)
    bar = pltpu.get_barrier_semaphore()
    greeted = greet_head(bar, hd)
    if n_stream:
        greeted = greeted + greet_blk(bar, bk)
    pl.semaphore_wait(bar, greeted)
    ring = None
    if n_stream:
        lsem, ssem, rsem = refs
        ring = BlkGather(bk, stream_out, ssem, rsem)
        for a in range(n_stream):
            ring.start(a, stream_in[a])
            pltpu.make_async_copy(stream_in[a], stream_out[a].at[:, bk.me], lsem.at[a]).start()

    def term(j):
        part[j] = dot(mix[j], w_out[...]).astype(bf16)

    summed = HeadSum(hd, part, near, mid, far, (ss, rs))
    term(hd.far_sib)
    summed.near_start(0)
    term(hd.sib)
    summed.near_start(1)
    term(hd.far)
    summed.middle()
    term(hd.me)
    gain, shift = table[layer + 1 : layer + 2], table[layer + 4 : layer + 5]
    spread = HeadGather(hd, normed, gs, gr)
    for p in range(PARTS):
        here = summed.half(p)
        v = base[here].astype(f32) + summed.total(p) + table[10 + layer : 11 + layer]
        total[here] = v
        normed[hd.me, here] = layer_norm(v, gain, shift).astype(bf16)
        spread.begin(p)

    def ask(j):
        if has_query:
            query[j] = (dot(normed[j], w_query[...]) + b_query[8:9]).astype(bf16)

    def step(k):
        for a in range(n_stream):
            ring.step(a, k)

    ask(hd.me)
    if n_stream:
        step(1)
    spread.forward()
    ask(hd.far)
    spread.arrive()
    ask(hd.sib)
    ask(hd.far_sib)
    if n_stream:
        for k in range(2, bk.Z):
            step(k)
        for a in range(n_stream):
            ring.arrive(a)
            ring.drain(a)
            pltpu.make_async_copy(stream_in[a], stream_out[a].at[:, bk.me], lsem.at[a]).wait()
    spread.drain()
    summed.finish()


def join_forward(mix, w_out, base, table, layer, count, cid, query=None, stream=()):
    rows, width = base.shape
    n = len(stream)
    ops = [mix, w_out, base, table] + list(query or ()) + list(stream)
    shapes = [
        jax.ShapeDtypeStruct((rows, width), f32),
        jax.ShapeDtypeStruct((4, rows, width), bf16),
    ]
    if query:
        shapes.append(jax.ShapeDtypeStruct(mix.shape, bf16))
    n_vmem = len(shapes)
    shapes += [jax.ShapeDtypeStruct((4, count) + a.shape[1:], bf16) for a in stream]
    scratch = [pltpu.VMEM((4, rows, width), bf16)] + head_sum_scratch(rows, width)
    scratch += head_gather_scratch()
    if n:
        scratch += [DMA((n,)), DMA((n, 3, count // 2)), DMA((n, count))]
    return pl.pallas_call(
        partial(forward_kernel, count, n, query is not None, layer),
        out_shape=shapes,
        in_specs=[VMEM] * (len(ops) - n) + [ANY] * n,
        out_specs=[VMEM] * n_vmem + [ANY] * n,
        scratch_shapes=scratch,
        compiler_params=params(cid),
        name="join_forward",
        cost_estimate=lasts(50 if n else 22),
    )(*ops)


def backward_kernel(count, layer, has_extra, *refs):
    refs = list(refs)
    if has_extra:
        part, extra = (refs.pop(0) for _ in range(2))
    else:
        dq, w_in, normed = (refs.pop(0) for _ in range(3))
    onward, v, table, w_out, mix = (refs.pop(0) for _ in range(5))
    back, stats, d_o, grad_out = (refs.pop(0) for _ in range(4))
    other = refs.pop(0)
    grad_all = refs.pop(0)
    sums = [refs.pop(0) for _ in range(5)]
    hd = Head()
    head_width = mix.shape[2]
    tokens = 4 * mix.shape[1]
    bar = pltpu.get_barrier_semaphore()
    pl.semaphore_wait(bar, greet_head(bar, hd))
    if has_extra:
        second = HeadSum(hd, extra, *refs[:3], refs[3:5])
        refs = refs[5:]
    else:
        part = refs.pop(0)
    summed = HeadSum(hd, part, *sums[:3], sums[3:])
    if has_extra:
        summed.begin()
        summed.middle()
        second.begin()
        second.middle()
    else:

        def term(j):
            part[j] = dot(dq[j], w_in[...], NT).astype(bf16)

        term(hd.far_sib)
        summed.near_start(0)
        term(hd.sib)
        summed.near_start(1)
        term(hd.far)
        summed.middle()
        term(hd.me)
        all_dq = dq[...].reshape(tokens, head_width)

        def weight(g, carry):
            lhs = normed[:, :, pl.ds(pl.multiple_of(g * head_width, head_width), head_width)]
            other[g] = (
                dot(lhs.reshape(tokens, head_width), all_dq, TN).reshape(other.shape[1:]).astype(bf16)
            )
            return carry

        lax.fori_loop(0, 4, weight, 0)
    gain = table[layer : layer + 1]
    spread = HeadGather(hd, grad_all, *refs)
    sums_here = []
    for p in range(PARTS):
        here = summed.half(p)
        dv, d_gain, d_shift = layer_norm_back(v[here], summed.total(p), gain)
        after = onward[here].astype(f32)
        d = dv + after
        back[here] = d
        rounded = d.astype(bf16)
        grad_all[hd.me, here] = rounded
        spread.begin(p)
        sums_here.append(
            (
                d_gain,
                d_shift,
                jnp.sum(rounded.astype(f32), axis=0, keepdims=True),
                jnp.sum(after, axis=0, keepdims=True),
            )
        )
    for i, terms in enumerate(zip(*sums_here)):
        stats[i : i + 1] = sum(terms[1:], terms[0])

    def out(j):
        d_o[j] = dot(grad_all[j], w_out[...], NT).astype(bf16)

    out(hd.me)
    if has_extra:
        other[...] = (v[...] + second.whole() + table[10 + layer : 11 + layer]).astype(bf16)
    spread.forward()
    out(hd.far)
    spread.arrive()
    out(hd.sib)
    out(hd.far_sib)
    grad = dot(mix[...].reshape(tokens, head_width), grad_all[...].reshape(tokens, -1), TN)
    grad_out[0] = grad.reshape(grad_out.shape[1:]).astype(bf16)
    spread.drain()
    summed.finish()
    if has_extra:
        second.finish()


def join_backward(terms, onward, v, table, layer, w_out, mix, count, cid):
    rows, width = onward.shape
    share, head_width = width // (4 * count), mix.shape[2]
    has_extra = len(terms) == 2
    ops = list(terms) + [onward, v, table, w_out, mix]
    other = ((rows, width), bf16) if has_extra else ((4, count, share, head_width), bf16)
    shapes = [
        ((rows, width), f32),
        ((8, width), f32),
        (mix.shape, bf16),
        ((1, count, share, width), bf16),
        other,
    ]
    scratch = [pltpu.VMEM((4, rows, width), bf16)] + head_sum_scratch(rows, width)
    if has_extra:
        scratch += head_sum_scratch(rows, width)
    else:
        scratch += [pltpu.VMEM((4, rows, width), bf16)]
    scratch += head_gather_scratch()
    return pl.pallas_call(
        partial(backward_kernel, count, layer, has_extra),
        out_shape=[jax.ShapeDtypeStruct(*s) for s in shapes],
        in_specs=[VMEM] * len(ops),
        out_specs=[VMEM] * len(shapes),
        scratch_shapes=scratch,
        compiler_params=params(cid),
        name="join_backward",
        cost_estimate=lasts(24),
    )(*ops)


def feed_forward_kernel(
    normed, d_output, w_in, w_out, b_hidden, out_part, d_part, mine, theirs, d_sum, act, dh
):
    rows, width = normed.shape[1:]
    tokens = 4 * rows
    share = mine.shape[1] // 8
    first = lax.axis_index("blk") % 2 == 0
    d_sum[...] = jnp.zeros_like(d_sum)

    def block(j, carry):
        hidden = dot(normed[j], w_in[...]) + b_hidden[...]
        phi = 0.5 * (1.0 + lax.erf(hidden * (0.5**0.5)))
        active = (hidden * phi).astype(bf16)
        slope = phi + hidden * jnp.exp(-0.5 * hidden * hidden) * ((0.5 / jnp.pi) ** 0.5)
        d_hidden = (dot(d_output[j], w_out[...], NT) * slope).astype(bf16)
        act[j] = active
        dh[j] = d_hidden
        d_sum[...] += jnp.sum(d_hidden.astype(f32), axis=0, keepdims=True)
        out_part[j] = dot(active, w_out[...]).astype(bf16)
        d_part[j] = dot(d_hidden, w_in[...], NT).astype(bf16)
        return carry

    lax.fori_loop(0, 4, block, 0)
    step = width // 4
    runs = step // (8 * share)

    def weight(g, carry):
        part = pl.ds(pl.multiple_of(g * step, step), step)
        def split(total, place):
            even, odd = total[:, 0].astype(bf16), total[:, 1].astype(bf16)
            mine[place] = jnp.where(first, even, odd)
            theirs[place] = jnp.where(first, odd, even)

        total = dot(normed[:, :, part].reshape(tokens, step), dh[...].reshape(tokens, -1), TN)
        place = (slice(None), pl.ds(pl.multiple_of(g * share, share), share))
        split(total.reshape(mine.shape[0], 2, share, -1), place)
        total = dot(act[:, :, part].reshape(tokens, step), d_output[...].reshape(tokens, -1), TN)
        place = (pl.ds(g * runs, runs), slice(4 * share, None))
        split(total.reshape(runs, 2, 4 * share, -1), place)
        return carry

    lax.fori_loop(0, 4, weight, 0)


def feed_forward(normed, d_output, w_in, w_out, b_hidden, count):
    rows, width = normed.shape[1:]
    share = width // (4 * count)
    return pl.pallas_call(
        feed_forward_kernel,
        out_shape=(
            jax.ShapeDtypeStruct(normed.shape, bf16),
            jax.ShapeDtypeStruct(normed.shape, bf16),
            jax.ShapeDtypeStruct((count // 2, 8 * share, width), bf16),
            jax.ShapeDtypeStruct((count // 2, 8 * share, width), bf16),
            jax.ShapeDtypeStruct((1, w_in.shape[1]), f32),
        ),
        in_specs=[VMEM] * 5,
        out_specs=(VMEM,) * 5,
        scratch_shapes=[
            pltpu.VMEM((4, rows, w_in.shape[1]), bf16),
            pltpu.VMEM((4, rows, w_in.shape[1]), bf16),
        ],
        compiler_params=pltpu.CompilerParams(vmem_limit_bytes=56 * 2**20),
        name="feed_forward",
        cost_estimate=lasts(15),
    )(normed, d_output, w_in, w_out, b_hidden)


def tie(value, *others):
    return lax.optimization_barrier((value,) + others)


def stack_heads(rows, scale):
    lane = lax.broadcasted_iota(jnp.int32, rows.shape, 1) // HEAD_DIM
    pieces = [
        jnp.where(lane == h, rows.astype(f32) * scale, 0.0).astype(bf16) for h in range(HEADS_HERE)
    ]
    return jnp.concatenate(pieces, axis=0)


def take_heads(wide, rows):
    pieces = [
        wide[h * HEAD_DIM : (h + 1) * HEAD_DIM, h * rows : (h + 1) * rows]
        for h in range(HEADS_HERE)
    ]
    return jnp.concatenate(pieces, axis=0).T


def wide_span(spans, which, i):
    return [jnp.concatenate([spans[which, e, i]] * HEADS_HERE, axis=1) for e in range(2)]


def masked_scores(keys, stacked, first, low, high):
    scores = dot(keys, stacked, NT)
    key_pos = first + lax.broadcasted_iota(jnp.int32, scores.shape, 0)
    return jnp.where((key_pos >= low) & (key_pos < high), scores, -1e30)


def attend_kernel(which, bounds, spans, q, k, v, o, mix, lse, acc):
    chunks, rows, width = q.shape

    def chunk(i, carry):
        stacked = stack_heads(q[i], HEAD_DIM ** (-0.5))
        lo, hi = wide_span(spans, which, i)
        acc[...] = jnp.zeros_like(acc)

        def step(kb, state):
            top, total = state
            first = pl.multiple_of(kb * KEY_BLOCK, KEY_BLOCK)
            scores = masked_scores(k[pl.ds(first, KEY_BLOCK), :], stacked, first, lo, hi)
            new_top = jnp.maximum(top, jnp.max(scores, axis=0, keepdims=True))
            fading = jnp.exp(top - new_top)
            weights = jnp.exp(scores - new_top)
            total = total * fading + jnp.sum(weights, axis=0, keepdims=True)
            acc[...] = acc[...] * fading + dot(
                v[pl.ds(first, KEY_BLOCK), :], weights.astype(bf16), TN
            )
            return new_top, total

        wide = HEADS_HERE * rows
        top, total = lax.fori_loop(
            bounds[which, 0, i],
            bounds[which, 1, i],
            step,
            (jnp.full((1, wide), -1e30, f32), jnp.zeros((1, wide), f32)),
        )
        lse[i] = top + jnp.log(total)
        result = take_heads(acc[...] / total, rows)
        o[i] = result
        mix[i] = result.astype(bf16)
        return carry

    lax.fori_loop(0, chunks, chunk, 0)


def attend(q, k, v, spans, which):
    bounds, spans = spans
    chunks, rows, width = q.shape
    wide = HEADS_HERE * rows
    return pl.pallas_call(
        partial(attend_kernel, which),
        out_shape=(
            jax.ShapeDtypeStruct(q.shape, f32),
            jax.ShapeDtypeStruct(q.shape, bf16),
            jax.ShapeDtypeStruct((chunks, 1, wide), f32),
        ),
        in_specs=[SMEM] + [VMEM] * 4,
        out_specs=(VMEM,) * 3,
        scratch_shapes=[pltpu.VMEM((width, wide), f32)],
        compiler_params=pltpu.CompilerParams(vmem_limit_bytes=56 * 2**20),
        name="attend",
        cost_estimate=lasts(12),
    )(bounds, spans, q, k, v)


def attend_back_kernel(
    which, bounds, spans, q, k, v, d_o, o, lse, dq, dk, dk_over, dv, dv_over, sums,
    qs, dos, delta, dq_acc, dk_acc, dv_acc
):
    chunks, rows, width = q.shape
    y = lax.axis_index("blk") % 2
    spread = KEY_BLOCK // (2 * rows)
    mine = [pl.ds(pl.multiple_of((2 * n + y) * rows, rows), rows) for n in range(spread)]
    theirs = [pl.ds(pl.multiple_of((2 * n + 1 - y) * rows, rows), rows) for n in range(spread)]
    sums[...] = jnp.zeros_like(sums)
    for i in range(chunks):
        qs[i] = stack_heads(q[i], HEAD_DIM ** (-0.5))
        dos[i] = stack_heads(d_o[i], 1.0)
        product = (d_o[i].astype(f32) * o[i]).T
        delta[i] = jnp.concatenate(
            [
                jnp.sum(product[h * HEAD_DIM : (h + 1) * HEAD_DIM], axis=0, keepdims=True)
                for h in range(HEADS_HERE)
            ],
            axis=1,
        )
    dq_acc[...] = jnp.zeros_like(dq_acc)

    def block(kb, carry):
        first = pl.multiple_of(kb * KEY_BLOCK, KEY_BLOCK)
        part = pl.ds(first, KEY_BLOCK)
        dk_acc[...] = jnp.zeros_like(dk_acc)
        dv_acc[...] = jnp.zeros_like(dv_acc)

        def chunk(i, inner):
            @pl.when((kb >= bounds[which, 0, i]) & (kb < bounds[which, 1, i]))
            def _():
                keys = k[part, :]
                lo, hi = wide_span(spans, which, i)
                scores = masked_scores(keys, qs[i], first, lo, hi)
                weights = jnp.exp(scores - lse[i])
                d_weights = dot(v[part, :], dos[i], NT)
                d_scores = (weights * (d_weights - delta[i])).astype(bf16)
                dv_acc[...] += dot(weights.astype(bf16), dos[i])
                dk_acc[...] += dot(d_scores, qs[i])
                dq_acc[i] += dot(keys, d_scores, TN)

            return inner

        lax.fori_loop(0, chunks, chunk, 0)
        for n in range(spread):
            dk[kb * spread + n] = dk_acc[mine[n], :].astype(bf16)
            dk_over[kb * spread + n] = dk_acc[theirs[n], :].astype(bf16)
            dv[kb * spread + n] = dv_acc[mine[n], :].astype(bf16)
            dv_over[kb * spread + n] = dv_acc[theirs[n], :].astype(bf16)
        sums[1:2] += jnp.sum(dv_acc[...], axis=0, keepdims=True)
        return carry

    lax.fori_loop(0, k.shape[0] // KEY_BLOCK, block, 0)
    for i in range(chunks):
        result = (take_heads(dq_acc[i], rows) * HEAD_DIM ** (-0.5)).astype(bf16)
        dq[i] = result
        sums[0:1] += jnp.sum(result.astype(f32), axis=0, keepdims=True)


def attend_back(q, k, v, spans, which, d_o, o, lse):
    bounds, spans = spans
    chunks, rows, width = q.shape
    wide = HEADS_HERE * rows
    half = (k.shape[0] // (2 * rows), rows, width)
    return pl.pallas_call(
        partial(attend_back_kernel, which),
        out_shape=(
            jax.ShapeDtypeStruct(q.shape, bf16),
            jax.ShapeDtypeStruct(half, bf16),
            jax.ShapeDtypeStruct(half, bf16),
            jax.ShapeDtypeStruct(half, bf16),
            jax.ShapeDtypeStruct(half, bf16),
            jax.ShapeDtypeStruct((8, width), f32),
        ),
        in_specs=[SMEM] + [VMEM] * 7,
        out_specs=(VMEM,) * 6,
        scratch_shapes=[
            pltpu.VMEM((chunks, wide, width), bf16),
            pltpu.VMEM((chunks, wide, width), bf16),
            pltpu.VMEM((chunks, 1, wide), f32),
            pltpu.VMEM((chunks, width, wide), f32),
            pltpu.VMEM((KEY_BLOCK, width), f32),
            pltpu.VMEM((KEY_BLOCK, width), f32),
        ],
        compiler_params=pltpu.CompilerParams(vmem_limit_bytes=60 * 2**20),
        name="attend_back",
        cost_estimate=lasts(14),
    )(bounds, spans, q, k, v, d_o, o, lse)


def key_spans(target_lengths, source_lengths, rows, count):
    ends = jnp.cumsum(target_lengths, dtype=jnp.int32)
    starts = ends - target_lengths
    chunk = jnp.arange(4, dtype=jnp.int32) * count + lax.axis_index("blk")

    def at(pos):
        past = (pos[..., None] >= ends).astype(jnp.int32)
        begun = (pos[..., None] >= starts).astype(jnp.int32)
        return (
            (jnp.sum(past * target_lengths, axis=-1), pos + 1),
            (jnp.sum(past * source_lengths, axis=-1), jnp.sum(begun * source_lengths, axis=-1)),
        )

    first, last = at(chunk * rows), at(chunk * rows + rows - 1)
    bounds = jnp.stack(
        [
            jnp.stack((low // KEY_BLOCK, (high + KEY_BLOCK - 1) // KEY_BLOCK))
            for (low, _), (_, high) in zip(first, last)
        ]
    ).astype(jnp.int32)
    spans = at(chunk[:, None] * rows + jnp.arange(rows, dtype=jnp.int32)[None, :])
    spans = jnp.stack([jnp.stack(s) for s in spans])
    return bounds, spans[:, :, :, None, :]


def body(
    count,
    inputs,
    encoded,
    d_output,
    target_lengths,
    source_lengths,
    norm_gain,
    norm_shift,
    self_qkv,
    self_bias,
    self_out,
    cross_q,
    cross_kv,
    cross_bias,
    cross_out,
    out_bias,
    ffn_in,
    ffn_in_bias,
    ffn_out,
):
    rows, width = inputs.shape
    devices = 4 * count
    share = width // devices
    head_width = width // 4
    hidden_width = ffn_in.shape[1]
    hidden_here = hidden_width // 4
    hidden_rows = hidden_width // width
    tokens_here = 4 * rows

    def split_cols(w):
        return jnp.transpose(w.reshape(share, -1, 4, w.shape[-1] // 4), (2, 0, 1, 3)).reshape(
            4, share, -1
        )

    small = jnp.concatenate(
        (
            norm_gain,
            norm_shift,
            self_bias,
            cross_bias,
            out_bias,
            ffn_in_bias.reshape(hidden_rows, share),
        )
    )
    n_small = small.shape[0]
    small = jnp.pad(small, ((0, N_SMALL - n_small), (0, 128 - share)))
    (
        table, here, b_hidden, w_qkv, w_cross_kv, w_cross_q, w_self_out, w_cross_out, w_ffn_in,
        inputs_all, encoded_all, d_output_all, normed_one, q1, k1, v1, k2, v2,
    ) = front(
        small,
        [split_cols(w) for w in (self_qkv, cross_kv, cross_q)],
        self_out[None],
        cross_out[None],
        split_cols(ffn_in),
        [inputs, encoded, d_output],
        count,
        0,
    )
    ffn_out, w_ffn_in = tie(ffn_out, w_ffn_in)
    w_ffn_out = lax.all_gather(ffn_out, "blk", axis=0, tiled=True)
    w_ffn_in = lax.all_gather(w_ffn_in, "blk", axis=1, tiled=True).reshape(width, -1)
    w_qkv, w_cross_kv, w_cross_q, w_self_out, w_cross_out = (
        w.reshape(-1, w.shape[-1]) for w in (w_qkv, w_cross_kv, w_cross_q, w_self_out, w_cross_out)
    )
    spans = key_spans(target_lengths, source_lengths, rows, count)

    k1, v1 = (a.reshape(-1, head_width) for a in (k1, v1))
    o1, mix1, lse1 = attend(q1, k1, v1, spans, 0)
    first, normed_two, q2, k2, v2 = join_forward(
        mix1, w_self_out, inputs, table, 0, count, 2, query=(w_cross_q, here), stream=(k2, v2)
    )
    k2, v2 = (a.reshape(-1, head_width) for a in (k2, v2))
    o2, mix2, lse2 = attend(q2, k2, v2, spans, 1)
    second, normed_three = join_forward(mix2, w_cross_out, first, table, 1, count, 3)

    out_part, d_part, ffn_mine, ffn_over, d_hidden = feed_forward(
        normed_three, d_output_all, w_ffn_in, w_ffn_out, b_hidden, count
    )
    swap = [(i, i ^ 1) for i in range(count)]
    ffn_over = lax.ppermute(ffn_over, "blk", swap)
    d_second, stats_three, d_o2, grad_cross_out, layer_output = join_backward(
        (d_part, out_part), d_output, second, table, 2, w_cross_out, mix2, count, 4
    )
    dq2, dk2, dk2_over, dv2, dv2_over, sums_two = attend_back(q2, k2, v2, spans, 1, d_o2, o2, lse2)
    inside = rows == 4 * share
    if inside:
        dk2_over, dv2_over = lax.ppermute((dk2_over, dv2_over), "blk", swap)
    dq2, ffn_over = tie(dq2, ffn_over)
    lines = [list(range(y, count, 2)) for y in range(2)]
    ffn_terms = lax.all_to_all(
        (ffn_mine.astype(f32) + ffn_over.astype(f32)).astype(bf16), "blk", 0, 0,
        axis_index_groups=lines, tiled=True,
    )
    d_first, stats_two, d_o1, grad_self_out, grad_cross_q = join_backward(
        (dq2, w_cross_q, normed_two), d_second, first, table, 1, w_self_out, mix1, count, 5
    )
    dq1, dk1, dk1_over, dv1, dv1_over, sums_one = attend_back(q1, k1, v1, spans, 0, d_o1, o1, lse1)
    pairs = (dk1, dv1, dk2, dv2, dk1_over, dv1_over, dk2_over, dv2_over)
    if inside:
        pairs = [a.reshape(4, count // 2, 4, share, head_width) for a in pairs]
    else:
        y = lax.axis_index("blk") % 2
        pairs = [
            jnp.where(y == 0, jnp.stack((a, b), axis=1), jnp.stack((b, a), axis=1)).reshape(
                4, count, rows, head_width
            )
            for a, b in zip(pairs[:4], pairs[4:])
        ]
        pairs = scatter_blk(pairs, count, 6)
    got = finale(
        count, pairs, grad_cross_out, grad_self_out, grad_cross_q, ffn_terms, dq1, normed_one,
        encoded_all, w_qkv, w_cross_kv, inputs, d_first, table, stats_two, stats_three,
        sums_one, sums_two, d_hidden, 7,
    )
    done = settle(got, layer_output, share, width, hidden_width)
    order = (
        "layer", "d_inputs", "d_encoded", "gain", "shift", "qkv", "self_bias", "so", "cq", "ckv",
        "cross_bias", "co", "out_bias", "ffn_in", "ffn_bias", "ffn_out",
    )
    outs = [done["out_" + n] for n in order]
    outs[14] = outs[14].reshape(-1)
    return tuple(outs)


def solution(mesh):
    both = ("head", "blk")
    rows2, rows3, cols2 = P(both, None), P(both, None, None), P(None, both)
    return jax.shard_map(
        partial(body, mesh.shape["blk"]),
        mesh=mesh,
        in_specs=(
            rows2, rows2, rows2, P(), P(), cols2, cols2, rows3, cols2, rows2, rows2, rows3,
            cols2, rows2, cols2, rows2, P(both), rows2,
        ),
        out_specs=(
            rows2, rows2, rows2, cols2, cols2, rows3, cols2, rows2, rows2, rows3, cols2, rows2,
            cols2, rows2, P(both), rows2,
        ),
        check_vma=False,
    )
```

```python
from functools import partial

import jax
import jax.numpy as jnp
from jax import lax
from jax.experimental import pallas as pl
from jax.experimental.pallas import tpu as pltpu
from jax.sharding import PartitionSpec as P

HEAD_DIM = 64
HEADS_HERE = 4
KEY_BLOCK = 512
AHEAD = 2
SKEW = 2
MESH = pl.DeviceIdType.MESH
ANY = pl.BlockSpec(memory_space=pl.ANY)
VMEM = pl.BlockSpec(memory_space=pltpu.VMEM)
SMEM = pl.BlockSpec(memory_space=pltpu.SMEM)
DMA = pltpu.SemaphoreType.DMA
f32 = jnp.float32
bf16 = jnp.bfloat16
NT = (((1,), (1,)), ((), ()))
NN = (((1,), (0,)), ((), ()))
TN = (((0,), (0,)), ((), ()))


def dot(a, b, dims=NN):
    return lax.dot_general(a, b, dims, preferred_element_type=f32)


def params(cid):
    return pltpu.CompilerParams(
        collective_id=cid, has_side_effects=True, vmem_limit_bytes=56 * 2**20
    )


def lasts(us):
    return pl.CostEstimate(flops=int(us * 3e8), bytes_accessed=int(us * 3e5), transcendentals=0)


def remote(src, dst, ssem, rsem, device):
    return pltpu.make_async_remote_copy(
        src, dst, ssem, rsem, device_id=device, device_id_type=MESH
    )


class Head:
    def __init__(self):
        self.me = lax.axis_index("head")
        self.core = self.me % 2
        self.x = self.me // 2
        self.sib = self.me + 1 - 2 * self.core
        self.far = self.me + 2 - 4 * self.x
        self.far_sib = self.sib + 2 - 4 * self.x


class Blk:
    def __init__(self, count):
        self.me = lax.axis_index("blk")
        self.z = self.me // 2
        self.y = self.me % 2
        self.Z = count // 2
        self.across = self.me + 1 - 2 * self.y


def signal(bar, **device):
    pl.semaphore_signal(bar, inc=1, device_id=device, device_id_type=MESH)


def greet_head(bar, hd):
    for k in range(1, 4):
        signal(bar, head=(hd.me + k) % 4)
    return 3


def greet_blk(bar, bk):
    signal(bar, blk=bk.across)

    @pl.when(bk.z > 0)
    def _():
        signal(bar, blk=bk.me - 2)

    @pl.when(bk.z < bk.Z - 1)
    def _():
        signal(bar, blk=bk.me + 2)

    return 1 + jnp.where(bk.z > 0, 1, 0) + jnp.where(bk.z < bk.Z - 1, 1, 0)


class BlkGather:
    def __init__(self, bk, outs, ssem, rsem, wide=()):
        self.bk, self.outs, self.ssem, self.rsem, self.wide = bk, outs, ssem, rsem, wide

    def copy(self, a, slot, way, device, src=None):
        view = self.outs[a].at[:, slot]
        return remote(
            view if src is None else src,
            view,
            self.ssem.at[a, way, slot],
            self.rsem.at[a, slot],
            {"blk": device},
        )

    def along(self, a, slot, upward, downward, src=None):
        bk = self.bk
        if upward:

            @pl.when(bk.z < bk.Z - 1)
            def _():
                self.copy(a, slot, 0, bk.me + 2, src).start()

        if downward:

            @pl.when(bk.z > 0)
            def _():
                self.copy(a, slot, 1, bk.me - 2, src).start()

    def start(self, a, src=None):
        self.along(a, self.bk.me, True, True, src)
        self.copy(a, self.bk.me, 2, self.bk.across, src).start()

    def step(self, a, k):
        bk = self.bk
        if k == 0:
            if a in self.wide:
                self.copy(a, bk.across, 2, bk.me).wait_recv()
                self.along(a, bk.across, True, True)
            return
        firsts = (bk.me, bk.across) if a in self.wide else (bk.me,)

        @pl.when(bk.z - k >= 0)
        def _():
            for first in firsts:
                slot = first - 2 * k
                self.copy(a, slot, 0, bk.me).wait_recv()
                self.along(a, slot, True, False)
                if a not in self.wide:
                    self.copy(a, slot, 2, bk.across).start()

        @pl.when(bk.z + k < bk.Z)
        def _():
            for first in firsts:
                slot = first + 2 * k
                self.copy(a, slot, 0, bk.me).wait_recv()
                self.along(a, slot, False, True)
                if a not in self.wide:
                    self.copy(a, slot, 2, bk.across).start()

    def arrive(self, a):
        if a not in self.wide:
            for s in range(self.bk.Z):
                self.copy(a, 2 * s + 1 - self.bk.y, 0, self.bk.me).wait_recv()

    def drain(self, a):
        bk = self.bk
        for s in range(bk.Z):
            for y in (bk.y, 1 - bk.y) if a in self.wide else (bk.y,):
                slot = 2 * s + y

                @pl.when((s <= bk.z) & (bk.z < bk.Z - 1))
                def _():
                    self.copy(a, slot, 0, bk.me).wait_send()

                @pl.when((s >= bk.z) & (bk.z > 0))
                def _():
                    self.copy(a, slot, 1, bk.me).wait_send()

            if a not in self.wide:
                self.copy(a, 2 * s + bk.y, 2, bk.me).wait_send()
        if a in self.wide:
            self.copy(a, bk.me, 2, bk.me).wait_send()


N_SMALL = 24


def front_kernel(
    count, small, qkv, ckv, cq, so, co, ffn_in, inputs, encoded, d_output, *refs
):
    (
        table, bias, b_hidden, w_qkv, w_ckv, w_cq, w_so, w_co, swapped, inputs_all, encoded_all,
        d_output_all, normed, q1, k1, v1, k2, v2, small_all, vectors, lsem, hs, hr, ssem, rsem,
    ) = refs
    hd, bk = Head(), Blk(count)
    share, head_width = cq.shape[0], q1.shape[2]
    rows, width = inputs.shape
    bar = pltpu.get_barrier_semaphore()
    pl.semaphore_wait(bar, greet_head(bar, hd) + greet_blk(bar, bk))
    ring = BlkGather(bk, (small_all, w_qkv, w_ckv, w_cq, w_so, w_co, k1, v1), ssem, rsem)
    K1, V1 = 6, 7
    pairs = (
        (small, small_all), (qkv, w_qkv), (ckv, w_ckv), (cq, w_cq), (so, w_so), (co, w_co),
        (inputs, inputs_all), (encoded, encoded_all), (ffn_in, swapped), (d_output, d_output_all),
    )
    SMALL, QKV, CKV, CQ, SO, CO, INPUTS, ENCODED, FFN_IN, D_OUTPUT = range(10)
    rows_only = (SO, CO)

    pieces = {QKV: 3, CKV: 2}

    def lanes(first, to, step):
        return pl.ds(pl.multiple_of(first + to * step, step), step)

    def source(a, to, i):
        if a == QKV:
            return qkv.at[i, :, lanes(0, to, head_width)]
        if a == CKV:
            return ckv.at[:, lanes(i * width, to, head_width)]
        if a == CQ:
            return cq.at[:, lanes(0, to, head_width)]
        if a == FFN_IN:
            return ffn_in.at[:, lanes(0, to, ffn_in.shape[1] // 4)]
        return pairs[a][0]

    def target(a, h, i):
        if a in rows_only:
            return pairs[a][1].at[:, bk.me]
        if a in pieces:
            return pairs[a][1].at[h, bk.me, :, i * head_width : (i + 1) * head_width]
        return pairs[a][1].at[h] if a >= INPUTS else pairs[a][1].at[h, bk.me]

    def own(a):
        return [
            pltpu.make_async_copy(source(a, hd.me, i), target(a, hd.me, i), lsem.at[a, i])
            for i in range(pieces.get(a, 1))
        ]

    def across_head(a, k, back):
        to = (hd.me + k) % 4
        here = to if back else hd.me
        return [
            remote(
                source(a, to, i), target(a, here, i), hs.at[a, k, i], hr.at[a, here, i], {"head": to}
            )
            for i in range(pieces.get(a, 1))
        ]

    def headed(a):
        for copy in own(a):
            copy.wait()
        for k in range(1, 4):
            for copy in across_head(a, k, True):
                copy.wait_recv()

    everything = (SMALL, QKV, CKV, CQ, INPUTS, ENCODED, FFN_IN, D_OUTPUT)
    for a in everything:
        for copy in own(a):
            copy.start()
        for k in (2, 1, 3):
            for copy in across_head(a, k, False):
                copy.start()
    for a in rows_only:
        own(a)[0].start()
    headed(SMALL)
    ring.start(SMALL)
    headed(QKV)
    ring.start(QKV)
    for a in rows_only:
        ring.start(a, pairs[a][0])
    headed(CKV)
    ring.start(CKV)
    headed(CQ)
    ring.start(CQ)
    for k in range(1, bk.Z):
        for a in (SMALL, QKV) + ((SO, CO, CKV, CQ) if k < bk.Z - 1 else ()):
            ring.step(a, k)
    ring.arrive(0)
    lane = lax.broadcasted_iota(jnp.int32, (N_SMALL, 128), 1)

    def assemble(h, carry):
        for group in range(head_width // 128):
            total = jnp.zeros((N_SMALL, 128), f32)
            for i in range(128 // share):
                piece = small_all[h, group * (128 // share) + i].astype(f32)
                if i:
                    piece = pltpu.roll(piece, i * share, 1)
                total = jnp.where(lane // share == i, piece, total)
            vectors[h, :, group * 128 : (group + 1) * 128] = total
        return carry

    lax.fori_loop(0, 4, assemble, 0)

    for h in range(4):
        table[:, h * head_width : (h + 1) * head_width] = vectors[h]
    bias[...] = vectors[hd.me]
    first = lax.broadcasted_iota(jnp.int32, (1, 128), 1)
    per_group = 128 // share
    for group in range(4 * count // per_group):
        total = jnp.zeros((1, 128), f32)
        for i in range(per_group):
            b, run = divmod(group * per_group + i, 4)
            piece = small_all[hd.me, b].astype(f32)[13 + run : 14 + run]
            if i:
                piece = pltpu.roll(piece, i * share, 1)
            total = jnp.where(first // share == i, piece, total)
        b_hidden[:, group * 128 : (group + 1) * 128] = total
    gain, shift = table[0:1], table[3:4]
    headed(INPUTS)

    def norm(j, carry):
        normed[j] = layer_norm(inputs_all[j].astype(f32), gain, shift).astype(bf16)
        return carry

    lax.fori_loop(0, 4, norm, 0)
    for a in (SO, CO, CKV, CQ):
        ring.step(a, bk.Z - 1)
    ring.arrive(QKV)

    def project(features, w, c, bias_row, store):
        cols = w[:, :, :, c * head_width : (c + 1) * head_width].reshape(width, head_width)

        def one(j, carry):
            out = dot(features[j], cols)
            if bias_row is not None:
                out = out + bias[bias_row : bias_row + 1, :]
            store(j, out.astype(bf16))
            return carry

        lax.fori_loop(0, 4, one, 0)

    def into(ref):
        def store(j, value):
            ref[j] = value

        return store

    def into_own(ref):
        def store(j, value):
            ref[j, bk.me] = value

        return store

    project(normed, w_qkv, 1, None, into_own(k1))
    ring.start(K1)
    project(normed, w_qkv, 2, 7, into_own(v1))
    ring.start(V1)
    project(normed, w_qkv, 0, 6, into(q1))
    headed(ENCODED)
    ring.step(K1, 1)
    ring.step(V1, 1)
    ring.arrive(CKV)
    project(encoded_all, w_ckv, 0, None, into(k2))
    project(encoded_all, w_ckv, 1, 9, into(v2))
    for k in range(2, bk.Z):
        ring.step(K1, k)
        ring.step(V1, k)
    for a in rows_only:
        own(a)[0].wait()
    for a in (FFN_IN, D_OUTPUT):
        headed(a)
    for a in (CQ, SO, CO, K1, V1):
        ring.arrive(a)
    for a in range(8):
        ring.drain(a)
    for a in everything:
        for k in range(1, 4):
            for copy in across_head(a, k, False):
                copy.wait_send()


def front(small, cols, so, co, ffn_in, acts, count, cid):
    rows, width = acts[0].shape
    share, head_width = so.shape[1], width // 4
    hidden_here = ffn_in.shape[1] // 4
    keys = (4, count, rows, head_width)
    tokens = (4, rows, width)
    block = (4, rows, head_width)
    bf = [(4, count, share, n * head_width) for n in (3, 2, 1)] + [(1, count) + a.shape[1:] for a in (so, co)]
    bf += [(4, share, hidden_here)] + [tokens] * 4 + [block, keys, keys, block, block]
    return pl.pallas_call(
        partial(front_kernel, count),
        out_shape=[
            jax.ShapeDtypeStruct((N_SMALL, width), f32),
            jax.ShapeDtypeStruct((N_SMALL, head_width), f32),
            jax.ShapeDtypeStruct((1, hidden_here), f32),
        ]
        + [jax.ShapeDtypeStruct(s, bf16) for s in bf],
        in_specs=[ANY] * 10,
        out_specs=[VMEM] * 5 + [ANY] * 4 + [VMEM] * 2 + [ANY] + [VMEM] * 6,
        scratch_shapes=[
            pltpu.VMEM((4, count, N_SMALL, 128), bf16),
            pltpu.VMEM((4, N_SMALL, head_width), f32),
            DMA((10, 3)),
            DMA((10, 4, 3)),
            DMA((10, 4, 3)),
            DMA((8, 3, count)),
            DMA((8, count)),
        ],
        compiler_params=params(cid),
        name="front",
        cost_estimate=lasts(90),
    )(small, *cols, so, co, ffn_in, *acts)


class BlkScatter:
    def __init__(self, bk, ins, bufs, sems):
        self.bk, self.ins = bk, ins
        self.own, self.over, self.side = bufs
        self.lsem, self.ys, self.yr, self.zs, self.ur, self.dr = sems

    def load(self, a, s):
        return pltpu.make_async_copy(
            self.ins[a].at[:, 2 * s + self.bk.y], self.own[a].at[s], self.lsem.at[a, s]
        )

    def cross(self, a, s):
        return remote(
            self.ins[a].at[:, 2 * s + 1 - self.bk.y],
            self.over[a].at[s],
            self.ys.at[a, s],
            self.yr.at[a, s],
            {"blk": self.bk.across},
        )

    def send(self, a, s, upward, slot=None):
        if slot is None:
            slot = s if upward else jnp.where(s == self.bk.z - 1, self.bk.Z, s)
        return remote(
            self.own[a].at[s],
            self.side[a].at[slot],
            self.zs.at[a, s],
            (self.ur if upward else self.dr).at[a, s],
            {"blk": self.bk.me + (2 if upward else -2)},
        )

    def order(self):
        for k in range((self.bk.Z + 1) // 2):
            yield self.bk.Z - 1 - k
            if k != self.bk.Z - 1 - k:
                yield k

    def begin(self, a):
        if a < len(self.ins):
            for s in self.order():
                self.cross(a, s).start()
                self.load(a, s).start()

    def add(self, a, s, extra, store):
        groups, rows = self.own[a].shape[1:3]
        step = min(rows, 32)

        def one(g, carry):
            for r in range(0, rows, step):
                part = pl.ds(r, step)
                total = self.own[a][s, g, part].astype(f32) + self.over[a][s, g, part].astype(f32)
                for slot in extra:
                    total = total + self.side[a][slot, g, part].astype(f32)
                store(g, part, total)
            return carry

        lax.fori_loop(0, groups, one, 0)

    def relay(self, a, s, upward):
        bk = self.bk
        self.load(a, s).wait()
        self.cross(a, s).wait_recv()
        inner = (bk.z > 0) if upward else (bk.z < bk.Z - 1)

        def store(g, part, total):
            self.own[a][s, g, part] = total.astype(bf16)

        @pl.when(inner)
        def _():
            self.send(a, s, upward, s).wait_recv()
            self.add(a, s, (s,), store)

        @pl.when(jnp.logical_not(inner))
        def _():
            self.add(a, s, (), store)

        self.send(a, s, upward).start()

    def run(self, finish):
        bk, n = self.bk, len(self.ins)
        for a in range(n):
            self.begin(a + AHEAD)
            for k in range(bk.Z - 1):

                @pl.when(bk.Z - 1 - k > bk.z)
                def _():
                    self.relay(a, bk.Z - 1 - k, True)

                @pl.when(k < bk.z)
                def _():
                    self.relay(a, k, False)

            if a > 0:
                finish(a - 1)
        finish(n - 1)

    def last(self, a, store):
        bk, s = self.bk, self.bk.z
        self.load(a, s).wait()
        self.cross(a, s).wait_recv()

        @pl.when(bk.z > 0)
        def _():
            self.send(a, s, True, s).wait_recv()

        @pl.when(bk.z < bk.Z - 1)
        def _():
            self.send(a, s, False, bk.Z).wait_recv()

        @pl.when((bk.z > 0) & (bk.z < bk.Z - 1))
        def _():
            self.add(a, s, (s, bk.Z), store)

        @pl.when((bk.z > 0) & (bk.z == bk.Z - 1))
        def _():
            self.add(a, s, (s,), store)

        @pl.when((bk.z == 0) & (bk.z < bk.Z - 1))
        def _():
            self.add(a, s, (bk.Z,), store)

    def finish(self):
        bk = self.bk
        for a in range(len(self.ins)):
            for s in range(bk.Z):
                self.cross(a, s).wait_send()

                @pl.when(s != bk.z)
                def _():
                    self.send(a, s, True, s).wait_send()


def scatter_scratch(items, count):
    Z = count // 2
    kinds = [
        pltpu.VMEM((slots, a.shape[0]) + a.shape[2:], bf16)
        for slots in (Z, Z, Z + 1)
        for a in items
    ]
    return kinds + [DMA((len(items), Z)) for _ in range(6)]


def scatter_parts(refs, n):
    bufs = tuple(refs[k * n : (k + 1) * n] for k in range(3))
    return bufs, refs[3 * n : 3 * n + 6], refs[3 * n + 6 :]


def scatter_blk_kernel(count, n, *refs):
    ins, outs = refs[:n], refs[n : 2 * n]
    bufs, sems, _ = scatter_parts(refs[2 * n :], n)
    bk = Blk(count)
    bar = pltpu.get_barrier_semaphore()
    pl.semaphore_wait(bar, greet_blk(bar, bk))
    ring = BlkScatter(bk, ins, bufs, sems)
    for a in range(AHEAD):
        ring.begin(a)

    def finish(a):
        def store(g, part, total):
            outs[a][g, part] = total.astype(outs[a].dtype)

        ring.last(a, store)

    ring.run(finish)
    ring.finish()


def scatter_blk(items, count, cid):
    n = len(items)
    return pl.pallas_call(
        partial(scatter_blk_kernel, count, n),
        out_shape=[
            jax.ShapeDtypeStruct((a.shape[0],) + a.shape[2:], a.dtype) for a in items
        ],
        in_specs=[ANY] * n,
        out_specs=[VMEM] * n,
        scratch_shapes=scatter_scratch(items, count),
        compiler_params=params(cid),
        name="scatter_blk",
        cost_estimate=lasts(60),
    )(*items)


PARTS = 2


class Halves:
    def half(self, p):
        rows = self.rows // PARTS
        return pl.ds(p * rows, rows)


class HeadSum(Halves):
    def __init__(self, hd, part, near, mid, far, sems):
        self.hd, self.part, self.near, self.mid, self.far = hd, part, near, mid, far
        self.ss, self.rs = sems
        self.rows = mid.shape[0]

    def near_copies(self, i):
        hd = self.hd
        block = hd.far_sib if i == 0 else hd.sib
        return [
            remote(
                self.part.at[block, self.half(p)],
                self.near.at[i, self.half(p)],
                self.ss.at[i, p],
                self.rs.at[i, p],
                {"head": hd.sib},
            )
            for p in range(PARTS)
        ]

    def near_start(self, i):
        for copy in self.near_copies(i):
            copy.start()

    def far_copy(self, p):
        return remote(
            self.mid.at[self.half(p)],
            self.far.at[self.half(p)],
            self.ss.at[2, p],
            self.rs.at[2, p],
            {"head": self.hd.far},
        )

    def begin(self):
        self.near_start(0)
        self.near_start(1)

    def middle(self):
        for p in range(PARTS):
            self.near_copies(0)[p].wait_recv()
            here = self.half(p)
            mine = self.part[self.hd.far, here].astype(f32)
            self.mid[here] = (mine + self.near[0, here].astype(f32)).astype(bf16)
            self.far_copy(p).start()

    def total(self, p):
        here = self.half(p)
        self.near_copies(1)[p].wait_recv()
        mine = self.part[self.hd.me, here].astype(f32) + self.near[1, here].astype(f32)
        self.far_copy(p).wait_recv()
        return mine + self.far[here].astype(f32)

    def whole(self):
        return jnp.concatenate([self.total(p) for p in range(PARTS)], axis=0)

    def finish(self):
        for p in range(PARTS):
            self.near_copies(0)[p].wait_send()
            self.near_copies(1)[p].wait_send()
            self.far_copy(p).wait_send()


def head_sum_scratch(rows, width):
    return [
        pltpu.VMEM((2, rows, width), bf16),
        pltpu.VMEM((rows, width), bf16),
        pltpu.VMEM((rows, width), bf16),
        DMA((3, PARTS)),
        DMA((3, PARTS)),
    ]


def head_gather_scratch():
    return [DMA((3, PARTS)), DMA((4, PARTS))]


class HeadGather(Halves):
    def __init__(self, hd, out, ss, rs):
        self.hd, self.out, self.ss, self.rs = hd, out, ss, rs
        self.rows = out.shape[1]

    def copy(self, slot, way, device, p):
        view = self.out.at[slot, self.half(p)]
        return remote(view, view, self.ss.at[way, p], self.rs.at[slot, p], {"head": device})

    def begin(self, p):
        hd = self.hd
        self.copy(hd.me, 0, hd.far, p).start()
        self.copy(hd.me, 1, hd.sib, p).start()

    def forward(self):
        hd = self.hd
        for p in range(PARTS):
            self.copy(hd.far, 0, hd.me, p).wait_recv()
            self.copy(hd.far, 2, hd.sib, p).start()

    def arrive(self):
        hd = self.hd
        for p in range(PARTS):
            self.copy(hd.sib, 0, hd.me, p).wait_recv()
            self.copy(hd.far_sib, 0, hd.me, p).wait_recv()

    def drain(self):
        hd = self.hd
        for p in range(PARTS):
            self.copy(hd.me, 0, hd.far, p).wait_send()
            self.copy(hd.me, 1, hd.sib, p).wait_send()
            self.copy(hd.far, 2, hd.sib, p).wait_send()


def row_stats(v):
    average = jnp.mean(v, axis=-1, keepdims=True)
    centred = v - average
    spread = jnp.mean(centred * centred, axis=-1, keepdims=True)
    return centred, lax.rsqrt(spread + 1e-05)


def layer_norm(v, gain, shift):
    centred, r = row_stats(v)
    return centred * r * gain + shift


def layer_norm_back(v, g, gain):
    centred, r = row_stats(v)
    u = centred * r
    c = g * gain
    dv = r * (c - jnp.mean(c, axis=-1, keepdims=True) - u * jnp.mean(c * u, axis=-1, keepdims=True))
    return dv, jnp.sum(g * u, axis=0, keepdims=True), jnp.sum(g, axis=0, keepdims=True)


SMALL_ROWS = (
    ("gain", 3), ("shift", 3), ("self_bias", 2), ("cross_bias", 2), ("out_bias", 3), ("ffn_bias", 4)
)
PAIRS = ("dk1", "dv1", "dk2", "dv2")


class PageScatter:
    def __init__(self, bk, feeds, bufs, sems, ready, crossed):
        self.bk, self.feeds, self.ready, self.crossed = bk, feeds, ready, crossed
        self.own, self.over, self.side = bufs
        self.lsem, self.ys, self.yr, self.zs, self.ur, self.dr = sems
        self.n = len(feeds)

    def load(self, a, s):
        copies = [
            pltpu.make_async_copy(src(s, True), self.own.at[(a, s) + dst], self.lsem.at[a, s, i])
            for i, (src, dst) in enumerate(self.feeds[a])
        ]
        if a in self.crossed:
            copies += [
                pltpu.make_async_copy(
                    src(s, False), self.over.at[(a, s) + dst], self.yr.at[a, s, i]
                )
                for i, (src, dst) in enumerate(self.feeds[a])
            ]
        return copies

    def cross(self, a, s):
        if a in self.crossed:
            return []
        return [
            remote(
                src(s, False),
                self.over.at[(a, s) + dst],
                self.ys.at[a, s, i],
                self.yr.at[a, s, i],
                {"blk": self.bk.across},
            )
            for i, (src, dst) in enumerate(self.feeds[a])
        ]

    def begin(self, a):
        Z = self.bk.Z
        for k in range(Z):
            s = Z - 1 - k // 2 if k % 2 == 0 else k // 2
            for copy in self.cross(a, s) + self.load(a, s):
                copy.start()

    def send(self, a, s, upward, slot=None):
        bk = self.bk
        if slot is None:
            slot = s if upward else jnp.where(s == bk.z - 1, bk.Z, s)
        return remote(
            self.own.at[a, s],
            self.side.at[a, slot],
            self.zs.at[a, s],
            (self.ur if upward else self.dr).at[a, s],
            {"blk": bk.me + (2 if upward else -2)},
        )

    def gathered(self, a):
        for s in range(self.bk.Z):
            for copy in self.load(a, s):
                copy.wait()
            for copy in self.cross(a, s):
                copy.wait_recv()

    def relay(self, a, s, upward):
        bk = self.bk
        inner = (bk.z > 0) if upward else (bk.z < bk.Z - 1)

        @pl.when(inner)
        def _():
            self.send(a, s, upward, s).wait_recv()
            self.own[a, s] = (
                self.own[a, s].astype(f32)
                + self.over[a, s].astype(f32)
                + self.side[a, s].astype(f32)
            ).astype(bf16)

        @pl.when(jnp.logical_not(inner))
        def _():
            self.own[a, s] = (
                self.own[a, s].astype(f32) + self.over[a, s].astype(f32)
            ).astype(bf16)

        self.send(a, s, upward).start()

    def wave(self, t):
        bk = self.bk
        if t < self.n:
            self.gathered(t)
        up, down = t - SKEW * bk.z, t - SKEW * (bk.Z - 1 - bk.z)

        @pl.when((up >= 0) & (up < self.n))
        def _():
            def one(i, carry):
                self.relay(up, bk.Z - 1 - i, True)
                return carry

            lax.fori_loop(0, bk.Z - 1 - bk.z, one, 0)

        @pl.when((down >= 0) & (down < self.n))
        def _():
            def one(i, carry):
                self.relay(down, i, False)
                return carry

            lax.fori_loop(0, bk.z, one, 0)

        a = t - SKEW * (bk.Z - 1)
        if a >= 0:
            self.last(a)

    def last(self, a):
        bk, s = self.bk, self.bk.z
        total = self.own[a, s].astype(f32) + self.over[a, s].astype(f32)

        @pl.when(bk.z > 0)
        def _():
            self.send(a, s, True, s).wait_recv()

        @pl.when(bk.z < bk.Z - 1)
        def _():
            self.send(a, s, False, bk.Z).wait_recv()

        total = total + jnp.where(bk.z > 0, self.side[a, s].astype(f32), 0.0)
        total = total + jnp.where(bk.z < bk.Z - 1, self.side[a, bk.Z].astype(f32), 0.0)
        self.ready[a](total)

    def drain(self):
        bk = self.bk
        for a in range(self.n):
            for s in range(bk.Z):
                for copy in self.cross(a, s):
                    copy.wait_send()

                @pl.when(s != bk.z)
                def _():
                    self.send(a, s, True, s).wait_send()


def finale_kernel(count, inside, names_in, names_out, names_scratch, *refs):
    r = dict(zip(names_in + names_out + names_scratch, refs))
    hd, bk = Head(), Blk(count)
    devices = 4 * count
    me = hd.me * count + bk.me
    rows, width = r["d_first"].shape
    head_width = width // 4
    share = width // devices
    bar = pltpu.get_barrier_semaphore()

    def place(k):
        to = (me + k) % devices
        return to, {"head": to // count, "blk": to % count}

    def greet(k, carry):
        signal(bar, **place(k)[1])
        return carry

    lax.fori_loop(1, devices, greet, 0)
    pl.semaphore_wait(bar, devices - 1)

    def tiles(src, dst, which):
        local = pltpu.make_async_copy(src.at[me], dst.at[me], r["tile_local"].at[which])

        def copy(k, back):
            to, device = place(k)
            return remote(
                src.at[to],
                dst.at[to if back else me],
                r["tile_send"].at[which, k],
                r["tile_recv"].at[which, to if back else me],
                device,
            )

        def start(k, carry):
            copy(k, False).start()
            return carry

        def end(k, carry):
            copy(k, False).wait_send()
            copy(k, True).wait_recv()
            return carry

        def begin():
            local.start()
            lax.fori_loop(1, devices, start, 0)

        def finish():
            local.wait()
            lax.fori_loop(1, devices, end, 0)

        return begin, finish

    headed = ["ffn_in", "cq", "qkv", "ckv"]

    def across_head(n, k, back):
        a = headed.index(n)
        to = (hd.me + k) % 4
        src = r["ffn_in"] if n == "ffn_in" else r["done_" + n]
        return remote(
            src.at[to],
            r["out_" + n].at[to if back else hd.me],
            r["head_send"].at[a, k],
            r["head_recv"].at[a, to if back else hd.me],
            {"head": to},
        )

    def send_heads(n):
        for k in range(1, 4):
            across_head(n, k, False).start()
        src = r["ffn_in"] if n == "ffn_in" else r["done_" + n]
        r["out_" + n][hd.me] = src[hd.me]

    def place_of(s, mine):
        return 2 * s + (bk.y if mine else 1 - bk.y)

    def col_page(ref, c):
        def src(s, mine):
            return ref.at[:, place_of(s, mine), :, c * head_width : (c + 1) * head_width]

        return [(src, ())]

    def row_page(ref):
        def src(j):
            return lambda s, mine: ref.at[
                0, place_of(s, mine), :, j * head_width : (j + 1) * head_width
            ]

        return [(src(j), (j,)) for j in range(4)]

    def pair_page(n, h):
        return [(lambda s, mine: r[n if mine else n + "_over"].at[h, s], ())]

    def store_pair(n, h):
        def store(total):
            r["sum_" + n][h] = total.reshape(rows, head_width).astype(bf16)

        return store

    def store_col(n, c):
        def store(total):
            r["done_" + n][:, :, c * head_width : (c + 1) * head_width] = total.astype(bf16)

        return store

    def store_row(n):
        def store(total):
            for j in range(4):
                r["out_" + n][0, :, j * head_width : (j + 1) * head_width] = total[j]

        return store

    feeds, ready, crossed, index = [], [], [], {}

    def item(name, feed, store):
        index[name] = len(feeds)
        feeds.append(feed)
        ready.append(store)

    if inside:
        for n, h in [(n, h) for n in ("dk2", "dk1", "dv1", "dv2") for h in range(4)]:
            if n in ("dk2", "dv2"):
                crossed.append(len(feeds))
            item(n, pair_page(n, h), store_pair(n, h))
    for n in ("so", "co"):
        item(n, row_page(r[n]), store_row(n))
    item("cq", col_page(r["cq"], 0), store_col("cq", 0))
    item("qkv0", col_page(r["grad_qkv"], 0), store_col("qkv", 0))
    item("ckv0", col_page(r["grad_ckv"], 0), store_col("ckv", 0))
    for c in (1, 2):
        item("qkv%d" % c, col_page(r["grad_qkv"], c), store_col("qkv", c))
    item("ckv1", col_page(r["grad_ckv"], 1), store_col("ckv", 1))
    ring = PageScatter(
        bk, feeds, (r["own"], r["over"], r["side"]), [r["ring%d" % i] for i in range(6)], ready,
        crossed,
    )

    def summed(n):
        return r["sum_" + n] if inside else r[n]

    def fill(joined, parts, first):
        for j in range(4):
            joined[j * rows : (j + 1) * rows, first : first + len(parts) * head_width] = (
                jnp.concatenate([p[j] for p in parts], axis=1)
            )

    def weight_grad(joined, cols, features, grad, g0, g1):
        def one(g, carry):
            lhs = features[:, :, pl.ds(pl.multiple_of(g * head_width, head_width), head_width)]
            total = dot(lhs.reshape(4 * rows, head_width), joined[:, cols], TN)
            grad[g, :, :, cols] = total.reshape(grad.shape[1:3] + (-1,)).astype(bf16)
            return carry

        lax.fori_loop(g0, g1, one, 0)

    def project(joined, w, summed_over_head):
        def term(j):
            def run():
                block = joined[pl.ds(pl.multiple_of(j * rows, rows), rows), :]
                summed_over_head.part[j] = dot(block, w[...], NT).astype(bf16)

            return run

        def near(i):
            return lambda: summed_over_head.near_start(i)

        return [
            [term(hd.far_sib), near(0)],
            [term(hd.sib), near(1)],
            [term(hd.far), summed_over_head.middle],
            [term(hd.me)],
        ]

    stats_begin, stats_finish = tiles(r["stats_tab"], r["stats_got"], 0)
    first, second = (
        HeadSum(
            hd, r["part%d" % (i + 1)], r["near%d" % i], r["mid%d" % i], r["far%d" % i],
            (r["sum_send%d" % i], r["sum_recv%d" % i]),
        )
        for i in range(2)
    )

    def query_part():
        fill(r["joined1"], [r["dq1"]], 0)
        weight_grad(r["joined1"], slice(0, head_width), r["normed"], r["grad_qkv"], 0, 4)
        ring.begin(index["qkv0"])

    def own_steps(n, c, joined, features, grad, page):
        cols = slice(c * head_width, (c + 1) * head_width)

        def half(g0, g1):
            return lambda: weight_grad(joined, cols, features, grad, g0, g1)

        return [
            [lambda: fill(joined, [summed(n)], c * head_width), half(0, 2)],
            [half(2, 4), lambda: ring.begin(index[page])],
        ]

    steps = dict(
        dk2=own_steps("dk2", 0, r["joined2"], r["encoded"], r["grad_ckv"], "ckv0"),
        dk1=own_steps("dk1", 1, r["joined1"], r["normed"], r["grad_qkv"], "qkv1"),
        dv1=own_steps("dv1", 2, r["joined1"], r["normed"], r["grad_qkv"], "qkv2"),
        dv2=own_steps("dv2", 1, r["joined2"], r["encoded"], r["grad_ckv"], "ckv1"),
    )
    steps["dv1"] += project(r["joined1"], r["w_qkv"], first)
    steps["dv2"] += project(r["joined2"], r["w_ckv"], second)

    def self_norm():
        dv, d_gain, d_shift = layer_norm_back(
            r["inputs"][...].astype(f32), first.whole(), r["table"][0:1]
        )
        r["out_d_inputs"][...] = dv + r["d_first"][...]
        r["own_stats"][0:1] = d_gain
        r["own_stats"][1:2] = d_shift

    def self_table():
        two, three = r["stats_two"], r["stats_three"]

        def placed(row):
            return jnp.concatenate(
                [jnp.where(hd.me == h, row, 0.0) for h in range(4)], axis=1
            )

        rows_of = [
            r["own_stats"][0:1], two[0:1], three[0:1], r["own_stats"][1:2], two[1:2], three[1:2],
            placed(r["sums_one"][0:1]), placed(r["sums_one"][1:2]),
            placed(r["sums_two"][0:1]), placed(r["sums_two"][1:2]),
            two[2:3], three[2:3], three[3:4],
        ]
        whole = jnp.concatenate(rows_of + [jnp.zeros((N_SMALL - 13, width), f32)], axis=0)
        hidden = r["d_hidden"][...]

        def turned(value, lane):
            tile = value[:, lane // 128 * 128 : lane // 128 * 128 + 128]
            return pltpu.roll(tile, 128 - lane % 128, 1) if lane % 128 else tile

        for d in range(devices):
            r["stats_tab"][d] = turned(whole, d * share)
            h, b = divmod(d, count)
            for run in range(4):
                mine = turned(hidden, (4 * b + run) * share)
                r["stats_tab"][d, 13 + run : 14 + run, :] = jnp.where(hd.me == h, mine, 0.0)

    def sum_ffn():
        def one(i, carry):
            part = pl.ds(pl.multiple_of(i * share, share), share)
            total = r["ffn_terms"][0, part, :].astype(f32)
            for b in range(1, count // 2):
                total = total + r["ffn_terms"][b, part, :].astype(f32)

            @pl.when(i < 4)
            def _():
                r["ffn_in"][i] = total.astype(bf16)

            @pl.when(i >= 4)
            def _():
                r["out_ffn_out"][pl.ds(pl.multiple_of((i - 4) * share, share), share), :] = total

            return carry

        lax.fori_loop(0, 8, one, 0)
        send_heads("ffn_in")

    lag = SKEW * (bk.Z - 1)
    lead = 4 if inside else index["cq"] + 1
    for a in range(lead):
        ring.begin(a)
    plan = {}

    def at(t, step):
        plan.setdefault(t, []).append(step)

    last = ring.n + lag - 1
    after_self = 0
    if inside:
        after_self = index["dv1"] + lag
        for n in PAIRS:
            for i, step in enumerate(steps[n]):
                at(index[n] + lag + (max(i - 1, 0) if n == "dv2" else i), step)
        at(3, [query_part])
        at(5, [sum_ffn])
    else:
        sum_ffn()
        query_part()
        for n in PAIRS:
            for step in steps[n]:
                for run in step:
                    run()
    for i, step in enumerate((self_norm, self_table, stats_begin)):
        at(min(after_self + 8 + i, last), [step])
    at(index["cq"] + lag, [lambda: send_heads("cq")])
    at(index["qkv2"] + lag, [lambda: send_heads("qkv")])
    for t in range(last + 1):
        for a in range(lead + 2 * t, min(lead + 2 * t + 2, index["cq"] + 1)):
            ring.begin(a)
        ring.wave(t)
        for step in plan.get(t, []):
            for run in step:
                run()
    send_heads("ckv")
    r["out_d_encoded"][...] = second.whole()
    ring.drain()
    first.finish()
    second.finish()
    for n in headed:
        for k in range(1, 4):
            across_head(n, k, False).wait_send()
            across_head(n, k, True).wait_recv()
    stats_finish()
    total = r["stats_got"][0]
    for d in range(1, devices):
        total = total + r["stats_got"][d]
    r["out_stats"][...] = total


def settle_kernel(names, *refs):
    r = dict(zip(names, refs[:-1]))
    sems = refs[-1]
    copies = [
        pltpu.make_async_copy(r[name], r["here_" + name[4:]], sems.at[i])
        for i, name in enumerate([n for n in names if n.startswith("got_")])
    ]
    for copy in copies:
        copy.start()
    for copy in copies:
        copy.wait()
    for name in ("ffn_in", "cq", "ckv", "qkv"):
        got, out = r["here_" + name], r["out_" + name]
        parts = dict(qkv=3, ckv=2).get(name, 1)
        step = got.shape[2] // parts
        for h in range(4):
            for c in range(parts):
                value = got[h, :, c * step : (c + 1) * step].astype(f32)
                if parts == 3:
                    out[c, :, h * step : (h + 1) * step] = value
                elif parts == 1:
                    out[:, h * step : (h + 1) * step] = value
                else:
                    out[:, c, h * step : (h + 1) * step] = value
    for name in ("d_inputs", "d_encoded", "ffn_out", "layer"):
        r["out_" + name][...] = r["here_" + name][...]
    for name in ("co", "so"):
        r["out_" + name][...] = r["here_" + name][0]
    row = 0
    for name, number in SMALL_ROWS:
        out = r["out_" + name]
        out[...] = r["here_stats"][row : row + number, : out.shape[1]]
        row += number


def settle(got, layer_output, share, width, hidden_width):
    rows = layer_output.shape[0]
    ins = {"got_" + n[4:]: a for n, a in got.items()}
    ins["got_layer"] = layer_output
    outs = dict(
        out_layer=((rows, width), bf16),
        out_d_inputs=((rows, width), f32),
        out_d_encoded=((rows, width), f32),
        out_qkv=((3, share, width), f32),
        out_ckv=((share, 2, width), f32),
        out_cq=((share, width), f32),
        out_ffn_in=((share, hidden_width), f32),
        out_ffn_out=(got["out_ffn_out"].shape, f32),
        out_co=((share, width), f32),
        out_so=((share, width), f32),
    )
    outs.update({"out_" + n: ((number, share), f32) for n, number in SMALL_ROWS})
    here = {"here_" + n[4:]: pltpu.VMEM(a.shape, a.dtype) for n, a in ins.items()}
    done = pl.pallas_call(
        partial(settle_kernel, tuple(ins) + tuple(outs) + tuple(here)),
        out_shape=[jax.ShapeDtypeStruct(*o) for o in outs.values()],
        in_specs=[ANY] * len(ins),
        out_specs=[VMEM] * len(outs),
        scratch_shapes=list(here.values()) + [DMA((len(ins),))],
        compiler_params=pltpu.CompilerParams(vmem_limit_bytes=60 * 2**20),
        name="settle",
        cost_estimate=lasts(4),
    )(*ins.values())
    return dict(zip(outs, done))


def finale(
    count, pairs, co, so, cq, ffn_terms, dq1, normed, encoded, w_qkv, w_ckv, inputs, d_first, table,
    stats_two, stats_three, sums_one, sums_two, d_hidden, cid,
):
    inside = len(pairs) == 8
    devices, Z = 4 * count, count // 2
    rows, width = inputs.shape
    share = width // devices
    head_width = w_ckv.shape[1] // 2
    hidden_width = ffn_terms.shape[2]
    ins = dict(zip(PAIRS + tuple(n + "_over" for n in PAIRS), pairs))
    ins.update(co=co, so=so, cq=cq)
    in_specs = [ANY if inside else VMEM] * len(pairs) + [ANY] * 3
    rest = dict(
        ffn_terms=ffn_terms, dq1=dq1, normed=normed, encoded=encoded, w_qkv=w_qkv, w_ckv=w_ckv,
        inputs=inputs, d_first=d_first, table=table, stats_two=stats_two, stats_three=stats_three,
        sums_one=sums_one, sums_two=sums_two, d_hidden=d_hidden,
    )
    ins.update(rest)
    in_specs += [VMEM] * len(rest)
    outs = dict(
        out_d_inputs=((rows, width), f32),
        out_d_encoded=((rows, width), f32),
        out_qkv=((4, share, 3 * head_width), bf16),
        out_ckv=((4, share, 2 * head_width), bf16),
        out_cq=((4, share, head_width), bf16),
        out_ffn_in=((4, share, hidden_width), bf16),
        out_ffn_out=((4 * share, width), f32),
        out_co=((1, share, width), f32),
        out_so=((1, share, width), f32),
        out_stats=((N_SMALL, 128), f32),
    )
    grads = dict(
        grad_qkv=(4, count, share, 3 * head_width), grad_ckv=(4, count, share, 2 * head_width)
    )
    scratch = {}
    n_items = 24 if inside else 8
    for kind, slots in (("own", Z), ("over", Z), ("side", Z + 1)):
        scratch[kind] = pltpu.VMEM((n_items, slots, 4, share, head_width), bf16)
    for n, wide in (("cq", 1), ("qkv", 3), ("ckv", 2)):
        scratch["done_" + n] = pltpu.VMEM((4, share, wide * head_width), bf16)
    scratch["ffn_in"] = pltpu.VMEM((4, share, hidden_width), bf16)
    if inside:
        for n in PAIRS:
            scratch["sum_" + n] = pltpu.VMEM((4, rows, head_width), bf16)
    for n, shape in grads.items():
        scratch[n] = pltpu.VMEM(shape, bf16)
    for i, n in enumerate(("1", "2")):
        scratch["part" + n] = pltpu.VMEM((4, rows, width), bf16)
        scratch["joined" + n] = pltpu.VMEM((4 * rows, (3 - i) * head_width), bf16)
        kinds = head_sum_scratch(rows, width)
        for name, kind in zip(("near", "mid", "far", "sum_send", "sum_recv"), kinds):
            scratch[name + str(i)] = kind
    scratch["own_stats"] = pltpu.VMEM((8, width), f32)
    for n in ("stats_tab", "stats_got"):
        scratch[n] = pltpu.VMEM((devices, N_SMALL, 128), f32)
    for i in range(6):
        scratch["ring%d" % i] = DMA((n_items, Z, 4) if i < 3 else (n_items, Z))
    scratch["tile_local"] = DMA((1,))
    scratch["tile_send"] = DMA((1, devices))
    scratch["tile_recv"] = DMA((1, devices))
    scratch["head_send"] = DMA((4, 4))
    scratch["head_recv"] = DMA((4, 4))
    got = pl.pallas_call(
        partial(finale_kernel, count, inside, tuple(ins), tuple(outs), tuple(scratch)),
        out_shape=[jax.ShapeDtypeStruct(*o) for o in outs.values()],
        in_specs=in_specs,
        out_specs=[VMEM] * len(outs),
        scratch_shapes=list(scratch.values()),
        compiler_params=params(cid),
        name="finale",
        cost_estimate=lasts(150),
    )(*ins.values())
    return dict(zip(outs, got))


def forward_kernel(count, n_stream, has_query, layer, *refs):
    refs = list(refs)
    mix, w_out, base, table = (refs.pop(0) for _ in range(4))
    w_query, b_query = (refs.pop(0) for _ in range(2)) if has_query else (None, None)
    stream_in = [refs.pop(0) for _ in range(n_stream)]
    total, normed = (refs.pop(0) for _ in range(2))
    query = refs.pop(0) if has_query else None
    stream_out = [refs.pop(0) for _ in range(n_stream)]
    part, near, mid, far, ss, rs, gs, gr = (refs.pop(0) for _ in range(8))
    hd, bk = Head(), Blk(count)
    bar = pltpu.get_barrier_semaphore()
    greeted = greet_head(bar, hd)
    if n_stream:
        greeted = greeted + greet_blk(bar, bk)
    pl.semaphore_wait(bar, greeted)
    ring = None
    if n_stream:
        lsem, ssem, rsem = refs
        ring = BlkGather(bk, stream_out, ssem, rsem)
        for a in range(n_stream):
            ring.start(a, stream_in[a])
            pltpu.make_async_copy(stream_in[a], stream_out[a].at[:, bk.me], lsem.at[a]).start()

    def term(j):
        part[j] = dot(mix[j], w_out[...]).astype(bf16)

    summed = HeadSum(hd, part, near, mid, far, (ss, rs))
    term(hd.far_sib)
    summed.near_start(0)
    term(hd.sib)
    summed.near_start(1)
    term(hd.far)
    summed.middle()
    term(hd.me)
    gain, shift = table[layer + 1 : layer + 2], table[layer + 4 : layer + 5]
    spread = HeadGather(hd, normed, gs, gr)
    for p in range(PARTS):
        here = summed.half(p)
        v = base[here].astype(f32) + summed.total(p) + table[10 + layer : 11 + layer]
        total[here] = v
        normed[hd.me, here] = layer_norm(v, gain, shift).astype(bf16)
        spread.begin(p)

    def ask(j):
        if has_query:
            query[j] = (dot(normed[j], w_query[...]) + b_query[8:9]).astype(bf16)

    def step(k):
        for a in range(n_stream):
            ring.step(a, k)

    ask(hd.me)
    if n_stream:
        step(1)
    spread.forward()
    ask(hd.far)
    spread.arrive()
    ask(hd.sib)
    ask(hd.far_sib)
    if n_stream:
        for k in range(2, bk.Z):
            step(k)
        for a in range(n_stream):
            ring.arrive(a)
            ring.drain(a)
            pltpu.make_async_copy(stream_in[a], stream_out[a].at[:, bk.me], lsem.at[a]).wait()
    spread.drain()
    summed.finish()


def join_forward(mix, w_out, base, table, layer, count, cid, query=None, stream=()):
    rows, width = base.shape
    n = len(stream)
    ops = [mix, w_out, base, table] + list(query or ()) + list(stream)
    shapes = [
        jax.ShapeDtypeStruct((rows, width), f32),
        jax.ShapeDtypeStruct((4, rows, width), bf16),
    ]
    if query:
        shapes.append(jax.ShapeDtypeStruct(mix.shape, bf16))
    n_vmem = len(shapes)
    shapes += [jax.ShapeDtypeStruct((4, count) + a.shape[1:], bf16) for a in stream]
    scratch = [pltpu.VMEM((4, rows, width), bf16)] + head_sum_scratch(rows, width)
    scratch += head_gather_scratch()
    if n:
        scratch += [DMA((n,)), DMA((n, 3, count)), DMA((n, count))]
    return pl.pallas_call(
        partial(forward_kernel, count, n, query is not None, layer),
        out_shape=shapes,
        in_specs=[VMEM] * (len(ops) - n) + [ANY] * n,
        out_specs=[VMEM] * n_vmem + [ANY] * n,
        scratch_shapes=scratch,
        compiler_params=params(cid),
        name="join_forward",
        cost_estimate=lasts(50 if n else 22),
    )(*ops)


def backward_kernel(count, layer, has_extra, *refs):
    refs = list(refs)
    if has_extra:
        part, extra = (refs.pop(0) for _ in range(2))
    else:
        dq, w_in, normed = (refs.pop(0) for _ in range(3))
    onward, v, table, w_out, mix = (refs.pop(0) for _ in range(5))
    back, stats, d_o, grad_out = (refs.pop(0) for _ in range(4))
    other = refs.pop(0)
    grad_all = refs.pop(0)
    sums = [refs.pop(0) for _ in range(5)]
    hd = Head()
    head_width = mix.shape[2]
    tokens = 4 * mix.shape[1]
    bar = pltpu.get_barrier_semaphore()
    pl.semaphore_wait(bar, greet_head(bar, hd))
    if has_extra:
        second = HeadSum(hd, extra, *refs[:3], refs[3:5])
        refs = refs[5:]
    else:
        part = refs.pop(0)
    summed = HeadSum(hd, part, *sums[:3], sums[3:])
    if has_extra:
        summed.begin()
        summed.middle()
        second.begin()
        second.middle()
    else:

        def term(j):
            part[j] = dot(dq[j], w_in[...], NT).astype(bf16)

        term(hd.far_sib)
        summed.near_start(0)
        term(hd.sib)
        summed.near_start(1)
        term(hd.far)
        summed.middle()
        term(hd.me)
        all_dq = dq[...].reshape(tokens, head_width)

        def weight(g, carry):
            lhs = normed[:, :, pl.ds(pl.multiple_of(g * head_width, head_width), head_width)]
            other[g] = (
                dot(lhs.reshape(tokens, head_width), all_dq, TN).reshape(other.shape[1:]).astype(bf16)
            )
            return carry

        lax.fori_loop(0, 4, weight, 0)
    gain = table[layer : layer + 1]
    spread = HeadGather(hd, grad_all, *refs)
    sums_here = []
    for p in range(PARTS):
        here = summed.half(p)
        dv, d_gain, d_shift = layer_norm_back(v[here], summed.total(p), gain)
        after = onward[here].astype(f32)
        d = dv + after
        back[here] = d
        rounded = d.astype(bf16)
        grad_all[hd.me, here] = rounded
        spread.begin(p)
        sums_here.append(
            (
                d_gain,
                d_shift,
                jnp.sum(rounded.astype(f32), axis=0, keepdims=True),
                jnp.sum(after, axis=0, keepdims=True),
            )
        )
    for i, terms in enumerate(zip(*sums_here)):
        stats[i : i + 1] = sum(terms[1:], terms[0])

    def out(j):
        d_o[j] = dot(grad_all[j], w_out[...], NT).astype(bf16)

    out(hd.me)
    if has_extra:
        other[...] = (v[...] + second.whole() + table[10 + layer : 11 + layer]).astype(bf16)
    spread.forward()
    out(hd.far)
    spread.arrive()
    out(hd.sib)
    out(hd.far_sib)
    grad = dot(mix[...].reshape(tokens, head_width), grad_all[...].reshape(tokens, -1), TN)
    grad_out[0] = grad.reshape(grad_out.shape[1:]).astype(bf16)
    spread.drain()
    summed.finish()
    if has_extra:
        second.finish()


def join_backward(terms, onward, v, table, layer, w_out, mix, count, cid):
    rows, width = onward.shape
    share, head_width = width // (4 * count), mix.shape[2]
    has_extra = len(terms) == 2
    ops = list(terms) + [onward, v, table, w_out, mix]
    other = ((rows, width), bf16) if has_extra else ((4, count, share, head_width), bf16)
    shapes = [
        ((rows, width), f32),
        ((8, width), f32),
        (mix.shape, bf16),
        ((1, count, share, width), bf16),
        other,
    ]
    scratch = [pltpu.VMEM((4, rows, width), bf16)] + head_sum_scratch(rows, width)
    if has_extra:
        scratch += head_sum_scratch(rows, width)
    else:
        scratch += [pltpu.VMEM((4, rows, width), bf16)]
    scratch += head_gather_scratch()
    return pl.pallas_call(
        partial(backward_kernel, count, layer, has_extra),
        out_shape=[jax.ShapeDtypeStruct(*s) for s in shapes],
        in_specs=[VMEM] * len(ops),
        out_specs=[VMEM] * len(shapes),
        scratch_shapes=scratch,
        compiler_params=params(cid),
        name="join_backward",
        cost_estimate=lasts(24),
    )(*ops)


def feed_forward_kernel(
    normed, d_output, w_in, w_out, b_hidden, out_part, d_part, mine, theirs, d_sum, act, dh
):
    rows, width = normed.shape[1:]
    tokens = 4 * rows
    share = mine.shape[1] // 8
    first = lax.axis_index("blk") % 2 == 0
    d_sum[...] = jnp.zeros_like(d_sum)

    def block(j, carry):
        hidden = dot(normed[j], w_in[...]) + b_hidden[...]
        phi = 0.5 * (1.0 + lax.erf(hidden * (0.5**0.5)))
        active = (hidden * phi).astype(bf16)
        slope = phi + hidden * jnp.exp(-0.5 * hidden * hidden) * ((0.5 / jnp.pi) ** 0.5)
        d_hidden = (dot(d_output[j], w_out[...], NT) * slope).astype(bf16)
        act[j] = active
        dh[j] = d_hidden
        d_sum[...] += jnp.sum(d_hidden.astype(f32), axis=0, keepdims=True)
        out_part[j] = dot(active, w_out[...]).astype(bf16)
        d_part[j] = dot(d_hidden, w_in[...], NT).astype(bf16)
        return carry

    lax.fori_loop(0, 4, block, 0)
    step = width // 4
    runs = step // (8 * share)

    def weight(g, carry):
        part = pl.ds(pl.multiple_of(g * step, step), step)
        def split(total, place):
            even, odd = total[:, 0].astype(bf16), total[:, 1].astype(bf16)
            mine[place] = jnp.where(first, even, odd)
            theirs[place] = jnp.where(first, odd, even)

        total = dot(normed[:, :, part].reshape(tokens, step), dh[...].reshape(tokens, -1), TN)
        place = (slice(None), pl.ds(pl.multiple_of(g * share, share), share))
        split(total.reshape(mine.shape[0], 2, share, -1), place)
        total = dot(act[:, :, part].reshape(tokens, step), d_output[...].reshape(tokens, -1), TN)
        place = (pl.ds(g * runs, runs), slice(4 * share, None))
        split(total.reshape(runs, 2, 4 * share, -1), place)
        return carry

    lax.fori_loop(0, 4, weight, 0)


def feed_forward(normed, d_output, w_in, w_out, b_hidden, count):
    rows, width = normed.shape[1:]
    share = width // (4 * count)
    return pl.pallas_call(
        feed_forward_kernel,
        out_shape=(
            jax.ShapeDtypeStruct(normed.shape, bf16),
            jax.ShapeDtypeStruct(normed.shape, bf16),
            jax.ShapeDtypeStruct((count // 2, 8 * share, width), bf16),
            jax.ShapeDtypeStruct((count // 2, 8 * share, width), bf16),
            jax.ShapeDtypeStruct((1, w_in.shape[1]), f32),
        ),
        in_specs=[VMEM] * 5,
        out_specs=(VMEM,) * 5,
        scratch_shapes=[
            pltpu.VMEM((4, rows, w_in.shape[1]), bf16),
            pltpu.VMEM((4, rows, w_in.shape[1]), bf16),
        ],
        compiler_params=pltpu.CompilerParams(vmem_limit_bytes=56 * 2**20),
        name="feed_forward",
        cost_estimate=lasts(15),
    )(normed, d_output, w_in, w_out, b_hidden)


def tie(value, *others):
    return lax.optimization_barrier((value,) + others)


def stack_heads(rows, scale):
    lane = lax.broadcasted_iota(jnp.int32, rows.shape, 1) // HEAD_DIM
    pieces = [
        jnp.where(lane == h, rows.astype(f32) * scale, 0.0).astype(bf16) for h in range(HEADS_HERE)
    ]
    return jnp.concatenate(pieces, axis=0)


def take_heads(wide, rows):
    pieces = [
        wide[h * HEAD_DIM : (h + 1) * HEAD_DIM, h * rows : (h + 1) * rows]
        for h in range(HEADS_HERE)
    ]
    return jnp.concatenate(pieces, axis=0).T


def wide_span(spans, which, i):
    return [jnp.concatenate([spans[which, e, i]] * HEADS_HERE, axis=1) for e in range(2)]


def masked_scores(keys, stacked, first, low, high):
    scores = dot(keys, stacked, NT)
    key_pos = first + lax.broadcasted_iota(jnp.int32, scores.shape, 0)
    return jnp.where((key_pos >= low) & (key_pos < high), scores, -1e30)


def attend_kernel(which, bounds, spans, q, k, v, o, mix, lse, acc):
    chunks, rows, width = q.shape

    def chunk(i, carry):
        stacked = stack_heads(q[i], HEAD_DIM ** (-0.5))
        lo, hi = wide_span(spans, which, i)
        acc[...] = jnp.zeros_like(acc)

        def step(kb, state):
            top, total = state
            first = pl.multiple_of(kb * KEY_BLOCK, KEY_BLOCK)
            scores = masked_scores(k[pl.ds(first, KEY_BLOCK), :], stacked, first, lo, hi)
            new_top = jnp.maximum(top, jnp.max(scores, axis=0, keepdims=True))
            fading = jnp.exp(top - new_top)
            weights = jnp.exp(scores - new_top)
            total = total * fading + jnp.sum(weights, axis=0, keepdims=True)
            acc[...] = acc[...] * fading + dot(
                v[pl.ds(first, KEY_BLOCK), :], weights.astype(bf16), TN
            )
            return new_top, total

        wide = HEADS_HERE * rows
        top, total = lax.fori_loop(
            bounds[which, 0, i],
            bounds[which, 1, i],
            step,
            (jnp.full((1, wide), -1e30, f32), jnp.zeros((1, wide), f32)),
        )
        lse[i] = top + jnp.log(total)
        result = take_heads(acc[...] / total, rows)
        o[i] = result
        mix[i] = result.astype(bf16)
        return carry

    lax.fori_loop(0, chunks, chunk, 0)


def attend(q, k, v, spans, which):
    bounds, spans = spans
    chunks, rows, width = q.shape
    wide = HEADS_HERE * rows
    return pl.pallas_call(
        partial(attend_kernel, which),
        out_shape=(
            jax.ShapeDtypeStruct(q.shape, f32),
            jax.ShapeDtypeStruct(q.shape, bf16),
            jax.ShapeDtypeStruct((chunks, 1, wide), f32),
        ),
        in_specs=[SMEM] + [VMEM] * 4,
        out_specs=(VMEM,) * 3,
        scratch_shapes=[pltpu.VMEM((width, wide), f32)],
        compiler_params=pltpu.CompilerParams(vmem_limit_bytes=56 * 2**20),
        name="attend",
        cost_estimate=lasts(12),
    )(bounds, spans, q, k, v)


def attend_back_kernel(
    which, bounds, spans, q, k, v, d_o, o, lse, dq, dk, dk_over, dv, dv_over, sums,
    qs, dos, delta, dq_acc, dk_acc, dv_acc
):
    chunks, rows, width = q.shape
    y = lax.axis_index("blk") % 2
    spread = KEY_BLOCK // (2 * rows)
    mine = [pl.ds(pl.multiple_of((2 * n + y) * rows, rows), rows) for n in range(spread)]
    theirs = [pl.ds(pl.multiple_of((2 * n + 1 - y) * rows, rows), rows) for n in range(spread)]
    sums[...] = jnp.zeros_like(sums)
    for i in range(chunks):
        qs[i] = stack_heads(q[i], HEAD_DIM ** (-0.5))
        dos[i] = stack_heads(d_o[i], 1.0)
        product = (d_o[i].astype(f32) * o[i]).T
        delta[i] = jnp.concatenate(
            [
                jnp.sum(product[h * HEAD_DIM : (h + 1) * HEAD_DIM], axis=0, keepdims=True)
                for h in range(HEADS_HERE)
            ],
            axis=1,
        )
    dq_acc[...] = jnp.zeros_like(dq_acc)

    def block(kb, carry):
        first = pl.multiple_of(kb * KEY_BLOCK, KEY_BLOCK)
        part = pl.ds(first, KEY_BLOCK)
        dk_acc[...] = jnp.zeros_like(dk_acc)
        dv_acc[...] = jnp.zeros_like(dv_acc)

        def chunk(i, inner):
            @pl.when((kb >= bounds[which, 0, i]) & (kb < bounds[which, 1, i]))
            def _():
                keys = k[part, :]
                lo, hi = wide_span(spans, which, i)
                scores = masked_scores(keys, qs[i], first, lo, hi)
                weights = jnp.exp(scores - lse[i])
                d_weights = dot(v[part, :], dos[i], NT)
                d_scores = (weights * (d_weights - delta[i])).astype(bf16)
                dv_acc[...] += dot(weights.astype(bf16), dos[i])
                dk_acc[...] += dot(d_scores, qs[i])
                dq_acc[i] += dot(keys, d_scores, TN)

            return inner

        lax.fori_loop(0, chunks, chunk, 0)
        for n in range(spread):
            dk[kb * spread + n] = dk_acc[mine[n], :].astype(bf16)
            dk_over[kb * spread + n] = dk_acc[theirs[n], :].astype(bf16)
            dv[kb * spread + n] = dv_acc[mine[n], :].astype(bf16)
            dv_over[kb * spread + n] = dv_acc[theirs[n], :].astype(bf16)
        sums[1:2] += jnp.sum(dv_acc[...], axis=0, keepdims=True)
        return carry

    lax.fori_loop(0, k.shape[0] // KEY_BLOCK, block, 0)
    for i in range(chunks):
        result = (take_heads(dq_acc[i], rows) * HEAD_DIM ** (-0.5)).astype(bf16)
        dq[i] = result
        sums[0:1] += jnp.sum(result.astype(f32), axis=0, keepdims=True)


def attend_back(q, k, v, spans, which, d_o, o, lse):
    bounds, spans = spans
    chunks, rows, width = q.shape
    wide = HEADS_HERE * rows
    half = (k.shape[0] // (2 * rows), rows, width)
    return pl.pallas_call(
        partial(attend_back_kernel, which),
        out_shape=(
            jax.ShapeDtypeStruct(q.shape, bf16),
            jax.ShapeDtypeStruct(half, bf16),
            jax.ShapeDtypeStruct(half, bf16),
            jax.ShapeDtypeStruct(half, bf16),
            jax.ShapeDtypeStruct(half, bf16),
            jax.ShapeDtypeStruct((8, width), f32),
        ),
        in_specs=[SMEM] + [VMEM] * 7,
        out_specs=(VMEM,) * 6,
        scratch_shapes=[
            pltpu.VMEM((chunks, wide, width), bf16),
            pltpu.VMEM((chunks, wide, width), bf16),
            pltpu.VMEM((chunks, 1, wide), f32),
            pltpu.VMEM((chunks, width, wide), f32),
            pltpu.VMEM((KEY_BLOCK, width), f32),
            pltpu.VMEM((KEY_BLOCK, width), f32),
        ],
        compiler_params=pltpu.CompilerParams(vmem_limit_bytes=60 * 2**20),
        name="attend_back",
        cost_estimate=lasts(14),
    )(bounds, spans, q, k, v, d_o, o, lse)


def key_spans(target_lengths, source_lengths, rows, count):
    ends = jnp.cumsum(target_lengths, dtype=jnp.int32)
    starts = ends - target_lengths
    chunk = jnp.arange(4, dtype=jnp.int32) * count + lax.axis_index("blk")

    def at(pos):
        past = (pos[..., None] >= ends).astype(jnp.int32)
        begun = (pos[..., None] >= starts).astype(jnp.int32)
        return (
            (jnp.sum(past * target_lengths, axis=-1), pos + 1),
            (jnp.sum(past * source_lengths, axis=-1), jnp.sum(begun * source_lengths, axis=-1)),
        )

    first, last = at(chunk * rows), at(chunk * rows + rows - 1)
    bounds = jnp.stack(
        [
            jnp.stack((low // KEY_BLOCK, (high + KEY_BLOCK - 1) // KEY_BLOCK))
            for (low, _), (_, high) in zip(first, last)
        ]
    ).astype(jnp.int32)
    spans = at(chunk[:, None] * rows + jnp.arange(rows, dtype=jnp.int32)[None, :])
    spans = jnp.stack([jnp.stack(s) for s in spans])
    return bounds, spans[:, :, :, None, :]


def body(
    count,
    inputs,
    encoded,
    d_output,
    target_lengths,
    source_lengths,
    norm_gain,
    norm_shift,
    self_qkv,
    self_bias,
    self_out,
    cross_q,
    cross_kv,
    cross_bias,
    cross_out,
    out_bias,
    ffn_in,
    ffn_in_bias,
    ffn_out,
):
    rows, width = inputs.shape
    devices = 4 * count
    share = width // devices
    head_width = width // 4
    hidden_width = ffn_in.shape[1]
    hidden_here = hidden_width // 4
    hidden_rows = hidden_width // width
    tokens_here = 4 * rows

    small = jnp.concatenate(
        (
            norm_gain,
            norm_shift,
            self_bias,
            cross_bias,
            out_bias,
            ffn_in_bias.reshape(hidden_rows, share),
        )
    )
    n_small = small.shape[0]
    small = jnp.pad(small, ((0, N_SMALL - n_small), (0, 128 - share)))
    (
        table, here, b_hidden, w_qkv, w_cross_kv, w_cross_q, w_self_out, w_cross_out, w_ffn_in,
        inputs_all, encoded_all, d_output_all, normed_one, q1, k1, v1, k2, v2,
    ) = front(
        small,
        [jnp.transpose(self_qkv, (1, 0, 2)), cross_kv.reshape(share, 2 * width), cross_q],
        self_out[None],
        cross_out[None],
        ffn_in,
        [inputs, encoded, d_output],
        count,
        0,
    )
    ffn_out, w_ffn_in = tie(ffn_out, w_ffn_in)
    w_ffn_out = lax.all_gather(ffn_out, "blk", axis=0, tiled=True)
    w_ffn_in = lax.all_gather(w_ffn_in, "blk", axis=1, tiled=True).reshape(width, -1)
    w_qkv, w_cross_kv, w_cross_q, w_self_out, w_cross_out = (
        w.reshape(-1, w.shape[-1]) for w in (w_qkv, w_cross_kv, w_cross_q, w_self_out, w_cross_out)
    )
    spans = key_spans(target_lengths, source_lengths, rows, count)

    k1, v1 = (a.reshape(-1, head_width) for a in (k1, v1))
    o1, mix1, lse1 = attend(q1, k1, v1, spans, 0)
    first, normed_two, q2, k2, v2 = join_forward(
        mix1, w_self_out, inputs, table, 0, count, 2, query=(w_cross_q, here), stream=(k2, v2)
    )
    k2, v2 = (a.reshape(-1, head_width) for a in (k2, v2))
    o2, mix2, lse2 = attend(q2, k2, v2, spans, 1)
    second, normed_three = join_forward(mix2, w_cross_out, first, table, 1, count, 3)

    out_part, d_part, ffn_mine, ffn_over, d_hidden = feed_forward(
        normed_three, d_output_all, w_ffn_in, w_ffn_out, b_hidden, count
    )
    swap = [(i, i ^ 1) for i in range(count)]
    ffn_over = lax.ppermute(ffn_over, "blk", swap)
    d_second, stats_three, d_o2, grad_cross_out, layer_output = join_backward(
        (d_part, out_part), d_output, second, table, 2, w_cross_out, mix2, count, 4
    )
    dq2, dk2, dk2_over, dv2, dv2_over, sums_two = attend_back(q2, k2, v2, spans, 1, d_o2, o2, lse2)
    inside = rows == 4 * share
    if inside:
        dk2_over, dv2_over = lax.ppermute((dk2_over, dv2_over), "blk", swap)
    dq2, ffn_over = tie(dq2, ffn_over)
    lines = [list(range(y, count, 2)) for y in range(2)]
    ffn_terms = lax.all_to_all(
        (ffn_mine.astype(f32) + ffn_over.astype(f32)).astype(bf16), "blk", 0, 0,
        axis_index_groups=lines, tiled=True,
    )
    d_first, stats_two, d_o1, grad_self_out, grad_cross_q = join_backward(
        (dq2, w_cross_q, normed_two), d_second, first, table, 1, w_self_out, mix1, count, 5
    )
    dq1, dk1, dk1_over, dv1, dv1_over, sums_one = attend_back(q1, k1, v1, spans, 0, d_o1, o1, lse1)
    pairs = (dk1, dv1, dk2, dv2, dk1_over, dv1_over, dk2_over, dv2_over)
    if inside:
        pairs = [a.reshape(4, count // 2, 4, share, head_width) for a in pairs]
    else:
        y = lax.axis_index("blk") % 2
        pairs = [
            jnp.where(y == 0, jnp.stack((a, b), axis=1), jnp.stack((b, a), axis=1)).reshape(
                4, count, rows, head_width
            )
            for a, b in zip(pairs[:4], pairs[4:])
        ]
        pairs = scatter_blk(pairs, count, 6)
    got = finale(
        count, pairs, grad_cross_out, grad_self_out, grad_cross_q, ffn_terms, dq1, normed_one,
        encoded_all, w_qkv, w_cross_kv, inputs, d_first, table, stats_two, stats_three,
        sums_one, sums_two, d_hidden, 7,
    )
    done = settle(got, layer_output, share, width, hidden_width)
    order = (
        "layer", "d_inputs", "d_encoded", "gain", "shift", "qkv", "self_bias", "so", "cq", "ckv",
        "cross_bias", "co", "out_bias", "ffn_in", "ffn_bias", "ffn_out",
    )
    outs = [done["out_" + n] for n in order]
    outs[5] = jnp.transpose(outs[5], (1, 0, 2))
    outs[14] = outs[14].reshape(-1)
    return tuple(outs)


def solution(mesh):
    both = ("head", "blk")
    rows2, rows3, cols2 = P(both, None), P(both, None, None), P(None, both)
    return jax.shard_map(
        partial(body, mesh.shape["blk"]),
        mesh=mesh,
        in_specs=(
            rows2, rows2, rows2, P(), P(), cols2, cols2, rows3, cols2, rows2, rows2, rows3,
            cols2, rows2, cols2, rows2, P(both), rows2,
        ),
        out_specs=(
            rows2, rows2, rows2, cols2, cols2, rows3, cols2, rows2, rows2, rows3, cols2, rows2,
            cols2, rows2, P(both), rows2,
        ),
        check_vma=False,
    )
```

```python
from functools import partial
from types import SimpleNamespace

import jax
import jax.numpy as jnp
from jax import lax
from jax.experimental import pallas as pl
from jax.experimental.pallas import tpu as pltpu
from jax.sharding import PartitionSpec as P

HEAD_DIM = 64
HEADS_HERE = 4
KEY_BLOCK = 512
AHEAD = 2
SKEW = 2
MESH = pl.DeviceIdType.MESH
ANY = pl.BlockSpec(memory_space=pl.ANY)
VMEM = pl.BlockSpec(memory_space=pltpu.VMEM)
SMEM = pl.BlockSpec(memory_space=pltpu.SMEM)
DMA = pltpu.SemaphoreType.DMA
f32 = jnp.float32
bf16 = jnp.bfloat16
NT = (((1,), (1,)), ((), ()))
NN = (((1,), (0,)), ((), ()))
TN = (((0,), (0,)), ((), ()))


def dot(a, b, dims=NN):
    return lax.dot_general(a, b, dims, preferred_element_type=f32)


def params(cid):
    return pltpu.CompilerParams(
        collective_id=cid, has_side_effects=True, vmem_limit_bytes=56 * 2**20
    )


def lasts(us):
    return pl.CostEstimate(flops=int(us * 3e8), bytes_accessed=int(us * 3e5), transcendentals=0)


def remote(src, dst, ssem, rsem, device):
    return pltpu.make_async_remote_copy(
        src, dst, ssem, rsem, device_id=device, device_id_type=MESH
    )


class Head:
    def __init__(self):
        self.me = lax.axis_index("head")
        self.core = self.me % 2
        self.x = self.me // 2
        self.sib = self.me + 1 - 2 * self.core
        self.far = self.me + 2 - 4 * self.x
        self.far_sib = self.sib + 2 - 4 * self.x


class Blk:
    def __init__(self, count):
        self.me = lax.axis_index("blk")
        self.z = self.me // 2
        self.y = self.me % 2
        self.Z = count // 2
        self.across = self.me + 1 - 2 * self.y


def signal(bar, **device):
    pl.semaphore_signal(bar, inc=1, device_id=device, device_id_type=MESH)


def greet_head(bar, hd):
    for k in range(1, 4):
        signal(bar, head=(hd.me + k) % 4)
    return 3


def greet_blk(bar, bk):
    signal(bar, blk=bk.across)

    @pl.when(bk.z > 0)
    def _():
        signal(bar, blk=bk.me - 2)

    @pl.when(bk.z < bk.Z - 1)
    def _():
        signal(bar, blk=bk.me + 2)

    return 1 + jnp.where(bk.z > 0, 1, 0) + jnp.where(bk.z < bk.Z - 1, 1, 0)


class BlkGather:
    def __init__(self, bk, outs, ssem, rsem, wide=()):
        self.bk, self.outs, self.ssem, self.rsem, self.wide = bk, outs, ssem, rsem, wide

    def copy(self, a, slot, way, device, src=None):
        view = self.outs[a].at[:, slot]
        return remote(
            view if src is None else src,
            view,
            self.ssem.at[a, way, slot],
            self.rsem.at[a, slot],
            {"blk": device},
        )

    def along(self, a, slot, upward, downward, src=None):
        bk = self.bk
        if upward:

            @pl.when(bk.z < bk.Z - 1)
            def _():
                self.copy(a, slot, 0, bk.me + 2, src).start()

        if downward:

            @pl.when(bk.z > 0)
            def _():
                self.copy(a, slot, 1, bk.me - 2, src).start()

    def start(self, a, src=None):
        self.along(a, self.bk.me, True, True, src)
        self.copy(a, self.bk.me, 2, self.bk.across, src).start()

    def step(self, a, k):
        bk = self.bk
        if k == 0:
            if a in self.wide:
                self.copy(a, bk.across, 2, bk.me).wait_recv()
                self.along(a, bk.across, True, True)
            return
        firsts = (bk.me, bk.across) if a in self.wide else (bk.me,)

        @pl.when(bk.z - k >= 0)
        def _():
            for first in firsts:
                slot = first - 2 * k
                self.copy(a, slot, 0, bk.me).wait_recv()
                self.along(a, slot, True, False)
                if a not in self.wide:
                    self.copy(a, slot, 2, bk.across).start()

        @pl.when(bk.z + k < bk.Z)
        def _():
            for first in firsts:
                slot = first + 2 * k
                self.copy(a, slot, 0, bk.me).wait_recv()
                self.along(a, slot, False, True)
                if a not in self.wide:
                    self.copy(a, slot, 2, bk.across).start()

    def arrive(self, a):
        if a not in self.wide:
            for s in range(self.bk.Z):
                self.copy(a, 2 * s + 1 - self.bk.y, 0, self.bk.me).wait_recv()

    def drain(self, a):
        bk = self.bk
        for s in range(bk.Z):
            for y in (bk.y, 1 - bk.y) if a in self.wide else (bk.y,):
                slot = 2 * s + y

                @pl.when((s <= bk.z) & (bk.z < bk.Z - 1))
                def _():
                    self.copy(a, slot, 0, bk.me).wait_send()

                @pl.when((s >= bk.z) & (bk.z > 0))
                def _():
                    self.copy(a, slot, 1, bk.me).wait_send()

            if a not in self.wide:
                self.copy(a, 2 * s + bk.y, 2, bk.me).wait_send()
        if a in self.wide:
            self.copy(a, bk.me, 2, bk.me).wait_send()


N_SMALL = 24


def front_kernel(
    count, small, qkv, ckv, cq, so, co, ffn_in, inputs, encoded, d_output, *refs
):
    (
        table, bias, b_hidden, w_qkv, w_ckv, w_cq, w_so, w_co, swapped, inputs_all, encoded_all,
        d_output_all, normed, q1, k1, v1, k2, v2, small_all, vectors, lsem, hs, hr, ssem, rsem,
    ) = refs
    hd, bk = Head(), Blk(count)
    share, head_width = cq.shape[0], q1.shape[2]
    rows, width = inputs.shape
    bar = pltpu.get_barrier_semaphore()
    pl.semaphore_wait(bar, greet_head(bar, hd) + greet_blk(bar, bk))
    ring = BlkGather(bk, (small_all, w_qkv, w_ckv, w_cq, w_so, w_co, k1, v1), ssem, rsem)
    K1, V1 = 6, 7
    pairs = (
        (small, small_all), (qkv, w_qkv), (ckv, w_ckv), (cq, w_cq), (so, w_so), (co, w_co),
        (inputs, inputs_all), (encoded, encoded_all), (ffn_in, swapped), (d_output, d_output_all),
    )
    SMALL, QKV, CKV, CQ, SO, CO, INPUTS, ENCODED, FFN_IN, D_OUTPUT = range(10)
    rows_only = (SO, CO)

    pieces = {QKV: 3, CKV: 2}

    def lanes(first, to, step):
        return pl.ds(pl.multiple_of(first + to * step, step), step)

    def source(a, to, i):
        if a == QKV:
            return qkv.at[i, :, lanes(0, to, head_width)]
        if a == CKV:
            return ckv.at[:, lanes(i * width, to, head_width)]
        if a == CQ:
            return cq.at[:, lanes(0, to, head_width)]
        if a == FFN_IN:
            return ffn_in.at[:, lanes(0, to, ffn_in.shape[1] // 4)]
        return pairs[a][0]

    def target(a, h, i):
        if a in rows_only:
            return pairs[a][1].at[:, bk.me]
        if a in pieces:
            return pairs[a][1].at[h, bk.me, :, i * head_width : (i + 1) * head_width]
        return pairs[a][1].at[h] if a >= INPUTS else pairs[a][1].at[h, bk.me]

    def own(a):
        return [
            pltpu.make_async_copy(source(a, hd.me, i), target(a, hd.me, i), lsem.at[a, i])
            for i in range(pieces.get(a, 1))
        ]

    def across_head(a, k, back):
        to = (hd.me + k) % 4
        here = to if back else hd.me
        return [
            remote(
                source(a, to, i), target(a, here, i), hs.at[a, k, i], hr.at[a, here, i], {"head": to}
            )
            for i in range(pieces.get(a, 1))
        ]

    def headed(a):
        for copy in own(a):
            copy.wait()
        for k in range(1, 4):
            for copy in across_head(a, k, True):
                copy.wait_recv()

    everything = (SMALL, QKV, CKV, CQ, INPUTS, ENCODED, FFN_IN, D_OUTPUT)
    for a in everything:
        for copy in own(a):
            copy.start()
        for k in (2, 1, 3):
            for copy in across_head(a, k, False):
                copy.start()
    for a in rows_only:
        own(a)[0].start()
    headed(SMALL)
    ring.start(SMALL)
    headed(QKV)
    ring.start(QKV)
    for a in rows_only:
        ring.start(a, pairs[a][0])
    headed(CKV)
    ring.start(CKV)
    headed(CQ)
    ring.start(CQ)
    for k in range(1, bk.Z):
        for a in (SMALL, QKV) + ((SO, CO, CKV, CQ) if k < bk.Z - 1 else ()):
            ring.step(a, k)
    ring.arrive(0)
    lane = lax.broadcasted_iota(jnp.int32, (N_SMALL, 128), 1)

    def assemble(h, carry):
        for group in range(head_width // 128):
            total = jnp.zeros((N_SMALL, 128), f32)
            for i in range(128 // share):
                piece = small_all[h, group * (128 // share) + i].astype(f32)
                if i:
                    piece = pltpu.roll(piece, i * share, 1)
                total = jnp.where(lane // share == i, piece, total)
            vectors[h, :, group * 128 : (group + 1) * 128] = total
        return carry

    lax.fori_loop(0, 4, assemble, 0)

    for h in range(4):
        table[:, h * head_width : (h + 1) * head_width] = vectors[h]
    bias[...] = vectors[hd.me]
    first = lax.broadcasted_iota(jnp.int32, (1, 128), 1)
    per_group = 128 // share
    for group in range(4 * count // per_group):
        total = jnp.zeros((1, 128), f32)
        for i in range(per_group):
            b, run = divmod(group * per_group + i, 4)
            piece = small_all[hd.me, b].astype(f32)[13 + run : 14 + run]
            if i:
                piece = pltpu.roll(piece, i * share, 1)
            total = jnp.where(first // share == i, piece, total)
        b_hidden[:, group * 128 : (group + 1) * 128] = total
    gain, shift = table[0:1], table[3:4]
    headed(INPUTS)

    def norm(j, carry):
        normed[j] = layer_norm(inputs_all[j].astype(f32), gain, shift).astype(bf16)
        return carry

    lax.fori_loop(0, 4, norm, 0)
    for a in (SO, CO, CKV, CQ):
        ring.step(a, bk.Z - 1)
    ring.arrive(QKV)

    def project(features, w, c, bias_row, store):
        cols = w[:, :, :, c * head_width : (c + 1) * head_width].reshape(width, head_width)

        def one(j, carry):
            out = dot(features[j], cols)
            if bias_row is not None:
                out = out + bias[bias_row : bias_row + 1, :]
            store(j, out.astype(bf16))
            return carry

        lax.fori_loop(0, 4, one, 0)

    def into(ref):
        def store(j, value):
            ref[j] = value

        return store

    def into_own(ref):
        def store(j, value):
            ref[j, bk.me] = value

        return store

    project(normed, w_qkv, 1, None, into_own(k1))
    ring.start(K1)
    project(normed, w_qkv, 2, 7, into_own(v1))
    ring.start(V1)
    project(normed, w_qkv, 0, 6, into(q1))
    headed(ENCODED)
    ring.step(K1, 1)
    ring.step(V1, 1)
    ring.arrive(CKV)
    project(encoded_all, w_ckv, 0, None, into(k2))
    project(encoded_all, w_ckv, 1, 9, into(v2))
    for k in range(2, bk.Z):
        ring.step(K1, k)
        ring.step(V1, k)
    for a in rows_only:
        own(a)[0].wait()
    for a in (FFN_IN, D_OUTPUT):
        headed(a)
    for a in (CQ, SO, CO, K1, V1):
        ring.arrive(a)
    for a in range(8):
        ring.drain(a)
    for a in everything:
        for k in range(1, 4):
            for copy in across_head(a, k, False):
                copy.wait_send()


def front(small, cols, so, co, ffn_in, acts, count, cid):
    rows, width = acts[0].shape
    share, head_width = so.shape[1], width // 4
    hidden_here = ffn_in.shape[1] // 4
    keys = (4, count, rows, head_width)
    tokens = (4, rows, width)
    block = (4, rows, head_width)
    bf = [(4, count, share, n * head_width) for n in (3, 2, 1)] + [(1, count) + a.shape[1:] for a in (so, co)]
    bf += [(4, share, hidden_here)] + [tokens] * 4 + [block, keys, keys, block, block]
    return pl.pallas_call(
        partial(front_kernel, count),
        out_shape=[
            jax.ShapeDtypeStruct((N_SMALL, width), f32),
            jax.ShapeDtypeStruct((N_SMALL, head_width), f32),
            jax.ShapeDtypeStruct((1, hidden_here), f32),
        ]
        + [jax.ShapeDtypeStruct(s, bf16) for s in bf],
        in_specs=[ANY] * 10,
        out_specs=[VMEM] * 5 + [ANY] * 4 + [VMEM] * 2 + [ANY] + [VMEM] * 6,
        scratch_shapes=[
            pltpu.VMEM((4, count, N_SMALL, 128), bf16),
            pltpu.VMEM((4, N_SMALL, head_width), f32),
            DMA((10, 3)),
            DMA((10, 4, 3)),
            DMA((10, 4, 3)),
            DMA((8, 3, count)),
            DMA((8, count)),
        ],
        compiler_params=params(cid),
        name="front",
        cost_estimate=lasts(90),
    )(small, *cols, so, co, ffn_in, *acts)


class BlkScatter:
    def __init__(self, bk, ins, bufs, sems):
        self.bk, self.ins = bk, ins
        self.own, self.over, self.side = bufs
        self.lsem, self.ys, self.yr, self.zs, self.ur, self.dr = sems

    def load(self, a, s):
        return pltpu.make_async_copy(
            self.ins[a].at[:, 2 * s + self.bk.y], self.own[a].at[s], self.lsem.at[a, s]
        )

    def cross(self, a, s):
        return remote(
            self.ins[a].at[:, 2 * s + 1 - self.bk.y],
            self.over[a].at[s],
            self.ys.at[a, s],
            self.yr.at[a, s],
            {"blk": self.bk.across},
        )

    def send(self, a, s, upward, slot=None):
        if slot is None:
            slot = s if upward else jnp.where(s == self.bk.z - 1, self.bk.Z, s)
        return remote(
            self.own[a].at[s],
            self.side[a].at[slot],
            self.zs.at[a, s],
            (self.ur if upward else self.dr).at[a, s],
            {"blk": self.bk.me + (2 if upward else -2)},
        )

    def order(self):
        for k in range((self.bk.Z + 1) // 2):
            yield self.bk.Z - 1 - k
            if k != self.bk.Z - 1 - k:
                yield k

    def begin(self, a):
        if a < len(self.ins):
            for s in self.order():
                self.cross(a, s).start()
                self.load(a, s).start()

    def add(self, a, s, extra, store):
        groups, rows = self.own[a].shape[1:3]
        step = min(rows, 32)

        def one(g, carry):
            for r in range(0, rows, step):
                part = pl.ds(r, step)
                total = self.own[a][s, g, part].astype(f32) + self.over[a][s, g, part].astype(f32)
                for slot in extra:
                    total = total + self.side[a][slot, g, part].astype(f32)
                store(g, part, total)
            return carry

        lax.fori_loop(0, groups, one, 0)

    def relay(self, a, s, upward):
        bk = self.bk
        self.load(a, s).wait()
        self.cross(a, s).wait_recv()
        inner = (bk.z > 0) if upward else (bk.z < bk.Z - 1)

        def store(g, part, total):
            self.own[a][s, g, part] = total.astype(bf16)

        @pl.when(inner)
        def _():
            self.send(a, s, upward, s).wait_recv()
            self.add(a, s, (s,), store)

        @pl.when(jnp.logical_not(inner))
        def _():
            self.add(a, s, (), store)

        self.send(a, s, upward).start()

    def run(self, finish):
        bk, n = self.bk, len(self.ins)
        for a in range(n):
            self.begin(a + AHEAD)
            for k in range(bk.Z - 1):

                @pl.when(bk.Z - 1 - k > bk.z)
                def _():
                    self.relay(a, bk.Z - 1 - k, True)

                @pl.when(k < bk.z)
                def _():
                    self.relay(a, k, False)

            if a > 0:
                finish(a - 1)
        finish(n - 1)

    def last(self, a, store):
        bk, s = self.bk, self.bk.z
        self.load(a, s).wait()
        self.cross(a, s).wait_recv()

        @pl.when(bk.z > 0)
        def _():
            self.send(a, s, True, s).wait_recv()

        @pl.when(bk.z < bk.Z - 1)
        def _():
            self.send(a, s, False, bk.Z).wait_recv()

        @pl.when((bk.z > 0) & (bk.z < bk.Z - 1))
        def _():
            self.add(a, s, (s, bk.Z), store)

        @pl.when((bk.z > 0) & (bk.z == bk.Z - 1))
        def _():
            self.add(a, s, (s,), store)

        @pl.when((bk.z == 0) & (bk.z < bk.Z - 1))
        def _():
            self.add(a, s, (bk.Z,), store)

    def finish(self):
        bk = self.bk
        for a in range(len(self.ins)):
            for s in range(bk.Z):
                self.cross(a, s).wait_send()

                @pl.when(s != bk.z)
                def _():
                    self.send(a, s, True, s).wait_send()


def scatter_scratch(items, count):
    Z = count // 2
    kinds = [
        pltpu.VMEM((slots, a.shape[0]) + a.shape[2:], bf16)
        for slots in (Z, Z, Z + 1)
        for a in items
    ]
    return kinds + [DMA((len(items), Z)) for _ in range(6)]


def scatter_parts(refs, n):
    bufs = tuple(refs[k * n : (k + 1) * n] for k in range(3))
    return bufs, refs[3 * n : 3 * n + 6], refs[3 * n + 6 :]


def scatter_blk_kernel(count, n, *refs):
    ins, outs = refs[:n], refs[n : 2 * n]
    bufs, sems, _ = scatter_parts(refs[2 * n :], n)
    bk = Blk(count)
    bar = pltpu.get_barrier_semaphore()
    pl.semaphore_wait(bar, greet_blk(bar, bk))
    ring = BlkScatter(bk, ins, bufs, sems)
    for a in range(AHEAD):
        ring.begin(a)

    def finish(a):
        def store(g, part, total):
            outs[a][g, part] = total.astype(outs[a].dtype)

        ring.last(a, store)

    ring.run(finish)
    ring.finish()


def scatter_blk(items, count, cid):
    n = len(items)
    return pl.pallas_call(
        partial(scatter_blk_kernel, count, n),
        out_shape=[
            jax.ShapeDtypeStruct((a.shape[0],) + a.shape[2:], a.dtype) for a in items
        ],
        in_specs=[ANY] * n,
        out_specs=[VMEM] * n,
        scratch_shapes=scatter_scratch(items, count),
        compiler_params=params(cid),
        name="scatter_blk",
        cost_estimate=lasts(60),
    )(*items)


PARTS = 2


class Halves:
    def half(self, p):
        rows = self.rows // PARTS
        return pl.ds(p * rows, rows)


class HeadSum(Halves):
    def __init__(self, hd, part, near, mid, far, sems):
        self.hd, self.part, self.near, self.mid, self.far = hd, part, near, mid, far
        self.ss, self.rs = sems
        self.rows = mid.shape[0]

    def near_copies(self, i):
        hd = self.hd
        block = hd.far_sib if i == 0 else hd.sib
        return [
            remote(
                self.part.at[block, self.half(p)],
                self.near.at[i, self.half(p)],
                self.ss.at[i, p],
                self.rs.at[i, p],
                {"head": hd.sib},
            )
            for p in range(PARTS)
        ]

    def near_start(self, i):
        for copy in self.near_copies(i):
            copy.start()

    def far_copy(self, p):
        return remote(
            self.mid.at[self.half(p)],
            self.far.at[self.half(p)],
            self.ss.at[2, p],
            self.rs.at[2, p],
            {"head": self.hd.far},
        )

    def begin(self):
        self.near_start(0)
        self.near_start(1)

    def middle(self):
        for p in range(PARTS):
            self.near_copies(0)[p].wait_recv()
            here = self.half(p)
            mine = self.part[self.hd.far, here].astype(f32)
            self.mid[here] = (mine + self.near[0, here].astype(f32)).astype(bf16)
            self.far_copy(p).start()

    def total(self, p):
        here = self.half(p)
        self.near_copies(1)[p].wait_recv()
        mine = self.part[self.hd.me, here].astype(f32) + self.near[1, here].astype(f32)
        self.far_copy(p).wait_recv()
        return mine + self.far[here].astype(f32)

    def whole(self):
        return jnp.concatenate([self.total(p) for p in range(PARTS)], axis=0)

    def finish(self):
        for p in range(PARTS):
            self.near_copies(0)[p].wait_send()
            self.near_copies(1)[p].wait_send()
            self.far_copy(p).wait_send()


def head_sum_scratch(rows, width):
    return [
        pltpu.VMEM((2, rows, width), bf16),
        pltpu.VMEM((rows, width), bf16),
        pltpu.VMEM((rows, width), bf16),
        DMA((3, PARTS)),
        DMA((3, PARTS)),
    ]


def head_gather_scratch():
    return [DMA((3, PARTS)), DMA((4, PARTS))]


class HeadGather(Halves):
    def __init__(self, hd, out, ss, rs):
        self.hd, self.out, self.ss, self.rs = hd, out, ss, rs
        self.rows = out.shape[1]

    def copy(self, slot, way, device, p):
        view = self.out.at[slot, self.half(p)]
        return remote(view, view, self.ss.at[way, p], self.rs.at[slot, p], {"head": device})

    def begin(self, p):
        hd = self.hd
        self.copy(hd.me, 0, hd.far, p).start()
        self.copy(hd.me, 1, hd.sib, p).start()

    def forward(self):
        hd = self.hd
        for p in range(PARTS):
            self.copy(hd.far, 0, hd.me, p).wait_recv()
            self.copy(hd.far, 2, hd.sib, p).start()

    def arrive(self):
        hd = self.hd
        for p in range(PARTS):
            self.copy(hd.sib, 0, hd.me, p).wait_recv()
            self.copy(hd.far_sib, 0, hd.me, p).wait_recv()

    def drain(self):
        hd = self.hd
        for p in range(PARTS):
            self.copy(hd.me, 0, hd.far, p).wait_send()
            self.copy(hd.me, 1, hd.sib, p).wait_send()
            self.copy(hd.far, 2, hd.sib, p).wait_send()


def row_stats(v):
    average = jnp.mean(v, axis=-1, keepdims=True)
    centred = v - average
    spread = jnp.mean(centred * centred, axis=-1, keepdims=True)
    return centred, lax.rsqrt(spread + 1e-05)


def layer_norm(v, gain, shift):
    centred, r = row_stats(v)
    return centred * r * gain + shift


def layer_norm_back(v, g, gain):
    centred, r = row_stats(v)
    u = centred * r
    c = g * gain
    dv = r * (c - jnp.mean(c, axis=-1, keepdims=True) - u * jnp.mean(c * u, axis=-1, keepdims=True))
    return dv, jnp.sum(g * u, axis=0, keepdims=True), jnp.sum(g, axis=0, keepdims=True)


SMALL_ROWS = (
    ("gain", 3), ("shift", 3), ("self_bias", 2), ("cross_bias", 2), ("out_bias", 3), ("ffn_bias", 4)
)
PAIRS = ("dk1", "dv1", "dk2", "dv2")


class PageScatter:
    def __init__(self, bk, feeds, bufs, sems, ready, crossed):
        self.bk, self.feeds, self.ready, self.crossed = bk, feeds, ready, crossed
        self.own, self.over, self.side = bufs
        self.lsem, self.ys, self.yr, self.zs, self.ur, self.dr = sems
        self.n = len(feeds)

    def load(self, a, s):
        copies = [
            pltpu.make_async_copy(src(s, True), self.own.at[(a, s) + dst], self.lsem.at[a, s, i])
            for i, (src, dst) in enumerate(self.feeds[a])
        ]
        if a in self.crossed:
            copies += [
                pltpu.make_async_copy(
                    src(s, False), self.over.at[(a, s) + dst], self.yr.at[a, s, i]
                )
                for i, (src, dst) in enumerate(self.feeds[a])
            ]
        return copies

    def cross(self, a, s):
        if a in self.crossed:
            return []
        return [
            remote(
                src(s, False),
                self.over.at[(a, s) + dst],
                self.ys.at[a, s, i],
                self.yr.at[a, s, i],
                {"blk": self.bk.across},
            )
            for i, (src, dst) in enumerate(self.feeds[a])
        ]

    def begin(self, a):
        Z = self.bk.Z
        for k in range(Z):
            s = Z - 1 - k // 2 if k % 2 == 0 else k // 2
            for copy in self.cross(a, s) + self.load(a, s):
                copy.start()

    def send(self, a, s, upward, slot=None):
        bk = self.bk
        if slot is None:
            slot = s if upward else jnp.where(s == bk.z - 1, bk.Z, s)
        return remote(
            self.own.at[a, s],
            self.side.at[a, slot],
            self.zs.at[a, s],
            (self.ur if upward else self.dr).at[a, s],
            {"blk": bk.me + (2 if upward else -2)},
        )

    def gathered(self, a):
        for s in range(self.bk.Z):
            for copy in self.load(a, s):
                copy.wait()
            for copy in self.cross(a, s):
                copy.wait_recv()

    def relay(self, a, s, upward):
        bk = self.bk
        inner = (bk.z > 0) if upward else (bk.z < bk.Z - 1)

        @pl.when(inner)
        def _():
            self.send(a, s, upward, s).wait_recv()
            self.own[a, s] = (
                self.own[a, s].astype(f32)
                + self.over[a, s].astype(f32)
                + self.side[a, s].astype(f32)
            ).astype(bf16)

        @pl.when(jnp.logical_not(inner))
        def _():
            self.own[a, s] = (
                self.own[a, s].astype(f32) + self.over[a, s].astype(f32)
            ).astype(bf16)

        self.send(a, s, upward).start()

    def wave(self, t):
        bk = self.bk
        if t < self.n:
            self.gathered(t)
        up, down = t - SKEW * bk.z, t - SKEW * (bk.Z - 1 - bk.z)

        @pl.when((up >= 0) & (up < self.n))
        def _():
            def one(i, carry):
                self.relay(up, bk.Z - 1 - i, True)
                return carry

            lax.fori_loop(0, bk.Z - 1 - bk.z, one, 0)

        @pl.when((down >= 0) & (down < self.n))
        def _():
            def one(i, carry):
                self.relay(down, i, False)
                return carry

            lax.fori_loop(0, bk.z, one, 0)

        a = t - SKEW * (bk.Z - 1)
        if a >= 0:
            self.last(a)

    def last(self, a):
        bk, s = self.bk, self.bk.z
        total = self.own[a, s].astype(f32) + self.over[a, s].astype(f32)

        @pl.when(bk.z > 0)
        def _():
            self.send(a, s, True, s).wait_recv()

        @pl.when(bk.z < bk.Z - 1)
        def _():
            self.send(a, s, False, bk.Z).wait_recv()

        total = total + jnp.where(bk.z > 0, self.side[a, s].astype(f32), 0.0)
        total = total + jnp.where(bk.z < bk.Z - 1, self.side[a, bk.Z].astype(f32), 0.0)
        self.ready[a](total)

    def drain(self):
        bk = self.bk
        for a in range(self.n):
            for s in range(bk.Z):
                for copy in self.cross(a, s):
                    copy.wait_send()

                @pl.when(s != bk.z)
                def _():
                    self.send(a, s, True, s).wait_send()


def finale_kernel(count, inside, names_in, names_out, names_scratch, *refs):
    r = SimpleNamespace(**dict(zip(names_in + names_out + names_scratch, refs)))
    hd, bk = Head(), Blk(count)
    devices = 4 * count
    me = hd.me * count + bk.me
    rows, width = r.d_first.shape
    head_width = width // 4
    share = width // devices
    bar = pltpu.get_barrier_semaphore()

    def place(k):
        to = (me + k) % devices
        return to, {"head": to // count, "blk": to % count}

    def greet(k, carry):
        signal(bar, **place(k)[1])
        return carry

    lax.fori_loop(1, devices, greet, 0)
    pl.semaphore_wait(bar, devices - 1)

    def tiles(src, dst, which):
        local = pltpu.make_async_copy(src.at[me], dst.at[me], r.tile_local.at[which])

        def copy(k, back):
            to, device = place(k)
            return remote(
                src.at[to],
                dst.at[to if back else me],
                r.tile_send.at[which, k],
                r.tile_recv.at[which, to if back else me],
                device,
            )

        def start(k, carry):
            copy(k, False).start()
            return carry

        def end(k, carry):
            copy(k, False).wait_send()
            copy(k, True).wait_recv()
            return carry

        def begin():
            local.start()
            lax.fori_loop(1, devices, start, 0)

        def finish():
            local.wait()
            lax.fori_loop(1, devices, end, 0)

        return begin, finish

    headed = ["ffn_in", "cq", "qkv", "ckv"]

    def across_head(n, k, back):
        a = headed.index(n)
        to = (hd.me + k) % 4
        src = r.ffn_in if n == "ffn_in" else getattr(r, "done_" + n)
        return remote(
            src.at[to],
            getattr(r, "out_" + n).at[to if back else hd.me],
            r.head_send.at[a, k],
            r.head_recv.at[a, to if back else hd.me],
            {"head": to},
        )

    def send_heads(n):
        for k in range(1, 4):
            across_head(n, k, False).start()
        src = r.ffn_in if n == "ffn_in" else getattr(r, "done_" + n)
        getattr(r, "out_" + n)[hd.me] = src[hd.me]

    def place_of(s, mine):
        return 2 * s + (bk.y if mine else 1 - bk.y)

    def col_page(ref, c):
        def src(s, mine):
            return ref.at[:, place_of(s, mine), :, c * head_width : (c + 1) * head_width]

        return [(src, ())]

    def row_page(ref):
        def src(j):
            return lambda s, mine: ref.at[
                0, place_of(s, mine), :, j * head_width : (j + 1) * head_width
            ]

        return [(src(j), (j,)) for j in range(4)]

    def pair_page(n, h):
        theirs = getattr(r, "over" + n[2]).at["kv".index(n[1])] if inside else None
        return [(lambda s, mine: (getattr(r, n) if mine else theirs).at[h, s], ())]

    def store_pair(n, h):
        def store(total):
            getattr(r, "sum_" + n)[h] = total.reshape(rows, head_width).astype(bf16)

        return store

    def store_col(n, c):
        def store(total):
            getattr(r, "done_" + n)[:, :, c * head_width : (c + 1) * head_width] = total.astype(bf16)

        return store

    def store_row(n):
        def store(total):
            for j in range(4):
                getattr(r, "out_" + n)[0, :, j * head_width : (j + 1) * head_width] = total[j]

        return store

    feeds, ready, crossed, index = [], [], [], {}

    def item(name, feed, store):
        index[name] = len(feeds)
        feeds.append(feed)
        ready.append(store)

    if inside:
        for n, h in [(n, h) for n in ("dk2", "dk1", "dv1", "dv2") for h in range(4)]:
            if n in ("dk2", "dv2"):
                crossed.append(len(feeds))
            item(n, pair_page(n, h), store_pair(n, h))
    for n in ("so", "co"):
        item(n, row_page(getattr(r, n)), store_row(n))
    item("cq", col_page(r.cq, 0), store_col("cq", 0))
    item("qkv0", col_page(r.grad_qkv, 0), store_col("qkv", 0))
    item("ckv0", col_page(r.grad_ckv, 0), store_col("ckv", 0))
    for c in (1, 2):
        item("qkv%d" % c, col_page(r.grad_qkv, c), store_col("qkv", c))
    item("ckv1", col_page(r.grad_ckv, 1), store_col("ckv", 1))
    ring = PageScatter(
        bk, feeds, (r.own, r.over, r.side), [getattr(r, "ring%d" % i) for i in range(6)], ready,
        crossed,
    )

    def summed(n):
        return getattr(r, "sum_" + n) if inside else getattr(r, n)

    def fill(joined, parts, first):
        for j in range(4):
            joined[j * rows : (j + 1) * rows, first : first + len(parts) * head_width] = (
                jnp.concatenate([p[j] for p in parts], axis=1)
            )

    def weight_grad(joined, cols, features, grad, g0, g1):
        def one(g, carry):
            lhs = features[:, :, pl.ds(pl.multiple_of(g * head_width, head_width), head_width)]
            total = dot(lhs.reshape(4 * rows, head_width), joined[:, cols], TN)
            grad[g, :, :, cols] = total.reshape(grad.shape[1:3] + (-1,)).astype(bf16)
            return carry

        lax.fori_loop(g0, g1, one, 0)

    def project(joined, w, summed_over_head):
        def term(j):
            def run():
                block = joined[pl.ds(pl.multiple_of(j * rows, rows), rows), :]
                summed_over_head.part[j] = dot(block, w[...], NT).astype(bf16)

            return run

        def near(i):
            return lambda: summed_over_head.near_start(i)

        return [
            [term(hd.far_sib), near(0)],
            [term(hd.sib), near(1)],
            [term(hd.far), summed_over_head.middle],
            [term(hd.me)],
        ]

    stats_begin, stats_finish = tiles(r.stats_tab, r.stats_got, 0)
    first, second = (
        HeadSum(
            hd, getattr(r, "part%d" % (i + 1)), getattr(r, "near%d" % i), getattr(r, "mid%d" % i), getattr(r, "far%d" % i),
            (getattr(r, "sum_send%d" % i), getattr(r, "sum_recv%d" % i)),
        )
        for i in range(2)
    )

    def query_part():
        fill(r.joined1, [r.dq1], 0)
        weight_grad(r.joined1, slice(0, head_width), r.normed, r.grad_qkv, 0, 4)
        ring.begin(index["qkv0"])

    def own_steps(n, c, joined, features, grad, page):
        cols = slice(c * head_width, (c + 1) * head_width)

        def half(g0, g1):
            return lambda: weight_grad(joined, cols, features, grad, g0, g1)

        return [
            [lambda: fill(joined, [summed(n)], c * head_width), half(0, 2)],
            [half(2, 4), lambda: ring.begin(index[page])],
        ]

    steps = dict(
        dk2=own_steps("dk2", 0, r.joined2, r.encoded, r.grad_ckv, "ckv0"),
        dk1=own_steps("dk1", 1, r.joined1, r.normed, r.grad_qkv, "qkv1"),
        dv1=own_steps("dv1", 2, r.joined1, r.normed, r.grad_qkv, "qkv2"),
        dv2=own_steps("dv2", 1, r.joined2, r.encoded, r.grad_ckv, "ckv1"),
    )
    steps["dv1"] += project(r.joined1, r.w_qkv, first)
    steps["dv2"] += project(r.joined2, r.w_ckv, second)

    def self_norm():
        dv, d_gain, d_shift = layer_norm_back(
            r.inputs[...].astype(f32), first.whole(), r.table[0:1]
        )
        r.out_d_inputs[...] = dv + r.d_first[...]
        r.own_stats[0:1] = d_gain
        r.own_stats[1:2] = d_shift

    def self_table():
        two, three = r.stats_two, r.stats_three

        def placed(row):
            return jnp.concatenate(
                [jnp.where(hd.me == h, row, 0.0) for h in range(4)], axis=1
            )

        rows_of = [
            r.own_stats[0:1], two[0:1], three[0:1], r.own_stats[1:2], two[1:2], three[1:2],
            placed(r.sums_one[0:1]), placed(r.sums_one[1:2]),
            placed(r.sums_two[0:1]), placed(r.sums_two[1:2]),
            two[2:3], three[2:3], three[3:4],
        ]
        whole = jnp.concatenate(rows_of + [jnp.zeros((N_SMALL - 13, width), f32)], axis=0)
        hidden = r.d_hidden[...]

        def turned(value, lane):
            tile = value[:, lane // 128 * 128 : lane // 128 * 128 + 128]
            return pltpu.roll(tile, 128 - lane % 128, 1) if lane % 128 else tile

        for d in range(devices):
            r.stats_tab[d] = turned(whole, d * share)
            h, b = divmod(d, count)
            for run in range(4):
                mine = turned(hidden, (4 * b + run) * share)
                r.stats_tab[d, 13 + run : 14 + run, :] = jnp.where(hd.me == h, mine, 0.0)

    def sum_ffn():
        def one(i, carry):
            part = pl.ds(pl.multiple_of(i * share, share), share)
            total = r.ffn_terms[0, part, :].astype(f32)
            for b in range(1, count // 2):
                total = total + r.ffn_terms[b, part, :].astype(f32)

            @pl.when(i < 4)
            def _():
                r.ffn_in[i] = total.astype(bf16)

            @pl.when(i >= 4)
            def _():
                r.out_ffn_out[pl.ds(pl.multiple_of((i - 4) * share, share), share), :] = total

            return carry

        lax.fori_loop(0, 8, one, 0)
        send_heads("ffn_in")

    lag = SKEW * (bk.Z - 1)
    lead = 4 if inside else index["cq"] + 1
    for a in range(lead):
        ring.begin(a)
    plan = {}

    def at(t, step):
        plan.setdefault(t, []).append(step)

    last = ring.n + lag - 1
    after_self = 0
    if inside:
        after_self = index["dv1"] + lag
        for n in PAIRS:
            for i, step in enumerate(steps[n]):
                at(index[n] + lag + (max(i - 1, 0) if n == "dv2" else i), step)
        at(3, [query_part])
        at(5, [sum_ffn])
    else:
        sum_ffn()
        query_part()
        for n in PAIRS:
            for step in steps[n]:
                for run in step:
                    run()
    for i, step in enumerate((self_norm, self_table, stats_begin)):
        at(min(after_self + 8 + i, last), [step])
    at(index["cq"] + lag, [lambda: send_heads("cq")])
    at(index["qkv2"] + lag, [lambda: send_heads("qkv")])
    for t in range(last + 1):
        for a in range(lead + 2 * t, min(lead + 2 * t + 2, index["cq"] + 1)):
            ring.begin(a)
        ring.wave(t)
        for step in plan.get(t, []):
            for run in step:
                run()
    send_heads("ckv")
    r.out_d_encoded[...] = second.whole()
    ring.drain()
    first.finish()
    second.finish()
    for n in headed:
        for k in range(1, 4):
            across_head(n, k, False).wait_send()
            across_head(n, k, True).wait_recv()
    stats_finish()
    total = r.stats_got[0]
    for d in range(1, devices):
        total = total + r.stats_got[d]
    r.out_stats[...] = total


def settle_kernel(names, *refs):
    r = SimpleNamespace(**dict(zip(names, refs[:-1])))
    sems = refs[-1]
    copies = [
        pltpu.make_async_copy(getattr(r, name), getattr(r, "here_" + name[4:]), sems.at[i])
        for i, name in enumerate([n for n in names if n.startswith("got_")])
    ]
    for copy in copies:
        copy.start()
    for copy in copies:
        copy.wait()
    for name in ("ffn_in", "cq", "ckv", "qkv"):
        got, out = getattr(r, "here_" + name), getattr(r, "out_" + name)
        parts = dict(qkv=3, ckv=2).get(name, 1)
        step = got.shape[2] // parts
        for h in range(4):
            for c in range(parts):
                value = got[h, :, c * step : (c + 1) * step].astype(f32)
                if parts == 3:
                    out[c, :, h * step : (h + 1) * step] = value
                elif parts == 1:
                    out[:, h * step : (h + 1) * step] = value
                else:
                    out[:, c, h * step : (h + 1) * step] = value
    for name in ("d_inputs", "d_encoded", "ffn_out", "layer"):
        getattr(r, "out_" + name)[...] = getattr(r, "here_" + name)[...]
    for name in ("co", "so"):
        getattr(r, "out_" + name)[...] = getattr(r, "here_" + name)[0]
    row = 0
    for name, number in SMALL_ROWS:
        out = getattr(r, "out_" + name)
        out[...] = r.here_stats[row : row + number, : out.shape[1]]
        row += number


def settle(got, layer_output, share, width, hidden_width):
    rows = layer_output.shape[0]
    ins = {"got_" + n[4:]: a for n, a in got.items()}
    ins["got_layer"] = layer_output
    outs = dict(
        out_layer=((rows, width), bf16),
        out_d_inputs=((rows, width), f32),
        out_d_encoded=((rows, width), f32),
        out_qkv=((3, share, width), f32),
        out_ckv=((share, 2, width), f32),
        out_cq=((share, width), f32),
        out_ffn_in=((share, hidden_width), f32),
        out_ffn_out=(got["out_ffn_out"].shape, f32),
        out_co=((share, width), f32),
        out_so=((share, width), f32),
    )
    outs.update({"out_" + n: ((number, share), f32) for n, number in SMALL_ROWS})
    here = {"here_" + n[4:]: pltpu.VMEM(a.shape, a.dtype) for n, a in ins.items()}
    done = pl.pallas_call(
        partial(settle_kernel, tuple(ins) + tuple(outs) + tuple(here)),
        out_shape=[jax.ShapeDtypeStruct(*o) for o in outs.values()],
        in_specs=[ANY] * len(ins),
        out_specs=[VMEM] * len(outs),
        scratch_shapes=list(here.values()) + [DMA((len(ins),))],
        compiler_params=pltpu.CompilerParams(vmem_limit_bytes=60 * 2**20),
        name="settle",
        cost_estimate=lasts(4),
    )(*ins.values())
    return dict(zip(outs, done))


def finale(
    count, pairs, co, so, cq, ffn_terms, dq1, normed, encoded, w_qkv, w_ckv, inputs, d_first, table,
    stats_two, stats_three, sums_one, sums_two, d_hidden, cid,
):
    inside = len(pairs) == 6
    devices, Z = 4 * count, count // 2
    rows, width = inputs.shape
    share = width // devices
    head_width = w_ckv.shape[1] // 2
    hidden_width = ffn_terms.shape[2]
    ins = dict(zip(PAIRS + ("over1", "over2"), pairs))
    ins.update(co=co, so=so, cq=cq)
    in_specs = [ANY if inside else VMEM] * len(pairs) + [ANY] * 3
    rest = dict(
        ffn_terms=ffn_terms, dq1=dq1, normed=normed, encoded=encoded, w_qkv=w_qkv, w_ckv=w_ckv,
        inputs=inputs, d_first=d_first, table=table, stats_two=stats_two, stats_three=stats_three,
        sums_one=sums_one, sums_two=sums_two, d_hidden=d_hidden,
    )
    ins.update(rest)
    in_specs += [VMEM] * len(rest)
    outs = dict(
        out_d_inputs=((rows, width), f32),
        out_d_encoded=((rows, width), f32),
        out_qkv=((4, share, 3 * head_width), bf16),
        out_ckv=((4, share, 2 * head_width), bf16),
        out_cq=((4, share, head_width), bf16),
        out_ffn_in=((4, share, hidden_width), bf16),
        out_ffn_out=((4 * share, width), f32),
        out_co=((1, share, width), f32),
        out_so=((1, share, width), f32),
        out_stats=((N_SMALL, 128), f32),
    )
    grads = dict(
        grad_qkv=(4, count, share, 3 * head_width), grad_ckv=(4, count, share, 2 * head_width)
    )
    scratch = {}
    n_items = 24 if inside else 8
    for kind, slots in (("own", Z), ("over", Z), ("side", Z + 1)):
        scratch[kind] = pltpu.VMEM((n_items, slots, 4, share, head_width), bf16)
    for n, wide in (("cq", 1), ("qkv", 3), ("ckv", 2)):
        scratch["done_" + n] = pltpu.VMEM((4, share, wide * head_width), bf16)
    scratch["ffn_in"] = pltpu.VMEM((4, share, hidden_width), bf16)
    if inside:
        for n in PAIRS:
            scratch["sum_" + n] = pltpu.VMEM((4, rows, head_width), bf16)
    for n, shape in grads.items():
        scratch[n] = pltpu.VMEM(shape, bf16)
    for i, n in enumerate(("1", "2")):
        scratch["part" + n] = pltpu.VMEM((4, rows, width), bf16)
        scratch["joined" + n] = pltpu.VMEM((4 * rows, (3 - i) * head_width), bf16)
        kinds = head_sum_scratch(rows, width)
        for name, kind in zip(("near", "mid", "far", "sum_send", "sum_recv"), kinds):
            scratch[name + str(i)] = kind
    scratch["own_stats"] = pltpu.VMEM((8, width), f32)
    for n in ("stats_tab", "stats_got"):
        scratch[n] = pltpu.VMEM((devices, N_SMALL, 128), f32)
    for i in range(6):
        scratch["ring%d" % i] = DMA((n_items, Z, 4) if i < 3 else (n_items, Z))
    scratch["tile_local"] = DMA((1,))
    scratch["tile_send"] = DMA((1, devices))
    scratch["tile_recv"] = DMA((1, devices))
    scratch["head_send"] = DMA((4, 4))
    scratch["head_recv"] = DMA((4, 4))
    got = pl.pallas_call(
        partial(finale_kernel, count, inside, tuple(ins), tuple(outs), tuple(scratch)),
        out_shape=[jax.ShapeDtypeStruct(*o) for o in outs.values()],
        in_specs=in_specs,
        out_specs=[VMEM] * len(outs),
        scratch_shapes=list(scratch.values()),
        compiler_params=params(cid),
        name="finale",
        cost_estimate=lasts(150),
    )(*ins.values())
    return dict(zip(outs, got))


def forward_kernel(count, n_stream, has_query, layer, *refs):
    refs = list(refs)
    mix, w_out, base, table = (refs.pop(0) for _ in range(4))
    w_query, b_query = (refs.pop(0) for _ in range(2)) if has_query else (None, None)
    stream_in = [refs.pop(0) for _ in range(n_stream)]
    total, normed = (refs.pop(0) for _ in range(2))
    query = refs.pop(0) if has_query else None
    stream_out = [refs.pop(0) for _ in range(n_stream)]
    part, near, mid, far, ss, rs, gs, gr = (refs.pop(0) for _ in range(8))
    hd, bk = Head(), Blk(count)
    bar = pltpu.get_barrier_semaphore()
    greeted = greet_head(bar, hd)
    if n_stream:
        greeted = greeted + greet_blk(bar, bk)
    pl.semaphore_wait(bar, greeted)
    ring = None
    if n_stream:
        lsem, ssem, rsem = refs
        ring = BlkGather(bk, stream_out, ssem, rsem)
        for a in range(n_stream):
            ring.start(a, stream_in[a])
            pltpu.make_async_copy(stream_in[a], stream_out[a].at[:, bk.me], lsem.at[a]).start()

    def term(j):
        part[j] = dot(mix[j], w_out[...]).astype(bf16)

    summed = HeadSum(hd, part, near, mid, far, (ss, rs))
    term(hd.far_sib)
    summed.near_start(0)
    term(hd.sib)
    summed.near_start(1)
    term(hd.far)
    summed.middle()
    term(hd.me)
    gain, shift = table[layer + 1 : layer + 2], table[layer + 4 : layer + 5]
    spread = HeadGather(hd, normed, gs, gr)
    for p in range(PARTS):
        here = summed.half(p)
        v = base[here].astype(f32) + summed.total(p) + table[10 + layer : 11 + layer]
        total[here] = v
        normed[hd.me, here] = layer_norm(v, gain, shift).astype(bf16)
        spread.begin(p)

    def ask(j):
        if has_query:
            query[j] = (dot(normed[j], w_query[...]) + b_query[8:9]).astype(bf16)

    def step(k):
        for a in range(n_stream):
            ring.step(a, k)

    ask(hd.me)
    if n_stream:
        step(1)
    spread.forward()
    ask(hd.far)
    spread.arrive()
    ask(hd.sib)
    ask(hd.far_sib)
    if n_stream:
        for k in range(2, bk.Z):
            step(k)
        for a in range(n_stream):
            ring.arrive(a)
            ring.drain(a)
            pltpu.make_async_copy(stream_in[a], stream_out[a].at[:, bk.me], lsem.at[a]).wait()
    spread.drain()
    summed.finish()


def join_forward(mix, w_out, base, table, layer, count, cid, query=None, stream=()):
    rows, width = base.shape
    n = len(stream)
    ops = [mix, w_out, base, table] + list(query or ()) + list(stream)
    shapes = [
        jax.ShapeDtypeStruct((rows, width), f32),
        jax.ShapeDtypeStruct((4, rows, width), bf16),
    ]
    if query:
        shapes.append(jax.ShapeDtypeStruct(mix.shape, bf16))
    n_vmem = len(shapes)
    shapes += [jax.ShapeDtypeStruct((4, count) + a.shape[1:], bf16) for a in stream]
    scratch = [pltpu.VMEM((4, rows, width), bf16)] + head_sum_scratch(rows, width)
    scratch += head_gather_scratch()
    if n:
        scratch += [DMA((n,)), DMA((n, 3, count)), DMA((n, count))]
    return pl.pallas_call(
        partial(forward_kernel, count, n, query is not None, layer),
        out_shape=shapes,
        in_specs=[VMEM] * (len(ops) - n) + [ANY] * n,
        out_specs=[VMEM] * n_vmem + [ANY] * n,
        scratch_shapes=scratch,
        compiler_params=params(cid),
        name="join_forward",
        cost_estimate=lasts(50 if n else 22),
    )(*ops)


def backward_kernel(count, layer, has_extra, *refs):
    refs = list(refs)
    if has_extra:
        part, extra = (refs.pop(0) for _ in range(2))
    else:
        dq, w_in, normed = (refs.pop(0) for _ in range(3))
    onward, v, table, w_out, mix = (refs.pop(0) for _ in range(5))
    back, stats, d_o, grad_out = (refs.pop(0) for _ in range(4))
    other = refs.pop(0)
    grad_all = refs.pop(0)
    sums = [refs.pop(0) for _ in range(5)]
    hd = Head()
    head_width = mix.shape[2]
    tokens = 4 * mix.shape[1]
    bar = pltpu.get_barrier_semaphore()
    pl.semaphore_wait(bar, greet_head(bar, hd))
    if has_extra:
        second = HeadSum(hd, extra, *refs[:3], refs[3:5])
        refs = refs[5:]
    else:
        part = refs.pop(0)
    summed = HeadSum(hd, part, *sums[:3], sums[3:])
    if has_extra:
        summed.begin()
        summed.middle()
        second.begin()
        second.middle()
    else:

        def term(j):
            part[j] = dot(dq[j], w_in[...], NT).astype(bf16)

        term(hd.far_sib)
        summed.near_start(0)
        term(hd.sib)
        summed.near_start(1)
        term(hd.far)
        summed.middle()
        term(hd.me)
        all_dq = dq[...].reshape(tokens, head_width)

        def weight(g, carry):
            lhs = normed[:, :, pl.ds(pl.multiple_of(g * head_width, head_width), head_width)]
            other[g] = (
                dot(lhs.reshape(tokens, head_width), all_dq, TN).reshape(other.shape[1:]).astype(bf16)
            )
            return carry

        lax.fori_loop(0, 4, weight, 0)
    gain = table[layer : layer + 1]
    spread = HeadGather(hd, grad_all, *refs)
    sums_here = []
    for p in range(PARTS):
        here = summed.half(p)
        dv, d_gain, d_shift = layer_norm_back(v[here], summed.total(p), gain)
        after = onward[here].astype(f32)
        d = dv + after
        back[here] = d
        rounded = d.astype(bf16)
        grad_all[hd.me, here] = rounded
        spread.begin(p)
        sums_here.append(
            (
                d_gain,
                d_shift,
                jnp.sum(rounded.astype(f32), axis=0, keepdims=True),
                jnp.sum(after, axis=0, keepdims=True),
            )
        )
    for i, terms in enumerate(zip(*sums_here)):
        stats[i : i + 1] = sum(terms[1:], terms[0])

    def out(j):
        d_o[j] = dot(grad_all[j], w_out[...], NT).astype(bf16)

    out(hd.me)
    if has_extra:
        other[...] = (v[...] + second.whole() + table[10 + layer : 11 + layer]).astype(bf16)
    spread.forward()
    out(hd.far)
    spread.arrive()
    out(hd.sib)
    out(hd.far_sib)
    grad = dot(mix[...].reshape(tokens, head_width), grad_all[...].reshape(tokens, -1), TN)
    grad_out[0] = grad.reshape(grad_out.shape[1:]).astype(bf16)
    spread.drain()
    summed.finish()
    if has_extra:
        second.finish()


def join_backward(terms, onward, v, table, layer, w_out, mix, count, cid):
    rows, width = onward.shape
    share, head_width = width // (4 * count), mix.shape[2]
    has_extra = len(terms) == 2
    ops = list(terms) + [onward, v, table, w_out, mix]
    other = ((rows, width), bf16) if has_extra else ((4, count, share, head_width), bf16)
    shapes = [
        ((rows, width), f32),
        ((8, width), f32),
        (mix.shape, bf16),
        ((1, count, share, width), bf16),
        other,
    ]
    scratch = [pltpu.VMEM((4, rows, width), bf16)] + head_sum_scratch(rows, width)
    if has_extra:
        scratch += head_sum_scratch(rows, width)
    else:
        scratch += [pltpu.VMEM((4, rows, width), bf16)]
    scratch += head_gather_scratch()
    return pl.pallas_call(
        partial(backward_kernel, count, layer, has_extra),
        out_shape=[jax.ShapeDtypeStruct(*s) for s in shapes],
        in_specs=[VMEM] * len(ops),
        out_specs=[VMEM] * len(shapes),
        scratch_shapes=scratch,
        compiler_params=params(cid),
        name="join_backward",
        cost_estimate=lasts(24),
    )(*ops)


def feed_forward_kernel(
    normed, d_output, w_in, w_out, b_hidden, out_part, d_part, mine, theirs, d_sum, out_sum, back_sum
):
    rows, width = normed.shape[1:]
    tokens = 4 * rows
    share = mine.shape[1] // 8
    step = width // 4
    runs = step // (8 * share)
    even_first = lax.axis_index("blk") % 2 == 0
    out_sum[...] = jnp.zeros_like(out_sum)
    back_sum[...] = jnp.zeros_like(back_sum)

    def split(total, place):
        even, odd = total[:, 0].astype(bf16), total[:, 1].astype(bf16)
        mine[place] = jnp.where(even_first, even, odd)
        theirs[place] = jnp.where(even_first, odd, even)

    def run(c, carry):
        part = pl.ds(pl.multiple_of(c * step, step), step)
        features = normed[...].reshape(tokens, width)
        after = d_output[...].reshape(tokens, width)
        hidden = dot(features, w_in[:, part]) + b_hidden[:, part]
        phi = 0.5 * (1.0 + lax.erf(hidden * (0.5**0.5)))
        active = (hidden * phi).astype(bf16)
        slope = phi + hidden * jnp.exp(-0.5 * hidden * hidden) * ((0.5 / jnp.pi) ** 0.5)
        d_hidden = (dot(after, w_out[part, :], NT) * slope).astype(bf16)
        d_sum[:, part] = jnp.sum(d_hidden.astype(f32), axis=0, keepdims=True)
        out_sum[...] += dot(active, w_out[part, :])
        back_sum[...] += dot(d_hidden, w_in[:, part], NT)
        split(
            dot(active, after, TN).reshape(runs, 2, 4 * share, -1),
            (pl.ds(c * runs, runs), slice(4 * share, None)),
        )
        for g in range(4):
            total = dot(features[:, g * step : (g + 1) * step], d_hidden, TN)
            split(
                total.reshape(mine.shape[0], 2, share, -1),
                (slice(None), slice(g * share, (g + 1) * share), part),
            )
        return carry

    lax.fori_loop(0, 4, run, 0)
    for j in range(4):
        out_part[j] = out_sum[j * rows : (j + 1) * rows].astype(bf16)
        d_part[j] = back_sum[j * rows : (j + 1) * rows].astype(bf16)


def feed_forward(normed, d_output, w_in, w_out, b_hidden, count):
    rows, width = normed.shape[1:]
    share = width // (4 * count)
    return pl.pallas_call(
        feed_forward_kernel,
        out_shape=(
            jax.ShapeDtypeStruct(normed.shape, bf16),
            jax.ShapeDtypeStruct(normed.shape, bf16),
            jax.ShapeDtypeStruct((count // 2, 8 * share, width), bf16),
            jax.ShapeDtypeStruct((count // 2, 8 * share, width), bf16),
            jax.ShapeDtypeStruct((1, w_in.shape[1]), f32),
        ),
        in_specs=[VMEM] * 5,
        out_specs=(VMEM,) * 5,
        scratch_shapes=[
            pltpu.VMEM((4 * rows, width), f32),
            pltpu.VMEM((4 * rows, width), f32),
        ],
        compiler_params=pltpu.CompilerParams(vmem_limit_bytes=56 * 2**20),
        name="feed_forward",
        cost_estimate=lasts(15),
    )(normed, d_output, w_in, w_out, b_hidden)


def tie(value, *others):
    return lax.optimization_barrier((value,) + others)


def stack_heads(rows, scale):
    lane = lax.broadcasted_iota(jnp.int32, rows.shape, 1) // HEAD_DIM
    pieces = [
        jnp.where(lane == h, rows.astype(f32) * scale, 0.0).astype(bf16) for h in range(HEADS_HERE)
    ]
    return jnp.concatenate(pieces, axis=0)


def take_heads(wide, rows):
    pieces = [
        wide[h * HEAD_DIM : (h + 1) * HEAD_DIM, h * rows : (h + 1) * rows]
        for h in range(HEADS_HERE)
    ]
    return jnp.concatenate(pieces, axis=0).T


def wide_span(spans, which, i):
    return [jnp.concatenate([spans[which, e, i]] * HEADS_HERE, axis=1) for e in range(2)]


def masked_scores(keys, stacked, first, low, high):
    scores = dot(keys, stacked, NT)
    key_pos = first + lax.broadcasted_iota(jnp.int32, scores.shape, 0)
    return jnp.where((key_pos >= low) & (key_pos < high), scores, -1e30)


def attend_kernel(which, bounds, spans, q, k, v, o, mix, lse, acc):
    chunks, rows, width = q.shape

    def chunk(i, carry):
        stacked = stack_heads(q[i], HEAD_DIM ** (-0.5))
        lo, hi = wide_span(spans, which, i)
        acc[...] = jnp.zeros_like(acc)

        def step(kb, state):
            top, total = state
            first = pl.multiple_of(kb * KEY_BLOCK, KEY_BLOCK)
            scores = masked_scores(k[pl.ds(first, KEY_BLOCK), :], stacked, first, lo, hi)
            new_top = jnp.maximum(top, jnp.max(scores, axis=0, keepdims=True))
            fading = jnp.exp(top - new_top)
            weights = jnp.exp(scores - new_top)
            total = total * fading + jnp.sum(weights, axis=0, keepdims=True)
            acc[...] = acc[...] * fading + dot(
                v[pl.ds(first, KEY_BLOCK), :], weights.astype(bf16), TN
            )
            return new_top, total

        wide = HEADS_HERE * rows
        top, total = lax.fori_loop(
            bounds[which, 0, i],
            bounds[which, 1, i],
            step,
            (jnp.full((1, wide), -1e30, f32), jnp.zeros((1, wide), f32)),
        )
        lse[i] = top + jnp.log(total)
        result = take_heads(acc[...] / total, rows)
        o[i] = result
        mix[i] = result.astype(bf16)
        return carry

    lax.fori_loop(0, chunks, chunk, 0)


def attend(q, k, v, spans, which):
    bounds, spans = spans
    chunks, rows, width = q.shape
    wide = HEADS_HERE * rows
    return pl.pallas_call(
        partial(attend_kernel, which),
        out_shape=(
            jax.ShapeDtypeStruct(q.shape, f32),
            jax.ShapeDtypeStruct(q.shape, bf16),
            jax.ShapeDtypeStruct((chunks, 1, wide), f32),
        ),
        in_specs=[SMEM] + [VMEM] * 4,
        out_specs=(VMEM,) * 3,
        scratch_shapes=[pltpu.VMEM((width, wide), f32)],
        compiler_params=pltpu.CompilerParams(vmem_limit_bytes=56 * 2**20),
        name="attend",
        cost_estimate=lasts(12),
    )(bounds, spans, q, k, v)


def attend_back_kernel(
    which, bounds, spans, q, k, v, d_o, o, lse, dq, dk, dv, over, sums,
    qs, dos, delta, dq_acc, dk_acc, dv_acc
):
    chunks, rows, width = q.shape
    y = lax.axis_index("blk") % 2
    spread = KEY_BLOCK // (2 * rows)
    mine = [pl.ds(pl.multiple_of((2 * n + y) * rows, rows), rows) for n in range(spread)]
    theirs = [pl.ds(pl.multiple_of((2 * n + 1 - y) * rows, rows), rows) for n in range(spread)]
    sums[...] = jnp.zeros_like(sums)
    for i in range(chunks):
        qs[i] = stack_heads(q[i], HEAD_DIM ** (-0.5))
        dos[i] = stack_heads(d_o[i], 1.0)
        product = (d_o[i].astype(f32) * o[i]).T
        delta[i] = jnp.concatenate(
            [
                jnp.sum(product[h * HEAD_DIM : (h + 1) * HEAD_DIM], axis=0, keepdims=True)
                for h in range(HEADS_HERE)
            ],
            axis=1,
        )
    dq_acc[...] = jnp.zeros_like(dq_acc)

    def block(kb, carry):
        first = pl.multiple_of(kb * KEY_BLOCK, KEY_BLOCK)
        part = pl.ds(first, KEY_BLOCK)
        dk_acc[...] = jnp.zeros_like(dk_acc)
        dv_acc[...] = jnp.zeros_like(dv_acc)

        def chunk(i, inner):
            @pl.when((kb >= bounds[which, 0, i]) & (kb < bounds[which, 1, i]))
            def _():
                keys = k[part, :]
                lo, hi = wide_span(spans, which, i)
                scores = masked_scores(keys, qs[i], first, lo, hi)
                weights = jnp.exp(scores - lse[i])
                d_weights = dot(v[part, :], dos[i], NT)
                d_scores = (weights * (d_weights - delta[i])).astype(bf16)
                dv_acc[...] += dot(weights.astype(bf16), dos[i])
                dk_acc[...] += dot(d_scores, qs[i])
                dq_acc[i] += dot(keys, d_scores, TN)

            return inner

        lax.fori_loop(0, chunks, chunk, 0)
        for n in range(spread):
            dk[kb * spread + n] = dk_acc[mine[n], :].astype(bf16)
            over[0, kb * spread + n] = dk_acc[theirs[n], :].astype(bf16)
            dv[kb * spread + n] = dv_acc[mine[n], :].astype(bf16)
            over[1, kb * spread + n] = dv_acc[theirs[n], :].astype(bf16)
        sums[1:2] += jnp.sum(dv_acc[...], axis=0, keepdims=True)
        return carry

    lax.fori_loop(0, k.shape[0] // KEY_BLOCK, block, 0)
    for i in range(chunks):
        result = (take_heads(dq_acc[i], rows) * HEAD_DIM ** (-0.5)).astype(bf16)
        dq[i] = result
        sums[0:1] += jnp.sum(result.astype(f32), axis=0, keepdims=True)


def attend_back(q, k, v, spans, which, d_o, o, lse):
    bounds, spans = spans
    chunks, rows, width = q.shape
    wide = HEADS_HERE * rows
    half = (k.shape[0] // (2 * rows), rows, width)
    return pl.pallas_call(
        partial(attend_back_kernel, which),
        out_shape=(
            jax.ShapeDtypeStruct(q.shape, bf16),
            jax.ShapeDtypeStruct(half, bf16),
            jax.ShapeDtypeStruct(half, bf16),
            jax.ShapeDtypeStruct((2,) + half, bf16),
            jax.ShapeDtypeStruct((8, width), f32),
        ),
        in_specs=[SMEM] + [VMEM] * 7,
        out_specs=(VMEM,) * 5,
        scratch_shapes=[
            pltpu.VMEM((chunks, wide, width), bf16),
            pltpu.VMEM((chunks, wide, width), bf16),
            pltpu.VMEM((chunks, 1, wide), f32),
            pltpu.VMEM((chunks, width, wide), f32),
            pltpu.VMEM((KEY_BLOCK, width), f32),
            pltpu.VMEM((KEY_BLOCK, width), f32),
        ],
        compiler_params=pltpu.CompilerParams(vmem_limit_bytes=60 * 2**20),
        name="attend_back",
        cost_estimate=lasts(14),
    )(bounds, spans, q, k, v, d_o, o, lse)


def key_spans(target_lengths, source_lengths, rows, count):
    ends = jnp.cumsum(target_lengths, dtype=jnp.int32)
    starts = ends - target_lengths
    chunk = jnp.arange(4, dtype=jnp.int32) * count + lax.axis_index("blk")

    def at(pos):
        past = (pos[..., None] >= ends).astype(jnp.int32)
        begun = (pos[..., None] >= starts).astype(jnp.int32)
        return (
            (jnp.sum(past * target_lengths, axis=-1), pos + 1),
            (jnp.sum(past * source_lengths, axis=-1), jnp.sum(begun * source_lengths, axis=-1)),
        )

    first, last = at(chunk * rows), at(chunk * rows + rows - 1)
    bounds = jnp.stack(
        [
            jnp.stack((low // KEY_BLOCK, (high + KEY_BLOCK - 1) // KEY_BLOCK))
            for (low, _), (_, high) in zip(first, last)
        ]
    ).astype(jnp.int32)
    spans = at(chunk[:, None] * rows + jnp.arange(rows, dtype=jnp.int32)[None, :])
    spans = jnp.stack([jnp.stack(s) for s in spans])
    return bounds, spans[:, :, :, None, :]


def body(
    count,
    inputs,
    encoded,
    d_output,
    target_lengths,
    source_lengths,
    norm_gain,
    norm_shift,
    self_qkv,
    self_bias,
    self_out,
    cross_q,
    cross_kv,
    cross_bias,
    cross_out,
    out_bias,
    ffn_in,
    ffn_in_bias,
    ffn_out,
):
    rows, width = inputs.shape
    devices = 4 * count
    share = width // devices
    head_width = width // 4
    hidden_width = ffn_in.shape[1]
    hidden_here = hidden_width // 4
    hidden_rows = hidden_width // width
    tokens_here = 4 * rows

    small = jnp.concatenate(
        (
            norm_gain,
            norm_shift,
            self_bias,
            cross_bias,
            out_bias,
            ffn_in_bias.reshape(hidden_rows, share),
        )
    )
    n_small = small.shape[0]
    small = jnp.pad(small, ((0, N_SMALL - n_small), (0, 128 - share)))
    (
        table, here, b_hidden, w_qkv, w_cross_kv, w_cross_q, w_self_out, w_cross_out, w_ffn_in,
        inputs_all, encoded_all, d_output_all, normed_one, q1, k1, v1, k2, v2,
    ) = front(
        small,
        [jnp.transpose(self_qkv, (1, 0, 2)), cross_kv.reshape(share, 2 * width), cross_q],
        self_out[None],
        cross_out[None],
        ffn_in,
        [inputs, encoded, d_output],
        count,
        0,
    )
    ffn_out, w_ffn_in = tie(ffn_out, w_ffn_in)
    w_ffn_out = lax.all_gather(ffn_out, "blk", axis=0, tiled=True)
    w_ffn_in = lax.all_gather(w_ffn_in, "blk", axis=1, tiled=True).reshape(width, -1)
    w_qkv, w_cross_kv, w_cross_q, w_self_out, w_cross_out = (
        w.reshape(-1, w.shape[-1]) for w in (w_qkv, w_cross_kv, w_cross_q, w_self_out, w_cross_out)
    )
    spans = key_spans(target_lengths, source_lengths, rows, count)

    k1, v1 = (a.reshape(-1, head_width) for a in (k1, v1))
    o1, mix1, lse1 = attend(q1, k1, v1, spans, 0)
    first, normed_two, q2, k2, v2 = join_forward(
        mix1, w_self_out, inputs, table, 0, count, 2, query=(w_cross_q, here), stream=(k2, v2)
    )
    k2, v2 = (a.reshape(-1, head_width) for a in (k2, v2))
    o2, mix2, lse2 = attend(q2, k2, v2, spans, 1)
    second, normed_three = join_forward(mix2, w_cross_out, first, table, 1, count, 3)

    out_part, d_part, ffn_mine, ffn_over, d_hidden = feed_forward(
        normed_three, d_output_all, w_ffn_in, w_ffn_out, b_hidden, count
    )
    swap = [(i, i ^ 1) for i in range(count)]
    ffn_over = lax.ppermute(ffn_over, "blk", swap)
    d_second, stats_three, d_o2, grad_cross_out, layer_output = join_backward(
        (d_part, out_part), d_output, second, table, 2, w_cross_out, mix2, count, 4
    )
    dq2, dk2, dv2, over2, sums_two = attend_back(q2, k2, v2, spans, 1, d_o2, o2, lse2)
    inside = rows == 4 * share
    if inside:
        over2 = lax.ppermute(over2, "blk", swap)
    dq2, ffn_over = tie(dq2, ffn_over)
    lines = [list(range(y, count, 2)) for y in range(2)]
    ffn_terms = lax.all_to_all(
        (ffn_mine.astype(f32) + ffn_over.astype(f32)).astype(bf16), "blk", 0, 0,
        axis_index_groups=lines, tiled=True,
    )
    d_first, stats_two, d_o1, grad_self_out, grad_cross_q = join_backward(
        (dq2, w_cross_q, normed_two), d_second, first, table, 1, w_self_out, mix1, count, 5
    )
    dq1, dk1, dv1, over1, sums_one = attend_back(q1, k1, v1, spans, 0, d_o1, o1, lse1)
    pairs = (dk1, dv1, dk2, dv2)
    lies = (4, count // 2, 4, share, head_width)
    if inside:
        pairs = [a.reshape(lies) for a in pairs]
        pairs += [a.reshape((2,) + lies) for a in (over1, over2)]
    else:
        y = lax.axis_index("blk") % 2
        pairs = [
            jnp.where(y == 0, jnp.stack((a, b), axis=1), jnp.stack((b, a), axis=1)).reshape(
                4, count, rows, head_width
            )
            for a, b in zip(pairs, (over1[0], over1[1], over2[0], over2[1]))
        ]
        pairs = scatter_blk(pairs, count, 6)
    got = finale(
        count, pairs, grad_cross_out, grad_self_out, grad_cross_q, ffn_terms, dq1, normed_one,
        encoded_all, w_qkv, w_cross_kv, inputs, d_first, table, stats_two, stats_three,
        sums_one, sums_two, d_hidden, 7,
    )
    done = settle(got, layer_output, share, width, hidden_width)
    order = (
        "layer", "d_inputs", "d_encoded", "gain", "shift", "qkv", "self_bias", "so", "cq", "ckv",
        "cross_bias", "co", "out_bias", "ffn_in", "ffn_bias", "ffn_out",
    )
    outs = [done["out_" + n] for n in order]
    outs[5] = jnp.transpose(outs[5], (1, 0, 2))
    outs[14] = outs[14].reshape(-1)
    return tuple(outs)


def solution(mesh):
    both = ("head", "blk")
    rows2, rows3, cols2 = P(both, None), P(both, None, None), P(None, both)
    return jax.shard_map(
        partial(body, mesh.shape["blk"]),
        mesh=mesh,
        in_specs=(
            rows2, rows2, rows2, P(), P(), cols2, cols2, rows3, cols2, rows2, rows2, rows3,
            cols2, rows2, cols2, rows2, P(both), rows2,
        ),
        out_specs=(
            rows2, rows2, rows2, cols2, cols2, rows3, cols2, rows2, rows2, rows3, cols2, rows2,
            cols2, rows2, P(both), rows2,
        ),
        check_vma=False,
    )
```
